32 devices in a mesh: ctx: 16 (over z, y, core), wsh: 2 (over x).
Axes of the slice: x: 2, y: 2, z: 4, core: 2. Of those that a mesh axis runs over, the one named last changes fastest.
Arguments:
- tokens: bfloat16 [2, 3, 1024, 1024], P('wsh', None, 'ctx'), may hold values from -6 to 6
- cotangent: bfloat16 [2, 3, 1024, 1024], P('wsh', None, 'ctx'), may hold values from -6 to 6
- lengths: int32 [2, 3, 2], P('wsh'), may hold values from 1 to 512, 768 in all within a row
- dealing: int32 [2, 3, 16], P('wsh'), may hold values from 0 to 15, each once within a row
- w_query: bfloat16 [1024, 1024], P('wsh'), may hold values from -0.1875 to 0.1875
- w_key: bfloat16 [1024, 1024], P('wsh'), may hold values from -0.1875 to 0.1875
- w_value: bfloat16 [1024, 1024], P('wsh'), may hold values from -0.1875 to 0.1875
- w_out: bfloat16 [1024, 1024], P('wsh'), may hold values from -1.5 to 1.5
- w_up: bfloat16 [1024, 4096], P('wsh'), may hold values from -0.1875 to 0.1875
- w_down: bfloat16 [4096, 1024], P('wsh'), may hold values from -0.09375 to 0.09375
- b_query: bfloat16 [1024], P('wsh'), may hold values from -2 to 2
- b_value: bfloat16 [1024], P('wsh'), may hold values from -2 to 2
- b_out: bfloat16 [1024], P('wsh'), may hold values from -2 to 2
- b_up: bfloat16 [4096], P('wsh'), may hold values from -2 to 2
- b_down: bfloat16 [1024], P('wsh'), may hold values from -2 to 2
- gain_one: bfloat16 [1024], P('wsh'), may hold values from 0.5 to 1.5
- shift_one: bfloat16 [1024], P('wsh'), may hold values from -2 to 2
- gain_two: bfloat16 [1024], P('wsh'), may hold values from 0.5 to 1.5
- shift_two: bfloat16 [1024], P('wsh'), may hold values from -2 to 2
Outputs:
- output: bfloat16 [2, 3, 1024, 1024], P('wsh', None, 'ctx')
- grad_tokens: bfloat16 [2, 3, 1024, 1024], P('wsh', None, 'ctx')
- grad_w_query: float32 [1024, 1024], P('wsh')
- grad_w_key: float32 [1024, 1024], P('wsh')
- grad_w_value: float32 [1024, 1024], P('wsh')
- grad_w_out: float32 [1024, 1024], P('wsh')
- grad_w_up: float32 [1024, 4096], P('wsh')
- grad_w_down: float32 [4096, 1024], P('wsh')
- grad_b_query: float32 [1024], P('wsh')
- grad_b_value: float32 [1024], P('wsh')
- grad_b_out: float32 [1024], P('wsh')
- grad_b_up: float32 [4096], P('wsh')
- grad_b_down: float32 [1024], P('wsh')
- grad_gain_one: float32 [1024], P('wsh')
- grad_shift_one: float32 [1024], P('wsh')
- grad_gain_two: float32 [1024], P('wsh')
- grad_shift_two: float32 [1024], P('wsh')
The draws below stay inside these ranges and needn't reach their ends.
Inputs may be any that keep to these rules, and one draw needn't show every extreme that they name: The 2 lengths of one group add up to 768. `dealing`: for each wsh index and micro-batch, a permutation of the 16 block numbers.
All inputs are finite; a program needn't handle non-finite values.
Results may differ from the reference program's by a relative error of at most 0.023.
Values may be sent and summed in bfloat16 or wider, within the bound.
A program may use at most 192 MiB of HBM per device.

```python
import math
import jax
import jax.numpy as jnp
import numpy as np
from jax import lax

D = 1024
HEADS = 16
FF = 4096
MAXLEN = 512
MB = 3
HD = 64
BLK = 64
NB = 16
NSEQ = 2
ROWS = 1024
N_WSH = 2


def block_levels(stream_key, shape, split, smallest, largest):
    loudness = 1.0
    for dim, shards_of in split:
        draws = jax.random.uniform(jax.random.fold_in(jax.random.fold_in(stream_key, 6), dim), (shards_of,), jnp.float32, smallest / len(split), largest / len(split))
        loudness = loudness * jnp.repeat(jnp.exp(draws), shape[dim] // shards_of).reshape((-1,) + (1,) * (len(shape) - 1 - dim))
    return loudness


def split_up(amount, total, limit, lean):
    loads = [(1 << 20) // math.isqrt(rank ** lean) + 1 for rank in range(2, amount + 1)]
    spare, holding = total - limit - (amount - 1), [1] * (amount - 1)
    while spare > 0:
        movable = [i for i in range(amount - 1) if holding[i] < limit]
        pool, budget = sum([loads[i] for i in movable]), spare
        for i in movable:
            more = min(limit - holding[i], max(1, budget * loads[i] // pool), spare)
            holding[i] = holding[i] + more
            spare = spare - more
    return np.array([limit] + holding)


def uneven_parts(stream_key, count, total, reach, skew):
    if count == 2:
        one = jax.random.randint(stream_key, (), max(1, total - reach), min(reach, total - 1) + 1)
        return jnp.stack([one, total - one])
    sizes = jnp.asarray(split_up(count, total, reach, skew), jnp.int32)
    couples = (count - 1) // 2
    giver, receiver = sizes[1:1 + 2 * couples:2], sizes[2:2 + 2 * couples:2]
    room = jnp.minimum(giver - 1, reach - receiver)
    moved = jax.random.randint(jax.random.fold_in(stream_key, 1), (couples,), 0, 1 << 20) % (room + 1)
    sizes = sizes.at[1:1 + 2 * couples:2].set(giver - moved).at[2:2 + 2 * couples:2].set(receiver + moved)
    return sizes[jax.random.permutation(jax.random.fold_in(stream_key, 2), count)]


def normal_values(stream_key, shape, scale, limit, pieces=(), kind=jnp.bfloat16):
    values = jax.random.normal(stream_key, shape, jnp.float32) * scale
    if len(pieces) > 0:
        values = block_levels(stream_key, shape, pieces, -0.22, 0.18) * values
    return jnp.clip(values, min=-limit, max=limit).astype(kind)


def setup_inputs(seed: int = 0) -> dict:
    key_of = jax.random.split(jax.random.key(seed), 20)
    return {
        "tokens": normal_values(key_of[0], (N_WSH, MB, ROWS, D), 1.0, 6.0, ((0, 2), (2, 16))),
        "cotangent": normal_values(key_of[1], (N_WSH, MB, ROWS, D), 1.0, 6.0, ((0, 2), (2, 16))),
        "lengths": jax.vmap(lambda own: uneven_parts(own, NSEQ, NSEQ * MAXLEN * 3 // 4, MAXLEN, 2))(jax.random.split(key_of[2], N_WSH * MB)).reshape((N_WSH, MB, NSEQ)).astype(jnp.int32),
        "dealing": jax.vmap(lambda own: jax.random.permutation(own, NB))(jax.random.split(key_of[3], N_WSH * MB)).reshape((N_WSH, MB, NB)).astype(jnp.int32),
        "w_query": normal_values(key_of[4], (D, D), D ** -0.5, 0.1875, ((0, 2),)),
        "w_key": normal_values(key_of[5], (D, D), D ** -0.5, 0.1875, ((0, 2),)),
        "w_value": normal_values(key_of[6], (D, D), D ** -0.5, 0.1875, ((0, 2),)),
        "w_out": normal_values(key_of[7], (D, D), (D // 64) ** -0.5, 1.5, ((0, 2),)),
        "w_up": normal_values(key_of[8], (D, FF), D ** -0.5, 0.1875, ((0, 2),)),
        "w_down": normal_values(key_of[9], (FF, D), FF ** -0.5, 0.09375, ((0, 2),)),
        "b_query": normal_values(key_of[10], (D,), 0.3, 2.0, ((0, 2),)),
        "b_value": normal_values(key_of[11], (D,), 0.3, 2.0, ((0, 2),)),
        "b_out": normal_values(key_of[12], (D,), 0.3, 2.0, ((0, 2),)),
        "b_up": normal_values(key_of[13], (FF,), 0.3, 2.0, ((0, 2),)),
        "b_down": normal_values(key_of[14], (D,), 0.3, 2.0, ((0, 2),)),
        "gain_one": jnp.clip(1.0 + 0.1 * jax.random.normal(key_of[15], (D,), jnp.float32), 0.5, 1.5).astype(jnp.bfloat16),
        "shift_one": normal_values(key_of[16], (D,), 0.3, 2.0, ((0, 2),)),
        "gain_two": jnp.clip(1.0 + 0.1 * jax.random.normal(key_of[17], (D,), jnp.float32), 0.5, 1.5).astype(jnp.bfloat16),
        "shift_two": normal_values(key_of[18], (D,), 0.3, 2.0, ((0, 2),)),
    }


@jax.custom_vjp
def low(v):
    return lax.optimization_barrier(v.astype(jnp.bfloat16)).astype(jnp.float32)

@jax.custom_vjp
def low_back(v):
    return v

def low_keep(v):
    return (low(v), None)

def low_pass(kept, grad):
    return (grad,)

def back_keep(v):
    return (v, None)

def back_low(kept, grad):
    return (low(grad),)
low.defvjp(low_keep, low_pass)
low_back.defvjp(back_keep, back_low)
EPSILON = 1e-12
NEG_FILL = -1e+30
HIGH = lax.Precision.HIGHEST

def layer_norm(summed, gain_vec, shift_vec):
    row_mean = lax.optimization_barrier(jnp.mean(summed, axis=-1, keepdims=True))
    centred = summed - row_mean
    row_var = lax.optimization_barrier(jnp.mean(centred * centred, axis=-1, keepdims=True))
    return centred * lax.rsqrt(row_var + EPSILON) * gain_vec + shift_vec

def softmax_rows(scores):
    shifted = scores - lax.optimization_barrier(jnp.max(scores, axis=-1, keepdims=True))
    raised = jnp.exp(shifted)
    return raised / lax.optimization_barrier(jnp.sum(raised, axis=-1, keepdims=True))

def layer_forward(param_set, token_set, key_valid):
    query_weight, key_weight, value_weight, out_weight, up_weight, down_weight, bias_query, bias_value, bias_out, bias_up, bias_down, gain_first, shift_first, gain_second, shift_second = param_set
    seq_count = token_set.shape[0]
    rows_flat = token_set.reshape(-1, D)
    queries = low(low_back(jnp.dot(rows_flat, query_weight, precision=HIGH) + bias_query))
    keys_all = low(low_back(jnp.dot(rows_flat, key_weight, precision=HIGH)))
    values_all = low(low_back(jnp.dot(rows_flat, value_weight, precision=HIGH) + bias_value))
    query_heads = queries.reshape(seq_count, MAXLEN, HEADS, HD)
    key_heads = keys_all.reshape(seq_count, MAXLEN, HEADS, HD)
    value_heads = values_all.reshape(seq_count, MAXLEN, HEADS, HD)
    scores = low_back(jnp.einsum('sqhd,skhd->shqk', query_heads, key_heads, precision=HIGH) * (1.0 / math.sqrt(HD)))
    scores = jnp.where(key_valid[:, None, None, :], scores, NEG_FILL)
    probs = softmax_rows(scores)
    attended = jnp.einsum('shqk,skhd->sqhd', low(probs), value_heads, precision=HIGH).reshape(-1, D)
    attended = low(low_back(attended))
    out_proj = low_back(jnp.dot(attended, out_weight, precision=HIGH) + bias_out)
    norm_one = layer_norm(rows_flat + out_proj, gain_first, shift_first)
    up_pre = low_back(jnp.dot(low(norm_one), up_weight, precision=HIGH) + bias_up)
    activated = low(jax.nn.gelu(up_pre, approximate=False))
    down_out = low_back(jnp.dot(activated, down_weight, precision=HIGH) + bias_down)
    result = layer_norm(norm_one + down_out, gain_second, shift_second)
    return result.reshape(seq_count, MAXLEN, D)

def reference(tokens, cotangent, lengths, dealing, w_query, w_key, w_value, w_out, w_up, w_down, b_query, b_value, b_out, b_up, b_down, gain_one, shift_one, gain_two, shift_two):
    params = tuple((item.astype(jnp.float32) for item in (w_query, w_key, w_value, w_out, w_up, w_down, b_query, b_value, b_out, b_up, b_down, gain_one, shift_one, gain_two, shift_two)))
    groups = N_WSH * MB
    slot_tokens = tokens.astype(jnp.float32).reshape(groups, NB, BLK, D)
    slot_cot = cotangent.astype(jnp.float32).reshape(groups, NB, BLK, D)
    dealt = dealing.reshape(groups, NB).astype(jnp.int32)
    inverse = jax.vmap(lambda order_row: jnp.zeros((NB,), jnp.int32).at[order_row].set(jnp.arange(NB, dtype=jnp.int32)))(dealt)
    nat_tokens = jnp.take_along_axis(slot_tokens, inverse[:, :, None, None], axis=1).reshape(groups, NSEQ, MAXLEN, D)
    nat_cot = jnp.take_along_axis(slot_cot, inverse[:, :, None, None], axis=1).reshape(groups, NSEQ, MAXLEN, D)
    seq_lengths = lengths.reshape(groups, NSEQ).astype(jnp.int32)

    def group_step(totals, inputs_now):
        group_tokens, group_cot, group_lengths = inputs_now
        key_valid = jnp.arange(MAXLEN, dtype=jnp.int32)[None, :] < group_lengths[:, None]
        result, back_fn = jax.vjp(lambda param_set, token_set: layer_forward(param_set, token_set, key_valid), params, group_tokens)
        grad_params, grad_input = back_fn(group_cot)
        totals = tuple((total_now + fresh for total_now, fresh in zip(totals, grad_params)))
        return (totals, (result, grad_input))
    zero_grads = tuple((jnp.zeros_like(item) for item in params))
    totals, (nat_out, nat_grad) = lax.scan(group_step, zero_grads, (nat_tokens, nat_cot, seq_lengths))
    slot_out = jnp.take_along_axis(nat_out.reshape(groups, NB, BLK, D), dealt[:, :, None, None], axis=1)
    slot_grad = jnp.take_along_axis(nat_grad.reshape(groups, NB, BLK, D), dealt[:, :, None, None], axis=1)
    output = slot_out.reshape(N_WSH, MB, ROWS, D).astype(jnp.bfloat16)
    grad_tokens = slot_grad.reshape(N_WSH, MB, ROWS, D).astype(jnp.bfloat16)
    return (output, grad_tokens, totals[0], totals[1], totals[2], totals[3], totals[4], totals[5], totals[6], totals[7], totals[8], totals[9], totals[10], totals[11], totals[12], totals[13], totals[14])
```

```python
import functools
import math

import jax
import jax.numpy as jnp
from jax import lax
from jax.experimental import pallas as pl
from jax.experimental.pallas import tpu as pltpu
from jax.sharding import PartitionSpec as P

HEADS = 16
BPS = 8
MB = 3
BLK = 64


EPSILON = 1e-12
NEG_FILL = -1e30


def as_sent(x):
    return jax.tree.map(lambda a: a.astype(jnp.bfloat16) if a.dtype == jnp.float32 else a, x)


def layer_norm(summed, gain_vec, shift_vec):
    row_mean = jnp.mean(summed, axis=-1, keepdims=True)
    centred = summed - row_mean
    row_var = jnp.mean(centred * centred, axis=-1, keepdims=True)
    return centred * lax.rsqrt(row_var + EPSILON) * gain_vec + shift_vec


def gelu_exact(values):
    return jax.nn.gelu(values, approximate=False)


def row_labels(dealt_order, seq_lengths):
    blocks_of_rows = jnp.repeat(dealt_order, BLK)
    within = jnp.tile(jnp.arange(BLK, dtype=jnp.int32), dealt_order.shape[0])
    seq_ids = blocks_of_rows // BPS
    places = blocks_of_rows % BPS * BLK + within
    numbers = jnp.arange(seq_lengths.shape[0], dtype=jnp.int32)
    seq_bound = jnp.sum(
        jnp.where(seq_ids[:, None] == numbers[None, :], seq_lengths[None, :], 0), axis=1
    )
    return (seq_ids, places < seq_bound)


def blockwise(carried, total_rows, step_rows, visit_block):
    return lax.fori_loop(
        0,
        total_rows // step_rows,
        lambda turn_index, running: visit_block(running, turn_index * step_rows),
        carried,
    )


def masked_scores(query_blk, key_blk, query_seq, key_seq, key_valid, scale_factor):
    allowed = (query_seq[:, None] == key_seq[None, :]) & key_valid[None, :]
    scores = (
        jnp.einsum("qhd,khd->hqk", query_blk, key_blk, preferred_element_type=jnp.float32)
        * scale_factor
    )
    return (jnp.where(allowed[None], scores, NEG_FILL), allowed[None].astype(jnp.float32))


def attention_grads(
    query_blk,
    grad_blk,
    key_blk,
    value_blk,
    query_seq,
    key_seq,
    key_valid,
    row_total,
    row_delta,
    scale_factor,
):
    scores, allowed = masked_scores(query_blk, key_blk, query_seq, key_seq, key_valid, scale_factor)
    probs = jnp.exp(scores - row_total[:, :, None]) * allowed
    grad_probs = jnp.einsum("qhd,khd->hqk", grad_blk, value_blk, preferred_element_type=jnp.float32)
    grad_scores = (probs * (grad_probs - row_delta[:, :, None])).astype(jnp.bfloat16)
    return (probs.astype(jnp.bfloat16), grad_scores)


def gather_params(params):
    return (
        lax.all_gather(params[0], "wsh", axis=0, tiled=True),
        lax.all_gather(params[1], "wsh", axis=0, tiled=True),
        lax.all_gather(params[2], "wsh", axis=0, tiled=True),
        lax.all_gather(params[3], "wsh", axis=0, tiled=True),
        lax.all_gather(params[4], "wsh", axis=0, tiled=True),
        lax.all_gather(params[5], "wsh", axis=0, tiled=True),
        lax.all_gather(params[6], "wsh", axis=0, tiled=True),
        lax.all_gather(params[7], "wsh", axis=0, tiled=True),
        lax.all_gather(params[8], "wsh", axis=0, tiled=True),
        lax.all_gather(params[9], "wsh", axis=0, tiled=True),
        lax.all_gather(params[10], "wsh", axis=0, tiled=True),
        lax.all_gather(params[11], "wsh", axis=0, tiled=True),
        lax.all_gather(params[12], "wsh", axis=0, tiled=True),
        lax.all_gather(params[13], "wsh", axis=0, tiled=True),
        lax.all_gather(params[14], "wsh", axis=0, tiled=True),
    )


def per_device(
    tokens,
    cotangent,
    lengths,
    dealing,
    w_query,
    w_key,
    w_value,
    w_out,
    w_up,
    w_down,
    b_query,
    b_value,
    b_out,
    b_up,
    b_down,
    gain_one,
    shift_one,
    gain_two,
    shift_two,
):
    params = (
        w_query,
        w_key,
        w_value,
        w_out,
        w_up,
        w_down,
        b_query,
        b_value,
        b_out,
        b_up,
        b_down,
        gain_one,
        shift_one,
        gain_two,
        shift_two,
    )
    own_rows = tokens.shape[2]
    width = tokens.shape[3]
    head_size = width // HEADS
    scale_factor = 1.0 / math.sqrt(head_size)
    my_start = lax.axis_index("ctx") * own_rows
    wsh_count = lax.axis_size("wsh")
    grads = tuple(
        (jnp.zeros((item.shape[0] * wsh_count,) + item.shape[1:], jnp.float32) for item in params)
    )
    results = []
    input_grads = []
    for micro in range(MB):
        whole = gather_params(params)
        query_weight, key_weight, value_weight, out_weight, up_weight, down_weight = whole[:6]
        (
            bias_query,
            bias_value,
            bias_out,
            bias_up,
            bias_down,
            gain_first,
            shift_first,
            gain_second,
            shift_second,
        ) = tuple((item.astype(jnp.float32) for item in whole[6:]))
        token_rows = tokens[0, micro]
        seq_all, valid_all = row_labels(dealing[0, micro], lengths[0, micro])
        my_seq = lax.dynamic_slice_in_dim(seq_all, my_start, own_rows)
        my_valid = lax.dynamic_slice_in_dim(valid_all, my_start, own_rows)
        query_low = (
            jnp.dot(token_rows, query_weight, preferred_element_type=jnp.float32) + bias_query
        ).astype(jnp.bfloat16)
        key_low = jnp.dot(token_rows, key_weight, preferred_element_type=jnp.float32).astype(
            jnp.bfloat16
        )
        value_low = (
            jnp.dot(token_rows, value_weight, preferred_element_type=jnp.float32) + bias_value
        ).astype(jnp.bfloat16)
        query_heads = query_low.reshape(own_rows, HEADS, head_size)
        my_key_heads = key_low.reshape(own_rows, HEADS, head_size)
        my_value_heads = value_low.reshape(own_rows, HEADS, head_size)
        start_state = (
            jnp.full((HEADS, own_rows), NEG_FILL, jnp.float32),
            jnp.zeros((HEADS, own_rows), jnp.float32),
            jnp.zeros((own_rows, HEADS, head_size), jnp.float32),
        )
        key_piece = lax.all_gather(key_low, "ctx", axis=0, tiled=True)
        value_piece = lax.all_gather(value_low, "ctx", axis=0, tiled=True)
        piece_rows = key_piece.shape[0]
        step_rows = math.gcd(piece_rows, 512)

        def visit_block(running, offset):
            run_max, run_sum, run_acc = running
            key_blk = lax.dynamic_slice_in_dim(key_piece, offset, step_rows).reshape(
                step_rows, HEADS, head_size
            )
            value_blk = lax.dynamic_slice_in_dim(value_piece, offset, step_rows).reshape(
                step_rows, HEADS, head_size
            )
            key_seq = lax.dynamic_slice_in_dim(seq_all, offset, step_rows)
            key_valid = lax.dynamic_slice_in_dim(valid_all, offset, step_rows)
            scores, allowed = masked_scores(
                query_heads, key_blk, my_seq, key_seq, key_valid, scale_factor
            )
            new_max = jnp.maximum(run_max, jnp.max(scores, axis=-1))
            rescale = jnp.exp(run_max - new_max)
            weights = jnp.exp(scores - new_max[:, :, None]) * allowed
            run_sum = run_sum * rescale + jnp.sum(weights, axis=-1)
            run_acc = run_acc * rescale.T[:, :, None] + jnp.einsum(
                "hqk,khd->qhd",
                weights.astype(jnp.bfloat16),
                value_blk,
                preferred_element_type=jnp.float32,
            )
            return (new_max, run_sum, run_acc)

        final_max, final_sum, final_acc = blockwise(start_state, piece_rows, step_rows, visit_block)
        attended = final_acc / final_sum.T[:, :, None]
        log_total = final_max + jnp.log(final_sum)
        attended_low = attended.reshape(own_rows, width).astype(jnp.bfloat16)
        out_proj = jnp.dot(attended_low, out_weight, preferred_element_type=jnp.float32) + bias_out
        first_sum = token_rows.astype(jnp.float32) + out_proj
        norm_one, norm_one_back = jax.vjp(layer_norm, first_sum, gain_first, shift_first)
        mlp_input = norm_one.astype(jnp.bfloat16)
        up_pre = jnp.dot(mlp_input, up_weight, preferred_element_type=jnp.float32) + bias_up
        activated, gelu_back = jax.vjp(gelu_exact, up_pre)
        activated_low = activated.astype(jnp.bfloat16)
        down_out = (
            jnp.dot(activated_low, down_weight, preferred_element_type=jnp.float32) + bias_down
        )
        result, norm_two_back = jax.vjp(layer_norm, norm_one + down_out, gain_second, shift_second)
        results.append(result.astype(jnp.bfloat16))
        grad_second, grad_gain_b, grad_shift_b = norm_two_back(
            cotangent[0, micro].astype(jnp.float32)
        )
        grad_down_low = grad_second.astype(jnp.bfloat16)
        grad_activated = jnp.einsum(
            "rd,fd->rf", grad_down_low, down_weight, preferred_element_type=jnp.float32
        )
        (grad_up_pre,) = gelu_back(grad_activated)
        grad_up_low = grad_up_pre.astype(jnp.bfloat16)
        grad_norm_one = (
            jnp.einsum("rf,df->rd", grad_up_low, up_weight, preferred_element_type=jnp.float32)
            + grad_second
        )
        grad_first, grad_gain_a, grad_shift_a = norm_one_back(grad_norm_one)
        grad_out_low = grad_first.astype(jnp.bfloat16)
        grad_att_low = jnp.einsum(
            "rd,ed->re", grad_out_low, out_weight, preferred_element_type=jnp.float32
        ).astype(jnp.bfloat16)
        grad_heads = grad_att_low.reshape(own_rows, HEADS, head_size)
        row_delta = jnp.sum(grad_heads.astype(jnp.float32) * attended, axis=-1).T
        empty_heads = jnp.zeros((own_rows, HEADS, head_size), jnp.float32)
        query_key_piece = lax.all_gather(key_low, "ctx", axis=0, tiled=True)
        query_value_piece = lax.all_gather(value_low, "ctx", axis=0, tiled=True)
        query_piece_rows = query_key_piece.shape[0]
        query_step_rows = math.gcd(query_piece_rows, 512)

        def query_visit_block(running, offset):
            key_blk = lax.dynamic_slice_in_dim(query_key_piece, offset, query_step_rows).reshape(
                query_step_rows, HEADS, head_size
            )
            value_blk = lax.dynamic_slice_in_dim(
                query_value_piece, offset, query_step_rows
            ).reshape(query_step_rows, HEADS, head_size)
            key_seq = lax.dynamic_slice_in_dim(seq_all, offset, query_step_rows)
            key_valid = lax.dynamic_slice_in_dim(valid_all, offset, query_step_rows)
            probs_low, grad_scores = attention_grads(
                query_heads,
                grad_heads,
                key_blk,
                value_blk,
                my_seq,
                key_seq,
                key_valid,
                log_total,
                row_delta,
                scale_factor,
            )
            return running + jnp.einsum(
                "hqk,khd->qhd", grad_scores, key_blk, preferred_element_type=jnp.float32
            )

        grad_query_sum = blockwise(
            empty_heads, query_piece_rows, query_step_rows, query_visit_block
        )
        total_all, delta_all = (
            lax.all_gather(log_total.T, "ctx", axis=0, tiled=True),
            lax.all_gather(row_delta.T, "ctx", axis=0, tiled=True),
        )
        query_piece = lax.all_gather(query_low, "ctx", axis=0, tiled=True)
        grad_piece = lax.all_gather(grad_att_low, "ctx", axis=0, tiled=True)
        key_piece_rows = query_piece.shape[0]
        key_step_rows = math.gcd(key_piece_rows, 512)

        def key_visit_block(running, offset):
            grad_key_run, grad_value_run = running
            query_blk = lax.dynamic_slice_in_dim(query_piece, offset, key_step_rows).reshape(
                key_step_rows, HEADS, head_size
            )
            grad_blk = lax.dynamic_slice_in_dim(grad_piece, offset, key_step_rows).reshape(
                key_step_rows, HEADS, head_size
            )
            total_blk = lax.dynamic_slice_in_dim(total_all, offset, key_step_rows)
            delta_blk = lax.dynamic_slice_in_dim(delta_all, offset, key_step_rows)
            query_seq = lax.dynamic_slice_in_dim(seq_all, offset, key_step_rows)
            probs_low, grad_scores = attention_grads(
                query_blk,
                grad_blk,
                my_key_heads,
                my_value_heads,
                query_seq,
                my_seq,
                my_valid,
                total_blk.T,
                delta_blk.T,
                scale_factor,
            )
            grad_key_run = grad_key_run + jnp.einsum(
                "hqk,qhd->khd", grad_scores, query_blk, preferred_element_type=jnp.float32
            )
            grad_value_run = grad_value_run + jnp.einsum(
                "hqk,qhd->khd", probs_low, grad_blk, preferred_element_type=jnp.float32
            )
            return (grad_key_run, grad_value_run)

        grad_key_sum, grad_value_sum = blockwise(
            (empty_heads, empty_heads), key_piece_rows, key_step_rows, key_visit_block
        )
        grad_key_flat = grad_key_sum.reshape(own_rows, width)
        grad_value_flat = grad_value_sum.reshape(own_rows, width)
        grad_query_low = (
            (grad_query_sum * scale_factor).reshape(own_rows, width).astype(jnp.bfloat16)
        )
        grad_key_low = (grad_key_flat * scale_factor).astype(jnp.bfloat16)
        grad_value_low = grad_value_flat.astype(jnp.bfloat16)
        terms = (
            jnp.einsum("rd,re->de", token_rows, grad_query_low, preferred_element_type=jnp.float32),
            jnp.einsum("rd,re->de", token_rows, grad_key_low, preferred_element_type=jnp.float32),
            jnp.einsum("rd,re->de", token_rows, grad_value_low, preferred_element_type=jnp.float32),
            jnp.einsum("rd,re->de", attended_low, grad_out_low, preferred_element_type=jnp.float32),
            jnp.einsum("rd,rf->df", mlp_input, grad_up_low, preferred_element_type=jnp.float32),
            jnp.einsum(
                "rf,rd->fd", activated_low, grad_down_low, preferred_element_type=jnp.float32
            ),
            jnp.sum(grad_query_low.astype(jnp.float32), axis=0),
            jnp.sum(grad_value_low.astype(jnp.float32), axis=0),
            jnp.sum(grad_out_low.astype(jnp.float32), axis=0),
            jnp.sum(grad_up_low.astype(jnp.float32), axis=0),
            jnp.sum(grad_down_low.astype(jnp.float32), axis=0),
            grad_gain_a,
            grad_shift_a,
            grad_gain_b,
            grad_shift_b,
        )
        grads = tuple((total_now + fresh for total_now, fresh in zip(grads, terms)))
        grad_rows = (
            grad_first
            + jnp.einsum(
                "re,de->rd", grad_query_low, query_weight, preferred_element_type=jnp.float32
            )
            + jnp.einsum("re,de->rd", grad_key_low, key_weight, preferred_element_type=jnp.float32)
            + jnp.einsum(
                "re,de->rd", grad_value_low, value_weight, preferred_element_type=jnp.float32
            )
        )
        input_grads.append(grad_rows.astype(jnp.bfloat16))
    shards = jax.tree.map(
        lambda part: part.astype(jnp.float32),
        lax.psum_scatter(as_sent(grads), "wsh", scatter_dimension=0, tiled=True),
    )
    summed = jax.tree.map(lambda part: part.astype(jnp.float32), lax.psum(as_sent(shards), "ctx"))
    return (jnp.stack(results)[None], jnp.stack(input_grads)[None]) + tuple(summed)


MESH_IDS = pl.DeviceIdType.MESH
F32 = jnp.float32
BF16 = jnp.bfloat16
HD = 64
VMEM_BYTES = 60 * 1024 * 1024


def flip(index, bit):
    return index + bit * (1 - 2 * lax.rem(lax.div(index, bit), 2))


def bit_of(index, bit):
    return lax.rem(lax.div(index, bit), 2)


def greet(peers):
    barrier = pltpu.get_barrier_semaphore()
    for peer in peers:
        pl.semaphore_signal(barrier, inc=1, device_id=peer, device_id_type=MESH_IDS)
    pl.semaphore_wait(barrier, len(peers))


def send(src, dst, send_sem, recv_sem, peer):
    copy = pltpu.make_async_remote_copy(
        src_ref=src,
        dst_ref=dst,
        send_sem=send_sem,
        recv_sem=recv_sem,
        device_id=peer,
        device_id_type=MESH_IDS,
    )
    copy.start()
    return copy


def gather_kernel(plan, n_weights, *refs):
    shards, small = refs[:n_weights], refs[n_weights]
    wholes, small_whole = refs[n_weights + 1 : 2 * n_weights + 1], refs[2 * n_weights + 1]
    send_sem, recv_sem, small_sems, local_sem = refs[2 * n_weights + 2 :]
    c, w = lax.axis_index("ctx"), lax.axis_index("wsh")
    o = 1 - w
    by_x, by_y, by_z, by_core = (c, o), (flip(c, 2), w), (flip(c, 4), w), (flip(c, 1), w)
    core, y, z = bit_of(c, 1), bit_of(c, 2), bit_of(c, 4)
    mine = core * 4 + z * 2 + y
    from_y, from_z = core * 4 + z * 2 + (1 - y), core * 4 + (1 - z) * 2 + y
    locals_ = []
    for index, (shard, whole) in enumerate(zip(shards, wholes)):
        rows = shard.shape[0]
        copy = pltpu.make_async_copy(
            shard, whole.at[pl.ds(pl.multiple_of(w * rows, rows), rows)], local_sem.at[index]
        )
        copy.start()
        locals_.append(copy)
    copy = pltpu.make_async_copy(small, small_whole.at[w], local_sem.at[n_weights])
    copy.start()
    locals_.append(copy)
    greet((by_x, by_y, by_z, by_core))
    sent = [send(small, small_whole.at[w], small_sems.at[0], small_sems.at[1], by_x)]

    def part(chunk, side, piece, start, count):
        tensor, first, rows = plan[chunk]
        size = rows // 8
        half = shards[tensor].shape[0]
        at = side * half + first + piece * size + start
        return wholes[tensor].at[pl.ds(pl.multiple_of(at, 8), count)]

    steps = {}
    for chunk, (tensor, first, rows) in enumerate(plan):
        size = rows // 8
        src = shards[tensor].at[pl.ds(pl.multiple_of(first + mine * size, 8), size)]
        steps[chunk, 0] = send(
            src, part(chunk, w, mine, 0, size), send_sem.at[0, chunk], recv_sem.at[0, chunk], by_x
        )

    def second(chunk):
        size = plan[chunk][2] // 8
        steps[chunk, 0].wait_recv()
        for kind, peer in ((1, by_y), (2, by_z)):
            ref = part(chunk, o, mine, 0, size)
            steps[chunk, kind] = send(
                ref, ref, send_sem.at[kind, chunk], recv_sem.at[kind, chunk], peer
            )

    def third(chunk):
        size = plan[chunk][2] // 8
        steps[chunk, 1].wait_recv()
        steps[chunk, 2].wait_recv()
        ref = part(chunk, o, from_z, 0, size // 2)
        steps[chunk, 3] = send(ref, ref, send_sem.at[3, chunk], recv_sem.at[3, chunk], by_y)
        ref = part(chunk, o, from_y, size // 2, size // 2)
        steps[chunk, 4] = send(ref, ref, send_sem.at[4, chunk], recv_sem.at[4, chunk], by_z)

    def fourth(chunk):
        size = plan[chunk][2] // 8
        steps[chunk, 3].wait_recv()
        steps[chunk, 4].wait_recv()
        ref = part(chunk, o, core * 4, 0, 4 * size)
        steps[chunk, 5] = send(ref, ref, send_sem.at[5, chunk], recv_sem.at[5, chunk], by_core)

    count = len(plan)
    for turn in range(count + 2):
        if turn < count:
            second(turn)
        if 0 <= turn - 1 < count:
            third(turn - 1)
        if 0 <= turn - 2 < count:
            fourth(turn - 2)
    for chunk in range(count):
        steps[chunk, 5].wait_recv()
        for kind in range(6):
            steps[chunk, kind].wait_send()
    sent[0].wait()
    for copy in locals_:
        copy.wait()


def gather_weights(shards, small):
    plan = []
    for index, shard in enumerate(shards):
        rows = shard.shape[0]
        parts = max(1, shard.shape[0] * shard.shape[1] // (1024 * 1024))
        for piece in range(parts):
            plan.append((index, piece * (rows // parts), rows // parts))
    count = len(shards)
    shapes = [jax.ShapeDtypeStruct((2 * s.shape[0],) + s.shape[1:], s.dtype) for s in shards]
    shapes.append(jax.ShapeDtypeStruct((2,) + small.shape, small.dtype))
    anywhere = pl.BlockSpec(memory_space=pl.ANY)
    return pl.pallas_call(
        functools.partial(gather_kernel, plan, count),
        out_shape=shapes,
        in_specs=[anywhere] * (count + 1),
        out_specs=[anywhere] * (count + 1),
        scratch_shapes=[
            pltpu.SemaphoreType.DMA((6, len(plan))),
            pltpu.SemaphoreType.DMA((6, len(plan))),
            pltpu.SemaphoreType.DMA((2,)),
            pltpu.SemaphoreType.DMA((count + 1,)),
        ],
        compiler_params=pltpu.CompilerParams(collective_id=0, has_side_effects=True),
        name="gather_weights",
    )(*shards, small)


def plane_peers(c, w, count):
    return [(lax.rem(c + step, count), w) for step in range(1, count)]


def pack_three(first, second, third, row, pair, out):
    cols = pl.ds(pair * 128, 128)
    a, b, d = (ref[pl.ds(row, BLK), cols] for ref in (first, second, third))
    half = BLK // 2
    for head in range(2):
        lane = slice(head * HD, head * HD + HD)
        out[2 * pair + head, 0:BLK, :] = jnp.concatenate([a[:, lane], b[:, lane]], axis=1)
        out[2 * pair + head, BLK : BLK + half, :] = jnp.concatenate(
            [d[:half, lane], d[half:, lane]], axis=1
        )


def unpack_fold(block):
    return jnp.concatenate([block[:, :HD], block[:, HD:]], axis=0)


def fold(rows):
    half = rows.shape[0] // 2
    return jnp.concatenate([rows[:half], rows[half:]], axis=1)


def all_bytes(ref, sem, peers):
    view = ref.at[pl.ds(0, peers)]
    return pltpu.make_async_copy(view, view, sem)


def attend_kernel(
    heads,
    lens_ref,
    slot_ref,
    block_ref,
    q_ref,
    k_ref,
    v_ref,
    a_ref,
    kept_ref,
    lse_ref,
    *scratch,
):
    in_buf = scratch[:MB]
    out_buf, back_out, back_in, q_s, k_s, v_s, a_s = scratch[MB : MB + 7]
    send_sem, recv_sem, back_send, back_recv, keep_sem = scratch[MB + 7 :]
    c, w = lax.axis_index("ctx"), lax.axis_index("wsh")
    peers = plane_peers(c, w, heads)
    greet(peers)
    blocks = heads
    for m in range(MB):
        for pair in range(heads // 2):
            pack_three(q_ref, k_ref, v_ref, m * BLK, pair, out_buf.at[m])
        for peer in peers:
            send(
                out_buf.at[m, peer[0]], in_buf[m].at[c], send_sem.at[m], recv_sem.at[m], peer
            )
        in_buf[m][c] = out_buf[m, c]
    for m in range(MB):
        all_bytes(in_buf[m], recv_sem.at[m], heads - 1).wait()
        keep = pltpu.make_async_copy(in_buf[m], kept_ref.at[m], keep_sem.at[m])
        keep.start()
        for b in range(blocks):
            got = in_buf[m][slot_ref[m, b]]
            q_s[b * BLK : (b + 1) * BLK, :] = got[:BLK, :HD]
            k_s[b * BLK : (b + 1) * BLK, :] = got[:BLK, HD:]
            v_s[b * BLK : (b + 1) * BLK, :] = unpack_fold(got[BLK:])
        span = BPS * BLK
        for s in range(blocks // BPS):
            rows = slice(s * span, (s + 1) * span)
            scores = lax.dot_general(
                k_s[rows, :], q_s[rows, :], (((1,), (1,)), ((), ())), preferred_element_type=F32
            ) * (1.0 / math.sqrt(HD))
            place = lax.broadcasted_iota(jnp.int32, scores.shape, 0)
            scores = jnp.where(place < lens_ref[m, s], scores, NEG_FILL)
            top = jnp.max(scores, axis=0, keepdims=True)
            weights = jnp.exp(scores - top)
            total = jnp.sum(weights, axis=0, keepdims=True)
            out_t = lax.dot_general(
                v_s[rows, :],
                weights.astype(BF16),
                (((0,), (0,)), ((), ())),
                preferred_element_type=F32,
            )
            a_s[s * BPS : (s + 1) * BPS] = (out_t / total).T.reshape(BPS, BLK, HD)
            lse_ref[pl.ds(m * (blocks // BPS) + s, 1), :] = top + jnp.log(total)
        for t in range(blocks):
            back_out[m, t] = fold(a_s[block_ref[m, t]]).astype(BF16)
        for peer in peers:
            send(
                back_out.at[m, peer[0]], back_in.at[m, c], back_send.at[m], back_recv.at[m], peer
            )
        back_in[m, c] = back_out[m, c]
    for m in range(MB):
        all_bytes(back_in.at[m], back_recv.at[m], heads - 1).wait()
        for pair in range(heads // 2):
            a_ref[m * BLK : (m + 1) * BLK, pair * 128 : (pair + 1) * 128] = jnp.concatenate(
                [unpack_fold(back_in[m, 2 * pair]), unpack_fold(back_in[m, 2 * pair + 1])], axis=1
            )
    for m in range(MB):
        all_bytes(out_buf.at[m], send_sem.at[m], heads - 1).wait()
        all_bytes(back_out.at[m], back_send.at[m], heads - 1).wait()
        pltpu.make_async_copy(in_buf[m], kept_ref.at[m], keep_sem.at[m]).wait()


def attend(lens, slot_of, block_of, q, k, v, heads):
    vmem, smem = pl.BlockSpec(memory_space=pltpu.VMEM), pl.BlockSpec(memory_space=pltpu.SMEM)
    rows, width = q.shape
    pack_rows = BLK + BLK // 2
    span = BPS * BLK
    return pl.pallas_call(
        functools.partial(attend_kernel, heads),
        out_shape=[
            jax.ShapeDtypeStruct((rows, width), BF16),
            jax.ShapeDtypeStruct((MB, heads, pack_rows, 128), BF16),
            jax.ShapeDtypeStruct((8, span), F32),
        ],
        in_specs=[smem] * 3 + [vmem] * 3,
        out_specs=[vmem, pl.BlockSpec(memory_space=pl.ANY), vmem],
        scratch_shapes=[pltpu.VMEM((heads, pack_rows, 128), BF16)] * MB
        + [
            pltpu.VMEM((MB, heads, pack_rows, 128), BF16),
            pltpu.VMEM((MB, heads, BLK // 2, 128), BF16),
            pltpu.VMEM((MB, heads, BLK // 2, 128), BF16),
            pltpu.VMEM((heads * BLK, HD), BF16),
            pltpu.VMEM((heads * BLK, HD), BF16),
            pltpu.VMEM((heads * BLK, HD), BF16),
            pltpu.VMEM((heads, BLK, HD), F32),
            pltpu.SemaphoreType.DMA((MB,)),
            pltpu.SemaphoreType.DMA((MB,)),
            pltpu.SemaphoreType.DMA((MB,)),
            pltpu.SemaphoreType.DMA((MB,)),
            pltpu.SemaphoreType.DMA((MB,)),
        ],
        compiler_params=pltpu.CompilerParams(
            collective_id=1, has_side_effects=True, vmem_limit_bytes=VMEM_BYTES
        ),
        name="attend",
    )(lens, slot_of, block_of, q, k, v)


def attend_back_kernel(heads, *refs):
    lens_ref, slot_ref, block_ref, da_ref, kept_ref, lse_ref = refs[:6]
    x_ref, a_ref, n_ref, g_ref, do_ref, du_ref, dm_ref = refs[6:13]
    dq_ref, dk_ref, dv_ref = refs[13:16]
    x_all, a_all, n_all, g_all, do_all, du_all, dm_all, dqkv_all = refs[16:24]
    in_buf = refs[24 : 24 + MB]
    out_buf, back_out, back_in = refs[24 + MB : 27 + MB]
    q_s, k_s, v_s, a_s, dq_s, dk_s, dv_s = refs[27 + MB : 34 + MB]
    send_sem, recv_sem, back_send, back_recv, mate_send, mate_recv, own_sem = refs[34 + MB :]
    c, w = lax.axis_index("ctx"), lax.axis_index("wsh")
    core = bit_of(c, 1)
    mate = (flip(c, 1), w)
    peers = plane_peers(c, w, heads)
    blocks = heads
    rows_own = da_ref.shape[0]
    greet(peers)

    place = pl.ds(pl.multiple_of(core * rows_own, rows_own), rows_own)
    moves = []

    def share(src, dst, lanes):
        for first, size, to, per_core in lanes:
            index = len(moves)
            step = size if per_core else 0
            own_from = pl.ds(pl.multiple_of(first + core * step, 128), size)
            mate_from = pl.ds(pl.multiple_of(first + (1 - core) * step, 128), size)
            spot = dst.at[place, pl.ds(to, size)]
            own = pltpu.make_async_copy(src.at[:, own_from], spot, own_sem.at[index])
            own.start()
            gone = send(
                src.at[:, mate_from], spot, mate_send.at[index], mate_recv.at[index], mate
            )
            moves.append((own, gone))

    width = da_ref.shape[1]
    hidden = g_ref.shape[1]
    for m in range(MB):
        row = slice(m * BLK, (m + 1) * BLK)
        for pair in range(heads // 2):
            both = da_ref[row, pair * 128 : (pair + 1) * 128]
            for head in range(2):
                out_buf[m, 2 * pair + head] = fold(both[:, head * HD : (head + 1) * HD])
        for peer in peers:
            send(out_buf.at[m, peer[0]], in_buf[m].at[c], send_sem.at[m], recv_sem.at[m], peer)
        in_buf[m][c] = out_buf[m, c]
    for src, dst in ((x_ref, x_all), (a_ref, a_all), (n_ref, n_all), (dm_ref, dm_all)):
        share(src, dst, ((0, width, 0, False),))
    share(do_ref, do_all, ((0, width // 2, 0, True),))
    share(du_ref, du_all, ((0, hidden // 2, 0, True),))
    share(g_ref, g_all, ((0, hidden // 4, 0, True), (hidden // 2, hidden // 4, hidden // 4, True)))
    for m in range(MB):
        all_bytes(in_buf[m], recv_sem.at[m], heads - 1).wait()
        for b in range(blocks):
            slot = slot_ref[m, b]
            got = kept_ref[m, slot]
            rows = slice(b * BLK, (b + 1) * BLK)
            q_s[rows, :] = got[:BLK, :HD]
            k_s[rows, :] = got[:BLK, HD:]
            v_s[rows, :] = unpack_fold(got[BLK:])
            a_s[rows, :] = unpack_fold(in_buf[m][slot])
        span = BPS * BLK
        for s in range(blocks // BPS):
            rows = slice(s * span, (s + 1) * span)
            qq, kk, vv, dd = q_s[rows, :], k_s[rows, :], v_s[rows, :], a_s[rows, :]
            scale = 1.0 / math.sqrt(HD)
            minor = (((1,), (1,)), ((), ()))
            scores = lax.dot_general(kk, qq, minor, preferred_element_type=F32) * scale
            spot = lax.broadcasted_iota(jnp.int32, scores.shape, 0)
            total = lse_ref[pl.ds(m * (blocks // BPS) + s, 1), :]
            probs = jnp.exp(jnp.where(spot < lens_ref[m, s], scores - total, NEG_FILL))
            dp = lax.dot_general(vv, dd, minor, preferred_element_type=F32)
            both = probs * dp
            delta = jnp.sum(both, axis=0, keepdims=True)
            ds = (both - probs * delta).astype(BF16)
            here = slice(s * BPS, (s + 1) * BPS)
            split = (BPS, BLK, HD)
            dv = jnp.dot(probs.astype(BF16), dd, preferred_element_type=F32)
            dv_s[here] = dv.reshape(split)
            dk_s[here] = (jnp.dot(ds, qq, preferred_element_type=F32) * scale).reshape(split)
            dq_t = lax.dot_general(kk, ds, (((0,), (0,)), ((), ())), preferred_element_type=F32)
            dq_s[here] = (dq_t.T * scale).reshape(split)
        for t in range(blocks):
            at = block_ref[m, t]
            back_out[m, t, 0:BLK, :] = jnp.concatenate([dq_s[at], dk_s[at]], axis=1).astype(BF16)
            back_out[m, t, BLK:, :] = fold(dv_s[at]).astype(BF16)
        for peer in peers:
            send(
                back_out.at[m, peer[0]], back_in.at[m, c], back_send.at[m], back_recv.at[m], peer
            )
        back_in[m, c] = back_out[m, c]
    for m in range(MB):
        all_bytes(back_in.at[m], back_recv.at[m], heads - 1).wait()
        row = slice(m * BLK, (m + 1) * BLK)
        for pair in range(heads // 2):
            lanes = slice(pair * 128, (pair + 1) * 128)
            one, two = back_in[m, 2 * pair], back_in[m, 2 * pair + 1]
            dq_ref[row, lanes] = jnp.concatenate([one[:BLK, :HD], two[:BLK, :HD]], axis=1)
            dk_ref[row, lanes] = jnp.concatenate([one[:BLK, HD:], two[:BLK, HD:]], axis=1)
            dv_ref[row, lanes] = jnp.concatenate(
                [unpack_fold(one[BLK:]), unpack_fold(two[BLK:])], axis=1
            )
    for index, ref in enumerate((dq_ref, dk_ref, dv_ref)):
        half = width // 2
        spot = dqkv_all.at[place, pl.ds(index * half, half)]
        number = len(moves)
        own_from = pl.ds(pl.multiple_of(core * half, 128), half)
        mate_from = pl.ds(pl.multiple_of((1 - core) * half, 128), half)
        own = pltpu.make_async_copy(ref.at[:, own_from], spot, own_sem.at[number])
        own.start()
        gone = send(ref.at[:, mate_from], spot, mate_send.at[number], mate_recv.at[number], mate)
        moves.append((own, gone))
    for m in range(MB):
        all_bytes(out_buf.at[m], send_sem.at[m], heads - 1).wait()
        all_bytes(back_out.at[m], back_send.at[m], heads - 1).wait()
    for own, gone in moves:
        own.wait()
        gone.wait()


def attend_back(lens, slot_of, block_of, da, kept, lse, x, a, n1, g, do, du, dm, heads):
    vmem, smem = pl.BlockSpec(memory_space=pltpu.VMEM), pl.BlockSpec(memory_space=pltpu.SMEM)
    anywhere = pl.BlockSpec(memory_space=pl.ANY)
    rows, width = da.shape
    hidden = g.shape[1]
    pack_rows = BLK + BLK // 2
    both = 2 * rows
    moves = 11
    shape = lambda *dims: jax.ShapeDtypeStruct(dims, BF16)
    return pl.pallas_call(
        functools.partial(attend_back_kernel, heads),
        out_shape=[shape(rows, width)] * 3
        + [
            shape(both, width),
            shape(both, width),
            shape(both, width),
            shape(both, hidden // 2),
            shape(both, width // 2),
            shape(both, hidden // 2),
            shape(both, width),
            shape(both, 3 * width // 2),
        ],
        in_specs=[smem] * 3 + [vmem] * 3 + [anywhere] * 7,
        out_specs=[vmem] * 3 + [anywhere] * 8,
        scratch_shapes=[pltpu.VMEM((heads, BLK // 2, 128), BF16)] * MB
        + [
            pltpu.VMEM((MB, heads, BLK // 2, 128), BF16),
            pltpu.VMEM((MB, heads, pack_rows, 128), BF16),
            pltpu.VMEM((MB, heads, pack_rows, 128), BF16),
        ]
        + [pltpu.VMEM((heads * BLK, HD), BF16)] * 4
        + [pltpu.VMEM((heads, BLK, HD), F32)] * 3
        + [pltpu.SemaphoreType.DMA((MB,))] * 4
        + [pltpu.SemaphoreType.DMA((moves,))] * 3,
        compiler_params=pltpu.CompilerParams(
            collective_id=2, has_side_effects=True, vmem_limit_bytes=VMEM_BYTES
        ),
        name="attend_back",
    )(lens, slot_of, block_of, da, kept, lse, x, a, n1, g, do, du, dm)


CHUNKS = 2


def reduce_kernel(ga1_ref, ga2_ref, gb_ref, gc_ref, vec_ref, *refs):
    o_a, o_b, o_c, vec_out = refs[:4]
    s_a, s_b, s_c = refs[4:7]
    r_bufs = (refs[7:11], refs[11:15], refs[15:19])
    v_recv, v_sum = refs[19:21]
    load_sem, rs_send, rs_recv, ag_send, ag_recv, v_send_sem, v_recv_sem, own_sem = refs[21:]
    c, x = lax.axis_index("ctx"), lax.axis_index("wsh")
    core, y, z, zz = bit_of(c, 1), bit_of(c, 2), bit_of(c, 4), bit_of(c, 8)
    by_x, by_y, by_z = (c, 1 - x), (flip(c, 2), x), (flip(c, 4), x)
    by_zz, by_core = (flip(c, 8), x), (flip(c, 1), x)
    shards = 8
    lanes1 = ga1_ref.shape[3]
    lanes2 = ga2_ref.shape[3]
    loads = [
        pltpu.make_async_copy(ga1_ref, s_a.at[:, :, :, pl.ds(0, lanes1)], load_sem.at[0]),
        pltpu.make_async_copy(ga2_ref, s_a.at[:, :, :, pl.ds(lanes1, lanes2)], load_sem.at[1]),
        pltpu.make_async_copy(gb_ref, s_b, load_sem.at[2]),
        pltpu.make_async_copy(gc_ref, s_c, load_sem.at[3]),
    ]
    for load in loads:
        load.start()
    greet((by_x, by_y, by_z, by_zz, by_core))
    vec_steps = [
        send(vec_ref.at[1 - x], v_recv.at[0], v_send_sem.at[0], v_recv_sem.at[0], by_x)
    ]

    def vec_next(step, peer):
        vec_steps[step].wait_recv()
        before = vec_ref[x] if step == 0 else v_sum[step - 1]
        v_sum[step] = before + v_recv[step]
        if peer is not None:
            vec_steps.append(
                send(
                    v_sum.at[step],
                    v_recv.at[step + 1],
                    v_send_sem.at[step + 1],
                    v_recv_sem.at[step + 1],
                    peer,
                )
            )

    for load in loads:
        load.wait()
    yz, zy = y * 4 + z * 2, z * 4 + y * 2
    plans = (
        (
            (by_x, 1 - x, x, 0, 0, 8),
            (by_y, x, x, (1 - y) * 4, y * 4, 4),
            (by_z, x, x, y * 4 + (1 - z) * 2, yz, 2),
            (by_zz, x, x, yz + 1 - zz, yz + zz, 1),
        ),
        (
            (by_y, None, None, (1 - y) * 4, y * 4, 4),
            (by_z, None, None, y * 4 + (1 - z) * 2, yz, 2),
            (by_x, 1 - x, x, yz, yz, 2),
            (by_zz, x, x, yz + 1 - zz, yz + zz, 1),
        ),
        (
            (by_z, None, None, (1 - z) * 4, z * 4, 4),
            (by_x, 1 - x, x, z * 4, z * 4, 4),
            (by_y, x, x, z * 4 + (1 - y) * 2, zy, 2),
            (by_zz, x, x, zy + 1 - zz, zy + zz, 1),
        ),
    )
    sums = (s_a, s_b, s_c)
    outs = (o_a, o_b, o_c)
    flights = {}

    def chunk_rows(part, chunk):
        rows = sums[part].shape[2] // CHUNKS
        return pl.ds(chunk * rows, rows)

    def reduce_send(part, step, chunk):
        peer, side, _, first, _, count = plans[part][step]
        rows = chunk_rows(part, chunk)
        if side is None:
            src = sums[part].at[:, pl.ds(first, count), rows]
            dst = r_bufs[part][step].at[:, :, rows]
        else:
            src = sums[part].at[side, pl.ds(first, count), rows]
            dst = r_bufs[part][step].at[0, :, rows]
        flights[part, step, chunk] = send(
            src, dst, rs_send.at[part, step, chunk], rs_recv.at[part, step, chunk], peer
        )

    def reduce_add(part, step, chunk):
        _, _, side, _, first, count = plans[part][step]
        rows = chunk_rows(part, chunk)
        flights[part, step, chunk].wait_recv()
        total, fresh = sums[part], r_bufs[part][step]
        sides = ((0, 0), (1, 1)) if side is None else ((side, 0),)
        for here, there in sides:

            def body(index, carry):
                spot = first + index
                total[here, spot, rows] = (
                    total[here, spot, rows].astype(F32) + fresh[there, index, rows].astype(F32)
                ).astype(BF16)
                return carry

            lax.fori_loop(0, count, body, 0)

    for chunk in range(CHUNKS):
        for part in range(3):
            reduce_send(part, 0, chunk)
    vec_peers = (by_y, by_z, by_zz, by_core, None)
    for step in range(1, 4):
        vec_next(step - 1, vec_peers[step - 1])
        for chunk in range(CHUNKS):
            for part in range(3):
                reduce_add(part, step - 1, chunk)
                reduce_send(part, step, chunk)
    gathers = (
        ((by_zz, yz + zz, 1), (by_z, yz, 2), (by_y, y * 4, 4)),
        ((by_zz, yz + zz, 1), (by_z, yz, 2), (by_y, y * 4, 4)),
        ((by_zz, zy + zz, 1), (by_y, zy, 2), (by_z, z * 4, 4)),
    )
    news = (
        (yz + 1 - zz, y * 4 + (1 - z) * 2, (1 - y) * 4),
        (yz + 1 - zz, y * 4 + (1 - z) * 2, (1 - y) * 4),
        (zy + 1 - zz, z * 4 + (1 - y) * 2, (1 - z) * 4),
    )
    owns, spread = [], {}
    vec_next(3, by_core)
    for chunk in range(CHUNKS):
        for part in range(3):
            reduce_add(part, 3, chunk)
            rows = chunk_rows(part, chunk)
            peer, first, count = gathers[part][0]
            src = sums[part].at[x, pl.ds(first, 1), rows]
            dst = outs[part].at[core, pl.ds(first, 1), rows]
            own = pltpu.make_async_copy(src, dst, own_sem.at[part, chunk])
            own.start()
            owns.append(own)
            sem = lambda kind: (ag_send.at[part, kind, chunk], ag_recv.at[part, kind, chunk])
            spread[part, 0, chunk] = send(src, dst, *sem(0), peer)
            spread[part, 3, chunk] = send(src, dst, *sem(3), by_core)
    vec_next(4, None)
    vec_out[...] = v_sum[4]
    for own in owns:
        own.wait()
    for step in range(1, 4):
        for chunk in range(CHUNKS):
            for part in range(3):
                rows = chunk_rows(part, chunk)
                spread[part, step - 1, chunk].wait_recv()
                sem = lambda kind: (ag_send.at[part, kind, chunk], ag_recv.at[part, kind, chunk])
                if step < 3:
                    peer, first, count = gathers[part][step]
                    ref = outs[part].at[core, pl.ds(first, count), rows]
                    spread[part, step, chunk] = send(ref, ref, *sem(step), peer)
                fresh = outs[part].at[
                    core, pl.ds(news[part][step - 1], gathers[part][step - 1][2]), rows
                ]
                spread[part, 3 + step, chunk] = send(fresh, fresh, *sem(3 + step), by_core)
    for key, flight in spread.items():
        if key[1] >= 3:
            flight.wait_recv()
        flight.wait_send()
    for flight in flights.values():
        flight.wait_send()
    for flight in vec_steps:
        flight.wait_send()


def reduce_grads(ga1, ga2, gb, gc, vec):
    vmem, anywhere = pl.BlockSpec(memory_space=pltpu.VMEM), pl.BlockSpec(memory_space=pl.ANY)
    lanes = ga1.shape[3] + ga2.shape[3]
    a_shape = ga1.shape[:3] + (lanes,)
    b_shape, c_shape = gb.shape, gc.shape
    scratch = [pltpu.VMEM(s, BF16) for s in (a_shape, b_shape, c_shape)]
    halves = (
        ((1, 8), (1, 4), (1, 2), (1, 1)),
        ((2, 4), (2, 2), (1, 2), (1, 1)),
        ((2, 4), (1, 4), (1, 2), (1, 1)),
    )
    for shape, steps in zip((a_shape, b_shape, c_shape), halves):
        scratch += [pltpu.VMEM(lead + shape[2:], BF16) for lead in steps]
    scratch += [
        pltpu.VMEM((5,) + vec.shape[1:], F32),
        pltpu.VMEM((5,) + vec.shape[1:], F32),
        pltpu.SemaphoreType.DMA((4,)),
        pltpu.SemaphoreType.DMA((3, 4, CHUNKS)),
        pltpu.SemaphoreType.DMA((3, 4, CHUNKS)),
        pltpu.SemaphoreType.DMA((3, 7, CHUNKS)),
        pltpu.SemaphoreType.DMA((3, 7, CHUNKS)),
        pltpu.SemaphoreType.DMA((5,)),
        pltpu.SemaphoreType.DMA((5,)),
        pltpu.SemaphoreType.DMA((3, CHUNKS)),
    ]
    return pl.pallas_call(
        reduce_kernel,
        out_shape=[
            jax.ShapeDtypeStruct(a_shape, BF16),
            jax.ShapeDtypeStruct(b_shape, BF16),
            jax.ShapeDtypeStruct(c_shape, BF16),
            jax.ShapeDtypeStruct(vec.shape[1:], F32),
        ],
        in_specs=[anywhere] * 4 + [vmem],
        out_specs=[anywhere] * 3 + [vmem],
        scratch_shapes=scratch,
        compiler_params=pltpu.CompilerParams(
            collective_id=3, has_side_effects=True, vmem_limit_bytes=VMEM_BYTES
        ),
        name="reduce_grads",
    )(ga1, ga2, gb, gc, vec)


def norm_parts(summed):
    row_mean = jnp.mean(summed, axis=-1, keepdims=True)
    centred = summed - row_mean
    row_var = jnp.mean(centred * centred, axis=-1, keepdims=True)
    scale = lax.rsqrt(row_var + EPSILON)
    return centred * scale, scale


def norm_back(grad, unit, scale, gain):
    inner = grad * gain
    mean_one = jnp.mean(inner, axis=-1, keepdims=True)
    mean_two = jnp.mean(inner * unit, axis=-1, keepdims=True)
    return scale * (inner - mean_one - unit * mean_two)


def dot(a, b, dims):
    return lax.dot_general(a, b, (dims, ((), ())), preferred_element_type=F32)


ROW_COL, COL_COL, ROW_ROW = ((1,), (0,)), ((1,), (1,)), ((0,), (0,))


def per_device_heads(tokens, cotangent, lengths, dealing, *params):
    rows_in = tokens.shape[2]
    width = tokens.shape[3]
    rows = MB * rows_in
    weights, vectors = params[:6], params[6:]
    sizes = [item.shape[0] for item in vectors]
    small = jnp.concatenate(vectors).reshape(-1, 128)
    *wholes, small_whole = gather_weights(weights, small)
    query_w, key_w, value_w, out_w, up_w, down_w = wholes
    flat = small_whole.reshape(2, -1).astype(F32)
    spots = [sum(sizes[:i]) for i in range(len(sizes) + 1)]
    bias_query, bias_value, bias_out, bias_up, bias_down, gain_one, shift_one, gain_two, shift_two = (
        flat[:, spots[i] : spots[i + 1]].reshape(1, -1) for i in range(len(sizes))
    )
    x = tokens.reshape(rows, width)
    lens = lengths[0]
    block_of = dealing[0]
    slot_of = jnp.argsort(block_of, axis=1).astype(jnp.int32)
    q = (dot(x, query_w, ROW_COL) + bias_query).astype(BF16)
    k = dot(x, key_w, ROW_COL).astype(BF16)
    v = (dot(x, value_w, ROW_COL) + bias_value).astype(BF16)
    a, kept, lse = attend(lens, slot_of, block_of, q, k, v, HEADS)

    h_one = x.astype(F32) + (dot(a, out_w, ROW_COL) + bias_out)
    unit_one, scale_one = norm_parts(h_one)
    n_one = unit_one * gain_one + shift_one
    n_low = n_one.astype(BF16)
    u = dot(n_low, up_w, ROW_COL) + bias_up
    act, act_back = jax.vjp(gelu_exact, u)
    g = act.astype(BF16)
    h_two = n_one + (dot(g, down_w, ROW_COL) + bias_down)
    unit_two, scale_two = norm_parts(h_two)
    output = (unit_two * gain_two + shift_two).astype(BF16)

    cot = cotangent.reshape(rows, width).astype(F32)
    dh_two = norm_back(cot, unit_two, scale_two, gain_two)
    dm = dh_two.astype(BF16)
    (du_full,) = act_back(dot(dm, down_w, COL_COL))
    du = du_full.astype(BF16)
    dn = dot(du, up_w, COL_COL) + dh_two
    dh_one = norm_back(dn, unit_one, scale_one, gain_one)
    do = dh_one.astype(BF16)
    da = dot(do, out_w, COL_COL).astype(BF16)

    dq, dk, dv, x_all, a_all, n_all, g_all, do_all, du_all, dm_all, dqkv_all = attend_back(
        lens, slot_of, block_of, da, kept, lse, x, a, n_low, g, do, du, dm, HEADS
    )
    total = lambda item: jnp.sum(item.astype(F32), axis=0)
    vec = [
        total(dq),
        total(dv),
        total(do),
        total(du),
        total(dm),
        total(dn * unit_one),
        total(dn),
        total(cot * unit_two),
        total(cot),
    ]
    vec = jnp.concatenate([item.reshape(2, -1) for item in vec], axis=1).reshape(2, -1, 128)
    ga1 = dot(x_all, dqkv_all, ROW_ROW).astype(BF16).reshape(2, 8, -1, dqkv_all.shape[1])
    ga2 = dot(a_all, do_all, ROW_ROW).astype(BF16).reshape(2, 8, -1, do_all.shape[1])
    gb = dot(n_all, du_all, ROW_ROW).astype(BF16).reshape(2, 8, -1, du_all.shape[1])
    gc = dot(g_all, dm_all, ROW_ROW).astype(BF16).reshape(2, 8, -1, dm_all.shape[1])
    o_a, o_b, o_c, vec_sum = reduce_grads(ga1, ga2, gb, gc, vec)
    grad_rows = (
        dh_one + dot(dq, query_w, COL_COL) + dot(dk, key_w, COL_COL) + dot(dv, value_w, COL_COL)
    )
    grad_tokens = grad_rows.astype(BF16)
    half = width // 2
    o_a = o_a.reshape(2, -1, o_a.shape[3])
    square = [
        jnp.concatenate([o_a[0, :, i * half : (i + 1) * half], o_a[1, :, i * half : (i + 1) * half]], axis=1)
        for i in range(4)
    ]
    o_b = o_b.reshape(2, -1, o_b.shape[3])
    up = jnp.concatenate([o_b[0], o_b[1]], axis=1)
    down = o_c.reshape(-1, width)
    vec_sum = vec_sum.reshape(-1)
    ends = [vec_sum[spots[i] : spots[i + 1]] for i in range(len(sizes))]
    shape = (1, MB, rows_in, width)
    return (
        (output.reshape(shape), grad_tokens.reshape(shape))
        + tuple(item.astype(F32) for item in square + [up, down])
        + tuple(ends)
    )


def solution(mesh):
    placed = (
        P("wsh", None, "ctx", None),
        P("wsh", None, "ctx", None),
        P("wsh", None, None),
        P("wsh", None, None),
        P("wsh", None),
        P("wsh", None),
        P("wsh", None),
        P("wsh", None),
        P("wsh", None),
        P("wsh", None),
        P("wsh"),
        P("wsh"),
        P("wsh"),
        P("wsh"),
        P("wsh"),
        P("wsh"),
        P("wsh"),
        P("wsh"),
        P("wsh"),
    )
    by_heads = mesh.shape["ctx"] == HEADS and mesh.shape["wsh"] == 2
    return jax.shard_map(
        per_device_heads if by_heads else per_device,
        mesh=mesh,
        in_specs=placed,
        out_specs=(
            P("wsh", None, "ctx", None),
            P("wsh", None, "ctx", None),
            P("wsh", None),
            P("wsh", None),
            P("wsh", None),
            P("wsh", None),
            P("wsh", None),
            P("wsh", None),
            P("wsh"),
            P("wsh"),
            P("wsh"),
            P("wsh"),
            P("wsh"),
            P("wsh"),
            P("wsh"),
            P("wsh"),
            P("wsh"),
        ),
        check_vma=False,
    )
```

```python
import functools
import math

import jax
import jax.numpy as jnp
from jax import lax
from jax.experimental import pallas as pl
from jax.experimental.pallas import tpu as pltpu
from jax.sharding import PartitionSpec as P

HEADS = 16
BPS = 8
MB = 3
BLK = 64


EPSILON = 1e-12
NEG_FILL = -1e30


def as_sent(x):
    return jax.tree.map(lambda a: a.astype(jnp.bfloat16) if a.dtype == jnp.float32 else a, x)


def layer_norm(summed, gain_vec, shift_vec):
    row_mean = jnp.mean(summed, axis=-1, keepdims=True)
    centred = summed - row_mean
    row_var = jnp.mean(centred * centred, axis=-1, keepdims=True)
    return centred * lax.rsqrt(row_var + EPSILON) * gain_vec + shift_vec


def gelu_exact(values):
    return jax.nn.gelu(values, approximate=False)


def row_labels(dealt_order, seq_lengths):
    blocks_of_rows = jnp.repeat(dealt_order, BLK)
    within = jnp.tile(jnp.arange(BLK, dtype=jnp.int32), dealt_order.shape[0])
    seq_ids = blocks_of_rows // BPS
    places = blocks_of_rows % BPS * BLK + within
    numbers = jnp.arange(seq_lengths.shape[0], dtype=jnp.int32)
    seq_bound = jnp.sum(
        jnp.where(seq_ids[:, None] == numbers[None, :], seq_lengths[None, :], 0), axis=1
    )
    return (seq_ids, places < seq_bound)


def blockwise(carried, total_rows, step_rows, visit_block):
    return lax.fori_loop(
        0,
        total_rows // step_rows,
        lambda turn_index, running: visit_block(running, turn_index * step_rows),
        carried,
    )


def masked_scores(query_blk, key_blk, query_seq, key_seq, key_valid, scale_factor):
    allowed = (query_seq[:, None] == key_seq[None, :]) & key_valid[None, :]
    scores = (
        jnp.einsum("qhd,khd->hqk", query_blk, key_blk, preferred_element_type=jnp.float32)
        * scale_factor
    )
    return (jnp.where(allowed[None], scores, NEG_FILL), allowed[None].astype(jnp.float32))


def attention_grads(
    query_blk,
    grad_blk,
    key_blk,
    value_blk,
    query_seq,
    key_seq,
    key_valid,
    row_total,
    row_delta,
    scale_factor,
):
    scores, allowed = masked_scores(query_blk, key_blk, query_seq, key_seq, key_valid, scale_factor)
    probs = jnp.exp(scores - row_total[:, :, None]) * allowed
    grad_probs = jnp.einsum("qhd,khd->hqk", grad_blk, value_blk, preferred_element_type=jnp.float32)
    grad_scores = (probs * (grad_probs - row_delta[:, :, None])).astype(jnp.bfloat16)
    return (probs.astype(jnp.bfloat16), grad_scores)


def gather_params(params):
    return (
        lax.all_gather(params[0], "wsh", axis=0, tiled=True),
        lax.all_gather(params[1], "wsh", axis=0, tiled=True),
        lax.all_gather(params[2], "wsh", axis=0, tiled=True),
        lax.all_gather(params[3], "wsh", axis=0, tiled=True),
        lax.all_gather(params[4], "wsh", axis=0, tiled=True),
        lax.all_gather(params[5], "wsh", axis=0, tiled=True),
        lax.all_gather(params[6], "wsh", axis=0, tiled=True),
        lax.all_gather(params[7], "wsh", axis=0, tiled=True),
        lax.all_gather(params[8], "wsh", axis=0, tiled=True),
        lax.all_gather(params[9], "wsh", axis=0, tiled=True),
        lax.all_gather(params[10], "wsh", axis=0, tiled=True),
        lax.all_gather(params[11], "wsh", axis=0, tiled=True),
        lax.all_gather(params[12], "wsh", axis=0, tiled=True),
        lax.all_gather(params[13], "wsh", axis=0, tiled=True),
        lax.all_gather(params[14], "wsh", axis=0, tiled=True),
    )


def per_device(
    tokens,
    cotangent,
    lengths,
    dealing,
    w_query,
    w_key,
    w_value,
    w_out,
    w_up,
    w_down,
    b_query,
    b_value,
    b_out,
    b_up,
    b_down,
    gain_one,
    shift_one,
    gain_two,
    shift_two,
):
    params = (
        w_query,
        w_key,
        w_value,
        w_out,
        w_up,
        w_down,
        b_query,
        b_value,
        b_out,
        b_up,
        b_down,
        gain_one,
        shift_one,
        gain_two,
        shift_two,
    )
    own_rows = tokens.shape[2]
    width = tokens.shape[3]
    head_size = width // HEADS
    scale_factor = 1.0 / math.sqrt(head_size)
    my_start = lax.axis_index("ctx") * own_rows
    wsh_count = lax.axis_size("wsh")
    grads = tuple(
        (jnp.zeros((item.shape[0] * wsh_count,) + item.shape[1:], jnp.float32) for item in params)
    )
    results = []
    input_grads = []
    for micro in range(MB):
        whole = gather_params(params)
        query_weight, key_weight, value_weight, out_weight, up_weight, down_weight = whole[:6]
        (
            bias_query,
            bias_value,
            bias_out,
            bias_up,
            bias_down,
            gain_first,
            shift_first,
            gain_second,
            shift_second,
        ) = tuple((item.astype(jnp.float32) for item in whole[6:]))
        token_rows = tokens[0, micro]
        seq_all, valid_all = row_labels(dealing[0, micro], lengths[0, micro])
        my_seq = lax.dynamic_slice_in_dim(seq_all, my_start, own_rows)
        my_valid = lax.dynamic_slice_in_dim(valid_all, my_start, own_rows)
        query_low = (
            jnp.dot(token_rows, query_weight, preferred_element_type=jnp.float32) + bias_query
        ).astype(jnp.bfloat16)
        key_low = jnp.dot(token_rows, key_weight, preferred_element_type=jnp.float32).astype(
            jnp.bfloat16
        )
        value_low = (
            jnp.dot(token_rows, value_weight, preferred_element_type=jnp.float32) + bias_value
        ).astype(jnp.bfloat16)
        query_heads = query_low.reshape(own_rows, HEADS, head_size)
        my_key_heads = key_low.reshape(own_rows, HEADS, head_size)
        my_value_heads = value_low.reshape(own_rows, HEADS, head_size)
        start_state = (
            jnp.full((HEADS, own_rows), NEG_FILL, jnp.float32),
            jnp.zeros((HEADS, own_rows), jnp.float32),
            jnp.zeros((own_rows, HEADS, head_size), jnp.float32),
        )
        key_piece = lax.all_gather(key_low, "ctx", axis=0, tiled=True)
        value_piece = lax.all_gather(value_low, "ctx", axis=0, tiled=True)
        piece_rows = key_piece.shape[0]
        step_rows = math.gcd(piece_rows, 512)

        def visit_block(running, offset):
            run_max, run_sum, run_acc = running
            key_blk = lax.dynamic_slice_in_dim(key_piece, offset, step_rows).reshape(
                step_rows, HEADS, head_size
            )
            value_blk = lax.dynamic_slice_in_dim(value_piece, offset, step_rows).reshape(
                step_rows, HEADS, head_size
            )
            key_seq = lax.dynamic_slice_in_dim(seq_all, offset, step_rows)
            key_valid = lax.dynamic_slice_in_dim(valid_all, offset, step_rows)
            scores, allowed = masked_scores(
                query_heads, key_blk, my_seq, key_seq, key_valid, scale_factor
            )
            new_max = jnp.maximum(run_max, jnp.max(scores, axis=-1))
            rescale = jnp.exp(run_max - new_max)
            weights = jnp.exp(scores - new_max[:, :, None]) * allowed
            run_sum = run_sum * rescale + jnp.sum(weights, axis=-1)
            run_acc = run_acc * rescale.T[:, :, None] + jnp.einsum(
                "hqk,khd->qhd",
                weights.astype(jnp.bfloat16),
                value_blk,
                preferred_element_type=jnp.float32,
            )
            return (new_max, run_sum, run_acc)

        final_max, final_sum, final_acc = blockwise(start_state, piece_rows, step_rows, visit_block)
        attended = final_acc / final_sum.T[:, :, None]
        log_total = final_max + jnp.log(final_sum)
        attended_low = attended.reshape(own_rows, width).astype(jnp.bfloat16)
        out_proj = jnp.dot(attended_low, out_weight, preferred_element_type=jnp.float32) + bias_out
        first_sum = token_rows.astype(jnp.float32) + out_proj
        norm_one, norm_one_back = jax.vjp(layer_norm, first_sum, gain_first, shift_first)
        mlp_input = norm_one.astype(jnp.bfloat16)
        up_pre = jnp.dot(mlp_input, up_weight, preferred_element_type=jnp.float32) + bias_up
        activated, gelu_back = jax.vjp(gelu_exact, up_pre)
        activated_low = activated.astype(jnp.bfloat16)
        down_out = (
            jnp.dot(activated_low, down_weight, preferred_element_type=jnp.float32) + bias_down
        )
        result, norm_two_back = jax.vjp(layer_norm, norm_one + down_out, gain_second, shift_second)
        results.append(result.astype(jnp.bfloat16))
        grad_second, grad_gain_b, grad_shift_b = norm_two_back(
            cotangent[0, micro].astype(jnp.float32)
        )
        grad_down_low = grad_second.astype(jnp.bfloat16)
        grad_activated = jnp.einsum(
            "rd,fd->rf", grad_down_low, down_weight, preferred_element_type=jnp.float32
        )
        (grad_up_pre,) = gelu_back(grad_activated)
        grad_up_low = grad_up_pre.astype(jnp.bfloat16)
        grad_norm_one = (
            jnp.einsum("rf,df->rd", grad_up_low, up_weight, preferred_element_type=jnp.float32)
            + grad_second
        )
        grad_first, grad_gain_a, grad_shift_a = norm_one_back(grad_norm_one)
        grad_out_low = grad_first.astype(jnp.bfloat16)
        grad_att_low = jnp.einsum(
            "rd,ed->re", grad_out_low, out_weight, preferred_element_type=jnp.float32
        ).astype(jnp.bfloat16)
        grad_heads = grad_att_low.reshape(own_rows, HEADS, head_size)
        row_delta = jnp.sum(grad_heads.astype(jnp.float32) * attended, axis=-1).T
        empty_heads = jnp.zeros((own_rows, HEADS, head_size), jnp.float32)
        query_key_piece = lax.all_gather(key_low, "ctx", axis=0, tiled=True)
        query_value_piece = lax.all_gather(value_low, "ctx", axis=0, tiled=True)
        query_piece_rows = query_key_piece.shape[0]
        query_step_rows = math.gcd(query_piece_rows, 512)

        def query_visit_block(running, offset):
            key_blk = lax.dynamic_slice_in_dim(query_key_piece, offset, query_step_rows).reshape(
                query_step_rows, HEADS, head_size
            )
            value_blk = lax.dynamic_slice_in_dim(
                query_value_piece, offset, query_step_rows
            ).reshape(query_step_rows, HEADS, head_size)
            key_seq = lax.dynamic_slice_in_dim(seq_all, offset, query_step_rows)
            key_valid = lax.dynamic_slice_in_dim(valid_all, offset, query_step_rows)
            probs_low, grad_scores = attention_grads(
                query_heads,
                grad_heads,
                key_blk,
                value_blk,
                my_seq,
                key_seq,
                key_valid,
                log_total,
                row_delta,
                scale_factor,
            )
            return running + jnp.einsum(
                "hqk,khd->qhd", grad_scores, key_blk, preferred_element_type=jnp.float32
            )

        grad_query_sum = blockwise(
            empty_heads, query_piece_rows, query_step_rows, query_visit_block
        )
        total_all, delta_all = (
            lax.all_gather(log_total.T, "ctx", axis=0, tiled=True),
            lax.all_gather(row_delta.T, "ctx", axis=0, tiled=True),
        )
        query_piece = lax.all_gather(query_low, "ctx", axis=0, tiled=True)
        grad_piece = lax.all_gather(grad_att_low, "ctx", axis=0, tiled=True)
        key_piece_rows = query_piece.shape[0]
        key_step_rows = math.gcd(key_piece_rows, 512)

        def key_visit_block(running, offset):
            grad_key_run, grad_value_run = running
            query_blk = lax.dynamic_slice_in_dim(query_piece, offset, key_step_rows).reshape(
                key_step_rows, HEADS, head_size
            )
            grad_blk = lax.dynamic_slice_in_dim(grad_piece, offset, key_step_rows).reshape(
                key_step_rows, HEADS, head_size
            )
            total_blk = lax.dynamic_slice_in_dim(total_all, offset, key_step_rows)
            delta_blk = lax.dynamic_slice_in_dim(delta_all, offset, key_step_rows)
            query_seq = lax.dynamic_slice_in_dim(seq_all, offset, key_step_rows)
            probs_low, grad_scores = attention_grads(
                query_blk,
                grad_blk,
                my_key_heads,
                my_value_heads,
                query_seq,
                my_seq,
                my_valid,
                total_blk.T,
                delta_blk.T,
                scale_factor,
            )
            grad_key_run = grad_key_run + jnp.einsum(
                "hqk,qhd->khd", grad_scores, query_blk, preferred_element_type=jnp.float32
            )
            grad_value_run = grad_value_run + jnp.einsum(
                "hqk,qhd->khd", probs_low, grad_blk, preferred_element_type=jnp.float32
            )
            return (grad_key_run, grad_value_run)

        grad_key_sum, grad_value_sum = blockwise(
            (empty_heads, empty_heads), key_piece_rows, key_step_rows, key_visit_block
        )
        grad_key_flat = grad_key_sum.reshape(own_rows, width)
        grad_value_flat = grad_value_sum.reshape(own_rows, width)
        grad_query_low = (
            (grad_query_sum * scale_factor).reshape(own_rows, width).astype(jnp.bfloat16)
        )
        grad_key_low = (grad_key_flat * scale_factor).astype(jnp.bfloat16)
        grad_value_low = grad_value_flat.astype(jnp.bfloat16)
        terms = (
            jnp.einsum("rd,re->de", token_rows, grad_query_low, preferred_element_type=jnp.float32),
            jnp.einsum("rd,re->de", token_rows, grad_key_low, preferred_element_type=jnp.float32),
            jnp.einsum("rd,re->de", token_rows, grad_value_low, preferred_element_type=jnp.float32),
            jnp.einsum("rd,re->de", attended_low, grad_out_low, preferred_element_type=jnp.float32),
            jnp.einsum("rd,rf->df", mlp_input, grad_up_low, preferred_element_type=jnp.float32),
            jnp.einsum(
                "rf,rd->fd", activated_low, grad_down_low, preferred_element_type=jnp.float32
            ),
            jnp.sum(grad_query_low.astype(jnp.float32), axis=0),
            jnp.sum(grad_value_low.astype(jnp.float32), axis=0),
            jnp.sum(grad_out_low.astype(jnp.float32), axis=0),
            jnp.sum(grad_up_low.astype(jnp.float32), axis=0),
            jnp.sum(grad_down_low.astype(jnp.float32), axis=0),
            grad_gain_a,
            grad_shift_a,
            grad_gain_b,
            grad_shift_b,
        )
        grads = tuple((total_now + fresh for total_now, fresh in zip(grads, terms)))
        grad_rows = (
            grad_first
            + jnp.einsum(
                "re,de->rd", grad_query_low, query_weight, preferred_element_type=jnp.float32
            )
            + jnp.einsum("re,de->rd", grad_key_low, key_weight, preferred_element_type=jnp.float32)
            + jnp.einsum(
                "re,de->rd", grad_value_low, value_weight, preferred_element_type=jnp.float32
            )
        )
        input_grads.append(grad_rows.astype(jnp.bfloat16))
    shards = jax.tree.map(
        lambda part: part.astype(jnp.float32),
        lax.psum_scatter(as_sent(grads), "wsh", scatter_dimension=0, tiled=True),
    )
    summed = jax.tree.map(lambda part: part.astype(jnp.float32), lax.psum(as_sent(shards), "ctx"))
    return (jnp.stack(results)[None], jnp.stack(input_grads)[None]) + tuple(summed)


MESH_IDS = pl.DeviceIdType.MESH
F32 = jnp.float32
BF16 = jnp.bfloat16
HD = 64
VMEM_BYTES = 60 * 1024 * 1024


def flip(index, bit):
    return index + bit * (1 - 2 * lax.rem(lax.div(index, bit), 2))


def bit_of(index, bit):
    return lax.rem(lax.div(index, bit), 2)


def greet(peers):
    barrier = pltpu.get_barrier_semaphore()
    for peer in peers:
        pl.semaphore_signal(barrier, inc=1, device_id=peer, device_id_type=MESH_IDS)
    pl.semaphore_wait(barrier, len(peers))


def send(src, dst, send_sem, recv_sem, peer):
    copy = pltpu.make_async_remote_copy(
        src_ref=src,
        dst_ref=dst,
        send_sem=send_sem,
        recv_sem=recv_sem,
        device_id=peer,
        device_id_type=MESH_IDS,
    )
    copy.start()
    return copy


def gather_kernel(plan, n_weights, *refs):
    shards, small = refs[:n_weights], refs[n_weights]
    wholes, small_whole = refs[n_weights + 1 : 2 * n_weights + 1], refs[2 * n_weights + 1]
    stages = refs[2 * n_weights + 2 : 3 * n_weights + 2]
    send_sem, recv_sem, small_sems, local_sem, stage_sem = refs[3 * n_weights + 2 :]
    c, w = lax.axis_index("ctx"), lax.axis_index("wsh")
    o = 1 - w
    by_x, by_y, by_z, by_core = (c, o), (flip(c, 2), w), (flip(c, 4), w), (flip(c, 1), w)
    core, y, z = bit_of(c, 1), bit_of(c, 2), bit_of(c, 4)
    mine = core * 4 + z * 2 + y
    from_y, from_z = core * 4 + z * 2 + (1 - y), core * 4 + (1 - z) * 2 + y
    staged, locals_ = [], []
    for index, (shard, stage) in enumerate(zip(shards, stages)):
        copy = pltpu.make_async_copy(shard, stage, stage_sem.at[index])
        copy.start()
        staged.append(copy)
    copy = pltpu.make_async_copy(small, small_whole.at[w], local_sem.at[n_weights])
    copy.start()
    locals_.append(copy)
    greet((by_x, by_y, by_z, by_core))
    sent = [send(small, small_whole.at[w], small_sems.at[0], small_sems.at[1], by_x)]

    def part(chunk, side, piece, start, count):
        tensor, first, rows = plan[chunk]
        size = rows // 8
        half = shards[tensor].shape[0]
        at = side * half + first + piece * size + start
        return wholes[tensor].at[pl.ds(pl.multiple_of(at, 8), count)]

    steps = {}
    for chunk, (tensor, first, rows) in enumerate(plan):
        size = rows // 8
        src = shards[tensor].at[pl.ds(pl.multiple_of(first + mine * size, 8), size)]
        steps[chunk, 0] = send(
            src, part(chunk, w, mine, 0, size), send_sem.at[0, chunk], recv_sem.at[0, chunk], by_x
        )

    for index, (stage, whole) in enumerate(zip(stages, wholes)):
        rows = stage.shape[0]
        staged[index].wait()
        copy = pltpu.make_async_copy(
            stage, whole.at[pl.ds(pl.multiple_of(w * rows, rows), rows)], local_sem.at[index]
        )
        copy.start()
        locals_.append(copy)

    def second(chunk):
        size = plan[chunk][2] // 8
        steps[chunk, 0].wait_recv()
        for kind, peer in ((1, by_y), (2, by_z)):
            ref = part(chunk, o, mine, 0, size)
            steps[chunk, kind] = send(
                ref, ref, send_sem.at[kind, chunk], recv_sem.at[kind, chunk], peer
            )

    def third(chunk):
        size = plan[chunk][2] // 8
        steps[chunk, 1].wait_recv()
        steps[chunk, 2].wait_recv()
        ref = part(chunk, o, from_z, 0, size // 2)
        steps[chunk, 3] = send(ref, ref, send_sem.at[3, chunk], recv_sem.at[3, chunk], by_y)
        ref = part(chunk, o, from_y, size // 2, size // 2)
        steps[chunk, 4] = send(ref, ref, send_sem.at[4, chunk], recv_sem.at[4, chunk], by_z)

    def fourth(chunk):
        size = plan[chunk][2] // 8
        steps[chunk, 3].wait_recv()
        steps[chunk, 4].wait_recv()
        ref = part(chunk, o, core * 4, 0, 4 * size)
        steps[chunk, 5] = send(ref, ref, send_sem.at[5, chunk], recv_sem.at[5, chunk], by_core)

    count = len(plan)
    for turn in range(count + 2):
        if turn < count:
            second(turn)
        if 0 <= turn - 1 < count:
            third(turn - 1)
        if 0 <= turn - 2 < count:
            fourth(turn - 2)
    for chunk in range(count):
        steps[chunk, 5].wait_recv()
        for kind in range(6):
            steps[chunk, kind].wait_send()
    sent[0].wait()
    for copy in locals_:
        copy.wait()


def gather_weights(shards, small):
    plan = []
    for index, shard in enumerate(shards):
        rows = shard.shape[0]
        parts = max(1, shard.shape[0] * shard.shape[1] // (1024 * 1024))
        for piece in range(parts):
            plan.append((index, piece * (rows // parts), rows // parts))
    count = len(shards)
    shapes = [jax.ShapeDtypeStruct((2 * s.shape[0],) + s.shape[1:], s.dtype) for s in shards]
    shapes.append(jax.ShapeDtypeStruct((2,) + small.shape, small.dtype))
    anywhere = pl.BlockSpec(memory_space=pl.ANY)
    return pl.pallas_call(
        functools.partial(gather_kernel, plan, count),
        out_shape=shapes,
        in_specs=[anywhere] * (count + 1),
        out_specs=[anywhere] * (count + 1),
        scratch_shapes=[pltpu.VMEM(s.shape, s.dtype) for s in shards]
        + [
            pltpu.SemaphoreType.DMA((6, len(plan))),
            pltpu.SemaphoreType.DMA((6, len(plan))),
            pltpu.SemaphoreType.DMA((2,)),
            pltpu.SemaphoreType.DMA((count + 1,)),
            pltpu.SemaphoreType.DMA((count,)),
        ],
        compiler_params=pltpu.CompilerParams(
            collective_id=0, has_side_effects=True, vmem_limit_bytes=VMEM_BYTES
        ),
        name="gather_weights",
    )(*shards, small)


def plane_peers(c, w, count):
    return [(lax.rem(c + step, count), w) for step in range(1, count)]


def pack_three(first, second, third, row, pair, out):
    cols = pl.ds(pair * 128, 128)
    a, b, d = (ref[pl.ds(row, BLK), cols] for ref in (first, second, third))
    half = BLK // 2
    for head in range(2):
        lane = slice(head * HD, head * HD + HD)
        out[2 * pair + head, 0:BLK, :] = jnp.concatenate([a[:, lane], b[:, lane]], axis=1)
        out[2 * pair + head, BLK : BLK + half, :] = jnp.concatenate(
            [d[:half, lane], d[half:, lane]], axis=1
        )


def unpack_fold(block):
    return jnp.concatenate([block[:, :HD], block[:, HD:]], axis=0)


def fold(rows):
    half = rows.shape[0] // 2
    return jnp.concatenate([rows[:half], rows[half:]], axis=1)


def all_bytes(ref, sem, peers):
    view = ref.at[pl.ds(0, peers)]
    return pltpu.make_async_copy(view, view, sem)


def attend_kernel(
    heads,
    lens_ref,
    slot_ref,
    block_ref,
    q_ref,
    k_ref,
    v_ref,
    a_ref,
    kept_ref,
    lse_ref,
    *scratch,
):
    in_buf = scratch[:MB]
    out_buf, back_out, back_in, q_s, k_s, v_s, a_s = scratch[MB : MB + 7]
    send_sem, recv_sem, back_send, back_recv, keep_sem = scratch[MB + 7 :]
    c, w = lax.axis_index("ctx"), lax.axis_index("wsh")
    peers = plane_peers(c, w, heads)
    greet(peers)
    blocks = heads
    for m in range(MB):
        for pair in range(heads // 2):
            pack_three(q_ref, k_ref, v_ref, m * BLK, pair, out_buf.at[m])
        for peer in peers:
            send(
                out_buf.at[m, peer[0]], in_buf[m].at[c], send_sem.at[m], recv_sem.at[m], peer
            )
        in_buf[m][c] = out_buf[m, c]
    for m in range(MB):
        all_bytes(in_buf[m], recv_sem.at[m], heads - 1).wait()
        keep = pltpu.make_async_copy(in_buf[m], kept_ref.at[m], keep_sem.at[m])
        keep.start()
        for b in range(blocks):
            got = in_buf[m][slot_ref[m, b]]
            q_s[b * BLK : (b + 1) * BLK, :] = got[:BLK, :HD]
            k_s[b * BLK : (b + 1) * BLK, :] = got[:BLK, HD:]
            v_s[b * BLK : (b + 1) * BLK, :] = unpack_fold(got[BLK:])
        span = BPS * BLK
        for s in range(blocks // BPS):
            rows = slice(s * span, (s + 1) * span)
            scores = lax.dot_general(
                k_s[rows, :], q_s[rows, :], (((1,), (1,)), ((), ())), preferred_element_type=F32
            ) * (1.0 / math.sqrt(HD))
            place = lax.broadcasted_iota(jnp.int32, scores.shape, 0)
            scores = jnp.where(place < lens_ref[m, s], scores, NEG_FILL)
            top = jnp.max(scores, axis=0, keepdims=True)
            weights = jnp.exp(scores - top)
            total = jnp.sum(weights, axis=0, keepdims=True)
            out_t = lax.dot_general(
                v_s[rows, :],
                weights.astype(BF16),
                (((0,), (0,)), ((), ())),
                preferred_element_type=F32,
            )
            a_s[s * BPS : (s + 1) * BPS] = (out_t / total).T.reshape(BPS, BLK, HD)
            lse_ref[pl.ds(m * (blocks // BPS) + s, 1), :] = top + jnp.log(total)
        for t in range(blocks):
            back_out[m, t] = fold(a_s[block_ref[m, t]]).astype(BF16)
        for peer in peers:
            send(
                back_out.at[m, peer[0]], back_in.at[m, c], back_send.at[m], back_recv.at[m], peer
            )
        back_in[m, c] = back_out[m, c]
    for m in range(MB):
        all_bytes(back_in.at[m], back_recv.at[m], heads - 1).wait()
        for pair in range(heads // 2):
            a_ref[m * BLK : (m + 1) * BLK, pair * 128 : (pair + 1) * 128] = jnp.concatenate(
                [unpack_fold(back_in[m, 2 * pair]), unpack_fold(back_in[m, 2 * pair + 1])], axis=1
            )
    for m in range(MB):
        all_bytes(out_buf.at[m], send_sem.at[m], heads - 1).wait()
        all_bytes(back_out.at[m], back_send.at[m], heads - 1).wait()
        pltpu.make_async_copy(in_buf[m], kept_ref.at[m], keep_sem.at[m]).wait()


def attend(lens, slot_of, block_of, q, k, v, heads):
    vmem, smem = pl.BlockSpec(memory_space=pltpu.VMEM), pl.BlockSpec(memory_space=pltpu.SMEM)
    rows, width = q.shape
    pack_rows = BLK + BLK // 2
    span = BPS * BLK
    return pl.pallas_call(
        functools.partial(attend_kernel, heads),
        out_shape=[
            jax.ShapeDtypeStruct((rows, width), BF16),
            jax.ShapeDtypeStruct((MB, heads, pack_rows, 128), BF16),
            jax.ShapeDtypeStruct((8, span), F32),
        ],
        in_specs=[smem] * 3 + [vmem] * 3,
        out_specs=[vmem, pl.BlockSpec(memory_space=pl.ANY), vmem],
        scratch_shapes=[pltpu.VMEM((heads, pack_rows, 128), BF16)] * MB
        + [
            pltpu.VMEM((MB, heads, pack_rows, 128), BF16),
            pltpu.VMEM((MB, heads, BLK // 2, 128), BF16),
            pltpu.VMEM((MB, heads, BLK // 2, 128), BF16),
            pltpu.VMEM((heads * BLK, HD), BF16),
            pltpu.VMEM((heads * BLK, HD), BF16),
            pltpu.VMEM((heads * BLK, HD), BF16),
            pltpu.VMEM((heads, BLK, HD), F32),
            pltpu.SemaphoreType.DMA((MB,)),
            pltpu.SemaphoreType.DMA((MB,)),
            pltpu.SemaphoreType.DMA((MB,)),
            pltpu.SemaphoreType.DMA((MB,)),
            pltpu.SemaphoreType.DMA((MB,)),
        ],
        compiler_params=pltpu.CompilerParams(
            collective_id=1, has_side_effects=True, vmem_limit_bytes=VMEM_BYTES
        ),
        name="attend",
    )(lens, slot_of, block_of, q, k, v)


def attend_back_kernel(heads, *refs):
    lens_ref, slot_ref, block_ref, da_ref, kept_ref, lse_ref = refs[:6]
    x_ref, a_ref, n_ref, g_ref, do_ref, du_ref, dm_ref = refs[6:13]
    dq_ref, dk_ref, dv_ref = refs[13:16]
    x_all, a_all, n_all, g_all, do_all, du_all, dm_all, dqkv_all = refs[16:24]
    in_buf = refs[24 : 24 + MB]
    out_buf, back_out, back_in = refs[24 + MB : 27 + MB]
    q_s, k_s, v_s, a_s, dq_s, dk_s, dv_s = refs[27 + MB : 34 + MB]
    send_sem, recv_sem, back_send, back_recv, mate_send, mate_recv, own_sem = refs[34 + MB :]
    c, w = lax.axis_index("ctx"), lax.axis_index("wsh")
    core = bit_of(c, 1)
    mate = (flip(c, 1), w)
    peers = plane_peers(c, w, heads)
    blocks = heads
    rows_own = da_ref.shape[0]
    greet(peers)

    place = pl.ds(pl.multiple_of(core * rows_own, rows_own), rows_own)
    moves = []

    def share(src, dst, lanes):
        for first, size, to, per_core in lanes:
            index = len(moves)
            step = size if per_core else 0
            own_from = pl.ds(pl.multiple_of(first + core * step, 128), size)
            mate_from = pl.ds(pl.multiple_of(first + (1 - core) * step, 128), size)
            spot = dst.at[place, pl.ds(to, size)]
            own = pltpu.make_async_copy(src.at[:, own_from], spot, own_sem.at[index])
            own.start()
            gone = send(
                src.at[:, mate_from], spot, mate_send.at[index], mate_recv.at[index], mate
            )
            moves.append((own, gone))

    width = da_ref.shape[1]
    hidden = g_ref.shape[1]
    for m in range(MB):
        row = slice(m * BLK, (m + 1) * BLK)
        for pair in range(heads // 2):
            both = da_ref[row, pair * 128 : (pair + 1) * 128]
            for head in range(2):
                out_buf[m, 2 * pair + head] = fold(both[:, head * HD : (head + 1) * HD])
        for peer in peers:
            send(out_buf.at[m, peer[0]], in_buf[m].at[c], send_sem.at[m], recv_sem.at[m], peer)
        in_buf[m][c] = out_buf[m, c]
    for src, dst in ((x_ref, x_all), (a_ref, a_all), (n_ref, n_all), (dm_ref, dm_all)):
        share(src, dst, ((0, width, 0, False),))
    share(do_ref, do_all, ((0, width // 2, 0, True),))
    share(du_ref, du_all, ((0, hidden // 2, 0, True),))
    share(g_ref, g_all, ((0, hidden // 4, 0, True), (hidden // 2, hidden // 4, hidden // 4, True)))
    for m in range(MB):
        all_bytes(in_buf[m], recv_sem.at[m], heads - 1).wait()
        for b in range(blocks):
            slot = slot_ref[m, b]
            got = kept_ref[m, slot]
            rows = slice(b * BLK, (b + 1) * BLK)
            q_s[rows, :] = got[:BLK, :HD]
            k_s[rows, :] = got[:BLK, HD:]
            v_s[rows, :] = unpack_fold(got[BLK:])
            a_s[rows, :] = unpack_fold(in_buf[m][slot])
        span = BPS * BLK
        for s in range(blocks // BPS):
            rows = slice(s * span, (s + 1) * span)
            qq, kk, vv, dd = q_s[rows, :], k_s[rows, :], v_s[rows, :], a_s[rows, :]
            scale = 1.0 / math.sqrt(HD)
            minor = (((1,), (1,)), ((), ()))
            scores = lax.dot_general(kk, qq, minor, preferred_element_type=F32) * scale
            spot = lax.broadcasted_iota(jnp.int32, scores.shape, 0)
            total = lse_ref[pl.ds(m * (blocks // BPS) + s, 1), :]
            probs = jnp.exp(jnp.where(spot < lens_ref[m, s], scores - total, NEG_FILL))
            dp = lax.dot_general(vv, dd, minor, preferred_element_type=F32)
            both = probs * dp
            delta = jnp.sum(both, axis=0, keepdims=True)
            ds = (both - probs * delta).astype(BF16)
            here = slice(s * BPS, (s + 1) * BPS)
            split = (BPS, BLK, HD)
            dv = jnp.dot(probs.astype(BF16), dd, preferred_element_type=F32)
            dv_s[here] = dv.reshape(split)
            dk_s[here] = (jnp.dot(ds, qq, preferred_element_type=F32) * scale).reshape(split)
            dq_t = lax.dot_general(kk, ds, (((0,), (0,)), ((), ())), preferred_element_type=F32)
            dq_s[here] = (dq_t.T * scale).reshape(split)
        for t in range(blocks):
            at = block_ref[m, t]
            back_out[m, t, 0:BLK, :] = jnp.concatenate([dq_s[at], dk_s[at]], axis=1).astype(BF16)
            back_out[m, t, BLK:, :] = fold(dv_s[at]).astype(BF16)
        for peer in peers:
            send(
                back_out.at[m, peer[0]], back_in.at[m, c], back_send.at[m], back_recv.at[m], peer
            )
        back_in[m, c] = back_out[m, c]
    for m in range(MB):
        all_bytes(back_in.at[m], back_recv.at[m], heads - 1).wait()
        row = slice(m * BLK, (m + 1) * BLK)
        for pair in range(heads // 2):
            lanes = slice(pair * 128, (pair + 1) * 128)
            one, two = back_in[m, 2 * pair], back_in[m, 2 * pair + 1]
            dq_ref[row, lanes] = jnp.concatenate([one[:BLK, :HD], two[:BLK, :HD]], axis=1)
            dk_ref[row, lanes] = jnp.concatenate([one[:BLK, HD:], two[:BLK, HD:]], axis=1)
            dv_ref[row, lanes] = jnp.concatenate(
                [unpack_fold(one[BLK:]), unpack_fold(two[BLK:])], axis=1
            )
    for index, ref in enumerate((dq_ref, dk_ref, dv_ref)):
        half = width // 2
        spot = dqkv_all.at[place, pl.ds(index * half, half)]
        number = len(moves)
        own_from = pl.ds(pl.multiple_of(core * half, 128), half)
        mate_from = pl.ds(pl.multiple_of((1 - core) * half, 128), half)
        own = pltpu.make_async_copy(ref.at[:, own_from], spot, own_sem.at[number])
        own.start()
        gone = send(ref.at[:, mate_from], spot, mate_send.at[number], mate_recv.at[number], mate)
        moves.append((own, gone))
    for m in range(MB):
        all_bytes(out_buf.at[m], send_sem.at[m], heads - 1).wait()
        all_bytes(back_out.at[m], back_send.at[m], heads - 1).wait()
    for own, gone in moves:
        own.wait()
        gone.wait()


def attend_back(lens, slot_of, block_of, da, kept, lse, x, a, n1, g, do, du, dm, heads):
    vmem, smem = pl.BlockSpec(memory_space=pltpu.VMEM), pl.BlockSpec(memory_space=pltpu.SMEM)
    anywhere = pl.BlockSpec(memory_space=pl.ANY)
    rows, width = da.shape
    hidden = g.shape[1]
    pack_rows = BLK + BLK // 2
    both = 2 * rows
    moves = 11
    shape = lambda *dims: jax.ShapeDtypeStruct(dims, BF16)
    return pl.pallas_call(
        functools.partial(attend_back_kernel, heads),
        out_shape=[shape(rows, width)] * 3
        + [
            shape(both, width),
            shape(both, width),
            shape(both, width),
            shape(both, hidden // 2),
            shape(both, width // 2),
            shape(both, hidden // 2),
            shape(both, width),
            shape(both, 3 * width // 2),
        ],
        in_specs=[smem] * 3 + [vmem] * 10,
        out_specs=[vmem] * 3 + [anywhere] * 8,
        scratch_shapes=[pltpu.VMEM((heads, BLK // 2, 128), BF16)] * MB
        + [
            pltpu.VMEM((MB, heads, BLK // 2, 128), BF16),
            pltpu.VMEM((MB, heads, pack_rows, 128), BF16),
            pltpu.VMEM((MB, heads, pack_rows, 128), BF16),
        ]
        + [pltpu.VMEM((heads * BLK, HD), BF16)] * 4
        + [pltpu.VMEM((heads, BLK, HD), F32)] * 3
        + [pltpu.SemaphoreType.DMA((MB,))] * 4
        + [pltpu.SemaphoreType.DMA((moves,))] * 3,
        compiler_params=pltpu.CompilerParams(
            collective_id=2, has_side_effects=True, vmem_limit_bytes=VMEM_BYTES
        ),
        name="attend_back",
    )(lens, slot_of, block_of, da, kept, lse, x, a, n1, g, do, du, dm)


CHUNKS = 2


def reduce_kernel(ga1_ref, ga2_ref, gb_ref, gc_ref, vec_ref, *refs):
    o_a, o_b, o_c, vec_out = refs[:4]
    s_a, s_b, s_c = refs[4:7]
    r_bufs = (refs[7:11], refs[11:15], refs[15:19])
    v_recv, v_sum = refs[19:21]
    load_sem, rs_send, rs_recv, ag_send, ag_recv, v_send_sem, v_recv_sem, own_sem = refs[21:]
    c, x = lax.axis_index("ctx"), lax.axis_index("wsh")
    core, y, z, zz = bit_of(c, 1), bit_of(c, 2), bit_of(c, 4), bit_of(c, 8)
    by_x, by_y, by_z = (c, 1 - x), (flip(c, 2), x), (flip(c, 4), x)
    by_zz, by_core = (flip(c, 8), x), (flip(c, 1), x)
    shards = 8
    lanes1 = ga1_ref.shape[3]
    lanes2 = ga2_ref.shape[3]
    loads = [
        pltpu.make_async_copy(ga1_ref, s_a.at[:, :, :, pl.ds(0, lanes1)], load_sem.at[0]),
        pltpu.make_async_copy(ga2_ref, s_a.at[:, :, :, pl.ds(lanes1, lanes2)], load_sem.at[1]),
        pltpu.make_async_copy(gb_ref, s_b, load_sem.at[2]),
        pltpu.make_async_copy(gc_ref, s_c, load_sem.at[3]),
    ]
    for load in loads:
        load.start()
    greet((by_x, by_y, by_z, by_zz, by_core))
    vec_steps = [
        send(vec_ref.at[1 - x], v_recv.at[0], v_send_sem.at[0], v_recv_sem.at[0], by_x)
    ]

    def vec_next(step, peer):
        vec_steps[step].wait_recv()
        before = vec_ref[x] if step == 0 else v_sum[step - 1]
        v_sum[step] = before + v_recv[step]
        if peer is not None:
            vec_steps.append(
                send(
                    v_sum.at[step],
                    v_recv.at[step + 1],
                    v_send_sem.at[step + 1],
                    v_recv_sem.at[step + 1],
                    peer,
                )
            )

    for load in loads:
        load.wait()
    yz, zy = y * 4 + z * 2, z * 4 + y * 2
    plans = (
        (
            (by_x, 1 - x, x, 0, 0, 8),
            (by_y, x, x, (1 - y) * 4, y * 4, 4),
            (by_z, x, x, y * 4 + (1 - z) * 2, yz, 2),
            (by_zz, x, x, yz + 1 - zz, yz + zz, 1),
        ),
        (
            (by_y, None, None, (1 - y) * 4, y * 4, 4),
            (by_z, None, None, y * 4 + (1 - z) * 2, yz, 2),
            (by_x, 1 - x, x, yz, yz, 2),
            (by_zz, x, x, yz + 1 - zz, yz + zz, 1),
        ),
        (
            (by_z, None, None, (1 - z) * 4, z * 4, 4),
            (by_x, 1 - x, x, z * 4, z * 4, 4),
            (by_y, x, x, z * 4 + (1 - y) * 2, zy, 2),
            (by_zz, x, x, zy + 1 - zz, zy + zz, 1),
        ),
    )
    sums = (s_a, s_b, s_c)
    outs = (o_a, o_b, o_c)
    flights = {}

    def chunk_rows(part, chunk):
        rows = sums[part].shape[2] // CHUNKS
        return pl.ds(chunk * rows, rows)

    def reduce_send(part, step, chunk):
        peer, side, _, first, _, count = plans[part][step]
        rows = chunk_rows(part, chunk)
        if side is None:
            src = sums[part].at[:, pl.ds(first, count), rows]
            dst = r_bufs[part][step].at[:, :, rows]
        else:
            src = sums[part].at[side, pl.ds(first, count), rows]
            dst = r_bufs[part][step].at[0, :, rows]
        flights[part, step, chunk] = send(
            src, dst, rs_send.at[part, step, chunk], rs_recv.at[part, step, chunk], peer
        )

    def reduce_add(part, step, chunk):
        _, _, side, _, first, count = plans[part][step]
        rows = chunk_rows(part, chunk)
        flights[part, step, chunk].wait_recv()
        total, fresh = sums[part], r_bufs[part][step]
        sides = ((0, 0), (1, 1)) if side is None else ((side, 0),)
        for here, there in sides:

            def body(index, carry):
                spot = first + index
                total[here, spot, rows] = (
                    total[here, spot, rows].astype(F32) + fresh[there, index, rows].astype(F32)
                ).astype(BF16)
                return carry

            lax.fori_loop(0, count, body, 0)

    for chunk in range(CHUNKS):
        for part in range(3):
            reduce_send(part, 0, chunk)
    vec_peers = (by_y, by_z, by_zz, by_core, None)
    for step in range(1, 4):
        vec_next(step - 1, vec_peers[step - 1])
        for chunk in range(CHUNKS):
            for part in range(3):
                reduce_add(part, step - 1, chunk)
                reduce_send(part, step, chunk)
    gathers = (
        ((by_zz, yz + zz, 1), (by_z, yz, 2), (by_y, y * 4, 4)),
        ((by_zz, yz + zz, 1), (by_z, yz, 2), (by_y, y * 4, 4)),
        ((by_zz, zy + zz, 1), (by_y, zy, 2), (by_z, z * 4, 4)),
    )
    news = (
        (yz + 1 - zz, y * 4 + (1 - z) * 2, (1 - y) * 4),
        (yz + 1 - zz, y * 4 + (1 - z) * 2, (1 - y) * 4),
        (zy + 1 - zz, z * 4 + (1 - y) * 2, (1 - z) * 4),
    )
    owns, spread = [], {}
    vec_next(3, by_core)
    for chunk in range(CHUNKS):
        for part in range(3):
            reduce_add(part, 3, chunk)
            rows = chunk_rows(part, chunk)
            peer, first, count = gathers[part][0]
            src = sums[part].at[x, pl.ds(first, 1), rows]
            dst = outs[part].at[core, pl.ds(first, 1), rows]
            own = pltpu.make_async_copy(src, dst, own_sem.at[part, chunk])
            own.start()
            owns.append(own)
            sem = lambda kind: (ag_send.at[part, kind, chunk], ag_recv.at[part, kind, chunk])
            spread[part, 0, chunk] = send(src, dst, *sem(0), peer)
            spread[part, 3, chunk] = send(src, dst, *sem(3), by_core)
    vec_next(4, None)
    vec_out[...] = v_sum[4]
    for own in owns:
        own.wait()
    for step in range(1, 4):
        for chunk in range(CHUNKS):
            for part in range(3):
                rows = chunk_rows(part, chunk)
                spread[part, step - 1, chunk].wait_recv()
                sem = lambda kind: (ag_send.at[part, kind, chunk], ag_recv.at[part, kind, chunk])
                if step < 3:
                    peer, first, count = gathers[part][step]
                    ref = outs[part].at[core, pl.ds(first, count), rows]
                    spread[part, step, chunk] = send(ref, ref, *sem(step), peer)
                fresh = outs[part].at[
                    core, pl.ds(news[part][step - 1], gathers[part][step - 1][2]), rows
                ]
                spread[part, 3 + step, chunk] = send(fresh, fresh, *sem(3 + step), by_core)
    for key, flight in spread.items():
        if key[1] >= 3:
            flight.wait_recv()
        flight.wait_send()
    for flight in flights.values():
        flight.wait_send()
    for flight in vec_steps:
        flight.wait_send()


def reduce_grads(ga1, ga2, gb, gc, vec):
    vmem, anywhere = pl.BlockSpec(memory_space=pltpu.VMEM), pl.BlockSpec(memory_space=pl.ANY)
    lanes = ga1.shape[3] + ga2.shape[3]
    a_shape = ga1.shape[:3] + (lanes,)
    b_shape, c_shape = gb.shape, gc.shape
    scratch = [pltpu.VMEM(s, BF16) for s in (a_shape, b_shape, c_shape)]
    halves = (
        ((1, 8), (1, 4), (1, 2), (1, 1)),
        ((2, 4), (2, 2), (1, 2), (1, 1)),
        ((2, 4), (1, 4), (1, 2), (1, 1)),
    )
    for shape, steps in zip((a_shape, b_shape, c_shape), halves):
        scratch += [pltpu.VMEM(lead + shape[2:], BF16) for lead in steps]
    scratch += [
        pltpu.VMEM((5,) + vec.shape[1:], F32),
        pltpu.VMEM((5,) + vec.shape[1:], F32),
        pltpu.SemaphoreType.DMA((4,)),
        pltpu.SemaphoreType.DMA((3, 4, CHUNKS)),
        pltpu.SemaphoreType.DMA((3, 4, CHUNKS)),
        pltpu.SemaphoreType.DMA((3, 7, CHUNKS)),
        pltpu.SemaphoreType.DMA((3, 7, CHUNKS)),
        pltpu.SemaphoreType.DMA((5,)),
        pltpu.SemaphoreType.DMA((5,)),
        pltpu.SemaphoreType.DMA((3, CHUNKS)),
    ]
    return pl.pallas_call(
        reduce_kernel,
        out_shape=[
            jax.ShapeDtypeStruct(a_shape, BF16),
            jax.ShapeDtypeStruct(b_shape, BF16),
            jax.ShapeDtypeStruct(c_shape, BF16),
            jax.ShapeDtypeStruct(vec.shape[1:], F32),
        ],
        in_specs=[anywhere] * 4 + [vmem],
        out_specs=[anywhere] * 3 + [vmem],
        scratch_shapes=scratch,
        compiler_params=pltpu.CompilerParams(
            collective_id=3, has_side_effects=True, vmem_limit_bytes=VMEM_BYTES
        ),
        name="reduce_grads",
    )(ga1, ga2, gb, gc, vec)


def norm_parts(summed):
    row_mean = jnp.mean(summed, axis=-1, keepdims=True)
    centred = summed - row_mean
    row_var = jnp.mean(centred * centred, axis=-1, keepdims=True)
    scale = lax.rsqrt(row_var + EPSILON)
    return centred * scale, scale


def norm_back(grad, unit, scale, gain):
    inner = grad * gain
    mean_one = jnp.mean(inner, axis=-1, keepdims=True)
    mean_two = jnp.mean(inner * unit, axis=-1, keepdims=True)
    return scale * (inner - mean_one - unit * mean_two)


def dot(a, b, dims):
    return lax.dot_general(a, b, (dims, ((), ())), preferred_element_type=F32)


ROW_COL, COL_COL, ROW_ROW = ((1,), (0,)), ((1,), (1,)), ((0,), (0,))


def per_device_heads(tokens, cotangent, lengths, dealing, *params):
    rows_in = tokens.shape[2]
    width = tokens.shape[3]
    rows = MB * rows_in
    weights, vectors = params[:6], params[6:]
    sizes = [item.shape[0] for item in vectors]
    small = jnp.concatenate(vectors).reshape(-1, 128)
    *wholes, small_whole = gather_weights(weights, small)
    query_w, key_w, value_w, out_w, up_w, down_w = wholes
    flat = small_whole.reshape(2, -1).astype(F32)
    spots = [sum(sizes[:i]) for i in range(len(sizes) + 1)]
    bias_query, bias_value, bias_out, bias_up, bias_down, gain_one, shift_one, gain_two, shift_two = (
        flat[:, spots[i] : spots[i + 1]].reshape(1, -1) for i in range(len(sizes))
    )
    x = tokens.reshape(rows, width)
    lens = lengths[0]
    block_of = dealing[0]
    slot_of = jnp.argsort(block_of, axis=1).astype(jnp.int32)
    q = (dot(x, query_w, ROW_COL) + bias_query).astype(BF16)
    k = dot(x, key_w, ROW_COL).astype(BF16)
    v = (dot(x, value_w, ROW_COL) + bias_value).astype(BF16)
    a, kept, lse = attend(lens, slot_of, block_of, q, k, v, HEADS)

    h_one = x.astype(F32) + (dot(a, out_w, ROW_COL) + bias_out)
    unit_one, scale_one = norm_parts(h_one)
    n_one = unit_one * gain_one + shift_one
    n_low = n_one.astype(BF16)
    u = dot(n_low, up_w, ROW_COL) + bias_up
    act, act_back = jax.vjp(gelu_exact, u)
    g = act.astype(BF16)
    h_two = n_one + (dot(g, down_w, ROW_COL) + bias_down)
    unit_two, scale_two = norm_parts(h_two)
    output = (unit_two * gain_two + shift_two).astype(BF16)

    cot = cotangent.reshape(rows, width).astype(F32)
    dh_two = norm_back(cot, unit_two, scale_two, gain_two)
    dm = dh_two.astype(BF16)
    (du_full,) = act_back(dot(dm, down_w, COL_COL))
    du = du_full.astype(BF16)
    dn = dot(du, up_w, COL_COL) + dh_two
    dh_one = norm_back(dn, unit_one, scale_one, gain_one)
    do = dh_one.astype(BF16)
    da = dot(do, out_w, COL_COL).astype(BF16)

    dq, dk, dv, x_all, a_all, n_all, g_all, do_all, du_all, dm_all, dqkv_all = attend_back(
        lens, slot_of, block_of, da, kept, lse, x, a, n_low, g, do, du, dm, HEADS
    )
    total = lambda item: jnp.sum(item.astype(F32), axis=0)
    vec = [
        total(dq),
        total(dv),
        total(do),
        total(du),
        total(dm),
        total(dn * unit_one),
        total(dn),
        total(cot * unit_two),
        total(cot),
    ]
    vec = jnp.concatenate([item.reshape(2, -1) for item in vec], axis=1).reshape(2, -1, 128)
    ga1 = dot(x_all, dqkv_all, ROW_ROW).astype(BF16).reshape(2, 8, -1, dqkv_all.shape[1])
    ga2 = dot(a_all, do_all, ROW_ROW).astype(BF16).reshape(2, 8, -1, do_all.shape[1])
    gb = dot(n_all, du_all, ROW_ROW).astype(BF16).reshape(2, 8, -1, du_all.shape[1])
    gc = dot(g_all, dm_all, ROW_ROW).astype(BF16).reshape(2, 8, -1, dm_all.shape[1])
    o_a, o_b, o_c, vec_sum = reduce_grads(ga1, ga2, gb, gc, vec)
    grad_rows = (
        dh_one + dot(dq, query_w, COL_COL) + dot(dk, key_w, COL_COL) + dot(dv, value_w, COL_COL)
    )
    grad_tokens = grad_rows.astype(BF16)
    half = width // 2
    o_a = o_a.reshape(2, -1, o_a.shape[3])
    square = [
        jnp.concatenate([o_a[0, :, i * half : (i + 1) * half], o_a[1, :, i * half : (i + 1) * half]], axis=1)
        for i in range(4)
    ]
    o_b = o_b.reshape(2, -1, o_b.shape[3])
    up = jnp.concatenate([o_b[0], o_b[1]], axis=1)
    down = o_c.reshape(-1, width)
    vec_sum = vec_sum.reshape(-1)
    ends = [vec_sum[spots[i] : spots[i + 1]] for i in range(len(sizes))]
    shape = (1, MB, rows_in, width)
    return (
        (output.reshape(shape), grad_tokens.reshape(shape))
        + tuple(item.astype(F32) for item in square + [up, down])
        + tuple(ends)
    )


def solution(mesh):
    placed = (
        P("wsh", None, "ctx", None),
        P("wsh", None, "ctx", None),
        P("wsh", None, None),
        P("wsh", None, None),
        P("wsh", None),
        P("wsh", None),
        P("wsh", None),
        P("wsh", None),
        P("wsh", None),
        P("wsh", None),
        P("wsh"),
        P("wsh"),
        P("wsh"),
        P("wsh"),
        P("wsh"),
        P("wsh"),
        P("wsh"),
        P("wsh"),
        P("wsh"),
    )
    by_heads = mesh.shape["ctx"] == HEADS and mesh.shape["wsh"] == 2
    return jax.shard_map(
        per_device_heads if by_heads else per_device,
        mesh=mesh,
        in_specs=placed,
        out_specs=(
            P("wsh", None, "ctx", None),
            P("wsh", None, "ctx", None),
            P("wsh", None),
            P("wsh", None),
            P("wsh", None),
            P("wsh", None),
            P("wsh", None),
            P("wsh", None),
            P("wsh"),
            P("wsh"),
            P("wsh"),
            P("wsh"),
            P("wsh"),
            P("wsh"),
            P("wsh"),
            P("wsh"),
            P("wsh"),
        ),
        check_vma=False,
    )
```

```python
import functools
import math

import jax
import jax.numpy as jnp
from jax import lax
from jax.experimental import pallas as pl
from jax.experimental.pallas import tpu as pltpu
from jax.sharding import PartitionSpec as P

HEADS = 16
BPS = 8
MB = 3
BLK = 64


EPSILON = 1e-12
NEG_FILL = -1e30


def as_sent(x):
    return jax.tree.map(lambda a: a.astype(jnp.bfloat16) if a.dtype == jnp.float32 else a, x)


def layer_norm(summed, gain_vec, shift_vec):
    row_mean = jnp.mean(summed, axis=-1, keepdims=True)
    centred = summed - row_mean
    row_var = jnp.mean(centred * centred, axis=-1, keepdims=True)
    return centred * lax.rsqrt(row_var + EPSILON) * gain_vec + shift_vec


def gelu_exact(values):
    return jax.nn.gelu(values, approximate=False)


def row_labels(dealt_order, seq_lengths):
    blocks_of_rows = jnp.repeat(dealt_order, BLK)
    within = jnp.tile(jnp.arange(BLK, dtype=jnp.int32), dealt_order.shape[0])
    seq_ids = blocks_of_rows // BPS
    places = blocks_of_rows % BPS * BLK + within
    numbers = jnp.arange(seq_lengths.shape[0], dtype=jnp.int32)
    seq_bound = jnp.sum(
        jnp.where(seq_ids[:, None] == numbers[None, :], seq_lengths[None, :], 0), axis=1
    )
    return (seq_ids, places < seq_bound)


def blockwise(carried, total_rows, step_rows, visit_block):
    return lax.fori_loop(
        0,
        total_rows // step_rows,
        lambda turn_index, running: visit_block(running, turn_index * step_rows),
        carried,
    )


def masked_scores(query_blk, key_blk, query_seq, key_seq, key_valid, scale_factor):
    allowed = (query_seq[:, None] == key_seq[None, :]) & key_valid[None, :]
    scores = (
        jnp.einsum("qhd,khd->hqk", query_blk, key_blk, preferred_element_type=jnp.float32)
        * scale_factor
    )
    return (jnp.where(allowed[None], scores, NEG_FILL), allowed[None].astype(jnp.float32))


def attention_grads(
    query_blk,
    grad_blk,
    key_blk,
    value_blk,
    query_seq,
    key_seq,
    key_valid,
    row_total,
    row_delta,
    scale_factor,
):
    scores, allowed = masked_scores(query_blk, key_blk, query_seq, key_seq, key_valid, scale_factor)
    probs = jnp.exp(scores - row_total[:, :, None]) * allowed
    grad_probs = jnp.einsum("qhd,khd->hqk", grad_blk, value_blk, preferred_element_type=jnp.float32)
    grad_scores = (probs * (grad_probs - row_delta[:, :, None])).astype(jnp.bfloat16)
    return (probs.astype(jnp.bfloat16), grad_scores)


def gather_params(params):
    return (
        lax.all_gather(params[0], "wsh", axis=0, tiled=True),
        lax.all_gather(params[1], "wsh", axis=0, tiled=True),
        lax.all_gather(params[2], "wsh", axis=0, tiled=True),
        lax.all_gather(params[3], "wsh", axis=0, tiled=True),
        lax.all_gather(params[4], "wsh", axis=0, tiled=True),
        lax.all_gather(params[5], "wsh", axis=0, tiled=True),
        lax.all_gather(params[6], "wsh", axis=0, tiled=True),
        lax.all_gather(params[7], "wsh", axis=0, tiled=True),
        lax.all_gather(params[8], "wsh", axis=0, tiled=True),
        lax.all_gather(params[9], "wsh", axis=0, tiled=True),
        lax.all_gather(params[10], "wsh", axis=0, tiled=True),
        lax.all_gather(params[11], "wsh", axis=0, tiled=True),
        lax.all_gather(params[12], "wsh", axis=0, tiled=True),
        lax.all_gather(params[13], "wsh", axis=0, tiled=True),
        lax.all_gather(params[14], "wsh", axis=0, tiled=True),
    )


def per_device(
    tokens,
    cotangent,
    lengths,
    dealing,
    w_query,
    w_key,
    w_value,
    w_out,
    w_up,
    w_down,
    b_query,
    b_value,
    b_out,
    b_up,
    b_down,
    gain_one,
    shift_one,
    gain_two,
    shift_two,
):
    params = (
        w_query,
        w_key,
        w_value,
        w_out,
        w_up,
        w_down,
        b_query,
        b_value,
        b_out,
        b_up,
        b_down,
        gain_one,
        shift_one,
        gain_two,
        shift_two,
    )
    own_rows = tokens.shape[2]
    width = tokens.shape[3]
    head_size = width // HEADS
    scale_factor = 1.0 / math.sqrt(head_size)
    my_start = lax.axis_index("ctx") * own_rows
    wsh_count = lax.axis_size("wsh")
    grads = tuple(
        (jnp.zeros((item.shape[0] * wsh_count,) + item.shape[1:], jnp.float32) for item in params)
    )
    results = []
    input_grads = []
    for micro in range(MB):
        whole = gather_params(params)
        query_weight, key_weight, value_weight, out_weight, up_weight, down_weight = whole[:6]
        (
            bias_query,
            bias_value,
            bias_out,
            bias_up,
            bias_down,
            gain_first,
            shift_first,
            gain_second,
            shift_second,
        ) = tuple((item.astype(jnp.float32) for item in whole[6:]))
        token_rows = tokens[0, micro]
        seq_all, valid_all = row_labels(dealing[0, micro], lengths[0, micro])
        my_seq = lax.dynamic_slice_in_dim(seq_all, my_start, own_rows)
        my_valid = lax.dynamic_slice_in_dim(valid_all, my_start, own_rows)
        query_low = (
            jnp.dot(token_rows, query_weight, preferred_element_type=jnp.float32) + bias_query
        ).astype(jnp.bfloat16)
        key_low = jnp.dot(token_rows, key_weight, preferred_element_type=jnp.float32).astype(
            jnp.bfloat16
        )
        value_low = (
            jnp.dot(token_rows, value_weight, preferred_element_type=jnp.float32) + bias_value
        ).astype(jnp.bfloat16)
        query_heads = query_low.reshape(own_rows, HEADS, head_size)
        my_key_heads = key_low.reshape(own_rows, HEADS, head_size)
        my_value_heads = value_low.reshape(own_rows, HEADS, head_size)
        start_state = (
            jnp.full((HEADS, own_rows), NEG_FILL, jnp.float32),
            jnp.zeros((HEADS, own_rows), jnp.float32),
            jnp.zeros((own_rows, HEADS, head_size), jnp.float32),
        )
        key_piece = lax.all_gather(key_low, "ctx", axis=0, tiled=True)
        value_piece = lax.all_gather(value_low, "ctx", axis=0, tiled=True)
        piece_rows = key_piece.shape[0]
        step_rows = math.gcd(piece_rows, 512)

        def visit_block(running, offset):
            run_max, run_sum, run_acc = running
            key_blk = lax.dynamic_slice_in_dim(key_piece, offset, step_rows).reshape(
                step_rows, HEADS, head_size
            )
            value_blk = lax.dynamic_slice_in_dim(value_piece, offset, step_rows).reshape(
                step_rows, HEADS, head_size
            )
            key_seq = lax.dynamic_slice_in_dim(seq_all, offset, step_rows)
            key_valid = lax.dynamic_slice_in_dim(valid_all, offset, step_rows)
            scores, allowed = masked_scores(
                query_heads, key_blk, my_seq, key_seq, key_valid, scale_factor
            )
            new_max = jnp.maximum(run_max, jnp.max(scores, axis=-1))
            rescale = jnp.exp(run_max - new_max)
            weights = jnp.exp(scores - new_max[:, :, None]) * allowed
            run_sum = run_sum * rescale + jnp.sum(weights, axis=-1)
            run_acc = run_acc * rescale.T[:, :, None] + jnp.einsum(
                "hqk,khd->qhd",
                weights.astype(jnp.bfloat16),
                value_blk,
                preferred_element_type=jnp.float32,
            )
            return (new_max, run_sum, run_acc)

        final_max, final_sum, final_acc = blockwise(start_state, piece_rows, step_rows, visit_block)
        attended = final_acc / final_sum.T[:, :, None]
        log_total = final_max + jnp.log(final_sum)
        attended_low = attended.reshape(own_rows, width).astype(jnp.bfloat16)
        out_proj = jnp.dot(attended_low, out_weight, preferred_element_type=jnp.float32) + bias_out
        first_sum = token_rows.astype(jnp.float32) + out_proj
        norm_one, norm_one_back = jax.vjp(layer_norm, first_sum, gain_first, shift_first)
        mlp_input = norm_one.astype(jnp.bfloat16)
        up_pre = jnp.dot(mlp_input, up_weight, preferred_element_type=jnp.float32) + bias_up
        activated, gelu_back = jax.vjp(gelu_exact, up_pre)
        activated_low = activated.astype(jnp.bfloat16)
        down_out = (
            jnp.dot(activated_low, down_weight, preferred_element_type=jnp.float32) + bias_down
        )
        result, norm_two_back = jax.vjp(layer_norm, norm_one + down_out, gain_second, shift_second)
        results.append(result.astype(jnp.bfloat16))
        grad_second, grad_gain_b, grad_shift_b = norm_two_back(
            cotangent[0, micro].astype(jnp.float32)
        )
        grad_down_low = grad_second.astype(jnp.bfloat16)
        grad_activated = jnp.einsum(
            "rd,fd->rf", grad_down_low, down_weight, preferred_element_type=jnp.float32
        )
        (grad_up_pre,) = gelu_back(grad_activated)
        grad_up_low = grad_up_pre.astype(jnp.bfloat16)
        grad_norm_one = (
            jnp.einsum("rf,df->rd", grad_up_low, up_weight, preferred_element_type=jnp.float32)
            + grad_second
        )
        grad_first, grad_gain_a, grad_shift_a = norm_one_back(grad_norm_one)
        grad_out_low = grad_first.astype(jnp.bfloat16)
        grad_att_low = jnp.einsum(
            "rd,ed->re", grad_out_low, out_weight, preferred_element_type=jnp.float32
        ).astype(jnp.bfloat16)
        grad_heads = grad_att_low.reshape(own_rows, HEADS, head_size)
        row_delta = jnp.sum(grad_heads.astype(jnp.float32) * attended, axis=-1).T
        empty_heads = jnp.zeros((own_rows, HEADS, head_size), jnp.float32)
        query_key_piece = lax.all_gather(key_low, "ctx", axis=0, tiled=True)
        query_value_piece = lax.all_gather(value_low, "ctx", axis=0, tiled=True)
        query_piece_rows = query_key_piece.shape[0]
        query_step_rows = math.gcd(query_piece_rows, 512)

        def query_visit_block(running, offset):
            key_blk = lax.dynamic_slice_in_dim(query_key_piece, offset, query_step_rows).reshape(
                query_step_rows, HEADS, head_size
            )
            value_blk = lax.dynamic_slice_in_dim(
                query_value_piece, offset, query_step_rows
            ).reshape(query_step_rows, HEADS, head_size)
            key_seq = lax.dynamic_slice_in_dim(seq_all, offset, query_step_rows)
            key_valid = lax.dynamic_slice_in_dim(valid_all, offset, query_step_rows)
            probs_low, grad_scores = attention_grads(
                query_heads,
                grad_heads,
                key_blk,
                value_blk,
                my_seq,
                key_seq,
                key_valid,
                log_total,
                row_delta,
                scale_factor,
            )
            return running + jnp.einsum(
                "hqk,khd->qhd", grad_scores, key_blk, preferred_element_type=jnp.float32
            )

        grad_query_sum = blockwise(
            empty_heads, query_piece_rows, query_step_rows, query_visit_block
        )
        total_all, delta_all = (
            lax.all_gather(log_total.T, "ctx", axis=0, tiled=True),
            lax.all_gather(row_delta.T, "ctx", axis=0, tiled=True),
        )
        query_piece = lax.all_gather(query_low, "ctx", axis=0, tiled=True)
        grad_piece = lax.all_gather(grad_att_low, "ctx", axis=0, tiled=True)
        key_piece_rows = query_piece.shape[0]
        key_step_rows = math.gcd(key_piece_rows, 512)

        def key_visit_block(running, offset):
            grad_key_run, grad_value_run = running
            query_blk = lax.dynamic_slice_in_dim(query_piece, offset, key_step_rows).reshape(
                key_step_rows, HEADS, head_size
            )
            grad_blk = lax.dynamic_slice_in_dim(grad_piece, offset, key_step_rows).reshape(
                key_step_rows, HEADS, head_size
            )
            total_blk = lax.dynamic_slice_in_dim(total_all, offset, key_step_rows)
            delta_blk = lax.dynamic_slice_in_dim(delta_all, offset, key_step_rows)
            query_seq = lax.dynamic_slice_in_dim(seq_all, offset, key_step_rows)
            probs_low, grad_scores = attention_grads(
                query_blk,
                grad_blk,
                my_key_heads,
                my_value_heads,
                query_seq,
                my_seq,
                my_valid,
                total_blk.T,
                delta_blk.T,
                scale_factor,
            )
            grad_key_run = grad_key_run + jnp.einsum(
                "hqk,qhd->khd", grad_scores, query_blk, preferred_element_type=jnp.float32
            )
            grad_value_run = grad_value_run + jnp.einsum(
                "hqk,qhd->khd", probs_low, grad_blk, preferred_element_type=jnp.float32
            )
            return (grad_key_run, grad_value_run)

        grad_key_sum, grad_value_sum = blockwise(
            (empty_heads, empty_heads), key_piece_rows, key_step_rows, key_visit_block
        )
        grad_key_flat = grad_key_sum.reshape(own_rows, width)
        grad_value_flat = grad_value_sum.reshape(own_rows, width)
        grad_query_low = (
            (grad_query_sum * scale_factor).reshape(own_rows, width).astype(jnp.bfloat16)
        )
        grad_key_low = (grad_key_flat * scale_factor).astype(jnp.bfloat16)
        grad_value_low = grad_value_flat.astype(jnp.bfloat16)
        terms = (
            jnp.einsum("rd,re->de", token_rows, grad_query_low, preferred_element_type=jnp.float32),
            jnp.einsum("rd,re->de", token_rows, grad_key_low, preferred_element_type=jnp.float32),
            jnp.einsum("rd,re->de", token_rows, grad_value_low, preferred_element_type=jnp.float32),
            jnp.einsum("rd,re->de", attended_low, grad_out_low, preferred_element_type=jnp.float32),
            jnp.einsum("rd,rf->df", mlp_input, grad_up_low, preferred_element_type=jnp.float32),
            jnp.einsum(
                "rf,rd->fd", activated_low, grad_down_low, preferred_element_type=jnp.float32
            ),
            jnp.sum(grad_query_low.astype(jnp.float32), axis=0),
            jnp.sum(grad_value_low.astype(jnp.float32), axis=0),
            jnp.sum(grad_out_low.astype(jnp.float32), axis=0),
            jnp.sum(grad_up_low.astype(jnp.float32), axis=0),
            jnp.sum(grad_down_low.astype(jnp.float32), axis=0),
            grad_gain_a,
            grad_shift_a,
            grad_gain_b,
            grad_shift_b,
        )
        grads = tuple((total_now + fresh for total_now, fresh in zip(grads, terms)))
        grad_rows = (
            grad_first
            + jnp.einsum(
                "re,de->rd", grad_query_low, query_weight, preferred_element_type=jnp.float32
            )
            + jnp.einsum("re,de->rd", grad_key_low, key_weight, preferred_element_type=jnp.float32)
            + jnp.einsum(
                "re,de->rd", grad_value_low, value_weight, preferred_element_type=jnp.float32
            )
        )
        input_grads.append(grad_rows.astype(jnp.bfloat16))
    shards = jax.tree.map(
        lambda part: part.astype(jnp.float32),
        lax.psum_scatter(as_sent(grads), "wsh", scatter_dimension=0, tiled=True),
    )
    summed = jax.tree.map(lambda part: part.astype(jnp.float32), lax.psum(as_sent(shards), "ctx"))
    return (jnp.stack(results)[None], jnp.stack(input_grads)[None]) + tuple(summed)


MESH_IDS = pl.DeviceIdType.MESH
F32 = jnp.float32
BF16 = jnp.bfloat16
HD = 64
VMEM_BYTES = 60 * 1024 * 1024


def flip(index, bit):
    return index + bit * (1 - 2 * lax.rem(lax.div(index, bit), 2))


def bit_of(index, bit):
    return lax.rem(lax.div(index, bit), 2)


def greet(peers):
    barrier = pltpu.get_barrier_semaphore()
    for peer in peers:
        pl.semaphore_signal(barrier, inc=1, device_id=peer, device_id_type=MESH_IDS)
    pl.semaphore_wait(barrier, len(peers))


def send(src, dst, send_sem, recv_sem, peer):
    copy = pltpu.make_async_remote_copy(
        src_ref=src,
        dst_ref=dst,
        send_sem=send_sem,
        recv_sem=recv_sem,
        device_id=peer,
        device_id_type=MESH_IDS,
    )
    copy.start()
    return copy


def gather_kernel(plan, n_weights, n_vectors, *refs):
    shards, vectors = refs[:n_weights], refs[n_weights : n_weights + n_vectors]
    refs = refs[n_weights + n_vectors :]
    wholes, small_whole = refs[:n_weights], refs[n_weights]
    stages = refs[n_weights + 1 : 2 * n_weights + 1]
    small, small_in = refs[2 * n_weights + 1 : 2 * n_weights + 3]
    send_sem, recv_sem, small_sems, local_sem, stage_sem = refs[2 * n_weights + 3 :]
    c, w = lax.axis_index("ctx"), lax.axis_index("wsh")
    o = 1 - w
    by_x, by_y, by_z, by_core = (c, o), (flip(c, 2), w), (flip(c, 4), w), (flip(c, 1), w)
    core, y, z = bit_of(c, 1), bit_of(c, 2), bit_of(c, 4)
    mine = core * 4 + z * 2 + y
    from_y, from_z = core * 4 + z * 2 + (1 - y), core * 4 + (1 - z) * 2 + y
    staged, locals_ = [], []
    for index, (shard, stage) in enumerate(zip(shards, stages)):
        copy = pltpu.make_async_copy(shard, stage, stage_sem.at[index])
        copy.start()
        staged.append(copy)
    line, lanes = 0, small.shape[1]
    for vector in vectors:
        for first in range(0, vector.shape[0], lanes):
            piece = vector[pl.ds(first, lanes)].astype(F32)
            small[line : line + 1, :] = piece.reshape(1, lanes)
            line += 1
    greet((by_x, by_y, by_z, by_core))
    small_sent = send(small, small_in, small_sems.at[0], small_sems.at[1], by_x)

    def part(chunk, side, piece, start, count):
        tensor, first, rows = plan[chunk]
        size = rows // 8
        half = shards[tensor].shape[0]
        at = side * half + first + piece * size + start
        return wholes[tensor].at[pl.ds(pl.multiple_of(at, 8), count)]

    steps = {}
    for chunk, (tensor, first, rows) in enumerate(plan):
        size = rows // 8
        src = shards[tensor].at[pl.ds(pl.multiple_of(first + mine * size, 8), size)]
        steps[chunk, 0] = send(
            src, part(chunk, w, mine, 0, size), send_sem.at[0, chunk], recv_sem.at[0, chunk], by_x
        )

    for index, (stage, whole) in enumerate(zip(stages, wholes)):
        rows = stage.shape[0]
        staged[index].wait()
        copy = pltpu.make_async_copy(
            stage, whole.at[pl.ds(pl.multiple_of(w * rows, rows), rows)], local_sem.at[index]
        )
        copy.start()
        locals_.append(copy)

    def second(chunk):
        size = plan[chunk][2] // 8
        steps[chunk, 0].wait_recv()
        for kind, peer in ((1, by_y), (2, by_z)):
            ref = part(chunk, o, mine, 0, size)
            steps[chunk, kind] = send(
                ref, ref, send_sem.at[kind, chunk], recv_sem.at[kind, chunk], peer
            )

    def third(chunk):
        size = plan[chunk][2] // 8
        steps[chunk, 1].wait_recv()
        steps[chunk, 2].wait_recv()
        ref = part(chunk, o, from_z, 0, size // 2)
        steps[chunk, 3] = send(ref, ref, send_sem.at[3, chunk], recv_sem.at[3, chunk], by_y)
        ref = part(chunk, o, from_y, size // 2, size // 2)
        steps[chunk, 4] = send(ref, ref, send_sem.at[4, chunk], recv_sem.at[4, chunk], by_z)

    def fourth(chunk):
        size = plan[chunk][2] // 8
        steps[chunk, 3].wait_recv()
        steps[chunk, 4].wait_recv()
        ref = part(chunk, o, core * 4, 0, 4 * size)
        steps[chunk, 5] = send(ref, ref, send_sem.at[5, chunk], recv_sem.at[5, chunk], by_core)

    count = len(plan)
    for turn in range(count + 2):
        if turn < count:
            second(turn)
        if 0 <= turn - 1 < count:
            third(turn - 1)
        if 0 <= turn - 2 < count:
            fourth(turn - 2)
    for chunk in range(count):
        steps[chunk, 5].wait_recv()
        for kind in range(6):
            steps[chunk, kind].wait_send()
    small_sent.wait()
    small_whole[w] = small[...]
    small_whole[o] = small_in[...]
    for copy in locals_:
        copy.wait()


def gather_weights(shards, vectors):
    plan = []
    for index, shard in enumerate(shards):
        rows = shard.shape[0]
        parts = max(1, shard.shape[0] * shard.shape[1] // (1024 * 1024))
        for piece in range(parts):
            plan.append((index, piece * (rows // parts), rows // parts))
    count = len(shards)
    shapes = [jax.ShapeDtypeStruct((2 * s.shape[0],) + s.shape[1:], s.dtype) for s in shards]
    lanes = min(item.shape[0] for item in vectors)
    lines = sum(item.shape[0] for item in vectors) // lanes
    shapes.append(jax.ShapeDtypeStruct((2, lines, lanes), F32))
    anywhere, vmem = pl.BlockSpec(memory_space=pl.ANY), pl.BlockSpec(memory_space=pltpu.VMEM)
    return pl.pallas_call(
        functools.partial(gather_kernel, plan, count, len(vectors)),
        out_shape=shapes,
        in_specs=[anywhere] * count + [vmem] * len(vectors),
        out_specs=[anywhere] * count + [vmem],
        scratch_shapes=[pltpu.VMEM(s.shape, s.dtype) for s in shards]
        + [pltpu.VMEM((lines, lanes), F32)] * 2
        + [
            pltpu.SemaphoreType.DMA((6, len(plan))),
            pltpu.SemaphoreType.DMA((6, len(plan))),
            pltpu.SemaphoreType.DMA((2,)),
            pltpu.SemaphoreType.DMA((count,)),
            pltpu.SemaphoreType.DMA((count,)),
        ],
        compiler_params=pltpu.CompilerParams(
            collective_id=0, has_side_effects=True, vmem_limit_bytes=VMEM_BYTES
        ),
        name="gather_weights",
    )(*shards, *vectors)


def plane_peers(c, w, count):
    return [(lax.rem(c + step, count), w) for step in range(1, count)]


def pack_three(first, second, third, row, pair, out):
    cols = pl.ds(pair * 128, 128)
    a, b, d = (ref[pl.ds(row, BLK), cols] for ref in (first, second, third))
    half = BLK // 2
    for head in range(2):
        lane = slice(head * HD, head * HD + HD)
        out[2 * pair + head, 0:BLK, :] = jnp.concatenate([a[:, lane], b[:, lane]], axis=1)
        out[2 * pair + head, BLK : BLK + half, :] = jnp.concatenate(
            [d[:half, lane], d[half:, lane]], axis=1
        )


def unpack_fold(block):
    return jnp.concatenate([block[:, :HD], block[:, HD:]], axis=0)


def fold(rows):
    half = rows.shape[0] // 2
    return jnp.concatenate([rows[:half], rows[half:]], axis=1)


def all_bytes(ref, sem, peers):
    view = ref.at[pl.ds(0, peers)]
    return pltpu.make_async_copy(view, view, sem)


def attend_kernel(
    heads,
    lens_ref,
    slot_ref,
    block_ref,
    q_ref,
    k_ref,
    v_ref,
    a_ref,
    kept_ref,
    lse_ref,
    *scratch,
):
    in_buf = scratch[:MB]
    out_buf, back_out, back_in, q_s, k_s, v_s, a_s = scratch[MB : MB + 7]
    send_sem, recv_sem, back_send, back_recv, keep_sem = scratch[MB + 7 :]
    c, w = lax.axis_index("ctx"), lax.axis_index("wsh")
    peers = plane_peers(c, w, heads)
    greet(peers)
    blocks = heads
    for m in range(MB):
        for pair in range(heads // 2):
            pack_three(q_ref, k_ref, v_ref, m * BLK, pair, out_buf.at[m])
        for peer in peers:
            send(
                out_buf.at[m, peer[0]], in_buf[m].at[c], send_sem.at[m], recv_sem.at[m], peer
            )
        in_buf[m][c] = out_buf[m, c]
    for m in range(MB):
        all_bytes(in_buf[m], recv_sem.at[m], heads - 1).wait()
        keep = pltpu.make_async_copy(in_buf[m], kept_ref.at[m], keep_sem.at[m])
        keep.start()
        for b in range(blocks):
            got = in_buf[m][slot_ref[0, m, b]]
            q_s[b * BLK : (b + 1) * BLK, :] = got[:BLK, :HD]
            k_s[b * BLK : (b + 1) * BLK, :] = got[:BLK, HD:]
            v_s[b * BLK : (b + 1) * BLK, :] = unpack_fold(got[BLK:])
        span = BPS * BLK
        for s in range(blocks // BPS):
            rows = slice(s * span, (s + 1) * span)
            scores = lax.dot_general(
                k_s[rows, :], q_s[rows, :], (((1,), (1,)), ((), ())), preferred_element_type=F32
            ) * (1.0 / math.sqrt(HD))
            place = lax.broadcasted_iota(jnp.int32, scores.shape, 0)
            scores = jnp.where(place < lens_ref[0, m, s], scores, NEG_FILL)
            top = jnp.max(scores, axis=0, keepdims=True)
            weights = jnp.exp(scores - top)
            total = jnp.sum(weights, axis=0, keepdims=True)
            out_t = lax.dot_general(
                v_s[rows, :],
                weights.astype(BF16),
                (((0,), (0,)), ((), ())),
                preferred_element_type=F32,
            )
            a_s[s * BPS : (s + 1) * BPS] = (out_t / total).T.reshape(BPS, BLK, HD)
            lse_ref[pl.ds(m * (blocks // BPS) + s, 1), :] = top + jnp.log(total)
        for t in range(blocks):
            back_out[m, t] = fold(a_s[block_ref[0, m, t]]).astype(BF16)
        for peer in peers:
            send(
                back_out.at[m, peer[0]], back_in.at[m, c], back_send.at[m], back_recv.at[m], peer
            )
        back_in[m, c] = back_out[m, c]
    for m in range(MB):
        all_bytes(back_in.at[m], back_recv.at[m], heads - 1).wait()
        for pair in range(heads // 2):
            a_ref[m * BLK : (m + 1) * BLK, pair * 128 : (pair + 1) * 128] = jnp.concatenate(
                [unpack_fold(back_in[m, 2 * pair]), unpack_fold(back_in[m, 2 * pair + 1])], axis=1
            )
    for m in range(MB):
        all_bytes(out_buf.at[m], send_sem.at[m], heads - 1).wait()
        all_bytes(back_out.at[m], back_send.at[m], heads - 1).wait()
        pltpu.make_async_copy(in_buf[m], kept_ref.at[m], keep_sem.at[m]).wait()


def attend(lens, slot_of, block_of, q, k, v, heads):
    vmem, smem = pl.BlockSpec(memory_space=pltpu.VMEM), pl.BlockSpec(memory_space=pltpu.SMEM)
    rows, width = q.shape
    pack_rows = BLK + BLK // 2
    span = BPS * BLK
    return pl.pallas_call(
        functools.partial(attend_kernel, heads),
        out_shape=[
            jax.ShapeDtypeStruct((rows, width), BF16),
            jax.ShapeDtypeStruct((MB, heads, pack_rows, 128), BF16),
            jax.ShapeDtypeStruct((8, span), F32),
        ],
        in_specs=[smem] * 3 + [vmem] * 3,
        out_specs=[vmem, pl.BlockSpec(memory_space=pl.ANY), vmem],
        scratch_shapes=[pltpu.VMEM((heads, pack_rows, 128), BF16)] * MB
        + [
            pltpu.VMEM((MB, heads, pack_rows, 128), BF16),
            pltpu.VMEM((MB, heads, BLK // 2, 128), BF16),
            pltpu.VMEM((MB, heads, BLK // 2, 128), BF16),
            pltpu.VMEM((heads * BLK, HD), BF16),
            pltpu.VMEM((heads * BLK, HD), BF16),
            pltpu.VMEM((heads * BLK, HD), BF16),
            pltpu.VMEM((heads, BLK, HD), F32),
            pltpu.SemaphoreType.DMA((MB,)),
            pltpu.SemaphoreType.DMA((MB,)),
            pltpu.SemaphoreType.DMA((MB,)),
            pltpu.SemaphoreType.DMA((MB,)),
            pltpu.SemaphoreType.DMA((MB,)),
        ],
        compiler_params=pltpu.CompilerParams(
            collective_id=1, has_side_effects=True, vmem_limit_bytes=VMEM_BYTES
        ),
        name="attend",
    )(lens, slot_of, block_of, q, k, v)


def attend_back_kernel(heads, *refs):
    lens_ref, slot_ref, block_ref, da_ref, kept_ref, lse_ref = refs[:6]
    x_ref, a_ref, n_ref, g_ref, do_ref, du_ref, dm_ref = refs[6:13]
    dq_ref, dk_ref, dv_ref = refs[13:16]
    x_all, a_all, n_all, g_all, do_all, du_all, dm_all, dqkv_all = refs[16:24]
    in_buf = refs[24 : 24 + MB]
    out_buf, back_out, back_in = refs[24 + MB : 27 + MB]
    q_s, k_s, v_s, a_s, dq_s, dk_s, dv_s = refs[27 + MB : 34 + MB]
    send_sem, recv_sem, back_send, back_recv, mate_send, mate_recv, own_sem = refs[34 + MB :]
    c, w = lax.axis_index("ctx"), lax.axis_index("wsh")
    core = bit_of(c, 1)
    mate = (flip(c, 1), w)
    peers = plane_peers(c, w, heads)
    blocks = heads
    rows_own = da_ref.shape[0]
    greet(peers)

    place = pl.ds(pl.multiple_of(core * rows_own, rows_own), rows_own)
    moves = []

    def share(src, dst, lanes):
        for first, size, to, per_core in lanes:
            index = len(moves)
            step = size if per_core else 0
            own_from = pl.ds(pl.multiple_of(first + core * step, 128), size)
            mate_from = pl.ds(pl.multiple_of(first + (1 - core) * step, 128), size)
            spot = dst.at[place, pl.ds(to, size)]
            own = pltpu.make_async_copy(src.at[:, own_from], spot, own_sem.at[index])
            own.start()
            gone = send(
                src.at[:, mate_from], spot, mate_send.at[index], mate_recv.at[index], mate
            )
            moves.append((own, gone))

    width = da_ref.shape[1]
    hidden = g_ref.shape[1]
    for m in range(MB):
        row = slice(m * BLK, (m + 1) * BLK)
        for pair in range(heads // 2):
            both = da_ref[row, pair * 128 : (pair + 1) * 128]
            for head in range(2):
                out_buf[m, 2 * pair + head] = fold(both[:, head * HD : (head + 1) * HD])
        for peer in peers:
            send(out_buf.at[m, peer[0]], in_buf[m].at[c], send_sem.at[m], recv_sem.at[m], peer)
        in_buf[m][c] = out_buf[m, c]
    for src, dst in ((x_ref, x_all), (a_ref, a_all), (n_ref, n_all), (dm_ref, dm_all)):
        share(src, dst, ((0, width, 0, False),))
    share(do_ref, do_all, ((0, width // 2, 0, True),))
    share(du_ref, du_all, ((0, hidden // 2, 0, True),))
    share(g_ref, g_all, ((0, hidden // 4, 0, True), (hidden // 2, hidden // 4, hidden // 4, True)))
    for m in range(MB):
        all_bytes(in_buf[m], recv_sem.at[m], heads - 1).wait()
        for b in range(blocks):
            slot = slot_ref[0, m, b]
            got = kept_ref[m, slot]
            rows = slice(b * BLK, (b + 1) * BLK)
            q_s[rows, :] = got[:BLK, :HD]
            k_s[rows, :] = got[:BLK, HD:]
            v_s[rows, :] = unpack_fold(got[BLK:])
            a_s[rows, :] = unpack_fold(in_buf[m][slot])
        span = BPS * BLK
        for s in range(blocks // BPS):
            rows = slice(s * span, (s + 1) * span)
            qq, kk, vv, dd = q_s[rows, :], k_s[rows, :], v_s[rows, :], a_s[rows, :]
            scale = 1.0 / math.sqrt(HD)
            minor = (((1,), (1,)), ((), ()))
            scores = lax.dot_general(kk, qq, minor, preferred_element_type=F32) * scale
            spot = lax.broadcasted_iota(jnp.int32, scores.shape, 0)
            total = lse_ref[pl.ds(m * (blocks // BPS) + s, 1), :]
            probs = jnp.exp(jnp.where(spot < lens_ref[0, m, s], scores - total, NEG_FILL))
            dp = lax.dot_general(vv, dd, minor, preferred_element_type=F32)
            both = probs * dp
            delta = jnp.sum(both, axis=0, keepdims=True)
            ds = (both - probs * delta).astype(BF16)
            here = slice(s * BPS, (s + 1) * BPS)
            split = (BPS, BLK, HD)
            dv = jnp.dot(probs.astype(BF16), dd, preferred_element_type=F32)
            dv_s[here] = dv.reshape(split)
            dk_s[here] = (jnp.dot(ds, qq, preferred_element_type=F32) * scale).reshape(split)
            dq_t = lax.dot_general(kk, ds, (((0,), (0,)), ((), ())), preferred_element_type=F32)
            dq_s[here] = (dq_t.T * scale).reshape(split)
        for t in range(blocks):
            at = block_ref[0, m, t]
            back_out[m, t, 0:BLK, :] = jnp.concatenate([dq_s[at], dk_s[at]], axis=1).astype(BF16)
            back_out[m, t, BLK:, :] = fold(dv_s[at]).astype(BF16)
        for peer in peers:
            send(
                back_out.at[m, peer[0]], back_in.at[m, c], back_send.at[m], back_recv.at[m], peer
            )
        back_in[m, c] = back_out[m, c]
    for m in range(MB):
        all_bytes(back_in.at[m], back_recv.at[m], heads - 1).wait()
        row = slice(m * BLK, (m + 1) * BLK)
        for pair in range(heads // 2):
            lanes = slice(pair * 128, (pair + 1) * 128)
            one, two = back_in[m, 2 * pair], back_in[m, 2 * pair + 1]
            dq_ref[row, lanes] = jnp.concatenate([one[:BLK, :HD], two[:BLK, :HD]], axis=1)
            dk_ref[row, lanes] = jnp.concatenate([one[:BLK, HD:], two[:BLK, HD:]], axis=1)
            dv_ref[row, lanes] = jnp.concatenate(
                [unpack_fold(one[BLK:]), unpack_fold(two[BLK:])], axis=1
            )
    for index, ref in enumerate((dq_ref, dk_ref, dv_ref)):
        half = width // 2
        spot = dqkv_all.at[place, pl.ds(index * half, half)]
        number = len(moves)
        own_from = pl.ds(pl.multiple_of(core * half, 128), half)
        mate_from = pl.ds(pl.multiple_of((1 - core) * half, 128), half)
        own = pltpu.make_async_copy(ref.at[:, own_from], spot, own_sem.at[number])
        own.start()
        gone = send(ref.at[:, mate_from], spot, mate_send.at[number], mate_recv.at[number], mate)
        moves.append((own, gone))
    for m in range(MB):
        all_bytes(out_buf.at[m], send_sem.at[m], heads - 1).wait()
        all_bytes(back_out.at[m], back_send.at[m], heads - 1).wait()
    for own, gone in moves:
        own.wait()
        gone.wait()


def attend_back(lens, slot_of, block_of, da, kept, lse, x, a, n1, g, do, du, dm, heads):
    vmem, smem = pl.BlockSpec(memory_space=pltpu.VMEM), pl.BlockSpec(memory_space=pltpu.SMEM)
    anywhere = pl.BlockSpec(memory_space=pl.ANY)
    rows, width = da.shape
    hidden = g.shape[1]
    pack_rows = BLK + BLK // 2
    both = 2 * rows
    moves = 11
    shape = lambda *dims: jax.ShapeDtypeStruct(dims, BF16)
    return pl.pallas_call(
        functools.partial(attend_back_kernel, heads),
        out_shape=[shape(rows, width)] * 3
        + [
            shape(both, width),
            shape(both, width),
            shape(both, width),
            shape(both, hidden // 2),
            shape(both, width // 2),
            shape(both, hidden // 2),
            shape(both, width),
            shape(both, 3 * width // 2),
        ],
        in_specs=[smem] * 3 + [vmem] * 10,
        out_specs=[vmem] * 3 + [anywhere] * 8,
        scratch_shapes=[pltpu.VMEM((heads, BLK // 2, 128), BF16)] * MB
        + [
            pltpu.VMEM((MB, heads, BLK // 2, 128), BF16),
            pltpu.VMEM((MB, heads, pack_rows, 128), BF16),
            pltpu.VMEM((MB, heads, pack_rows, 128), BF16),
        ]
        + [pltpu.VMEM((heads * BLK, HD), BF16)] * 4
        + [pltpu.VMEM((heads, BLK, HD), F32)] * 3
        + [pltpu.SemaphoreType.DMA((MB,))] * 4
        + [pltpu.SemaphoreType.DMA((moves,))] * 3,
        compiler_params=pltpu.CompilerParams(
            collective_id=2, has_side_effects=True, vmem_limit_bytes=VMEM_BYTES
        ),
        name="attend_back",
    )(lens, slot_of, block_of, da, kept, lse, x, a, n1, g, do, du, dm)


CHUNKS = 2
ORDERS = {
    (0, 0): "xyzZ",
    (0, 1): "xzyZ",
    (1, 0): "yxZz",
    (1, 1): "yZxz",
    (2, 0): "zxyZ",
    (2, 1): "Zyxz",
}


def landing_shapes(order, shape):
    shards, sides, shapes = 8, 2, []
    for name in order:
        if name == "x":
            sides = 1
        else:
            shards //= 2
        shapes.append((sides, shards, shape[2] // CHUNKS, shape[3]))
    return shapes


def reduce_kernel(ga1_ref, ga2_ref, gb_ref, gc_ref, vec_ref, *refs):
    o_a, o_b, o_c, vec_out = refs[:4]
    s_a, s_b, s_c = refs[4:7]
    r_bufs = {key: refs[7 + 4 * i : 11 + 4 * i] for i, key in enumerate(ORDERS)}
    rest = refs[7 + 4 * len(ORDERS) :]
    v_recv, v_sum = rest[:2]
    load_sem, rs_send, rs_recv, ag_send, ag_recv, v_send_sem, v_recv_sem, own_sem = rest[2:]
    c, x = lax.axis_index("ctx"), lax.axis_index("wsh")
    core, y, z, zz = bit_of(c, 1), bit_of(c, 2), bit_of(c, 4), bit_of(c, 8)
    by_x, by_y, by_z = (c, 1 - x), (flip(c, 2), x), (flip(c, 4), x)
    by_zz, by_core = (flip(c, 8), x), (flip(c, 1), x)
    shards = 8
    lanes1 = ga1_ref.shape[3]
    lanes2 = ga2_ref.shape[3]
    loads = [
        pltpu.make_async_copy(ga1_ref, s_a.at[:, :, :, pl.ds(0, lanes1)], load_sem.at[0]),
        pltpu.make_async_copy(ga2_ref, s_a.at[:, :, :, pl.ds(lanes1, lanes2)], load_sem.at[1]),
        pltpu.make_async_copy(gb_ref, s_b, load_sem.at[2]),
        pltpu.make_async_copy(gc_ref, s_c, load_sem.at[3]),
    ]
    for load in loads:
        load.start()
    greet((by_x, by_y, by_z, by_zz, by_core))
    vec_steps = [
        send(vec_ref.at[1 - x], v_recv.at[0], v_send_sem.at[0], v_recv_sem.at[0], by_x)
    ]

    def vec_next(step, peer):
        vec_steps[step].wait_recv()
        before = vec_ref[x] if step == 0 else v_sum[step - 1]
        v_sum[step] = before + v_recv[step]
        if peer is not None:
            vec_steps.append(
                send(
                    v_sum.at[step],
                    v_recv.at[step + 1],
                    v_send_sem.at[step + 1],
                    v_recv_sem.at[step + 1],
                    peer,
                )
            )

    for load in loads:
        load.wait()
    bits = {"y": y, "z": z, "Z": zz}
    peers = {"x": by_x, "y": by_y, "z": by_z, "Z": by_zz}
    plans, gathers = {}, {}
    for key, order in ORDERS.items():
        first, count, sided = 0, 8, False
        plans[key], back = [], []
        for name in order:
            if name == "x":
                plans[key].append((by_x, 1 - x, x, first, first, count))
                sided = True
                continue
            count //= 2
            out, keep = first + (1 - bits[name]) * count, first + bits[name] * count
            side = x if sided else None
            plans[key].append((peers[name], side, side, out, keep, count))
            back.append((peers[name], keep, out, count))
            first = keep
        gathers[key] = back[::-1]
    sums = (s_a, s_b, s_c)
    outs = (o_a, o_b, o_c)
    flights = {}

    def chunk_rows(part, chunk):
        rows = sums[part].shape[2] // CHUNKS
        return pl.ds(chunk * rows, rows)

    def reduce_send(part, step, chunk):
        peer, side, _, first, _, count = plans[part, chunk][step]
        rows = chunk_rows(part, chunk)
        dst = r_bufs[part, chunk][step]
        if side is None:
            src = sums[part].at[:, pl.ds(first, count), rows]
        else:
            src, dst = sums[part].at[side, pl.ds(first, count), rows], dst.at[0]
        flights[part, step, chunk] = send(
            src, dst, rs_send.at[part, step, chunk], rs_recv.at[part, step, chunk], peer
        )

    def reduce_add(part, step, chunk):
        _, _, side, _, first, count = plans[part, chunk][step]
        rows = chunk_rows(part, chunk)
        flights[part, step, chunk].wait_recv()
        total, fresh = sums[part], r_bufs[part, chunk][step]
        sides = ((0, 0), (1, 1)) if side is None else ((side, 0),)
        for here, there in sides:

            def body(index, carry):
                spot = first + index
                total[here, spot, rows] = (
                    total[here, spot, rows].astype(F32) + fresh[there, index].astype(F32)
                ).astype(BF16)
                return carry

            lax.fori_loop(0, count, body, 0)

    for chunk in range(CHUNKS):
        for part in range(3):
            reduce_send(part, 0, chunk)
    vec_peers = (by_y, by_z, by_zz, by_core, None)
    for step in range(1, 4):
        vec_next(step - 1, vec_peers[step - 1])
        for chunk in range(CHUNKS):
            for part in range(3):
                reduce_add(part, step - 1, chunk)
                reduce_send(part, step, chunk)
    owns, spread = [], {}
    vec_next(3, by_core)
    for chunk in range(CHUNKS):
        for part in range(3):
            reduce_add(part, 3, chunk)
            rows = chunk_rows(part, chunk)
            peer, first, _, _ = gathers[part, chunk][0]
            src = sums[part].at[x, pl.ds(first, 1), rows]
            dst = outs[part].at[core, pl.ds(first, 1), rows]
            own = pltpu.make_async_copy(src, dst, own_sem.at[part, chunk])
            own.start()
            owns.append(own)
            sem = lambda kind: (ag_send.at[part, kind, chunk], ag_recv.at[part, kind, chunk])
            spread[part, 0, chunk] = send(src, dst, *sem(0), peer)
            spread[part, 3, chunk] = send(src, dst, *sem(3), by_core)
    vec_next(4, None)
    vec_out[...] = v_sum[4]
    for own in owns:
        own.wait()
    for step in range(1, 4):
        for chunk in range(CHUNKS):
            for part in range(3):
                rows = chunk_rows(part, chunk)
                spread[part, step - 1, chunk].wait_recv()
                sem = lambda kind: (ag_send.at[part, kind, chunk], ag_recv.at[part, kind, chunk])
                if step < 3:
                    peer, first, _, count = gathers[part, chunk][step]
                    ref = outs[part].at[core, pl.ds(first, count), rows]
                    spread[part, step, chunk] = send(ref, ref, *sem(step), peer)
                _, _, first, count = gathers[part, chunk][step - 1]
                fresh = outs[part].at[core, pl.ds(first, count), rows]
                spread[part, 3 + step, chunk] = send(fresh, fresh, *sem(3 + step), by_core)
    for key, flight in spread.items():
        if key[1] >= 3:
            flight.wait_recv()
        flight.wait_send()
    for flight in flights.values():
        flight.wait_send()
    for flight in vec_steps:
        flight.wait_send()


def reduce_grads(ga1, ga2, gb, gc, vec):
    vmem, anywhere = pl.BlockSpec(memory_space=pltpu.VMEM), pl.BlockSpec(memory_space=pl.ANY)
    lanes = ga1.shape[3] + ga2.shape[3]
    a_shape = ga1.shape[:3] + (lanes,)
    b_shape, c_shape = gb.shape, gc.shape
    scratch = [pltpu.VMEM(s, BF16) for s in (a_shape, b_shape, c_shape)]
    shapes = (a_shape, b_shape, c_shape)
    for (part, _), order in ORDERS.items():
        scratch += [pltpu.VMEM(shape, BF16) for shape in landing_shapes(order, shapes[part])]
    scratch += [
        pltpu.VMEM((5,) + vec.shape[1:], F32),
        pltpu.VMEM((5,) + vec.shape[1:], F32),
        pltpu.SemaphoreType.DMA((4,)),
        pltpu.SemaphoreType.DMA((3, 4, CHUNKS)),
        pltpu.SemaphoreType.DMA((3, 4, CHUNKS)),
        pltpu.SemaphoreType.DMA((3, 7, CHUNKS)),
        pltpu.SemaphoreType.DMA((3, 7, CHUNKS)),
        pltpu.SemaphoreType.DMA((5,)),
        pltpu.SemaphoreType.DMA((5,)),
        pltpu.SemaphoreType.DMA((3, CHUNKS)),
    ]
    return pl.pallas_call(
        reduce_kernel,
        out_shape=[
            jax.ShapeDtypeStruct(a_shape, BF16),
            jax.ShapeDtypeStruct(b_shape, BF16),
            jax.ShapeDtypeStruct(c_shape, BF16),
            jax.ShapeDtypeStruct(vec.shape[1:], F32),
        ],
        in_specs=[anywhere] * 4 + [vmem],
        out_specs=[anywhere] * 3 + [vmem],
        scratch_shapes=scratch,
        compiler_params=pltpu.CompilerParams(
            collective_id=3, has_side_effects=True, vmem_limit_bytes=VMEM_BYTES
        ),
        name="reduce_grads",
    )(ga1, ga2, gb, gc, vec)


def widen_kernel(a_ref, b_ref, c_ref, *outs):
    half = outs[0].shape[1] // 2
    for index, out in enumerate(outs[:4]):
        for core in range(2):
            out[:, core * half : (core + 1) * half] = a_ref[
                core, 0, :, index * half : (index + 1) * half
            ].astype(F32)
    up, down = outs[4:]
    half = up.shape[1] // 2
    for core in range(2):
        up[:, core * half : (core + 1) * half] = b_ref[core, 0].astype(F32)
        down[core, 0] = c_ref[core, 0].astype(F32)


def widen(o_a, o_b, o_c):
    shards = o_a.shape[1]
    block = lambda item: pl.BlockSpec((2, 1) + item.shape[2:], lambda i: (0, i, 0, 0))
    rows = o_a.shape[2]
    square = (shards * rows, o_a.shape[3] // 2)
    wide = (shards * rows, 2 * o_b.shape[3])
    return pl.pallas_call(
        widen_kernel,
        grid=(shards,),
        out_shape=[jax.ShapeDtypeStruct(square, F32)] * 4
        + [jax.ShapeDtypeStruct(wide, F32), jax.ShapeDtypeStruct(o_c.shape, F32)],
        in_specs=[block(o_a), block(o_b), block(o_c)],
        out_specs=[pl.BlockSpec((rows, square[1]), lambda i: (i, 0))] * 4
        + [pl.BlockSpec((rows, wide[1]), lambda i: (i, 0)), block(o_c)],
        compiler_params=pltpu.CompilerParams(vmem_limit_bytes=VMEM_BYTES),
        name="widen",
    )(o_a, o_b, o_c)


def norm_parts(summed):
    row_mean = jnp.mean(summed, axis=-1, keepdims=True)
    centred = summed - row_mean
    row_var = jnp.mean(centred * centred, axis=-1, keepdims=True)
    scale = lax.rsqrt(row_var + EPSILON)
    return centred * scale, scale


def norm_back(grad, unit, scale, gain):
    inner = grad * gain
    mean_one = jnp.mean(inner, axis=-1, keepdims=True)
    mean_two = jnp.mean(inner * unit, axis=-1, keepdims=True)
    return scale * (inner - mean_one - unit * mean_two)


def dot(a, b, dims):
    return lax.dot_general(a, b, (dims, ((), ())), preferred_element_type=F32)


ROW_COL, COL_COL, ROW_ROW = ((1,), (0,)), ((1,), (1,)), ((0,), (0,))


def per_device_heads(tokens, cotangent, lengths, dealing, *params):
    rows_in = tokens.shape[2]
    width = tokens.shape[3]
    rows = MB * rows_in
    weights, vectors = params[:6], params[6:]
    sizes = [item.shape[0] for item in vectors]
    *wholes, small_whole = gather_weights(weights, vectors)
    query_w, key_w, value_w, out_w, up_w, down_w = wholes
    spots = [sum(sizes[:i]) for i in range(len(sizes) + 1)]
    lines = [spot // small_whole.shape[2] for spot in spots]
    bias_query, bias_value, bias_out, bias_up, bias_down, gain_one, shift_one, gain_two, shift_two = (
        small_whole[:, lines[i] : lines[i + 1]].reshape(1, -1) for i in range(len(sizes))
    )
    x = tokens.reshape(rows, width)
    lens, block_of = lengths, dealing
    slot_of = jnp.argsort(block_of, axis=2).astype(jnp.int32)
    q = (dot(x, query_w, ROW_COL) + bias_query).astype(BF16)
    k = dot(x, key_w, ROW_COL).astype(BF16)
    v = (dot(x, value_w, ROW_COL) + bias_value).astype(BF16)
    a, kept, lse = attend(lens, slot_of, block_of, q, k, v, HEADS)

    h_one = x.astype(F32) + (dot(a, out_w, ROW_COL) + bias_out)
    unit_one, scale_one = norm_parts(h_one)
    n_one = unit_one * gain_one + shift_one
    n_low = n_one.astype(BF16)
    u = dot(n_low, up_w, ROW_COL) + bias_up
    below = 0.5 * (1.0 + lax.erf(u * math.sqrt(0.5)))
    slope = below + u * jnp.exp(-0.5 * u * u) * (1.0 / math.sqrt(2.0 * math.pi))
    g, slope = lax.optimization_barrier(((u * below).astype(BF16), slope))
    h_two = n_one + (dot(g, down_w, ROW_COL) + bias_down)
    unit_two, scale_two = norm_parts(h_two)
    output = (unit_two * gain_two + shift_two).astype(BF16)

    cot = cotangent.reshape(rows, width).astype(F32)
    dh_two = norm_back(cot, unit_two, scale_two, gain_two)
    dm = dh_two.astype(BF16)
    du = lax.optimization_barrier((slope * dot(dm, down_w, COL_COL)).astype(BF16))
    dn = lax.optimization_barrier(dot(du, up_w, COL_COL)) + dh_two
    dh_one = norm_back(dn, unit_one, scale_one, gain_one)
    do = dh_one.astype(BF16)
    da = dot(do, out_w, COL_COL).astype(BF16)

    dq, dk, dv, x_all, a_all, n_all, g_all, do_all, du_all, dm_all, dqkv_all = attend_back(
        lens, slot_of, block_of, da, kept, lse, x, a, n_low, g, do, du, dm, HEADS
    )
    total = lambda item: jnp.sum(item.astype(F32), axis=0)
    vec = [
        total(dq),
        total(dv),
        total(do),
        total(du),
        total(dm),
        total(dn * unit_one),
        total(dn),
        total(cot * unit_two),
        total(cot),
    ]
    vec = jnp.concatenate([item.reshape(2, -1) for item in vec], axis=1).reshape(2, -1, 128)
    ga1 = dot(x_all, dqkv_all, ROW_ROW).astype(BF16).reshape(2, 8, -1, dqkv_all.shape[1])
    ga2 = dot(a_all, do_all, ROW_ROW).astype(BF16).reshape(2, 8, -1, do_all.shape[1])
    gb = dot(n_all, du_all, ROW_ROW).astype(BF16).reshape(2, 8, -1, du_all.shape[1])
    gc = dot(g_all, dm_all, ROW_ROW).astype(BF16).reshape(2, 8, -1, dm_all.shape[1])
    o_a, o_b, o_c, vec_sum = reduce_grads(ga1, ga2, gb, gc, vec)
    grad_rows = (
        dh_one + dot(dq, query_w, COL_COL) + dot(dk, key_w, COL_COL) + dot(dv, value_w, COL_COL)
    )
    grad_tokens = grad_rows.astype(BF16)
    *square, up, down = widen(o_a, o_b, o_c)
    down = down.reshape(-1, width)
    vec_sum = vec_sum.reshape(-1)
    ends = [vec_sum[spots[i] : spots[i + 1]] for i in range(len(sizes))]
    shape = (1, MB, rows_in, width)
    return (
        (output.reshape(shape), grad_tokens.reshape(shape))
        + (*square, up, down)
        + tuple(ends)
    )


def solution(mesh):
    placed = (
        P("wsh", None, "ctx", None),
        P("wsh", None, "ctx", None),
        P("wsh", None, None),
        P("wsh", None, None),
        P("wsh", None),
        P("wsh", None),
        P("wsh", None),
        P("wsh", None),
        P("wsh", None),
        P("wsh", None),
        P("wsh"),
        P("wsh"),
        P("wsh"),
        P("wsh"),
        P("wsh"),
        P("wsh"),
        P("wsh"),
        P("wsh"),
        P("wsh"),
    )
    by_heads = mesh.shape["ctx"] == HEADS and mesh.shape["wsh"] == 2
    return jax.shard_map(
        per_device_heads if by_heads else per_device,
        mesh=mesh,
        in_specs=placed,
        out_specs=(
            P("wsh", None, "ctx", None),
            P("wsh", None, "ctx", None),
            P("wsh", None),
            P("wsh", None),
            P("wsh", None),
            P("wsh", None),
            P("wsh", None),
            P("wsh", None),
            P("wsh"),
            P("wsh"),
            P("wsh"),
            P("wsh"),
            P("wsh"),
            P("wsh"),
            P("wsh"),
            P("wsh"),
            P("wsh"),
        ),
        check_vma=False,
    )
```

```python
import functools
import math

import jax
import jax.numpy as jnp
from jax import lax
from jax.experimental import pallas as pl
from jax.experimental.pallas import tpu as pltpu
from jax.sharding import PartitionSpec as P

HEADS = 16
BPS = 8
MB = 3
BLK = 64


EPSILON = 1e-12
NEG_FILL = -1e30


def as_sent(x):
    return jax.tree.map(lambda a: a.astype(jnp.bfloat16) if a.dtype == jnp.float32 else a, x)


def layer_norm(summed, gain_vec, shift_vec):
    row_mean = jnp.mean(summed, axis=-1, keepdims=True)
    centred = summed - row_mean
    row_var = jnp.mean(centred * centred, axis=-1, keepdims=True)
    return centred * lax.rsqrt(row_var + EPSILON) * gain_vec + shift_vec


def gelu_exact(values):
    return jax.nn.gelu(values, approximate=False)


def row_labels(dealt_order, seq_lengths):
    blocks_of_rows = jnp.repeat(dealt_order, BLK)
    within = jnp.tile(jnp.arange(BLK, dtype=jnp.int32), dealt_order.shape[0])
    seq_ids = blocks_of_rows // BPS
    places = blocks_of_rows % BPS * BLK + within
    numbers = jnp.arange(seq_lengths.shape[0], dtype=jnp.int32)
    seq_bound = jnp.sum(
        jnp.where(seq_ids[:, None] == numbers[None, :], seq_lengths[None, :], 0), axis=1
    )
    return (seq_ids, places < seq_bound)


def blockwise(carried, total_rows, step_rows, visit_block):
    return lax.fori_loop(
        0,
        total_rows // step_rows,
        lambda turn_index, running: visit_block(running, turn_index * step_rows),
        carried,
    )


def masked_scores(query_blk, key_blk, query_seq, key_seq, key_valid, scale_factor):
    allowed = (query_seq[:, None] == key_seq[None, :]) & key_valid[None, :]
    scores = (
        jnp.einsum("qhd,khd->hqk", query_blk, key_blk, preferred_element_type=jnp.float32)
        * scale_factor
    )
    return (jnp.where(allowed[None], scores, NEG_FILL), allowed[None].astype(jnp.float32))


def attention_grads(
    query_blk,
    grad_blk,
    key_blk,
    value_blk,
    query_seq,
    key_seq,
    key_valid,
    row_total,
    row_delta,
    scale_factor,
):
    scores, allowed = masked_scores(query_blk, key_blk, query_seq, key_seq, key_valid, scale_factor)
    probs = jnp.exp(scores - row_total[:, :, None]) * allowed
    grad_probs = jnp.einsum("qhd,khd->hqk", grad_blk, value_blk, preferred_element_type=jnp.float32)
    grad_scores = (probs * (grad_probs - row_delta[:, :, None])).astype(jnp.bfloat16)
    return (probs.astype(jnp.bfloat16), grad_scores)


def gather_params(params):
    return (
        lax.all_gather(params[0], "wsh", axis=0, tiled=True),
        lax.all_gather(params[1], "wsh", axis=0, tiled=True),
        lax.all_gather(params[2], "wsh", axis=0, tiled=True),
        lax.all_gather(params[3], "wsh", axis=0, tiled=True),
        lax.all_gather(params[4], "wsh", axis=0, tiled=True),
        lax.all_gather(params[5], "wsh", axis=0, tiled=True),
        lax.all_gather(params[6], "wsh", axis=0, tiled=True),
        lax.all_gather(params[7], "wsh", axis=0, tiled=True),
        lax.all_gather(params[8], "wsh", axis=0, tiled=True),
        lax.all_gather(params[9], "wsh", axis=0, tiled=True),
        lax.all_gather(params[10], "wsh", axis=0, tiled=True),
        lax.all_gather(params[11], "wsh", axis=0, tiled=True),
        lax.all_gather(params[12], "wsh", axis=0, tiled=True),
        lax.all_gather(params[13], "wsh", axis=0, tiled=True),
        lax.all_gather(params[14], "wsh", axis=0, tiled=True),
    )


def per_device(
    tokens,
    cotangent,
    lengths,
    dealing,
    w_query,
    w_key,
    w_value,
    w_out,
    w_up,
    w_down,
    b_query,
    b_value,
    b_out,
    b_up,
    b_down,
    gain_one,
    shift_one,
    gain_two,
    shift_two,
):
    params = (
        w_query,
        w_key,
        w_value,
        w_out,
        w_up,
        w_down,
        b_query,
        b_value,
        b_out,
        b_up,
        b_down,
        gain_one,
        shift_one,
        gain_two,
        shift_two,
    )
    own_rows = tokens.shape[2]
    width = tokens.shape[3]
    head_size = width // HEADS
    scale_factor = 1.0 / math.sqrt(head_size)
    my_start = lax.axis_index("ctx") * own_rows
    wsh_count = lax.axis_size("wsh")
    grads = tuple(
        (jnp.zeros((item.shape[0] * wsh_count,) + item.shape[1:], jnp.float32) for item in params)
    )
    results = []
    input_grads = []
    for micro in range(MB):
        whole = gather_params(params)
        query_weight, key_weight, value_weight, out_weight, up_weight, down_weight = whole[:6]
        (
            bias_query,
            bias_value,
            bias_out,
            bias_up,
            bias_down,
            gain_first,
            shift_first,
            gain_second,
            shift_second,
        ) = tuple((item.astype(jnp.float32) for item in whole[6:]))
        token_rows = tokens[0, micro]
        seq_all, valid_all = row_labels(dealing[0, micro], lengths[0, micro])
        my_seq = lax.dynamic_slice_in_dim(seq_all, my_start, own_rows)
        my_valid = lax.dynamic_slice_in_dim(valid_all, my_start, own_rows)
        query_low = (
            jnp.dot(token_rows, query_weight, preferred_element_type=jnp.float32) + bias_query
        ).astype(jnp.bfloat16)
        key_low = jnp.dot(token_rows, key_weight, preferred_element_type=jnp.float32).astype(
            jnp.bfloat16
        )
        value_low = (
            jnp.dot(token_rows, value_weight, preferred_element_type=jnp.float32) + bias_value
        ).astype(jnp.bfloat16)
        query_heads = query_low.reshape(own_rows, HEADS, head_size)
        my_key_heads = key_low.reshape(own_rows, HEADS, head_size)
        my_value_heads = value_low.reshape(own_rows, HEADS, head_size)
        start_state = (
            jnp.full((HEADS, own_rows), NEG_FILL, jnp.float32),
            jnp.zeros((HEADS, own_rows), jnp.float32),
            jnp.zeros((own_rows, HEADS, head_size), jnp.float32),
        )
        key_piece = lax.all_gather(key_low, "ctx", axis=0, tiled=True)
        value_piece = lax.all_gather(value_low, "ctx", axis=0, tiled=True)
        piece_rows = key_piece.shape[0]
        step_rows = math.gcd(piece_rows, 512)

        def visit_block(running, offset):
            run_max, run_sum, run_acc = running
            key_blk = lax.dynamic_slice_in_dim(key_piece, offset, step_rows).reshape(
                step_rows, HEADS, head_size
            )
            value_blk = lax.dynamic_slice_in_dim(value_piece, offset, step_rows).reshape(
                step_rows, HEADS, head_size
            )
            key_seq = lax.dynamic_slice_in_dim(seq_all, offset, step_rows)
            key_valid = lax.dynamic_slice_in_dim(valid_all, offset, step_rows)
            scores, allowed = masked_scores(
                query_heads, key_blk, my_seq, key_seq, key_valid, scale_factor
            )
            new_max = jnp.maximum(run_max, jnp.max(scores, axis=-1))
            rescale = jnp.exp(run_max - new_max)
            weights = jnp.exp(scores - new_max[:, :, None]) * allowed
            run_sum = run_sum * rescale + jnp.sum(weights, axis=-1)
            run_acc = run_acc * rescale.T[:, :, None] + jnp.einsum(
                "hqk,khd->qhd",
                weights.astype(jnp.bfloat16),
                value_blk,
                preferred_element_type=jnp.float32,
            )
            return (new_max, run_sum, run_acc)

        final_max, final_sum, final_acc = blockwise(start_state, piece_rows, step_rows, visit_block)
        attended = final_acc / final_sum.T[:, :, None]
        log_total = final_max + jnp.log(final_sum)
        attended_low = attended.reshape(own_rows, width).astype(jnp.bfloat16)
        out_proj = jnp.dot(attended_low, out_weight, preferred_element_type=jnp.float32) + bias_out
        first_sum = token_rows.astype(jnp.float32) + out_proj
        norm_one, norm_one_back = jax.vjp(layer_norm, first_sum, gain_first, shift_first)
        mlp_input = norm_one.astype(jnp.bfloat16)
        up_pre = jnp.dot(mlp_input, up_weight, preferred_element_type=jnp.float32) + bias_up
        activated, gelu_back = jax.vjp(gelu_exact, up_pre)
        activated_low = activated.astype(jnp.bfloat16)
        down_out = (
            jnp.dot(activated_low, down_weight, preferred_element_type=jnp.float32) + bias_down
        )
        result, norm_two_back = jax.vjp(layer_norm, norm_one + down_out, gain_second, shift_second)
        results.append(result.astype(jnp.bfloat16))
        grad_second, grad_gain_b, grad_shift_b = norm_two_back(
            cotangent[0, micro].astype(jnp.float32)
        )
        grad_down_low = grad_second.astype(jnp.bfloat16)
        grad_activated = jnp.einsum(
            "rd,fd->rf", grad_down_low, down_weight, preferred_element_type=jnp.float32
        )
        (grad_up_pre,) = gelu_back(grad_activated)
        grad_up_low = grad_up_pre.astype(jnp.bfloat16)
        grad_norm_one = (
            jnp.einsum("rf,df->rd", grad_up_low, up_weight, preferred_element_type=jnp.float32)
            + grad_second
        )
        grad_first, grad_gain_a, grad_shift_a = norm_one_back(grad_norm_one)
        grad_out_low = grad_first.astype(jnp.bfloat16)
        grad_att_low = jnp.einsum(
            "rd,ed->re", grad_out_low, out_weight, preferred_element_type=jnp.float32
        ).astype(jnp.bfloat16)
        grad_heads = grad_att_low.reshape(own_rows, HEADS, head_size)
        row_delta = jnp.sum(grad_heads.astype(jnp.float32) * attended, axis=-1).T
        empty_heads = jnp.zeros((own_rows, HEADS, head_size), jnp.float32)
        query_key_piece = lax.all_gather(key_low, "ctx", axis=0, tiled=True)
        query_value_piece = lax.all_gather(value_low, "ctx", axis=0, tiled=True)
        query_piece_rows = query_key_piece.shape[0]
        query_step_rows = math.gcd(query_piece_rows, 512)

        def query_visit_block(running, offset):
            key_blk = lax.dynamic_slice_in_dim(query_key_piece, offset, query_step_rows).reshape(
                query_step_rows, HEADS, head_size
            )
            value_blk = lax.dynamic_slice_in_dim(
                query_value_piece, offset, query_step_rows
            ).reshape(query_step_rows, HEADS, head_size)
            key_seq = lax.dynamic_slice_in_dim(seq_all, offset, query_step_rows)
            key_valid = lax.dynamic_slice_in_dim(valid_all, offset, query_step_rows)
            probs_low, grad_scores = attention_grads(
                query_heads,
                grad_heads,
                key_blk,
                value_blk,
                my_seq,
                key_seq,
                key_valid,
                log_total,
                row_delta,
                scale_factor,
            )
            return running + jnp.einsum(
                "hqk,khd->qhd", grad_scores, key_blk, preferred_element_type=jnp.float32
            )

        grad_query_sum = blockwise(
            empty_heads, query_piece_rows, query_step_rows, query_visit_block
        )
        total_all, delta_all = (
            lax.all_gather(log_total.T, "ctx", axis=0, tiled=True),
            lax.all_gather(row_delta.T, "ctx", axis=0, tiled=True),
        )
        query_piece = lax.all_gather(query_low, "ctx", axis=0, tiled=True)
        grad_piece = lax.all_gather(grad_att_low, "ctx", axis=0, tiled=True)
        key_piece_rows = query_piece.shape[0]
        key_step_rows = math.gcd(key_piece_rows, 512)

        def key_visit_block(running, offset):
            grad_key_run, grad_value_run = running
            query_blk = lax.dynamic_slice_in_dim(query_piece, offset, key_step_rows).reshape(
                key_step_rows, HEADS, head_size
            )
            grad_blk = lax.dynamic_slice_in_dim(grad_piece, offset, key_step_rows).reshape(
                key_step_rows, HEADS, head_size
            )
            total_blk = lax.dynamic_slice_in_dim(total_all, offset, key_step_rows)
            delta_blk = lax.dynamic_slice_in_dim(delta_all, offset, key_step_rows)
            query_seq = lax.dynamic_slice_in_dim(seq_all, offset, key_step_rows)
            probs_low, grad_scores = attention_grads(
                query_blk,
                grad_blk,
                my_key_heads,
                my_value_heads,
                query_seq,
                my_seq,
                my_valid,
                total_blk.T,
                delta_blk.T,
                scale_factor,
            )
            grad_key_run = grad_key_run + jnp.einsum(
                "hqk,qhd->khd", grad_scores, query_blk, preferred_element_type=jnp.float32
            )
            grad_value_run = grad_value_run + jnp.einsum(
                "hqk,qhd->khd", probs_low, grad_blk, preferred_element_type=jnp.float32
            )
            return (grad_key_run, grad_value_run)

        grad_key_sum, grad_value_sum = blockwise(
            (empty_heads, empty_heads), key_piece_rows, key_step_rows, key_visit_block
        )
        grad_key_flat = grad_key_sum.reshape(own_rows, width)
        grad_value_flat = grad_value_sum.reshape(own_rows, width)
        grad_query_low = (
            (grad_query_sum * scale_factor).reshape(own_rows, width).astype(jnp.bfloat16)
        )
        grad_key_low = (grad_key_flat * scale_factor).astype(jnp.bfloat16)
        grad_value_low = grad_value_flat.astype(jnp.bfloat16)
        terms = (
            jnp.einsum("rd,re->de", token_rows, grad_query_low, preferred_element_type=jnp.float32),
            jnp.einsum("rd,re->de", token_rows, grad_key_low, preferred_element_type=jnp.float32),
            jnp.einsum("rd,re->de", token_rows, grad_value_low, preferred_element_type=jnp.float32),
            jnp.einsum("rd,re->de", attended_low, grad_out_low, preferred_element_type=jnp.float32),
            jnp.einsum("rd,rf->df", mlp_input, grad_up_low, preferred_element_type=jnp.float32),
            jnp.einsum(
                "rf,rd->fd", activated_low, grad_down_low, preferred_element_type=jnp.float32
            ),
            jnp.sum(grad_query_low.astype(jnp.float32), axis=0),
            jnp.sum(grad_value_low.astype(jnp.float32), axis=0),
            jnp.sum(grad_out_low.astype(jnp.float32), axis=0),
            jnp.sum(grad_up_low.astype(jnp.float32), axis=0),
            jnp.sum(grad_down_low.astype(jnp.float32), axis=0),
            grad_gain_a,
            grad_shift_a,
            grad_gain_b,
            grad_shift_b,
        )
        grads = tuple((total_now + fresh for total_now, fresh in zip(grads, terms)))
        grad_rows = (
            grad_first
            + jnp.einsum(
                "re,de->rd", grad_query_low, query_weight, preferred_element_type=jnp.float32
            )
            + jnp.einsum("re,de->rd", grad_key_low, key_weight, preferred_element_type=jnp.float32)
            + jnp.einsum(
                "re,de->rd", grad_value_low, value_weight, preferred_element_type=jnp.float32
            )
        )
        input_grads.append(grad_rows.astype(jnp.bfloat16))
    shards = jax.tree.map(
        lambda part: part.astype(jnp.float32),
        lax.psum_scatter(as_sent(grads), "wsh", scatter_dimension=0, tiled=True),
    )
    summed = jax.tree.map(lambda part: part.astype(jnp.float32), lax.psum(as_sent(shards), "ctx"))
    return (jnp.stack(results)[None], jnp.stack(input_grads)[None]) + tuple(summed)


MESH_IDS = pl.DeviceIdType.MESH
F32 = jnp.float32
BF16 = jnp.bfloat16
HD = 64
VMEM_BYTES = 60 * 1024 * 1024


def flip(index, bit):
    return index + bit * (1 - 2 * lax.rem(lax.div(index, bit), 2))


def bit_of(index, bit):
    return lax.rem(lax.div(index, bit), 2)


def greet(peers):
    barrier = pltpu.get_barrier_semaphore()
    for peer in peers:
        pl.semaphore_signal(barrier, inc=1, device_id=peer, device_id_type=MESH_IDS)
    pl.semaphore_wait(barrier, len(peers))


def send(src, dst, send_sem, recv_sem, peer):
    copy = pltpu.make_async_remote_copy(
        src_ref=src,
        dst_ref=dst,
        send_sem=send_sem,
        recv_sem=recv_sem,
        device_id=peer,
        device_id_type=MESH_IDS,
    )
    copy.start()
    return copy


def plane_peers(c, w, count):
    return [(lax.rem(c + step, count), w) for step in range(1, count)]


def pack_three(first, second, third, row, pair, out):
    cols = pl.ds(pair * 128, 128)
    a, b, d = (ref[pl.ds(row, BLK), cols] for ref in (first, second, third))
    half = BLK // 2
    for head in range(2):
        lane = slice(head * HD, head * HD + HD)
        out[2 * pair + head, 0:BLK, :] = jnp.concatenate([a[:, lane], b[:, lane]], axis=1)
        out[2 * pair + head, BLK : BLK + half, :] = jnp.concatenate(
            [d[:half, lane], d[half:, lane]], axis=1
        )


def unpack_fold(block):
    return jnp.concatenate([block[:, :HD], block[:, HD:]], axis=0)


def fold(rows):
    half = rows.shape[0] // 2
    return jnp.concatenate([rows[:half], rows[half:]], axis=1)


def all_bytes(ref, sem, peers):
    view = ref.at[pl.ds(0, peers)]
    return pltpu.make_async_copy(view, view, sem)


SQUARE, PAIR, ALONE = 8, 4, 2


def weight_plan(shards):
    plan, first_bulk = [], 3
    for index in range(first_bulk):
        plan.append((index, 0, shards[index].shape[0], SQUARE))
    unit = shards[0].shape[0] * shards[0].shape[1]
    bulk = []
    for index in range(first_bulk, len(shards)):
        rows, cols = shards[index].shape
        parts = max(1, rows * cols // unit)
        for part in range(parts):
            bulk.append((index, part * (rows // parts), rows // parts))
    squares, alone = BULK_WAYS
    for number, item in enumerate(bulk):
        if number < squares:
            way = SQUARE
        elif number >= len(bulk) - alone:
            way = ALONE
        else:
            way = PAIR
        plan.append(item + (way,))
    return plan


BULK_WAYS = (2, 2)


def forward_kernel(heads, plan, n_weights, n_vectors, *refs):
    lens_ref, slot_ref, block_ref, x_ref = refs[:4]
    refs = refs[4:]
    shards, vectors = refs[:n_weights], refs[n_weights : n_weights + n_vectors]
    refs = refs[n_weights + n_vectors :]
    wholes, small_whole, a_ref, kept_ref, lse_ref = refs[:n_weights], *refs[n_weights : n_weights + 4]
    refs = refs[n_weights + 4 :]
    near, stages, refs = refs[:3], refs[3:n_weights], refs[n_weights:]
    small, small_in, bias, q_ref, k_ref, v_ref = refs[:6]
    in_buf = refs[6 : 6 + MB]
    out_buf, back_out, back_in, q_s, k_s, v_s, a_s = refs[6 + MB : 13 + MB]
    (
        w_send,
        w_recv,
        small_sems,
        local_sem,
        stage_sem,
        send_sem,
        recv_sem,
        back_send,
        back_recv,
        keep_sem,
    ) = refs[13 + MB :]
    c, w = lax.axis_index("ctx"), lax.axis_index("wsh")
    o = 1 - w
    by_x, by_y, by_z, by_core = (c, o), (flip(c, 2), w), (flip(c, 4), w), (flip(c, 1), w)
    core, y, z = bit_of(c, 1), bit_of(c, 2), bit_of(c, 4)
    peers = plane_peers(c, w, heads)
    targets = tuple(near) + tuple(wholes[3:])
    staged, locals_ = [], []
    for index, shard in enumerate(shards):
        rows = shard.shape[0]
        spot = pl.ds(pl.multiple_of(w * rows, rows), rows)
        dst = near[index].at[spot] if index < 3 else stages[index - 3]
        copy = pltpu.make_async_copy(shard, dst, stage_sem.at[index])
        copy.start()
        staged.append(copy)
    line, lanes = 0, small.shape[1]
    for vector in vectors:
        for first in range(0, vector.shape[0], lanes):
            piece = vector[pl.ds(first, lanes)].astype(F32)
            small[line : line + 1, :] = piece.reshape(1, lanes)
            line += 1
    greet(peers + [by_x])
    small_sent = send(small, small_in, small_sems.at[0], small_sems.at[1], by_x)

    def part(chunk, side, piece, start, count):
        tensor, first, rows, way = plan[chunk]
        half = shards[tensor].shape[0]
        at = side * half + first + piece * (rows // way) + start
        return targets[tensor].at[pl.ds(pl.multiple_of(at, 8), count)]

    steps = {}

    def sem(kind, chunk):
        return w_send.at[kind, chunk], w_recv.at[kind, chunk]

    def own_piece(way):
        return {SQUARE: core * 4 + z * 2 + y, PAIR: core * 2 + y, ALONE: core}[way]

    for chunk, (tensor, first, rows, way) in enumerate(plan):
        size, mine = rows // way, own_piece(way)
        src = shards[tensor].at[pl.ds(pl.multiple_of(first + mine * size, 8), size)]
        steps[chunk, 0] = send(src, part(chunk, w, mine, 0, size), *sem(0, chunk), by_x)

    def second(chunk):
        _, _, rows, way = plan[chunk]
        if way == ALONE:
            return
        steps[chunk, 0].wait_recv()
        ref = part(chunk, o, own_piece(way), 0, rows // way)
        steps[chunk, 1] = send(ref, ref, *sem(1, chunk), by_y)
        if way == SQUARE:
            steps[chunk, 2] = send(ref, ref, *sem(2, chunk), by_z)

    def third(chunk):
        _, _, rows, way = plan[chunk]
        if way != SQUARE:
            return
        size = rows // way
        steps[chunk, 1].wait_recv()
        steps[chunk, 2].wait_recv()
        ref = part(chunk, o, core * 4 + (1 - z) * 2 + y, 0, size // 2)
        steps[chunk, 3] = send(ref, ref, *sem(3, chunk), by_y)
        ref = part(chunk, o, core * 4 + z * 2 + (1 - y), size // 2, size // 2)
        steps[chunk, 4] = send(ref, ref, *sem(4, chunk), by_z)

    def fourth(chunk):
        _, _, rows, way = plan[chunk]
        for kind in {SQUARE: (3, 4), PAIR: (1,), ALONE: (0,)}[way]:
            steps[chunk, kind].wait_recv()
        ref = part(chunk, o, core * (way // 2), 0, rows // 2)
        steps[chunk, 5] = send(ref, ref, *sem(5, chunk), by_core)

    for index in range(3):
        staged[index].wait()
    for turn in range(5):
        for stage, act in enumerate((second, third, fourth)):
            if 0 <= turn - stage < 3:
                act(turn - stage)
    small_sent.wait()
    small_whole[w] = small[...]
    small_whole[o] = small_in[...]
    for side in range(2):
        for row in range(2):
            bias[row : row + 1, side * lanes : (side + 1) * lanes] = small_whole[
                side, row : row + 1, :
            ]
    width = x_ref.shape[1]
    step = 256
    for index, (weight, out) in enumerate(zip(near, (q_ref, k_ref, v_ref))):
        steps[index, 5].wait_recv()

        def project(turn, carry):
            cols = pl.ds(pl.multiple_of(turn * step, step), step)
            total = jnp.dot(x_ref[...], weight[:, cols], preferred_element_type=F32)
            if index != 1:
                total = total + bias[index // 2 : index // 2 + 1, cols]
            out[:, cols] = total.astype(BF16)
            return carry

        lax.fori_loop(0, width // step, project, 0)
    for m in range(MB):
        for pair in range(heads // 2):
            pack_three(q_ref, k_ref, v_ref, m * BLK, pair, out_buf.at[m])
        for peer in peers:
            send(out_buf.at[m, peer[0]], in_buf[m].at[c], send_sem.at[m], recv_sem.at[m], peer)
        in_buf[m][c] = out_buf[m, c]
    for index in range(n_weights):
        if index < 3:
            copy = pltpu.make_async_copy(near[index], wholes[index], local_sem.at[index])
        else:
            rows = shards[index].shape[0]
            spot = pl.ds(pl.multiple_of(w * rows, rows), rows)
            staged[index].wait()
            copy = pltpu.make_async_copy(
                stages[index - 3], wholes[index].at[spot], local_sem.at[index]
            )
        copy.start()
        locals_.append(copy)

    bulk = range(3, len(plan))
    kinds = {way: [i for i in bulk if plan[i][3] == way] for way in (SQUARE, PAIR, ALONE)}
    squares, pairs, alone = kinds[SQUARE], kinds[PAIR], kinds[ALONE]
    moves = [(second, i) for i in squares + pairs[:2]]
    moves += [None]
    moves += [(third, i) for i in squares] + [(second, i) for i in pairs[2:3]]
    moves += [None]
    moves += [(fourth, i) for i in squares] + [(second, i) for i in pairs[3:4]]
    moves += [(fourth, i) for i in pairs[:2]]
    moves += [None]
    moves += [(second, i) for i in pairs[4:]] + [(fourth, i) for i in pairs[2:]]
    moves += [(fourth, i) for i in alone]

    def pump():
        while moves:
            move = moves.pop(0)
            if move is None:
                return
            move[0](move[1])

    blocks = heads
    span = BPS * BLK
    for m in range(MB):
        pump()
        all_bytes(in_buf[m], recv_sem.at[m], heads - 1).wait()
        keep = pltpu.make_async_copy(in_buf[m], kept_ref.at[m], keep_sem.at[m])
        keep.start()
        for b in range(blocks):
            got = in_buf[m][slot_ref[0, m, b]]
            q_s[b * BLK : (b + 1) * BLK, :] = got[:BLK, :HD]
            k_s[b * BLK : (b + 1) * BLK, :] = got[:BLK, HD:]
            v_s[b * BLK : (b + 1) * BLK, :] = unpack_fold(got[BLK:])

        def one_sequence(s, carry):
            rows = pl.ds(pl.multiple_of(s * span, span), span)
            scores = lax.dot_general(
                k_s[rows, :], q_s[rows, :], (((1,), (1,)), ((), ())), preferred_element_type=F32
            ) * (1.0 / math.sqrt(HD))
            place = lax.broadcasted_iota(jnp.int32, scores.shape, 0)
            scores = jnp.where(place < lens_ref[0, m, s], scores, NEG_FILL)
            top = jnp.max(scores, axis=0, keepdims=True)
            weights = jnp.exp(scores - top)
            total = jnp.sum(weights, axis=0, keepdims=True)
            out_t = lax.dot_general(
                v_s[rows, :],
                weights.astype(BF16),
                (((0,), (0,)), ((), ())),
                preferred_element_type=F32,
            )
            a_s[pl.ds(s * BPS, BPS)] = (out_t / total).T.reshape(BPS, BLK, HD)
            lse_ref[pl.ds(m * (blocks // BPS) + s, 1), :] = top + jnp.log(total)
            return carry

        lax.fori_loop(0, blocks // BPS, one_sequence, 0)
        for t in range(blocks):
            back_out[m, t] = fold(a_s[block_ref[0, m, t]]).astype(BF16)
        for peer in peers:
            send(
                back_out.at[m, peer[0]], back_in.at[m, c], back_send.at[m], back_recv.at[m], peer
            )
        back_in[m, c] = back_out[m, c]
    pump()
    for m in range(MB):
        all_bytes(back_in.at[m], back_recv.at[m], heads - 1).wait()
        for pair in range(heads // 2):
            a_ref[m * BLK : (m + 1) * BLK, pair * 128 : (pair + 1) * 128] = jnp.concatenate(
                [unpack_fold(back_in[m, 2 * pair]), unpack_fold(back_in[m, 2 * pair + 1])], axis=1
            )
    for m in range(MB):
        all_bytes(out_buf.at[m], send_sem.at[m], heads - 1).wait()
        all_bytes(back_out.at[m], back_send.at[m], heads - 1).wait()
        pltpu.make_async_copy(in_buf[m], kept_ref.at[m], keep_sem.at[m]).wait()
    for chunk in bulk:
        steps[chunk, 5].wait_recv()
    for flight in steps.values():
        flight.wait_send()
    for copy in locals_:
        copy.wait()


def forward(lens, slot_of, block_of, x, shards, vectors, heads):
    plan = weight_plan(shards)
    count = len(shards)
    anywhere, vmem = pl.BlockSpec(memory_space=pl.ANY), pl.BlockSpec(memory_space=pltpu.VMEM)
    smem = pl.BlockSpec(memory_space=pltpu.SMEM)
    rows, width = x.shape
    pack_rows = BLK + BLK // 2
    span = BPS * BLK
    lanes = min(item.shape[0] for item in vectors)
    lines = sum(item.shape[0] for item in vectors) // lanes
    whole = lambda s: (2 * s.shape[0],) + s.shape[1:]
    return pl.pallas_call(
        functools.partial(forward_kernel, heads, plan, count, len(vectors)),
        out_shape=[jax.ShapeDtypeStruct(whole(s), s.dtype) for s in shards]
        + [
            jax.ShapeDtypeStruct((2, lines, lanes), F32),
            jax.ShapeDtypeStruct((rows, width), BF16),
            jax.ShapeDtypeStruct((MB, heads, pack_rows, 128), BF16),
            jax.ShapeDtypeStruct((8, span), F32),
        ],
        in_specs=[smem] * 3 + [vmem] + [anywhere] * count + [vmem] * len(vectors),
        out_specs=[anywhere] * count + [vmem, vmem, anywhere, vmem],
        scratch_shapes=[pltpu.VMEM(whole(s), s.dtype) for s in shards[:3]]
        + [pltpu.VMEM(s.shape, s.dtype) for s in shards[3:]]
        + [pltpu.VMEM((lines, lanes), F32)] * 2
        + [pltpu.VMEM((2, width), F32)]
        + [pltpu.VMEM((rows, width), BF16)] * 3
        + [pltpu.VMEM((heads, pack_rows, 128), BF16)] * MB
        + [
            pltpu.VMEM((MB, heads, pack_rows, 128), BF16),
            pltpu.VMEM((MB, heads, BLK // 2, 128), BF16),
            pltpu.VMEM((MB, heads, BLK // 2, 128), BF16),
            pltpu.VMEM((heads * BLK, HD), BF16),
            pltpu.VMEM((heads * BLK, HD), BF16),
            pltpu.VMEM((heads * BLK, HD), BF16),
            pltpu.VMEM((heads, BLK, HD), F32),
            pltpu.SemaphoreType.DMA((6, len(plan))),
            pltpu.SemaphoreType.DMA((6, len(plan))),
            pltpu.SemaphoreType.DMA((2,)),
            pltpu.SemaphoreType.DMA((count,)),
            pltpu.SemaphoreType.DMA((count,)),
        ]
        + [pltpu.SemaphoreType.DMA((MB,))] * 5,
        compiler_params=pltpu.CompilerParams(
            collective_id=1, has_side_effects=True, vmem_limit_bytes=VMEM_BYTES
        ),
        name="forward",
    )(lens, slot_of, block_of, x, *shards, *vectors)


def attend_back_kernel(heads, *refs):
    lens_ref, slot_ref, block_ref, da_ref, kept_ref, lse_ref = refs[:6]
    x_ref, a_ref, n_ref, g_ref, do_ref, du_ref, dm_ref = refs[6:13]
    dq_ref, dk_ref, dv_ref = refs[13:16]
    x_all, a_all, n_all, g_all, do_all, du_all, dm_all, dqkv_all = refs[16:24]
    in_buf = refs[24 : 24 + MB]
    out_buf, back_out, back_in = refs[24 + MB : 27 + MB]
    q_s, k_s, v_s, a_s, dq_s, dk_s, dv_s = refs[27 + MB : 34 + MB]
    send_sem, recv_sem, back_send, back_recv, mate_send, mate_recv, own_sem = refs[34 + MB :]
    c, w = lax.axis_index("ctx"), lax.axis_index("wsh")
    core = bit_of(c, 1)
    mate = (flip(c, 1), w)
    peers = plane_peers(c, w, heads)
    blocks = heads
    rows_own = da_ref.shape[0]
    greet(peers)

    place = pl.ds(pl.multiple_of(core * rows_own, rows_own), rows_own)
    moves = []

    def share(src, dst, lanes):
        for first, size, to, per_core in lanes:
            index = len(moves)
            step = size if per_core else 0
            own_from = pl.ds(pl.multiple_of(first + core * step, 128), size)
            mate_from = pl.ds(pl.multiple_of(first + (1 - core) * step, 128), size)
            spot = dst.at[place, pl.ds(to, size)]
            own = pltpu.make_async_copy(src.at[:, own_from], spot, own_sem.at[index])
            own.start()
            gone = send(
                src.at[:, mate_from], spot, mate_send.at[index], mate_recv.at[index], mate
            )
            moves.append((own, gone))

    width = da_ref.shape[1]
    hidden = g_ref.shape[1]
    for m in range(MB):
        row = slice(m * BLK, (m + 1) * BLK)
        for pair in range(heads // 2):
            both = da_ref[row, pair * 128 : (pair + 1) * 128]
            for head in range(2):
                out_buf[m, 2 * pair + head] = fold(both[:, head * HD : (head + 1) * HD])
        for peer in peers:
            send(out_buf.at[m, peer[0]], in_buf[m].at[c], send_sem.at[m], recv_sem.at[m], peer)
        in_buf[m][c] = out_buf[m, c]
    for src, dst in ((x_ref, x_all), (a_ref, a_all), (n_ref, n_all), (dm_ref, dm_all)):
        share(src, dst, ((0, width, 0, False),))
    share(do_ref, do_all, ((0, width // 2, 0, True),))
    share(du_ref, du_all, ((0, hidden // 2, 0, True),))
    share(g_ref, g_all, ((0, hidden // 4, 0, True), (hidden // 2, hidden // 4, hidden // 4, True)))
    for m in range(MB):
        all_bytes(in_buf[m], recv_sem.at[m], heads - 1).wait()
        for b in range(blocks):
            slot = slot_ref[0, m, b]
            got = kept_ref[m, slot]
            rows = slice(b * BLK, (b + 1) * BLK)
            q_s[rows, :] = got[:BLK, :HD]
            k_s[rows, :] = got[:BLK, HD:]
            v_s[rows, :] = unpack_fold(got[BLK:])
            a_s[rows, :] = unpack_fold(in_buf[m][slot])
        span = BPS * BLK

        def one_sequence(s, carry):
            rows = pl.ds(pl.multiple_of(s * span, span), span)
            qq, kk, vv, dd = q_s[rows, :], k_s[rows, :], v_s[rows, :], a_s[rows, :]
            scale = 1.0 / math.sqrt(HD)
            minor = (((1,), (1,)), ((), ()))
            scores = lax.dot_general(kk, qq, minor, preferred_element_type=F32) * scale
            spot = lax.broadcasted_iota(jnp.int32, scores.shape, 0)
            total = lse_ref[pl.ds(m * (blocks // BPS) + s, 1), :]
            probs = jnp.exp(jnp.where(spot < lens_ref[0, m, s], scores - total, NEG_FILL))
            dp = lax.dot_general(vv, dd, minor, preferred_element_type=F32)
            both = probs * dp
            delta = jnp.sum(both, axis=0, keepdims=True)
            ds = (both - probs * delta).astype(BF16)
            here = pl.ds(s * BPS, BPS)
            split = (BPS, BLK, HD)
            dv = jnp.dot(probs.astype(BF16), dd, preferred_element_type=F32)
            dv_s[here] = dv.reshape(split)
            dk_s[here] = (jnp.dot(ds, qq, preferred_element_type=F32) * scale).reshape(split)
            dq_t = lax.dot_general(kk, ds, (((0,), (0,)), ((), ())), preferred_element_type=F32)
            dq_s[here] = (dq_t.T * scale).reshape(split)
            return carry

        lax.fori_loop(0, blocks // BPS, one_sequence, 0)
        for t in range(blocks):
            at = block_ref[0, m, t]
            back_out[m, t, 0:BLK, :] = jnp.concatenate([dq_s[at], dk_s[at]], axis=1).astype(BF16)
            back_out[m, t, BLK:, :] = fold(dv_s[at]).astype(BF16)
        for peer in peers:
            send(
                back_out.at[m, peer[0]], back_in.at[m, c], back_send.at[m], back_recv.at[m], peer
            )
        back_in[m, c] = back_out[m, c]
    for m in range(MB):
        all_bytes(back_in.at[m], back_recv.at[m], heads - 1).wait()
        row = slice(m * BLK, (m + 1) * BLK)
        for pair in range(heads // 2):
            lanes = slice(pair * 128, (pair + 1) * 128)
            one, two = back_in[m, 2 * pair], back_in[m, 2 * pair + 1]
            dq_ref[row, lanes] = jnp.concatenate([one[:BLK, :HD], two[:BLK, :HD]], axis=1)
            dk_ref[row, lanes] = jnp.concatenate([one[:BLK, HD:], two[:BLK, HD:]], axis=1)
            dv_ref[row, lanes] = jnp.concatenate(
                [unpack_fold(one[BLK:]), unpack_fold(two[BLK:])], axis=1
            )
    for index, ref in enumerate((dq_ref, dk_ref, dv_ref)):
        half = width // 2
        spot = dqkv_all.at[place, pl.ds(index * half, half)]
        number = len(moves)
        own_from = pl.ds(pl.multiple_of(core * half, 128), half)
        mate_from = pl.ds(pl.multiple_of((1 - core) * half, 128), half)
        own = pltpu.make_async_copy(ref.at[:, own_from], spot, own_sem.at[number])
        own.start()
        gone = send(ref.at[:, mate_from], spot, mate_send.at[number], mate_recv.at[number], mate)
        moves.append((own, gone))
    for m in range(MB):
        all_bytes(out_buf.at[m], send_sem.at[m], heads - 1).wait()
        all_bytes(back_out.at[m], back_send.at[m], heads - 1).wait()
    for own, gone in moves:
        own.wait()
        gone.wait()


def attend_back(lens, slot_of, block_of, da, kept, lse, x, a, n1, g, do, du, dm, heads):
    vmem, smem = pl.BlockSpec(memory_space=pltpu.VMEM), pl.BlockSpec(memory_space=pltpu.SMEM)
    anywhere = pl.BlockSpec(memory_space=pl.ANY)
    rows, width = da.shape
    hidden = g.shape[1]
    pack_rows = BLK + BLK // 2
    both = 2 * rows
    moves = 11
    shape = lambda *dims: jax.ShapeDtypeStruct(dims, BF16)
    return pl.pallas_call(
        functools.partial(attend_back_kernel, heads),
        out_shape=[shape(rows, width)] * 3
        + [
            shape(both, width),
            shape(both, width),
            shape(both, width),
            shape(both, hidden // 2),
            shape(both, width // 2),
            shape(both, hidden // 2),
            shape(both, width),
            shape(both, 3 * width // 2),
        ],
        in_specs=[smem] * 3 + [vmem] * 10,
        out_specs=[vmem] * 3 + [anywhere] * 8,
        scratch_shapes=[pltpu.VMEM((heads, BLK // 2, 128), BF16)] * MB
        + [
            pltpu.VMEM((MB, heads, BLK // 2, 128), BF16),
            pltpu.VMEM((MB, heads, pack_rows, 128), BF16),
            pltpu.VMEM((MB, heads, pack_rows, 128), BF16),
        ]
        + [pltpu.VMEM((heads * BLK, HD), BF16)] * 4
        + [pltpu.VMEM((heads, BLK, HD), F32)] * 3
        + [pltpu.SemaphoreType.DMA((MB,))] * 4
        + [pltpu.SemaphoreType.DMA((moves,))] * 3,
        compiler_params=pltpu.CompilerParams(
            collective_id=2, has_side_effects=True, vmem_limit_bytes=VMEM_BYTES
        ),
        name="attend_back",
    )(lens, slot_of, block_of, da, kept, lse, x, a, n1, g, do, du, dm)


CHUNKS = 2
ORDERS = {
    (0, 0): "xyzZ",
    (0, 1): "xzyZ",
    (1, 0): "yxZz",
    (1, 1): "yZxz",
    (2, 0): "zxyZ",
    (2, 1): "Zyxz",
}


def landing_shapes(order, shape):
    shards, sides, shapes = 8, 2, []
    for name in order:
        if name == "x":
            sides = 1
        else:
            shards //= 2
        shapes.append((sides, shards, shape[2] // CHUNKS, shape[3]))
    return shapes


def reduce_kernel(ga1_ref, ga2_ref, gb_ref, gc_ref, vec_ref, *refs):
    o_a, o_b, o_c, vec_out = refs[:4]
    s_a, s_b, s_c = refs[4:7]
    r_bufs = {key: refs[7 + 4 * i : 11 + 4 * i] for i, key in enumerate(ORDERS)}
    rest = refs[7 + 4 * len(ORDERS) :]
    v_recv, v_sum = rest[:2]
    load_sem, rs_send, rs_recv, ag_send, ag_recv, v_send_sem, v_recv_sem, own_sem = rest[2:]
    c, x = lax.axis_index("ctx"), lax.axis_index("wsh")
    core, y, z, zz = bit_of(c, 1), bit_of(c, 2), bit_of(c, 4), bit_of(c, 8)
    by_x, by_y, by_z = (c, 1 - x), (flip(c, 2), x), (flip(c, 4), x)
    by_zz, by_core = (flip(c, 8), x), (flip(c, 1), x)
    shards = 8
    lanes1 = ga1_ref.shape[3]
    lanes2 = ga2_ref.shape[3]
    loads = [
        pltpu.make_async_copy(ga1_ref, s_a.at[:, :, :, pl.ds(0, lanes1)], load_sem.at[0]),
        pltpu.make_async_copy(ga2_ref, s_a.at[:, :, :, pl.ds(lanes1, lanes2)], load_sem.at[1]),
        pltpu.make_async_copy(gb_ref, s_b, load_sem.at[2]),
        pltpu.make_async_copy(gc_ref, s_c, load_sem.at[3]),
    ]
    for load in loads:
        load.start()
    greet((by_x, by_y, by_z, by_zz, by_core))
    vec_steps = [
        send(vec_ref.at[1 - x], v_recv.at[0], v_send_sem.at[0], v_recv_sem.at[0], by_x)
    ]

    def vec_next(step, peer):
        vec_steps[step].wait_recv()
        before = vec_ref[x] if step == 0 else v_sum[step - 1]
        v_sum[step] = before + v_recv[step]
        if peer is not None:
            vec_steps.append(
                send(
                    v_sum.at[step],
                    v_recv.at[step + 1],
                    v_send_sem.at[step + 1],
                    v_recv_sem.at[step + 1],
                    peer,
                )
            )

    for load in loads:
        load.wait()
    bits = {"y": y, "z": z, "Z": zz}
    peers = {"x": by_x, "y": by_y, "z": by_z, "Z": by_zz}
    plans, gathers = {}, {}
    for key, order in ORDERS.items():
        first, count, sided = 0, 8, False
        plans[key], back = [], []
        for name in order:
            if name == "x":
                plans[key].append((by_x, 1 - x, x, first, first, count))
                sided = True
                continue
            count //= 2
            out, keep = first + (1 - bits[name]) * count, first + bits[name] * count
            side = x if sided else None
            plans[key].append((peers[name], side, side, out, keep, count))
            back.append((peers[name], keep, out, count))
            first = keep
        gathers[key] = back[::-1]
    sums = (s_a, s_b, s_c)
    outs = (o_a, o_b, o_c)
    flights = {}

    def chunk_rows(part, chunk):
        rows = sums[part].shape[2] // CHUNKS
        return pl.ds(chunk * rows, rows)

    def reduce_send(part, step, chunk):
        peer, side, _, first, _, count = plans[part, chunk][step]
        rows = chunk_rows(part, chunk)
        dst = r_bufs[part, chunk][step]
        if side is None:
            src = sums[part].at[:, pl.ds(first, count), rows]
        else:
            src, dst = sums[part].at[side, pl.ds(first, count), rows], dst.at[0]
        flights[part, step, chunk] = send(
            src, dst, rs_send.at[part, step, chunk], rs_recv.at[part, step, chunk], peer
        )

    def reduce_add(part, step, chunk):
        _, _, side, _, first, count = plans[part, chunk][step]
        rows = chunk_rows(part, chunk)
        flights[part, step, chunk].wait_recv()
        total, fresh = sums[part], r_bufs[part, chunk][step]
        sides = ((0, 0), (1, 1)) if side is None else ((side, 0),)
        for here, there in sides:

            def body(index, carry):
                spot = first + index
                total[here, spot, rows] = (
                    total[here, spot, rows].astype(F32) + fresh[there, index].astype(F32)
                ).astype(BF16)
                return carry

            lax.fori_loop(0, count, body, 0)

    for chunk in range(CHUNKS):
        for part in range(3):
            reduce_send(part, 0, chunk)
    vec_peers = (by_y, by_z, by_zz, by_core, None)
    for step in range(1, 4):
        vec_next(step - 1, vec_peers[step - 1])
        for chunk in range(CHUNKS):
            for part in range(3):
                reduce_add(part, step - 1, chunk)
                reduce_send(part, step, chunk)
    owns, spread = [], {}
    vec_next(3, by_core)
    for chunk in range(CHUNKS):
        for part in range(3):
            reduce_add(part, 3, chunk)
            rows = chunk_rows(part, chunk)
            peer, first, _, _ = gathers[part, chunk][0]
            src = sums[part].at[x, pl.ds(first, 1), rows]
            dst = outs[part].at[core, pl.ds(first, 1), rows]
            own = pltpu.make_async_copy(src, dst, own_sem.at[part, chunk])
            own.start()
            owns.append(own)
            sem = lambda kind: (ag_send.at[part, kind, chunk], ag_recv.at[part, kind, chunk])
            spread[part, 0, chunk] = send(src, dst, *sem(0), peer)
            spread[part, 3, chunk] = send(src, dst, *sem(3), by_core)
    vec_next(4, None)
    vec_out[...] = v_sum[4]
    for own in owns:
        own.wait()
    for step in range(1, 4):
        for chunk in range(CHUNKS):
            for part in range(3):
                rows = chunk_rows(part, chunk)
                spread[part, step - 1, chunk].wait_recv()
                sem = lambda kind: (ag_send.at[part, kind, chunk], ag_recv.at[part, kind, chunk])
                if step < 3:
                    peer, first, _, count = gathers[part, chunk][step]
                    ref = outs[part].at[core, pl.ds(first, count), rows]
                    spread[part, step, chunk] = send(ref, ref, *sem(step), peer)
                _, _, first, count = gathers[part, chunk][step - 1]
                fresh = outs[part].at[core, pl.ds(first, count), rows]
                spread[part, 3 + step, chunk] = send(fresh, fresh, *sem(3 + step), by_core)
    for key, flight in spread.items():
        if key[1] >= 3:
            flight.wait_recv()
        flight.wait_send()
    for flight in flights.values():
        flight.wait_send()
    for flight in vec_steps:
        flight.wait_send()


def reduce_grads(ga1, ga2, gb, gc, vec):
    vmem, anywhere = pl.BlockSpec(memory_space=pltpu.VMEM), pl.BlockSpec(memory_space=pl.ANY)
    lanes = ga1.shape[3] + ga2.shape[3]
    a_shape = ga1.shape[:3] + (lanes,)
    b_shape, c_shape = gb.shape, gc.shape
    scratch = [pltpu.VMEM(s, BF16) for s in (a_shape, b_shape, c_shape)]
    shapes = (a_shape, b_shape, c_shape)
    for (part, _), order in ORDERS.items():
        scratch += [pltpu.VMEM(shape, BF16) for shape in landing_shapes(order, shapes[part])]
    scratch += [
        pltpu.VMEM((5,) + vec.shape[1:], F32),
        pltpu.VMEM((5,) + vec.shape[1:], F32),
        pltpu.SemaphoreType.DMA((4,)),
        pltpu.SemaphoreType.DMA((3, 4, CHUNKS)),
        pltpu.SemaphoreType.DMA((3, 4, CHUNKS)),
        pltpu.SemaphoreType.DMA((3, 7, CHUNKS)),
        pltpu.SemaphoreType.DMA((3, 7, CHUNKS)),
        pltpu.SemaphoreType.DMA((5,)),
        pltpu.SemaphoreType.DMA((5,)),
        pltpu.SemaphoreType.DMA((3, CHUNKS)),
    ]
    return pl.pallas_call(
        reduce_kernel,
        out_shape=[
            jax.ShapeDtypeStruct(a_shape, BF16),
            jax.ShapeDtypeStruct(b_shape, BF16),
            jax.ShapeDtypeStruct(c_shape, BF16),
            jax.ShapeDtypeStruct(vec.shape[1:], F32),
        ],
        in_specs=[anywhere] * 4 + [vmem],
        out_specs=[anywhere] * 3 + [vmem],
        scratch_shapes=scratch,
        compiler_params=pltpu.CompilerParams(
            collective_id=3, has_side_effects=True, vmem_limit_bytes=VMEM_BYTES
        ),
        name="reduce_grads",
    )(ga1, ga2, gb, gc, vec)


def widen_kernel(a_ref, b_ref, c_ref, *outs):
    half = outs[0].shape[1] // 2
    for index, out in enumerate(outs[:4]):
        for core in range(2):
            out[:, core * half : (core + 1) * half] = a_ref[
                core, 0, :, index * half : (index + 1) * half
            ].astype(F32)
    up, down = outs[4:]
    half = up.shape[1] // 2
    for core in range(2):
        up[:, core * half : (core + 1) * half] = b_ref[core, 0].astype(F32)
        down[core, 0] = c_ref[core, 0].astype(F32)


def widen(o_a, o_b, o_c):
    shards = o_a.shape[1]
    block = lambda item: pl.BlockSpec((2, 1) + item.shape[2:], lambda i: (0, i, 0, 0))
    rows = o_a.shape[2]
    square = (shards * rows, o_a.shape[3] // 2)
    wide = (shards * rows, 2 * o_b.shape[3])
    return pl.pallas_call(
        widen_kernel,
        grid=(shards,),
        out_shape=[jax.ShapeDtypeStruct(square, F32)] * 4
        + [jax.ShapeDtypeStruct(wide, F32), jax.ShapeDtypeStruct(o_c.shape, F32)],
        in_specs=[block(o_a), block(o_b), block(o_c)],
        out_specs=[pl.BlockSpec((rows, square[1]), lambda i: (i, 0))] * 4
        + [pl.BlockSpec((rows, wide[1]), lambda i: (i, 0)), block(o_c)],
        compiler_params=pltpu.CompilerParams(vmem_limit_bytes=VMEM_BYTES),
        name="widen",
    )(o_a, o_b, o_c)


def norm_parts(summed):
    row_mean = jnp.mean(summed, axis=-1, keepdims=True)
    centred = summed - row_mean
    row_var = jnp.mean(centred * centred, axis=-1, keepdims=True)
    scale = lax.rsqrt(row_var + EPSILON)
    return centred * scale, scale


def norm_back(grad, unit, scale, gain):
    inner = grad * gain
    mean_one = jnp.mean(inner, axis=-1, keepdims=True)
    mean_two = jnp.mean(inner * unit, axis=-1, keepdims=True)
    return scale * (inner - mean_one - unit * mean_two)


def dot(a, b, dims):
    return lax.dot_general(a, b, (dims, ((), ())), preferred_element_type=F32)


ROW_COL, COL_COL, ROW_ROW = ((1,), (0,)), ((1,), (1,)), ((0,), (0,))


def per_device_heads(tokens, cotangent, lengths, dealing, *params):
    rows_in = tokens.shape[2]
    width = tokens.shape[3]
    rows = MB * rows_in
    weights, vectors = params[:6], params[6:]
    sizes = [item.shape[0] for item in vectors]
    x = tokens.reshape(rows, width)
    lens, block_of = lengths, dealing
    slot_of = jnp.argsort(block_of, axis=2).astype(jnp.int32)
    *wholes, small_whole, a, kept, lse = forward(
        lens, slot_of, block_of, x, weights, vectors, HEADS
    )
    query_w, key_w, value_w, out_w, up_w, down_w = wholes
    spots = [sum(sizes[:i]) for i in range(len(sizes) + 1)]
    lines = [spot // small_whole.shape[2] for spot in spots]
    _, _, bias_out, bias_up, bias_down, gain_one, shift_one, gain_two, shift_two = (
        small_whole[:, lines[i] : lines[i + 1]].reshape(1, -1) for i in range(len(sizes))
    )
    h_one = x.astype(F32) + (dot(a, out_w, ROW_COL) + bias_out)
    unit_one, scale_one = norm_parts(h_one)
    n_one = unit_one * gain_one + shift_one
    n_low = n_one.astype(BF16)
    u = dot(n_low, up_w, ROW_COL) + bias_up
    below = 0.5 * (1.0 + lax.erf(u * math.sqrt(0.5)))
    slope = below + u * jnp.exp(-0.5 * u * u) * (1.0 / math.sqrt(2.0 * math.pi))
    g, slope = lax.optimization_barrier(((u * below).astype(BF16), slope))
    h_two = n_one + (dot(g, down_w, ROW_COL) + bias_down)
    unit_two, scale_two = norm_parts(h_two)
    output = (unit_two * gain_two + shift_two).astype(BF16)

    cot = cotangent.reshape(rows, width).astype(F32)
    dh_two = norm_back(cot, unit_two, scale_two, gain_two)
    dm = dh_two.astype(BF16)
    du = lax.optimization_barrier((slope * dot(dm, down_w, COL_COL)).astype(BF16))
    dn = lax.optimization_barrier(dot(du, up_w, COL_COL)) + dh_two
    dh_one = norm_back(dn, unit_one, scale_one, gain_one)
    do = dh_one.astype(BF16)
    da = dot(do, out_w, COL_COL).astype(BF16)

    dq, dk, dv, x_all, a_all, n_all, g_all, do_all, du_all, dm_all, dqkv_all = attend_back(
        lens, slot_of, block_of, da, kept, lse, x, a, n_low, g, do, du, dm, HEADS
    )
    total = lambda item: jnp.sum(item.astype(F32), axis=0)
    vec = [
        total(dq),
        total(dv),
        total(do),
        total(du),
        total(dm),
        total(dn * unit_one),
        total(dn),
        total(cot * unit_two),
        total(cot),
    ]
    vec = jnp.concatenate([item.reshape(2, -1) for item in vec], axis=1).reshape(2, -1, 128)
    ga1 = dot(x_all, dqkv_all, ROW_ROW).astype(BF16).reshape(2, 8, -1, dqkv_all.shape[1])
    ga2 = dot(a_all, do_all, ROW_ROW).astype(BF16).reshape(2, 8, -1, do_all.shape[1])
    gb = dot(n_all, du_all, ROW_ROW).astype(BF16).reshape(2, 8, -1, du_all.shape[1])
    gc = dot(g_all, dm_all, ROW_ROW).astype(BF16).reshape(2, 8, -1, dm_all.shape[1])
    o_a, o_b, o_c, vec_sum = reduce_grads(ga1, ga2, gb, gc, vec)
    grad_rows = (
        dh_one + dot(dq, query_w, COL_COL) + dot(dk, key_w, COL_COL) + dot(dv, value_w, COL_COL)
    )
    grad_tokens = grad_rows.astype(BF16)
    *square, up, down = widen(o_a, o_b, o_c)
    down = down.reshape(-1, width)
    vec_sum = vec_sum.reshape(-1)
    ends = [vec_sum[spots[i] : spots[i + 1]] for i in range(len(sizes))]
    shape = (1, MB, rows_in, width)
    return (
        (output.reshape(shape), grad_tokens.reshape(shape))
        + (*square, up, down)
        + tuple(ends)
    )


def solution(mesh):
    placed = (
        P("wsh", None, "ctx", None),
        P("wsh", None, "ctx", None),
        P("wsh", None, None),
        P("wsh", None, None),
        P("wsh", None),
        P("wsh", None),
        P("wsh", None),
        P("wsh", None),
        P("wsh", None),
        P("wsh", None),
        P("wsh"),
        P("wsh"),
        P("wsh"),
        P("wsh"),
        P("wsh"),
        P("wsh"),
        P("wsh"),
        P("wsh"),
        P("wsh"),
    )
    by_heads = mesh.shape["ctx"] == HEADS and mesh.shape["wsh"] == 2
    return jax.shard_map(
        per_device_heads if by_heads else per_device,
        mesh=mesh,
        in_specs=placed,
        out_specs=(
            P("wsh", None, "ctx", None),
            P("wsh", None, "ctx", None),
            P("wsh", None),
            P("wsh", None),
            P("wsh", None),
            P("wsh", None),
            P("wsh", None),
            P("wsh", None),
            P("wsh"),
            P("wsh"),
            P("wsh"),
            P("wsh"),
            P("wsh"),
            P("wsh"),
            P("wsh"),
            P("wsh"),
            P("wsh"),
        ),
        check_vma=False,
    )
```

```python
import functools
import math

import jax
import jax.numpy as jnp
from jax import lax
from jax.experimental import pallas as pl
from jax.experimental.pallas import tpu as pltpu
from jax.sharding import PartitionSpec as P

HEADS = 16
BPS = 8
MB = 3
BLK = 64


EPSILON = 1e-12
NEG_FILL = -1e30


def as_sent(x):
    return jax.tree.map(lambda a: a.astype(jnp.bfloat16) if a.dtype == jnp.float32 else a, x)


def layer_norm(summed, gain_vec, shift_vec):
    row_mean = jnp.mean(summed, axis=-1, keepdims=True)
    centred = summed - row_mean
    row_var = jnp.mean(centred * centred, axis=-1, keepdims=True)
    return centred * lax.rsqrt(row_var + EPSILON) * gain_vec + shift_vec


def gelu_exact(values):
    return jax.nn.gelu(values, approximate=False)


def row_labels(dealt_order, seq_lengths):
    blocks_of_rows = jnp.repeat(dealt_order, BLK)
    within = jnp.tile(jnp.arange(BLK, dtype=jnp.int32), dealt_order.shape[0])
    seq_ids = blocks_of_rows // BPS
    places = blocks_of_rows % BPS * BLK + within
    numbers = jnp.arange(seq_lengths.shape[0], dtype=jnp.int32)
    seq_bound = jnp.sum(
        jnp.where(seq_ids[:, None] == numbers[None, :], seq_lengths[None, :], 0), axis=1
    )
    return (seq_ids, places < seq_bound)


def blockwise(carried, total_rows, step_rows, visit_block):
    return lax.fori_loop(
        0,
        total_rows // step_rows,
        lambda turn_index, running: visit_block(running, turn_index * step_rows),
        carried,
    )


def masked_scores(query_blk, key_blk, query_seq, key_seq, key_valid, scale_factor):
    allowed = (query_seq[:, None] == key_seq[None, :]) & key_valid[None, :]
    scores = (
        jnp.einsum("qhd,khd->hqk", query_blk, key_blk, preferred_element_type=jnp.float32)
        * scale_factor
    )
    return (jnp.where(allowed[None], scores, NEG_FILL), allowed[None].astype(jnp.float32))


def attention_grads(
    query_blk,
    grad_blk,
    key_blk,
    value_blk,
    query_seq,
    key_seq,
    key_valid,
    row_total,
    row_delta,
    scale_factor,
):
    scores, allowed = masked_scores(query_blk, key_blk, query_seq, key_seq, key_valid, scale_factor)
    probs = jnp.exp(scores - row_total[:, :, None]) * allowed
    grad_probs = jnp.einsum("qhd,khd->hqk", grad_blk, value_blk, preferred_element_type=jnp.float32)
    grad_scores = (probs * (grad_probs - row_delta[:, :, None])).astype(jnp.bfloat16)
    return (probs.astype(jnp.bfloat16), grad_scores)


def gather_params(params):
    return (
        lax.all_gather(params[0], "wsh", axis=0, tiled=True),
        lax.all_gather(params[1], "wsh", axis=0, tiled=True),
        lax.all_gather(params[2], "wsh", axis=0, tiled=True),
        lax.all_gather(params[3], "wsh", axis=0, tiled=True),
        lax.all_gather(params[4], "wsh", axis=0, tiled=True),
        lax.all_gather(params[5], "wsh", axis=0, tiled=True),
        lax.all_gather(params[6], "wsh", axis=0, tiled=True),
        lax.all_gather(params[7], "wsh", axis=0, tiled=True),
        lax.all_gather(params[8], "wsh", axis=0, tiled=True),
        lax.all_gather(params[9], "wsh", axis=0, tiled=True),
        lax.all_gather(params[10], "wsh", axis=0, tiled=True),
        lax.all_gather(params[11], "wsh", axis=0, tiled=True),
        lax.all_gather(params[12], "wsh", axis=0, tiled=True),
        lax.all_gather(params[13], "wsh", axis=0, tiled=True),
        lax.all_gather(params[14], "wsh", axis=0, tiled=True),
    )


def per_device(
    tokens,
    cotangent,
    lengths,
    dealing,
    w_query,
    w_key,
    w_value,
    w_out,
    w_up,
    w_down,
    b_query,
    b_value,
    b_out,
    b_up,
    b_down,
    gain_one,
    shift_one,
    gain_two,
    shift_two,
):
    params = (
        w_query,
        w_key,
        w_value,
        w_out,
        w_up,
        w_down,
        b_query,
        b_value,
        b_out,
        b_up,
        b_down,
        gain_one,
        shift_one,
        gain_two,
        shift_two,
    )
    own_rows = tokens.shape[2]
    width = tokens.shape[3]
    head_size = width // HEADS
    scale_factor = 1.0 / math.sqrt(head_size)
    my_start = lax.axis_index("ctx") * own_rows
    wsh_count = lax.axis_size("wsh")
    grads = tuple(
        (jnp.zeros((item.shape[0] * wsh_count,) + item.shape[1:], jnp.float32) for item in params)
    )
    results = []
    input_grads = []
    for micro in range(MB):
        whole = gather_params(params)
        query_weight, key_weight, value_weight, out_weight, up_weight, down_weight = whole[:6]
        (
            bias_query,
            bias_value,
            bias_out,
            bias_up,
            bias_down,
            gain_first,
            shift_first,
            gain_second,
            shift_second,
        ) = tuple((item.astype(jnp.float32) for item in whole[6:]))
        token_rows = tokens[0, micro]
        seq_all, valid_all = row_labels(dealing[0, micro], lengths[0, micro])
        my_seq = lax.dynamic_slice_in_dim(seq_all, my_start, own_rows)
        my_valid = lax.dynamic_slice_in_dim(valid_all, my_start, own_rows)
        query_low = (
            jnp.dot(token_rows, query_weight, preferred_element_type=jnp.float32) + bias_query
        ).astype(jnp.bfloat16)
        key_low = jnp.dot(token_rows, key_weight, preferred_element_type=jnp.float32).astype(
            jnp.bfloat16
        )
        value_low = (
            jnp.dot(token_rows, value_weight, preferred_element_type=jnp.float32) + bias_value
        ).astype(jnp.bfloat16)
        query_heads = query_low.reshape(own_rows, HEADS, head_size)
        my_key_heads = key_low.reshape(own_rows, HEADS, head_size)
        my_value_heads = value_low.reshape(own_rows, HEADS, head_size)
        start_state = (
            jnp.full((HEADS, own_rows), NEG_FILL, jnp.float32),
            jnp.zeros((HEADS, own_rows), jnp.float32),
            jnp.zeros((own_rows, HEADS, head_size), jnp.float32),
        )
        key_piece = lax.all_gather(key_low, "ctx", axis=0, tiled=True)
        value_piece = lax.all_gather(value_low, "ctx", axis=0, tiled=True)
        piece_rows = key_piece.shape[0]
        step_rows = math.gcd(piece_rows, 512)

        def visit_block(running, offset):
            run_max, run_sum, run_acc = running
            key_blk = lax.dynamic_slice_in_dim(key_piece, offset, step_rows).reshape(
                step_rows, HEADS, head_size
            )
            value_blk = lax.dynamic_slice_in_dim(value_piece, offset, step_rows).reshape(
                step_rows, HEADS, head_size
            )
            key_seq = lax.dynamic_slice_in_dim(seq_all, offset, step_rows)
            key_valid = lax.dynamic_slice_in_dim(valid_all, offset, step_rows)
            scores, allowed = masked_scores(
                query_heads, key_blk, my_seq, key_seq, key_valid, scale_factor
            )
            new_max = jnp.maximum(run_max, jnp.max(scores, axis=-1))
            rescale = jnp.exp(run_max - new_max)
            weights = jnp.exp(scores - new_max[:, :, None]) * allowed
            run_sum = run_sum * rescale + jnp.sum(weights, axis=-1)
            run_acc = run_acc * rescale.T[:, :, None] + jnp.einsum(
                "hqk,khd->qhd",
                weights.astype(jnp.bfloat16),
                value_blk,
                preferred_element_type=jnp.float32,
            )
            return (new_max, run_sum, run_acc)

        final_max, final_sum, final_acc = blockwise(start_state, piece_rows, step_rows, visit_block)
        attended = final_acc / final_sum.T[:, :, None]
        log_total = final_max + jnp.log(final_sum)
        attended_low = attended.reshape(own_rows, width).astype(jnp.bfloat16)
        out_proj = jnp.dot(attended_low, out_weight, preferred_element_type=jnp.float32) + bias_out
        first_sum = token_rows.astype(jnp.float32) + out_proj
        norm_one, norm_one_back = jax.vjp(layer_norm, first_sum, gain_first, shift_first)
        mlp_input = norm_one.astype(jnp.bfloat16)
        up_pre = jnp.dot(mlp_input, up_weight, preferred_element_type=jnp.float32) + bias_up
        activated, gelu_back = jax.vjp(gelu_exact, up_pre)
        activated_low = activated.astype(jnp.bfloat16)
        down_out = (
            jnp.dot(activated_low, down_weight, preferred_element_type=jnp.float32) + bias_down
        )
        result, norm_two_back = jax.vjp(layer_norm, norm_one + down_out, gain_second, shift_second)
        results.append(result.astype(jnp.bfloat16))
        grad_second, grad_gain_b, grad_shift_b = norm_two_back(
            cotangent[0, micro].astype(jnp.float32)
        )
        grad_down_low = grad_second.astype(jnp.bfloat16)
        grad_activated = jnp.einsum(
            "rd,fd->rf", grad_down_low, down_weight, preferred_element_type=jnp.float32
        )
        (grad_up_pre,) = gelu_back(grad_activated)
        grad_up_low = grad_up_pre.astype(jnp.bfloat16)
        grad_norm_one = (
            jnp.einsum("rf,df->rd", grad_up_low, up_weight, preferred_element_type=jnp.float32)
            + grad_second
        )
        grad_first, grad_gain_a, grad_shift_a = norm_one_back(grad_norm_one)
        grad_out_low = grad_first.astype(jnp.bfloat16)
        grad_att_low = jnp.einsum(
            "rd,ed->re", grad_out_low, out_weight, preferred_element_type=jnp.float32
        ).astype(jnp.bfloat16)
        grad_heads = grad_att_low.reshape(own_rows, HEADS, head_size)
        row_delta = jnp.sum(grad_heads.astype(jnp.float32) * attended, axis=-1).T
        empty_heads = jnp.zeros((own_rows, HEADS, head_size), jnp.float32)
        query_key_piece = lax.all_gather(key_low, "ctx", axis=0, tiled=True)
        query_value_piece = lax.all_gather(value_low, "ctx", axis=0, tiled=True)
        query_piece_rows = query_key_piece.shape[0]
        query_step_rows = math.gcd(query_piece_rows, 512)

        def query_visit_block(running, offset):
            key_blk = lax.dynamic_slice_in_dim(query_key_piece, offset, query_step_rows).reshape(
                query_step_rows, HEADS, head_size
            )
            value_blk = lax.dynamic_slice_in_dim(
                query_value_piece, offset, query_step_rows
            ).reshape(query_step_rows, HEADS, head_size)
            key_seq = lax.dynamic_slice_in_dim(seq_all, offset, query_step_rows)
            key_valid = lax.dynamic_slice_in_dim(valid_all, offset, query_step_rows)
            probs_low, grad_scores = attention_grads(
                query_heads,
                grad_heads,
                key_blk,
                value_blk,
                my_seq,
                key_seq,
                key_valid,
                log_total,
                row_delta,
                scale_factor,
            )
            return running + jnp.einsum(
                "hqk,khd->qhd", grad_scores, key_blk, preferred_element_type=jnp.float32
            )

        grad_query_sum = blockwise(
            empty_heads, query_piece_rows, query_step_rows, query_visit_block
        )
        total_all, delta_all = (
            lax.all_gather(log_total.T, "ctx", axis=0, tiled=True),
            lax.all_gather(row_delta.T, "ctx", axis=0, tiled=True),
        )
        query_piece = lax.all_gather(query_low, "ctx", axis=0, tiled=True)
        grad_piece = lax.all_gather(grad_att_low, "ctx", axis=0, tiled=True)
        key_piece_rows = query_piece.shape[0]
        key_step_rows = math.gcd(key_piece_rows, 512)

        def key_visit_block(running, offset):
            grad_key_run, grad_value_run = running
            query_blk = lax.dynamic_slice_in_dim(query_piece, offset, key_step_rows).reshape(
                key_step_rows, HEADS, head_size
            )
            grad_blk = lax.dynamic_slice_in_dim(grad_piece, offset, key_step_rows).reshape(
                key_step_rows, HEADS, head_size
            )
            total_blk = lax.dynamic_slice_in_dim(total_all, offset, key_step_rows)
            delta_blk = lax.dynamic_slice_in_dim(delta_all, offset, key_step_rows)
            query_seq = lax.dynamic_slice_in_dim(seq_all, offset, key_step_rows)
            probs_low, grad_scores = attention_grads(
                query_blk,
                grad_blk,
                my_key_heads,
                my_value_heads,
                query_seq,
                my_seq,
                my_valid,
                total_blk.T,
                delta_blk.T,
                scale_factor,
            )
            grad_key_run = grad_key_run + jnp.einsum(
                "hqk,qhd->khd", grad_scores, query_blk, preferred_element_type=jnp.float32
            )
            grad_value_run = grad_value_run + jnp.einsum(
                "hqk,qhd->khd", probs_low, grad_blk, preferred_element_type=jnp.float32
            )
            return (grad_key_run, grad_value_run)

        grad_key_sum, grad_value_sum = blockwise(
            (empty_heads, empty_heads), key_piece_rows, key_step_rows, key_visit_block
        )
        grad_key_flat = grad_key_sum.reshape(own_rows, width)
        grad_value_flat = grad_value_sum.reshape(own_rows, width)
        grad_query_low = (
            (grad_query_sum * scale_factor).reshape(own_rows, width).astype(jnp.bfloat16)
        )
        grad_key_low = (grad_key_flat * scale_factor).astype(jnp.bfloat16)
        grad_value_low = grad_value_flat.astype(jnp.bfloat16)
        terms = (
            jnp.einsum("rd,re->de", token_rows, grad_query_low, preferred_element_type=jnp.float32),
            jnp.einsum("rd,re->de", token_rows, grad_key_low, preferred_element_type=jnp.float32),
            jnp.einsum("rd,re->de", token_rows, grad_value_low, preferred_element_type=jnp.float32),
            jnp.einsum("rd,re->de", attended_low, grad_out_low, preferred_element_type=jnp.float32),
            jnp.einsum("rd,rf->df", mlp_input, grad_up_low, preferred_element_type=jnp.float32),
            jnp.einsum(
                "rf,rd->fd", activated_low, grad_down_low, preferred_element_type=jnp.float32
            ),
            jnp.sum(grad_query_low.astype(jnp.float32), axis=0),
            jnp.sum(grad_value_low.astype(jnp.float32), axis=0),
            jnp.sum(grad_out_low.astype(jnp.float32), axis=0),
            jnp.sum(grad_up_low.astype(jnp.float32), axis=0),
            jnp.sum(grad_down_low.astype(jnp.float32), axis=0),
            grad_gain_a,
            grad_shift_a,
            grad_gain_b,
            grad_shift_b,
        )
        grads = tuple((total_now + fresh for total_now, fresh in zip(grads, terms)))
        grad_rows = (
            grad_first
            + jnp.einsum(
                "re,de->rd", grad_query_low, query_weight, preferred_element_type=jnp.float32
            )
            + jnp.einsum("re,de->rd", grad_key_low, key_weight, preferred_element_type=jnp.float32)
            + jnp.einsum(
                "re,de->rd", grad_value_low, value_weight, preferred_element_type=jnp.float32
            )
        )
        input_grads.append(grad_rows.astype(jnp.bfloat16))
    shards = jax.tree.map(
        lambda part: part.astype(jnp.float32),
        lax.psum_scatter(as_sent(grads), "wsh", scatter_dimension=0, tiled=True),
    )
    summed = jax.tree.map(lambda part: part.astype(jnp.float32), lax.psum(as_sent(shards), "ctx"))
    return (jnp.stack(results)[None], jnp.stack(input_grads)[None]) + tuple(summed)


MESH_IDS = pl.DeviceIdType.MESH
F32 = jnp.float32
BF16 = jnp.bfloat16
HD = 64
VMEM_BYTES = 60 * 1024 * 1024


def flip(index, bit):
    return index + bit * (1 - 2 * lax.rem(lax.div(index, bit), 2))


def bit_of(index, bit):
    return lax.rem(lax.div(index, bit), 2)


def greet(peers):
    barrier = pltpu.get_barrier_semaphore()
    for peer in peers:
        pl.semaphore_signal(barrier, inc=1, device_id=peer, device_id_type=MESH_IDS)
    pl.semaphore_wait(barrier, len(peers))


def send(src, dst, send_sem, recv_sem, peer):
    copy = pltpu.make_async_remote_copy(
        src_ref=src,
        dst_ref=dst,
        send_sem=send_sem,
        recv_sem=recv_sem,
        device_id=peer,
        device_id_type=MESH_IDS,
    )
    copy.start()
    return copy


def plane_peers(c, w, count):
    return [(lax.rem(c + step, count), w) for step in range(1, count)]


def pack_three(first, second, third, row, pair, out):
    cols = pl.ds(pair * 128, 128)
    a, b, d = (ref[pl.ds(row, BLK), cols] for ref in (first, second, third))
    half = BLK // 2
    for head in range(2):
        lane = slice(head * HD, head * HD + HD)
        out[2 * pair + head, 0:BLK, :] = jnp.concatenate([a[:, lane], b[:, lane]], axis=1)
        out[2 * pair + head, BLK : BLK + half, :] = jnp.concatenate(
            [d[:half, lane], d[half:, lane]], axis=1
        )


def unpack_fold(block):
    return jnp.concatenate([block[:, :HD], block[:, HD:]], axis=0)


def fold(rows):
    half = rows.shape[0] // 2
    return jnp.concatenate([rows[:half], rows[half:]], axis=1)


def all_bytes(ref, sem, peers):
    view = ref.at[pl.ds(0, peers)]
    return pltpu.make_async_copy(view, view, sem)


SQUARE, PAIR, ALONE = 8, 4, 2


def weight_plan(shards):
    plan, first_bulk = [], 3
    for index in range(first_bulk):
        plan.append((index, 0, shards[index].shape[0], SQUARE))
    unit = shards[0].shape[0] * shards[0].shape[1]
    bulk = []
    for index in range(first_bulk, len(shards)):
        rows, cols = shards[index].shape
        parts = max(1, rows * cols // unit)
        for part in range(parts):
            bulk.append((index, part * (rows // parts), rows // parts))
    squares, alone = BULK_WAYS
    for number, item in enumerate(bulk):
        if number < squares:
            way = SQUARE
        elif number >= len(bulk) - alone:
            way = ALONE
        else:
            way = PAIR
        plan.append(item + (way,))
    return plan


BULK_WAYS = (2, 2)


def forward_kernel(heads, plan, n_weights, n_vectors, *refs):
    lens_ref, slot_ref, block_ref, x_ref = refs[:4]
    refs = refs[4:]
    shards, vectors = refs[:n_weights], refs[n_weights : n_weights + n_vectors]
    refs = refs[n_weights + n_vectors :]
    wholes, small_whole, a_ref, kept_ref, lse_ref = refs[:n_weights], *refs[n_weights : n_weights + 4]
    refs = refs[n_weights + 4 :]
    near, stages, refs = refs[:3], refs[3:n_weights], refs[n_weights:]
    small, small_in, bias, q_ref, k_ref, v_ref = refs[:6]
    in_buf = refs[6 : 6 + MB]
    out_buf, back_out, back_in, q_s, k_s, v_s, a_s = refs[6 + MB : 13 + MB]
    (
        w_send,
        w_recv,
        small_sems,
        local_sem,
        stage_sem,
        send_sem,
        recv_sem,
        back_send,
        back_recv,
        keep_sem,
    ) = refs[13 + MB :]
    c, w = lax.axis_index("ctx"), lax.axis_index("wsh")
    o = 1 - w
    by_x, by_y, by_z, by_core = (c, o), (flip(c, 2), w), (flip(c, 4), w), (flip(c, 1), w)
    core, y, z = bit_of(c, 1), bit_of(c, 2), bit_of(c, 4)
    peers = plane_peers(c, w, heads)
    targets = tuple(near) + tuple(wholes[3:])
    staged, locals_ = [], []
    for index, shard in enumerate(shards):
        rows = shard.shape[0]
        spot = pl.ds(pl.multiple_of(w * rows, rows), rows)
        dst = near[index].at[spot] if index < 3 else stages[index - 3]
        copy = pltpu.make_async_copy(shard, dst, stage_sem.at[index])
        copy.start()
        staged.append(copy)
    line, lanes = 0, small.shape[1]
    for vector in vectors:
        for first in range(0, vector.shape[0], lanes):
            piece = vector[pl.ds(first, lanes)].astype(F32)
            small[line : line + 1, :] = piece.reshape(1, lanes)
            line += 1
    greet(peers + [by_x])
    small_sent = send(small, small_in, small_sems.at[0], small_sems.at[1], by_x)

    def part(chunk, side, piece, start, count):
        tensor, first, rows, way = plan[chunk]
        half = shards[tensor].shape[0]
        at = side * half + first + piece * (rows // way) + start
        return targets[tensor].at[pl.ds(pl.multiple_of(at, 8), count)]

    steps = {}

    def sem(kind, chunk):
        return w_send.at[kind, chunk], w_recv.at[kind, chunk]

    def own_piece(way):
        return {SQUARE: core * 4 + z * 2 + y, PAIR: core * 2 + y, ALONE: core}[way]

    for chunk, (tensor, first, rows, way) in enumerate(plan):
        size, mine = rows // way, own_piece(way)
        src = shards[tensor].at[pl.ds(pl.multiple_of(first + mine * size, 8), size)]
        steps[chunk, 0] = send(src, part(chunk, w, mine, 0, size), *sem(0, chunk), by_x)

    def second(chunk):
        _, _, rows, way = plan[chunk]
        if way == ALONE:
            return
        steps[chunk, 0].wait_recv()
        ref = part(chunk, o, own_piece(way), 0, rows // way)
        steps[chunk, 1] = send(ref, ref, *sem(1, chunk), by_y)
        if way == SQUARE:
            steps[chunk, 2] = send(ref, ref, *sem(2, chunk), by_z)

    def third(chunk):
        _, _, rows, way = plan[chunk]
        if way != SQUARE:
            return
        size = rows // way
        steps[chunk, 1].wait_recv()
        steps[chunk, 2].wait_recv()
        ref = part(chunk, o, core * 4 + (1 - z) * 2 + y, 0, size // 2)
        steps[chunk, 3] = send(ref, ref, *sem(3, chunk), by_y)
        ref = part(chunk, o, core * 4 + z * 2 + (1 - y), size // 2, size // 2)
        steps[chunk, 4] = send(ref, ref, *sem(4, chunk), by_z)

    def fourth(chunk):
        _, _, rows, way = plan[chunk]
        for kind in {SQUARE: (3, 4), PAIR: (1,), ALONE: (0,)}[way]:
            steps[chunk, kind].wait_recv()
        ref = part(chunk, o, core * (way // 2), 0, rows // 2)
        steps[chunk, 5] = send(ref, ref, *sem(5, chunk), by_core)

    for index in range(3):
        staged[index].wait()
    for turn in range(5):
        for stage, act in enumerate((second, third, fourth)):
            if 0 <= turn - stage < 3:
                act(turn - stage)
    small_sent.wait()
    small_whole[w] = small[...]
    small_whole[o] = small_in[...]
    for side in range(2):
        for row in range(2):
            bias[row : row + 1, side * lanes : (side + 1) * lanes] = small_whole[
                side, row : row + 1, :
            ]
    width = x_ref.shape[1]
    step = 256
    for index, (weight, out) in enumerate(zip(near, (q_ref, k_ref, v_ref))):
        steps[index, 5].wait_recv()

        def project(turn, carry):
            cols = pl.ds(pl.multiple_of(turn * step, step), step)
            total = jnp.dot(x_ref[...], weight[:, cols], preferred_element_type=F32)
            if index != 1:
                total = total + bias[index // 2 : index // 2 + 1, cols]
            out[:, cols] = total.astype(BF16)
            return carry

        lax.fori_loop(0, width // step, project, 0)
    for m in range(MB):
        for pair in range(heads // 2):
            pack_three(q_ref, k_ref, v_ref, m * BLK, pair, out_buf.at[m])
        for peer in peers:
            send(out_buf.at[m, peer[0]], in_buf[m].at[c], send_sem.at[m], recv_sem.at[m], peer)
        in_buf[m][c] = out_buf[m, c]
    for index in range(n_weights):
        if index < 3:
            copy = pltpu.make_async_copy(near[index], wholes[index], local_sem.at[index])
        else:
            rows = shards[index].shape[0]
            spot = pl.ds(pl.multiple_of(w * rows, rows), rows)
            staged[index].wait()
            copy = pltpu.make_async_copy(
                stages[index - 3], wholes[index].at[spot], local_sem.at[index]
            )
        copy.start()
        locals_.append(copy)

    bulk = range(3, len(plan))
    kinds = {way: [i for i in bulk if plan[i][3] == way] for way in (SQUARE, PAIR, ALONE)}
    squares, pairs, alone = kinds[SQUARE], kinds[PAIR], kinds[ALONE]
    moves = [(second, i) for i in squares + pairs[:2]]
    moves += [None]
    moves += [(third, i) for i in squares] + [(second, i) for i in pairs[2:3]]
    moves += [None]
    moves += [(fourth, i) for i in squares] + [(second, i) for i in pairs[3:4]]
    moves += [(fourth, i) for i in pairs[:2]]
    moves += [None]
    moves += [(second, i) for i in pairs[4:]] + [(fourth, i) for i in pairs[2:]]
    moves += [(fourth, i) for i in alone]

    def pump():
        while moves:
            move = moves.pop(0)
            if move is None:
                return
            move[0](move[1])

    blocks = heads
    span = BPS * BLK
    for m in range(MB):
        pump()
        all_bytes(in_buf[m], recv_sem.at[m], heads - 1).wait()
        keep = pltpu.make_async_copy(in_buf[m], kept_ref.at[m], keep_sem.at[m])
        keep.start()
        for b in range(blocks):
            got = in_buf[m][slot_ref[0, m, b]]
            q_s[b * BLK : (b + 1) * BLK, :] = got[:BLK, :HD]
            k_s[b * BLK : (b + 1) * BLK, :] = got[:BLK, HD:]
            v_s[b * BLK : (b + 1) * BLK, :] = unpack_fold(got[BLK:])

        def one_sequence(s, carry):
            rows = pl.ds(pl.multiple_of(s * span, span), span)
            scores = lax.dot_general(
                k_s[rows, :], q_s[rows, :], (((1,), (1,)), ((), ())), preferred_element_type=F32
            ) * (1.0 / math.sqrt(HD))
            place = lax.broadcasted_iota(jnp.int32, scores.shape, 0)
            scores = jnp.where(place < lens_ref[0, m, s], scores, NEG_FILL)
            top = jnp.max(scores, axis=0, keepdims=True)
            weights = jnp.exp(scores - top)
            total = jnp.sum(weights, axis=0, keepdims=True)
            out_t = lax.dot_general(
                v_s[rows, :],
                weights.astype(BF16),
                (((0,), (0,)), ((), ())),
                preferred_element_type=F32,
            )
            a_s[pl.ds(s * BPS, BPS)] = (out_t / total).T.reshape(BPS, BLK, HD)
            lse_ref[pl.ds(m * (blocks // BPS) + s, 1), :] = top + jnp.log(total)
            return carry

        lax.fori_loop(0, blocks // BPS, one_sequence, 0)
        for t in range(blocks):
            back_out[m, t] = fold(a_s[block_ref[0, m, t]]).astype(BF16)
        for peer in peers:
            send(
                back_out.at[m, peer[0]], back_in.at[m, c], back_send.at[m], back_recv.at[m], peer
            )
        back_in[m, c] = back_out[m, c]
    pump()
    for m in range(MB):
        all_bytes(back_in.at[m], back_recv.at[m], heads - 1).wait()
        for pair in range(heads // 2):
            a_ref[m * BLK : (m + 1) * BLK, pair * 128 : (pair + 1) * 128] = jnp.concatenate(
                [unpack_fold(back_in[m, 2 * pair]), unpack_fold(back_in[m, 2 * pair + 1])], axis=1
            )
    for m in range(MB):
        all_bytes(out_buf.at[m], send_sem.at[m], heads - 1).wait()
        all_bytes(back_out.at[m], back_send.at[m], heads - 1).wait()
        pltpu.make_async_copy(in_buf[m], kept_ref.at[m], keep_sem.at[m]).wait()
    for chunk in bulk:
        steps[chunk, 5].wait_recv()
    for flight in steps.values():
        flight.wait_send()
    for copy in locals_:
        copy.wait()


def forward(lens, slot_of, block_of, x, shards, vectors, heads):
    plan = weight_plan(shards)
    count = len(shards)
    anywhere, vmem = pl.BlockSpec(memory_space=pl.ANY), pl.BlockSpec(memory_space=pltpu.VMEM)
    smem = pl.BlockSpec(memory_space=pltpu.SMEM)
    rows, width = x.shape
    pack_rows = BLK + BLK // 2
    span = BPS * BLK
    lanes = min(item.shape[0] for item in vectors)
    lines = sum(item.shape[0] for item in vectors) // lanes
    whole = lambda s: (2 * s.shape[0],) + s.shape[1:]
    return pl.pallas_call(
        functools.partial(forward_kernel, heads, plan, count, len(vectors)),
        out_shape=[jax.ShapeDtypeStruct(whole(s), s.dtype) for s in shards]
        + [
            jax.ShapeDtypeStruct((2, lines, lanes), F32),
            jax.ShapeDtypeStruct((rows, width), BF16),
            jax.ShapeDtypeStruct((MB, heads, pack_rows, 128), BF16),
            jax.ShapeDtypeStruct((8, span), F32),
        ],
        in_specs=[smem] * 3 + [vmem] + [anywhere] * count + [vmem] * len(vectors),
        out_specs=[anywhere] * count + [vmem, vmem, anywhere, vmem],
        scratch_shapes=[pltpu.VMEM(whole(s), s.dtype) for s in shards[:3]]
        + [pltpu.VMEM(s.shape, s.dtype) for s in shards[3:]]
        + [pltpu.VMEM((lines, lanes), F32)] * 2
        + [pltpu.VMEM((2, width), F32)]
        + [pltpu.VMEM((rows, width), BF16)] * 3
        + [pltpu.VMEM((heads, pack_rows, 128), BF16)] * MB
        + [
            pltpu.VMEM((MB, heads, pack_rows, 128), BF16),
            pltpu.VMEM((MB, heads, BLK // 2, 128), BF16),
            pltpu.VMEM((MB, heads, BLK // 2, 128), BF16),
            pltpu.VMEM((heads * BLK, HD), BF16),
            pltpu.VMEM((heads * BLK, HD), BF16),
            pltpu.VMEM((heads * BLK, HD), BF16),
            pltpu.VMEM((heads, BLK, HD), F32),
            pltpu.SemaphoreType.DMA((6, len(plan))),
            pltpu.SemaphoreType.DMA((6, len(plan))),
            pltpu.SemaphoreType.DMA((2,)),
            pltpu.SemaphoreType.DMA((count,)),
            pltpu.SemaphoreType.DMA((count,)),
        ]
        + [pltpu.SemaphoreType.DMA((MB,))] * 5,
        compiler_params=pltpu.CompilerParams(
            collective_id=1, has_side_effects=True, vmem_limit_bytes=VMEM_BYTES
        ),
        name="forward",
    )(lens, slot_of, block_of, x, *shards, *vectors)


ORDERS = (
    ("yxzZ", "zxyZ"),
    ("xyzZ", "xzyZ"),
    ("yxZz", "zxyZ"),
)
PIECES = len(ORDERS[0])
KEYS = tuple((part, piece) for part in range(3) for piece in range(PIECES))


def default_schedule():
    early = [(part, piece) for piece in range(PIECES) for part in (1, 2)]
    late = [(0, piece) for piece in range(PIECES)]
    events = ["up", 0, "down", 1, 2] + early + ["back", "qkv", "rows"]
    for step in range(6):
        events += early + ["vec"] + late
    return events + late


def landing_shapes(order, shape):
    shards, sides, shapes = 8, 2, []
    for name in order:
        if name == "x":
            sides = 1
        else:
            shards //= 2
        shapes.append((sides, shards, shape[2] // PIECES, shape[3]))
    return shapes


def dot_t(a, b):
    return lax.dot_general(a, b, (((0,), (0,)), ((), ())), preferred_element_type=F32)


def lanes_at(first, size):
    return pl.ds(pl.multiple_of(first, 128), size)


def backward_kernel(heads, *refs):
    lens_ref, slot_ref, block_ref, da_ref, kept_ref, lse_ref = refs[:6]
    x_ref, a_ref, n_ref, g_ref, do_ref, du_ref, dm_ref, vec_ref, dh_ref = refs[6:15]
    weights = refs[15:18]
    rows_out, o_a, o_b, o_c, vec_out = refs[18:23]
    refs = refs[23:]
    in_buf = refs[:MB]
    out_buf, back_out, back_in, q_s, k_s, v_s, a_s, dq_s, dk_s, dv_s = refs[MB : MB + 10]
    refs = refs[MB + 10 :]
    dq_ref, dk_ref, dv_ref, m_x, m_a, m_n, m_dm, m_do, m_du, m_g, m_dqkv = refs[:11]
    near, (vec_s, v_recv, v_sum, s_a, s_b, s_c) = refs[11:14], refs[14:20]
    refs = refs[20:]
    r_bufs = {key: refs[4 * i : 4 * i + 4] for i, key in enumerate(KEYS)}
    (
        send_sem,
        recv_sem,
        back_send,
        back_recv,
        mate_send,
        mate_recv,
        near_sem,
        rs_send,
        rs_recv,
        ag_send,
        ag_recv,
        own_sem,
        v_send_sem,
        v_recv_sem,
    ) = refs[4 * len(KEYS) :]
    c, x = lax.axis_index("ctx"), lax.axis_index("wsh")
    core, y, z, zz = bit_of(c, 1), bit_of(c, 2), bit_of(c, 4), bit_of(c, 8)
    by_core = (flip(c, 1), x)
    by = {"x": (c, 1 - x), "y": (flip(c, 2), x), "z": (flip(c, 4), x), "Z": (flip(c, 8), x)}
    bits = {"y": y, "z": z, "Z": zz}
    peers = plane_peers(c, x, heads)
    blocks, span = heads, BPS * BLK
    width, hidden = da_ref.shape[1], g_ref.shape[1]
    for index, weight in enumerate(weights):
        pltpu.make_async_copy(weight, near[index], near_sem.at[index]).start()
    greet(peers + [by["x"]])

    for m in range(MB):
        row = slice(m * BLK, (m + 1) * BLK)
        for pair in range(heads // 2):
            both = da_ref[row, pair * 128 : (pair + 1) * 128]
            for head in range(2):
                out_buf[m, 2 * pair + head] = fold(both[:, head * HD : (head + 1) * HD])
        for peer in peers:
            send(out_buf.at[m, peer[0]], in_buf[m].at[c], send_sem.at[m], recv_sem.at[m], peer)
        in_buf[m][c] = out_buf[m, c]

    shared = {}

    def share(name, src, dst):
        index = len(shared)
        shared[name] = send(src, dst, mate_send.at[index], mate_recv.at[index], by_core)

    other = 1 - core
    share("n", n_ref, m_n)
    share("du", du_ref.at[:, lanes_at(other * (hidden // 2), hidden // 2)], m_du)
    for half in range(2):
        share(
            "g" + str(half),
            g_ref.at[:, lanes_at(half * (hidden // 2) + other * (hidden // 4), hidden // 4)],
            m_g.at[:, pl.ds(half * (hidden // 4), hidden // 4)],
        )
    share("dm", dm_ref, m_dm)
    share("a", a_ref, m_a)
    share("do", do_ref.at[:, lanes_at(other * (width // 2), width // 2)], m_do)
    share("x", x_ref, m_x)

    sums, outs = (s_a, s_b, s_c), (o_a, o_b, o_c)
    wide = 256

    def tile(pairs, out, first, count):
        def body(turn, carry):
            at = turn * wide
            total = sum(dot_t(lhs[...], rhs[:, lanes_at(col + at, wide)]) for lhs, rhs, col in pairs)
            cols = lanes_at(first + at, wide)
            out[..., cols] = total.astype(BF16).reshape(out.shape[:-1] + (wide,))
            return carry

        lax.fori_loop(0, count, body, 0)

    def grads_up():
        shared["n"].wait_recv()
        shared["du"].wait_recv()
        half = hidden // 2
        tile(((n_ref, du_ref, core * half), (m_n, m_du, 0)), s_b, 0, half // wide)

    def grads_down():
        for name in ("g0", "g1", "dm"):
            shared[name].wait_recv()
        quarter = hidden // 4
        for half in range(2):
            mine = g_ref.at[:, lanes_at(half * 2 * quarter + core * quarter, quarter)]
            others = m_g.at[:, pl.ds(half * quarter, quarter)]
            tile(((mine, dm_ref, 0), (others, m_dm, 0)), s_c.at[half], 0, width // wide)

    def grads_qkv():
        half = width // 2
        for name in ("a", "do", "x", "dq", "dk", "dv"):
            shared[name].wait_recv()
        tile(((a_ref, do_ref, core * half), (m_a, m_do, 0)), s_a, 3 * half, half // wide)
        for index, ref in enumerate((dq_ref, dk_ref, dv_ref)):
            pairs = ((x_ref, ref, core * half), (m_x, m_dqkv, index * half))
            tile(pairs, s_a, index * half, half // wide)

    def attention(m):
        all_bytes(in_buf[m], recv_sem.at[m], heads - 1).wait()
        for b in range(blocks):
            slot = slot_ref[0, m, b]
            got = kept_ref[m, slot]
            rows = slice(b * BLK, (b + 1) * BLK)
            q_s[rows, :] = got[:BLK, :HD]
            k_s[rows, :] = got[:BLK, HD:]
            v_s[rows, :] = unpack_fold(got[BLK:])
            a_s[rows, :] = unpack_fold(in_buf[m][slot])

        def one_sequence(s, carry):
            rows = pl.ds(pl.multiple_of(s * span, span), span)
            qq, kk, vv, dd = q_s[rows, :], k_s[rows, :], v_s[rows, :], a_s[rows, :]
            scale = 1.0 / math.sqrt(HD)
            minor = (((1,), (1,)), ((), ()))
            scores = lax.dot_general(kk, qq, minor, preferred_element_type=F32) * scale
            spot = lax.broadcasted_iota(jnp.int32, scores.shape, 0)
            total = lse_ref[pl.ds(m * (blocks // BPS) + s, 1), :]
            probs = jnp.exp(jnp.where(spot < lens_ref[0, m, s], scores - total, NEG_FILL))
            dp = lax.dot_general(vv, dd, minor, preferred_element_type=F32)
            both = probs * dp
            delta = jnp.sum(both, axis=0, keepdims=True)
            ds = (both - probs * delta).astype(BF16)
            here, split = pl.ds(s * BPS, BPS), (BPS, BLK, HD)
            dv = jnp.dot(probs.astype(BF16), dd, preferred_element_type=F32)
            dv_s[here] = dv.reshape(split)
            dk_s[here] = (jnp.dot(ds, qq, preferred_element_type=F32) * scale).reshape(split)
            dq_s[here] = (dot_t(kk, ds).T * scale).reshape(split)
            return carry

        lax.fori_loop(0, blocks // BPS, one_sequence, 0)
        for t in range(blocks):
            at = block_ref[0, m, t]
            back_out[m, t, 0:BLK, :] = jnp.concatenate([dq_s[at], dk_s[at]], axis=1).astype(BF16)
            back_out[m, t, BLK:, :] = fold(dv_s[at]).astype(BF16)
        for peer in peers:
            send(
                back_out.at[m, peer[0]], back_in.at[m, c], back_send.at[m], back_recv.at[m], peer
            )
        back_in[m, c] = back_out[m, c]

    vec_peers = (by["x"], by["y"], by["z"], by["Z"], by_core)
    vec_steps = []

    def vec_send(src):
        step = len(vec_steps)
        vec_steps.append(
            send(
                src, v_recv.at[step], v_send_sem.at[step], v_recv_sem.at[step], vec_peers[step]
            )
        )

    def vec_next():
        step = len(vec_steps) - 1
        vec_steps[step].wait_recv()
        before = vec_s[x] if step == 0 else v_sum[step - 1]
        v_sum[step] = before + v_recv[step]
        if step + 1 < len(vec_peers):
            vec_send(v_sum.at[step])

    def come_back():
        for m in range(MB):
            all_bytes(back_in.at[m], back_recv.at[m], heads - 1).wait()
            row = slice(m * BLK, (m + 1) * BLK)
            for pair in range(heads // 2):
                lanes = slice(pair * 128, (pair + 1) * 128)
                one, two = back_in[m, 2 * pair], back_in[m, 2 * pair + 1]
                dq_ref[row, lanes] = jnp.concatenate([one[:BLK, :HD], two[:BLK, :HD]], axis=1)
                dk_ref[row, lanes] = jnp.concatenate([one[:BLK, HD:], two[:BLK, HD:]], axis=1)
                dv_ref[row, lanes] = jnp.concatenate(
                    [unpack_fold(one[BLK:]), unpack_fold(two[BLK:])], axis=1
                )
        half = width // 2
        for index, (name, ref) in enumerate((("dq", dq_ref), ("dk", dk_ref), ("dv", dv_ref))):
            share(
                name,
                ref.at[:, lanes_at(other * half, half)],
                m_dqkv.at[:, pl.ds(index * half, half)],
            )
        vec_s[...] = vec_ref[...]
        lanes = vec_s.shape[2]
        for index, ref in enumerate((dq_ref, dv_ref)):
            total = jnp.sum(ref[...].astype(F32), axis=0, keepdims=True)
            for side in range(2):
                vec_s[side, index : index + 1, :] = total[:, side * lanes : (side + 1) * lanes]
        vec_send(vec_s.at[1 - x])

    def grad_rows():
        total = dh_ref[...]
        for index, ref in enumerate((dq_ref, dk_ref, dv_ref)):
            pltpu.make_async_copy(weights[index], near[index], near_sem.at[index]).wait()
            total = total + lax.dot_general(
                ref[...], near[index][...], (((1,), (1,)), ((), ())), preferred_element_type=F32
            )
        rows_out[...] = total.astype(BF16)

    plans, gathers = {}, {}
    for key in KEYS:
        first, count, sided = 0, 8, False
        plans[key], back = [], []
        for name in ORDERS[key[0]][key[1]]:
            if name == "x":
                plans[key].append((by["x"], 1 - x, x, first, first, count))
                sided = True
                continue
            count //= 2
            out, keep = first + (1 - bits[name]) * count, first + bits[name] * count
            side = x if sided else None
            plans[key].append((by[name], side, side, out, keep, count))
            back.append((by[name], keep, out, count))
            first = keep
        gathers[key] = back[::-1]
    flights, spread, owns, state = {}, {}, {}, {}

    def piece_rows(key):
        rows = sums[key[0]].shape[2] // PIECES
        return pl.ds(key[1] * rows, rows)

    def reduce_send(key, step):
        peer, side, _, first, _, count = plans[key][step]
        dst = r_bufs[key][step]
        if side is None:
            src = sums[key[0]].at[:, pl.ds(first, count), piece_rows(key)]
        else:
            src, dst = sums[key[0]].at[side, pl.ds(first, count), piece_rows(key)], dst.at[0]
        sems = rs_send.at[key[0], key[1], step], rs_recv.at[key[0], key[1], step]
        flights[key, step] = send(src, dst, *sems, peer)
        state[key] = step

    def reduce_add(key, step):
        _, _, side, _, first, count = plans[key][step]
        flights[key, step].wait_recv()
        total, fresh, rows = sums[key[0]], r_bufs[key][step], piece_rows(key)
        sides = ((0, 0), (1, 1)) if side is None else ((side, 0),)
        for here, there in sides:

            def body(index, carry):
                spot = first + index
                total[here, spot, rows] = (
                    total[here, spot, rows].astype(F32) + fresh[there, index].astype(F32)
                ).astype(BF16)
                return carry

            lax.fori_loop(0, count, body, 0)

    def spread_send(key, kind, src, dst, peer):
        sems = ag_send.at[key[0], key[1], kind], ag_recv.at[key[0], key[1], kind]
        spread[key, kind] = send(src, dst, *sems, peer)

    def advance(key):
        step = state[key]
        out, rows = outs[key[0]], piece_rows(key)
        if step < 4:
            reduce_add(key, step)
            if step < 3:
                reduce_send(key, step + 1)
                return
            peer, first, _, _ = gathers[key][0]
            src = sums[key[0]].at[x, pl.ds(first, 1), rows]
            dst = out.at[core, pl.ds(first, 1), rows]
            owns[key] = pltpu.make_async_copy(src, dst, own_sem.at[key[0], key[1]])
            owns[key].start()
            spread_send(key, 0, src, dst, peer)
            spread_send(key, 3, src, dst, by_core)
        else:
            turn = step - 3
            spread[key, turn - 1].wait_recv()
            if turn == 1:
                owns[key].wait()
            if turn < 3:
                peer, first, _, count = gathers[key][turn]
                ref = out.at[core, pl.ds(first, count), rows]
                spread_send(key, turn, ref, ref, peer)
            _, _, first, count = gathers[key][turn - 1]
            ref = out.at[core, pl.ds(first, count), rows]
            spread_send(key, 3 + turn, ref, ref, by_core)
        state[key] = step + 1

    actions = {
        "up": (grads_up, 1),
        "down": (grads_down, 2),
        "qkv": (grads_qkv, 0),
        "back": (come_back, None),
        "rows": (grad_rows, None),
        "vec": (vec_next, None),
    }
    for event in SCHEDULE:
        if isinstance(event, tuple):
            advance(event)
        elif isinstance(event, int):
            attention(event)
        else:
            action, part = actions[event]
            if event == "vec" and len(vec_steps) == len(vec_peers) and "vec" in state:
                continue
            if event == "vec" and len(vec_steps) == len(vec_peers):
                state["vec"] = True
            action()
            if part is not None:
                for piece in range(PIECES):
                    reduce_send((part, piece), 0)
    vec_out[...] = v_sum[len(vec_peers) - 1]
    for m in range(MB):
        all_bytes(out_buf.at[m], send_sem.at[m], heads - 1).wait()
        all_bytes(back_out.at[m], back_send.at[m], heads - 1).wait()
    for flight in shared.values():
        flight.wait_send()
    for flight in vec_steps:
        flight.wait_send()
    for flight in flights.values():
        flight.wait_send()
    for (_, kind), flight in spread.items():
        if kind >= 3:
            flight.wait_recv()
        flight.wait_send()


SCHEDULE = default_schedule()


def backward(lens, slot_of, block_of, da, kept, lse, x, a, n1, g, do, du, dm, vec, dh, weights, heads):
    vmem, smem = pl.BlockSpec(memory_space=pltpu.VMEM), pl.BlockSpec(memory_space=pltpu.SMEM)
    anywhere = pl.BlockSpec(memory_space=pl.ANY)
    rows, width = da.shape
    hidden = g.shape[1]
    pack_rows = BLK + BLK // 2
    low = lambda *dims: pltpu.VMEM(dims, BF16)
    a_shape, b_shape = (2, 8, width // 16, 2 * width), (2, 8, width // 16, hidden // 2)
    c_shape = (2, 8, hidden // 32, width)
    scratch = [low(heads, BLK // 2, 128)] * MB
    scratch += [low(MB, heads, BLK // 2, 128)]
    scratch += [low(MB, heads, pack_rows, 128)] * 2
    scratch += [low(heads * BLK, HD)] * 4
    scratch += [pltpu.VMEM((heads, BLK, HD), F32)] * 3
    scratch += [low(rows, width)] * 7
    scratch += [low(rows, width // 2), low(rows, hidden // 2), low(rows, hidden // 2)]
    scratch += [low(rows, 3 * width // 2)]
    scratch += [low(*item.shape) for item in weights]
    scratch += [pltpu.VMEM(vec.shape, F32)] + [pltpu.VMEM((5,) + vec.shape[1:], F32)] * 2
    scratch += [low(*shape) for shape in (a_shape, b_shape, c_shape)]
    for key in KEYS:
        shape = (a_shape, b_shape, c_shape)[key[0]]
        scratch += [low(*item) for item in landing_shapes(ORDERS[key[0]][key[1]], shape)]
    sems = lambda *dims: pltpu.SemaphoreType.DMA(dims)
    scratch += [sems(MB)] * 4 + [sems(11)] * 2 + [sems(3)]
    scratch += [sems(3, PIECES, 4)] * 2 + [sems(3, PIECES, 7)] * 2 + [sems(3, PIECES)]
    scratch += [sems(5)] * 2
    return pl.pallas_call(
        functools.partial(backward_kernel, heads),
        out_shape=[
            jax.ShapeDtypeStruct((rows, width), BF16),
            jax.ShapeDtypeStruct(a_shape, BF16),
            jax.ShapeDtypeStruct(b_shape, BF16),
            jax.ShapeDtypeStruct(c_shape, BF16),
            jax.ShapeDtypeStruct(vec.shape[1:], F32),
        ],
        in_specs=[smem] * 3 + [vmem] * 12 + [anywhere] * 3,
        out_specs=[vmem] + [anywhere] * 3 + [vmem],
        scratch_shapes=scratch,
        compiler_params=pltpu.CompilerParams(
            collective_id=2, has_side_effects=True, vmem_limit_bytes=VMEM_BYTES
        ),
        name="backward",
    )(lens, slot_of, block_of, da, kept, lse, x, a, n1, g, do, du, dm, vec, dh, *weights)


def widen_kernel(a_ref, b_ref, c_ref, *outs):
    half = outs[0].shape[1] // 2
    for index, out in enumerate(outs[:4]):
        for core in range(2):
            out[:, core * half : (core + 1) * half] = a_ref[
                core, 0, :, index * half : (index + 1) * half
            ].astype(F32)
    up, down = outs[4:]
    half = up.shape[1] // 2
    for core in range(2):
        up[:, core * half : (core + 1) * half] = b_ref[core, 0].astype(F32)
        down[core, 0] = c_ref[core, 0].astype(F32)


def widen(o_a, o_b, o_c):
    shards = o_a.shape[1]
    block = lambda item: pl.BlockSpec((2, 1) + item.shape[2:], lambda i: (0, i, 0, 0))
    rows = o_a.shape[2]
    square = (shards * rows, o_a.shape[3] // 2)
    wide = (shards * rows, 2 * o_b.shape[3])
    return pl.pallas_call(
        widen_kernel,
        grid=(shards,),
        out_shape=[jax.ShapeDtypeStruct(square, F32)] * 4
        + [jax.ShapeDtypeStruct(wide, F32), jax.ShapeDtypeStruct(o_c.shape, F32)],
        in_specs=[block(o_a), block(o_b), block(o_c)],
        out_specs=[pl.BlockSpec((rows, square[1]), lambda i: (i, 0))] * 4
        + [pl.BlockSpec((rows, wide[1]), lambda i: (i, 0)), block(o_c)],
        compiler_params=pltpu.CompilerParams(vmem_limit_bytes=VMEM_BYTES),
        name="widen",
    )(o_a, o_b, o_c)


def norm_parts(summed):
    row_mean = jnp.mean(summed, axis=-1, keepdims=True)
    centred = summed - row_mean
    row_var = jnp.mean(centred * centred, axis=-1, keepdims=True)
    scale = lax.rsqrt(row_var + EPSILON)
    return centred * scale, scale


def norm_back(grad, unit, scale, gain):
    inner = grad * gain
    mean_one = jnp.mean(inner, axis=-1, keepdims=True)
    mean_two = jnp.mean(inner * unit, axis=-1, keepdims=True)
    return scale * (inner - mean_one - unit * mean_two)


def dot(a, b, dims):
    return lax.dot_general(a, b, (dims, ((), ())), preferred_element_type=F32)


ROW_COL, COL_COL, ROW_ROW = ((1,), (0,)), ((1,), (1,)), ((0,), (0,))


def per_device_heads(tokens, cotangent, lengths, dealing, *params):
    rows_in = tokens.shape[2]
    width = tokens.shape[3]
    rows = MB * rows_in
    weights, vectors = params[:6], params[6:]
    sizes = [item.shape[0] for item in vectors]
    x = tokens.reshape(rows, width)
    lens, block_of = lengths, dealing
    slot_of = jnp.argsort(block_of, axis=2).astype(jnp.int32)
    *wholes, small_whole, a, kept, lse = forward(
        lens, slot_of, block_of, x, weights, vectors, HEADS
    )
    query_w, key_w, value_w, out_w, up_w, down_w = wholes
    spots = [sum(sizes[:i]) for i in range(len(sizes) + 1)]
    lines = [spot // small_whole.shape[2] for spot in spots]
    _, _, bias_out, bias_up, bias_down, gain_one, shift_one, gain_two, shift_two = (
        small_whole[:, lines[i] : lines[i + 1]].reshape(1, -1) for i in range(len(sizes))
    )
    h_one = x.astype(F32) + (dot(a, out_w, ROW_COL) + bias_out)
    unit_one, scale_one = norm_parts(h_one)
    n_one = unit_one * gain_one + shift_one
    n_low = n_one.astype(BF16)
    u = dot(n_low, up_w, ROW_COL) + bias_up
    below = 0.5 * (1.0 + lax.erf(u * math.sqrt(0.5)))
    slope = below + u * jnp.exp(-0.5 * u * u) * (1.0 / math.sqrt(2.0 * math.pi))
    g, slope = lax.optimization_barrier(((u * below).astype(BF16), slope))
    h_two = n_one + (dot(g, down_w, ROW_COL) + bias_down)
    unit_two, scale_two = norm_parts(h_two)
    output = (unit_two * gain_two + shift_two).astype(BF16)

    cot = cotangent.reshape(rows, width).astype(F32)
    dh_two = norm_back(cot, unit_two, scale_two, gain_two)
    dm = dh_two.astype(BF16)
    du = lax.optimization_barrier((slope * dot(dm, down_w, COL_COL)).astype(BF16))
    dn = lax.optimization_barrier(dot(du, up_w, COL_COL)) + dh_two
    dh_one = norm_back(dn, unit_one, scale_one, gain_one)
    do = dh_one.astype(BF16)
    da = dot(do, out_w, COL_COL).astype(BF16)

    total = lambda item: jnp.sum(item.astype(F32), axis=0).reshape(2, -1, small_whole.shape[2])
    nothing = jnp.zeros((2, 2, small_whole.shape[2]), F32)
    vec = [nothing] + [
        total(item)
        for item in (do, du, dm, dn * unit_one, dn, cot * unit_two, cot)
    ]
    grad_tokens, o_a, o_b, o_c, vec_sum = backward(
        lens,
        slot_of,
        block_of,
        da,
        kept,
        lse,
        x,
        a,
        n_low,
        g,
        do,
        du,
        dm,
        jnp.concatenate(vec, axis=1),
        dh_one,
        (query_w, key_w, value_w),
        HEADS,
    )
    *square, up, down = widen(o_a, o_b, o_c)
    down = down.reshape(-1, width)
    vec_sum = vec_sum.reshape(-1)
    ends = [vec_sum[spots[i] : spots[i + 1]] for i in range(len(sizes))]
    shape = (1, MB, rows_in, width)
    return (
        (output.reshape(shape), grad_tokens.reshape(shape))
        + (*square, up, down)
        + tuple(ends)
    )


def solution(mesh):
    placed = (
        P("wsh", None, "ctx", None),
        P("wsh", None, "ctx", None),
        P("wsh", None, None),
        P("wsh", None, None),
        P("wsh", None),
        P("wsh", None),
        P("wsh", None),
        P("wsh", None),
        P("wsh", None),
        P("wsh", None),
        P("wsh"),
        P("wsh"),
        P("wsh"),
        P("wsh"),
        P("wsh"),
        P("wsh"),
        P("wsh"),
        P("wsh"),
        P("wsh"),
    )
    by_heads = mesh.shape["ctx"] == HEADS and mesh.shape["wsh"] == 2
    return jax.shard_map(
        per_device_heads if by_heads else per_device,
        mesh=mesh,
        in_specs=placed,
        out_specs=(
            P("wsh", None, "ctx", None),
            P("wsh", None, "ctx", None),
            P("wsh", None),
            P("wsh", None),
            P("wsh", None),
            P("wsh", None),
            P("wsh", None),
            P("wsh", None),
            P("wsh"),
            P("wsh"),
            P("wsh"),
            P("wsh"),
            P("wsh"),
            P("wsh"),
            P("wsh"),
            P("wsh"),
            P("wsh"),
        ),
        check_vma=False,
    )
```

```python
import functools
import math

import jax
import jax.numpy as jnp
from jax import lax
from jax.experimental import pallas as pl
from jax.experimental.pallas import tpu as pltpu
from jax.sharding import PartitionSpec as P

HEADS = 16
BPS = 8
MB = 3
BLK = 64


EPSILON = 1e-12
NEG_FILL = -1e30


def as_sent(x):
    return jax.tree.map(lambda a: a.astype(jnp.bfloat16) if a.dtype == jnp.float32 else a, x)


def layer_norm(summed, gain_vec, shift_vec):
    row_mean = jnp.mean(summed, axis=-1, keepdims=True)
    centred = summed - row_mean
    row_var = jnp.mean(centred * centred, axis=-1, keepdims=True)
    return centred * lax.rsqrt(row_var + EPSILON) * gain_vec + shift_vec


def gelu_exact(values):
    return jax.nn.gelu(values, approximate=False)


def row_labels(dealt_order, seq_lengths):
    blocks_of_rows = jnp.repeat(dealt_order, BLK)
    within = jnp.tile(jnp.arange(BLK, dtype=jnp.int32), dealt_order.shape[0])
    seq_ids = blocks_of_rows // BPS
    places = blocks_of_rows % BPS * BLK + within
    numbers = jnp.arange(seq_lengths.shape[0], dtype=jnp.int32)
    seq_bound = jnp.sum(
        jnp.where(seq_ids[:, None] == numbers[None, :], seq_lengths[None, :], 0), axis=1
    )
    return (seq_ids, places < seq_bound)


def blockwise(carried, total_rows, step_rows, visit_block):
    return lax.fori_loop(
        0,
        total_rows // step_rows,
        lambda turn_index, running: visit_block(running, turn_index * step_rows),
        carried,
    )


def masked_scores(query_blk, key_blk, query_seq, key_seq, key_valid, scale_factor):
    allowed = (query_seq[:, None] == key_seq[None, :]) & key_valid[None, :]
    scores = (
        jnp.einsum("qhd,khd->hqk", query_blk, key_blk, preferred_element_type=jnp.float32)
        * scale_factor
    )
    return (jnp.where(allowed[None], scores, NEG_FILL), allowed[None].astype(jnp.float32))


def attention_grads(
    query_blk,
    grad_blk,
    key_blk,
    value_blk,
    query_seq,
    key_seq,
    key_valid,
    row_total,
    row_delta,
    scale_factor,
):
    scores, allowed = masked_scores(query_blk, key_blk, query_seq, key_seq, key_valid, scale_factor)
    probs = jnp.exp(scores - row_total[:, :, None]) * allowed
    grad_probs = jnp.einsum("qhd,khd->hqk", grad_blk, value_blk, preferred_element_type=jnp.float32)
    grad_scores = (probs * (grad_probs - row_delta[:, :, None])).astype(jnp.bfloat16)
    return (probs.astype(jnp.bfloat16), grad_scores)


def gather_params(params):
    return (
        lax.all_gather(params[0], "wsh", axis=0, tiled=True),
        lax.all_gather(params[1], "wsh", axis=0, tiled=True),
        lax.all_gather(params[2], "wsh", axis=0, tiled=True),
        lax.all_gather(params[3], "wsh", axis=0, tiled=True),
        lax.all_gather(params[4], "wsh", axis=0, tiled=True),
        lax.all_gather(params[5], "wsh", axis=0, tiled=True),
        lax.all_gather(params[6], "wsh", axis=0, tiled=True),
        lax.all_gather(params[7], "wsh", axis=0, tiled=True),
        lax.all_gather(params[8], "wsh", axis=0, tiled=True),
        lax.all_gather(params[9], "wsh", axis=0, tiled=True),
        lax.all_gather(params[10], "wsh", axis=0, tiled=True),
        lax.all_gather(params[11], "wsh", axis=0, tiled=True),
        lax.all_gather(params[12], "wsh", axis=0, tiled=True),
        lax.all_gather(params[13], "wsh", axis=0, tiled=True),
        lax.all_gather(params[14], "wsh", axis=0, tiled=True),
    )


def per_device(
    tokens,
    cotangent,
    lengths,
    dealing,
    w_query,
    w_key,
    w_value,
    w_out,
    w_up,
    w_down,
    b_query,
    b_value,
    b_out,
    b_up,
    b_down,
    gain_one,
    shift_one,
    gain_two,
    shift_two,
):
    params = (
        w_query,
        w_key,
        w_value,
        w_out,
        w_up,
        w_down,
        b_query,
        b_value,
        b_out,
        b_up,
        b_down,
        gain_one,
        shift_one,
        gain_two,
        shift_two,
    )
    own_rows = tokens.shape[2]
    width = tokens.shape[3]
    head_size = width // HEADS
    scale_factor = 1.0 / math.sqrt(head_size)
    my_start = lax.axis_index("ctx") * own_rows
    wsh_count = lax.axis_size("wsh")
    grads = tuple(
        (jnp.zeros((item.shape[0] * wsh_count,) + item.shape[1:], jnp.float32) for item in params)
    )
    results = []
    input_grads = []
    for micro in range(MB):
        whole = gather_params(params)
        query_weight, key_weight, value_weight, out_weight, up_weight, down_weight = whole[:6]
        (
            bias_query,
            bias_value,
            bias_out,
            bias_up,
            bias_down,
            gain_first,
            shift_first,
            gain_second,
            shift_second,
        ) = tuple((item.astype(jnp.float32) for item in whole[6:]))
        token_rows = tokens[0, micro]
        seq_all, valid_all = row_labels(dealing[0, micro], lengths[0, micro])
        my_seq = lax.dynamic_slice_in_dim(seq_all, my_start, own_rows)
        my_valid = lax.dynamic_slice_in_dim(valid_all, my_start, own_rows)
        query_low = (
            jnp.dot(token_rows, query_weight, preferred_element_type=jnp.float32) + bias_query
        ).astype(jnp.bfloat16)
        key_low = jnp.dot(token_rows, key_weight, preferred_element_type=jnp.float32).astype(
            jnp.bfloat16
        )
        value_low = (
            jnp.dot(token_rows, value_weight, preferred_element_type=jnp.float32) + bias_value
        ).astype(jnp.bfloat16)
        query_heads = query_low.reshape(own_rows, HEADS, head_size)
        my_key_heads = key_low.reshape(own_rows, HEADS, head_size)
        my_value_heads = value_low.reshape(own_rows, HEADS, head_size)
        start_state = (
            jnp.full((HEADS, own_rows), NEG_FILL, jnp.float32),
            jnp.zeros((HEADS, own_rows), jnp.float32),
            jnp.zeros((own_rows, HEADS, head_size), jnp.float32),
        )
        key_piece = lax.all_gather(key_low, "ctx", axis=0, tiled=True)
        value_piece = lax.all_gather(value_low, "ctx", axis=0, tiled=True)
        piece_rows = key_piece.shape[0]
        step_rows = math.gcd(piece_rows, 512)

        def visit_block(running, offset):
            run_max, run_sum, run_acc = running
            key_blk = lax.dynamic_slice_in_dim(key_piece, offset, step_rows).reshape(
                step_rows, HEADS, head_size
            )
            value_blk = lax.dynamic_slice_in_dim(value_piece, offset, step_rows).reshape(
                step_rows, HEADS, head_size
            )
            key_seq = lax.dynamic_slice_in_dim(seq_all, offset, step_rows)
            key_valid = lax.dynamic_slice_in_dim(valid_all, offset, step_rows)
            scores, allowed = masked_scores(
                query_heads, key_blk, my_seq, key_seq, key_valid, scale_factor
            )
            new_max = jnp.maximum(run_max, jnp.max(scores, axis=-1))
            rescale = jnp.exp(run_max - new_max)
            weights = jnp.exp(scores - new_max[:, :, None]) * allowed
            run_sum = run_sum * rescale + jnp.sum(weights, axis=-1)
            run_acc = run_acc * rescale.T[:, :, None] + jnp.einsum(
                "hqk,khd->qhd",
                weights.astype(jnp.bfloat16),
                value_blk,
                preferred_element_type=jnp.float32,
            )
            return (new_max, run_sum, run_acc)

        final_max, final_sum, final_acc = blockwise(start_state, piece_rows, step_rows, visit_block)
        attended = final_acc / final_sum.T[:, :, None]
        log_total = final_max + jnp.log(final_sum)
        attended_low = attended.reshape(own_rows, width).astype(jnp.bfloat16)
        out_proj = jnp.dot(attended_low, out_weight, preferred_element_type=jnp.float32) + bias_out
        first_sum = token_rows.astype(jnp.float32) + out_proj
        norm_one, norm_one_back = jax.vjp(layer_norm, first_sum, gain_first, shift_first)
        mlp_input = norm_one.astype(jnp.bfloat16)
        up_pre = jnp.dot(mlp_input, up_weight, preferred_element_type=jnp.float32) + bias_up
        activated, gelu_back = jax.vjp(gelu_exact, up_pre)
        activated_low = activated.astype(jnp.bfloat16)
        down_out = (
            jnp.dot(activated_low, down_weight, preferred_element_type=jnp.float32) + bias_down
        )
        result, norm_two_back = jax.vjp(layer_norm, norm_one + down_out, gain_second, shift_second)
        results.append(result.astype(jnp.bfloat16))
        grad_second, grad_gain_b, grad_shift_b = norm_two_back(
            cotangent[0, micro].astype(jnp.float32)
        )
        grad_down_low = grad_second.astype(jnp.bfloat16)
        grad_activated = jnp.einsum(
            "rd,fd->rf", grad_down_low, down_weight, preferred_element_type=jnp.float32
        )
        (grad_up_pre,) = gelu_back(grad_activated)
        grad_up_low = grad_up_pre.astype(jnp.bfloat16)
        grad_norm_one = (
            jnp.einsum("rf,df->rd", grad_up_low, up_weight, preferred_element_type=jnp.float32)
            + grad_second
        )
        grad_first, grad_gain_a, grad_shift_a = norm_one_back(grad_norm_one)
        grad_out_low = grad_first.astype(jnp.bfloat16)
        grad_att_low = jnp.einsum(
            "rd,ed->re", grad_out_low, out_weight, preferred_element_type=jnp.float32
        ).astype(jnp.bfloat16)
        grad_heads = grad_att_low.reshape(own_rows, HEADS, head_size)
        row_delta = jnp.sum(grad_heads.astype(jnp.float32) * attended, axis=-1).T
        empty_heads = jnp.zeros((own_rows, HEADS, head_size), jnp.float32)
        query_key_piece = lax.all_gather(key_low, "ctx", axis=0, tiled=True)
        query_value_piece = lax.all_gather(value_low, "ctx", axis=0, tiled=True)
        query_piece_rows = query_key_piece.shape[0]
        query_step_rows = math.gcd(query_piece_rows, 512)

        def query_visit_block(running, offset):
            key_blk = lax.dynamic_slice_in_dim(query_key_piece, offset, query_step_rows).reshape(
                query_step_rows, HEADS, head_size
            )
            value_blk = lax.dynamic_slice_in_dim(
                query_value_piece, offset, query_step_rows
            ).reshape(query_step_rows, HEADS, head_size)
            key_seq = lax.dynamic_slice_in_dim(seq_all, offset, query_step_rows)
            key_valid = lax.dynamic_slice_in_dim(valid_all, offset, query_step_rows)
            probs_low, grad_scores = attention_grads(
                query_heads,
                grad_heads,
                key_blk,
                value_blk,
                my_seq,
                key_seq,
                key_valid,
                log_total,
                row_delta,
                scale_factor,
            )
            return running + jnp.einsum(
                "hqk,khd->qhd", grad_scores, key_blk, preferred_element_type=jnp.float32
            )

        grad_query_sum = blockwise(
            empty_heads, query_piece_rows, query_step_rows, query_visit_block
        )
        total_all, delta_all = (
            lax.all_gather(log_total.T, "ctx", axis=0, tiled=True),
            lax.all_gather(row_delta.T, "ctx", axis=0, tiled=True),
        )
        query_piece = lax.all_gather(query_low, "ctx", axis=0, tiled=True)
        grad_piece = lax.all_gather(grad_att_low, "ctx", axis=0, tiled=True)
        key_piece_rows = query_piece.shape[0]
        key_step_rows = math.gcd(key_piece_rows, 512)

        def key_visit_block(running, offset):
            grad_key_run, grad_value_run = running
            query_blk = lax.dynamic_slice_in_dim(query_piece, offset, key_step_rows).reshape(
                key_step_rows, HEADS, head_size
            )
            grad_blk = lax.dynamic_slice_in_dim(grad_piece, offset, key_step_rows).reshape(
                key_step_rows, HEADS, head_size
            )
            total_blk = lax.dynamic_slice_in_dim(total_all, offset, key_step_rows)
            delta_blk = lax.dynamic_slice_in_dim(delta_all, offset, key_step_rows)
            query_seq = lax.dynamic_slice_in_dim(seq_all, offset, key_step_rows)
            probs_low, grad_scores = attention_grads(
                query_blk,
                grad_blk,
                my_key_heads,
                my_value_heads,
                query_seq,
                my_seq,
                my_valid,
                total_blk.T,
                delta_blk.T,
                scale_factor,
            )
            grad_key_run = grad_key_run + jnp.einsum(
                "hqk,qhd->khd", grad_scores, query_blk, preferred_element_type=jnp.float32
            )
            grad_value_run = grad_value_run + jnp.einsum(
                "hqk,qhd->khd", probs_low, grad_blk, preferred_element_type=jnp.float32
            )
            return (grad_key_run, grad_value_run)

        grad_key_sum, grad_value_sum = blockwise(
            (empty_heads, empty_heads), key_piece_rows, key_step_rows, key_visit_block
        )
        grad_key_flat = grad_key_sum.reshape(own_rows, width)
        grad_value_flat = grad_value_sum.reshape(own_rows, width)
        grad_query_low = (
            (grad_query_sum * scale_factor).reshape(own_rows, width).astype(jnp.bfloat16)
        )
        grad_key_low = (grad_key_flat * scale_factor).astype(jnp.bfloat16)
        grad_value_low = grad_value_flat.astype(jnp.bfloat16)
        terms = (
            jnp.einsum("rd,re->de", token_rows, grad_query_low, preferred_element_type=jnp.float32),
            jnp.einsum("rd,re->de", token_rows, grad_key_low, preferred_element_type=jnp.float32),
            jnp.einsum("rd,re->de", token_rows, grad_value_low, preferred_element_type=jnp.float32),
            jnp.einsum("rd,re->de", attended_low, grad_out_low, preferred_element_type=jnp.float32),
            jnp.einsum("rd,rf->df", mlp_input, grad_up_low, preferred_element_type=jnp.float32),
            jnp.einsum(
                "rf,rd->fd", activated_low, grad_down_low, preferred_element_type=jnp.float32
            ),
            jnp.sum(grad_query_low.astype(jnp.float32), axis=0),
            jnp.sum(grad_value_low.astype(jnp.float32), axis=0),
            jnp.sum(grad_out_low.astype(jnp.float32), axis=0),
            jnp.sum(grad_up_low.astype(jnp.float32), axis=0),
            jnp.sum(grad_down_low.astype(jnp.float32), axis=0),
            grad_gain_a,
            grad_shift_a,
            grad_gain_b,
            grad_shift_b,
        )
        grads = tuple((total_now + fresh for total_now, fresh in zip(grads, terms)))
        grad_rows = (
            grad_first
            + jnp.einsum(
                "re,de->rd", grad_query_low, query_weight, preferred_element_type=jnp.float32
            )
            + jnp.einsum("re,de->rd", grad_key_low, key_weight, preferred_element_type=jnp.float32)
            + jnp.einsum(
                "re,de->rd", grad_value_low, value_weight, preferred_element_type=jnp.float32
            )
        )
        input_grads.append(grad_rows.astype(jnp.bfloat16))
    shards = jax.tree.map(
        lambda part: part.astype(jnp.float32),
        lax.psum_scatter(as_sent(grads), "wsh", scatter_dimension=0, tiled=True),
    )
    summed = jax.tree.map(lambda part: part.astype(jnp.float32), lax.psum(as_sent(shards), "ctx"))
    return (jnp.stack(results)[None], jnp.stack(input_grads)[None]) + tuple(summed)


MESH_IDS = pl.DeviceIdType.MESH
F32 = jnp.float32
BF16 = jnp.bfloat16
HD = 64
VMEM_BYTES = 60 * 1024 * 1024


def flip(index, bit):
    return index + bit * (1 - 2 * lax.rem(lax.div(index, bit), 2))


def bit_of(index, bit):
    return lax.rem(lax.div(index, bit), 2)


def greet(peers):
    barrier = pltpu.get_barrier_semaphore()
    for peer in peers:
        pl.semaphore_signal(barrier, inc=1, device_id=peer, device_id_type=MESH_IDS)
    pl.semaphore_wait(barrier, len(peers))


def send(src, dst, send_sem, recv_sem, peer):
    copy = pltpu.make_async_remote_copy(
        src_ref=src,
        dst_ref=dst,
        send_sem=send_sem,
        recv_sem=recv_sem,
        device_id=peer,
        device_id_type=MESH_IDS,
    )
    copy.start()
    return copy


SEQS = HEADS // BPS


def plane_peers(c, w, count):
    return [(lax.rem(c + step, count), w) for step in range(1, count)]


def pack_three(first, second, third, row, pair, out):
    cols = pl.ds(pair * 128, 128)
    a, b, d = (ref[pl.ds(row, BLK), cols] for ref in (first, second, third))
    half = BLK // 2
    for head in range(2):
        lane = slice(head * HD, head * HD + HD)
        out[2 * pair + head, 0:BLK, :] = jnp.concatenate([a[:, lane], b[:, lane]], axis=1)
        out[2 * pair + head, BLK : BLK + half, :] = jnp.concatenate(
            [d[:half, lane], d[half:, lane]], axis=1
        )


def unpack_fold(block):
    return jnp.concatenate([block[:, :HD], block[:, HD:]], axis=0)


def fold(rows):
    half = rows.shape[0] // 2
    return jnp.concatenate([rows[:half], rows[half:]], axis=1)


def all_bytes(ref, sem, peers):
    view = ref.at[pl.ds(0, peers)]
    return pltpu.make_async_copy(view, view, sem)


SQUARE, PAIR, ALONE = 8, 4, 2


def weight_plan(shards):
    plan, first_bulk = [], 3
    for index in range(first_bulk):
        plan.append((index, 0, shards[index].shape[0], SQUARE))
    unit = shards[0].shape[0] * shards[0].shape[1]
    bulk = []
    for index in range(first_bulk, len(shards)):
        rows, cols = shards[index].shape
        parts = max(1, rows * cols // unit)
        for part in range(parts):
            bulk.append((index, part * (rows // parts), rows // parts))
    squares, alone = BULK_WAYS
    for number, item in enumerate(bulk):
        if number < squares:
            way = SQUARE
        elif number >= len(bulk) - alone:
            way = ALONE
        else:
            way = PAIR
        plan.append(item + (way,))
    return plan


BULK_WAYS = (4, 2)


def forward_kernel(heads, plan, n_weights, n_vectors, *refs):
    table_ref, x_ref = refs[:2]
    refs = refs[2:]
    shards, vectors = refs[:n_weights], refs[n_weights : n_weights + n_vectors]
    refs = refs[n_weights + n_vectors :]
    wholes, small_whole, a_ref, kept_ref, lse_ref = refs[:n_weights], *refs[n_weights : n_weights + 4]
    refs = refs[n_weights + 4 :]
    near, stages, refs = refs[:3], refs[3:n_weights], refs[n_weights:]
    small, small_in, bias, q_ref, k_ref, v_ref = refs[:6]
    in_buf = refs[6 : 6 + MB]
    out_buf, back_out, back_in, q_s, k_s, v_s, a_s = refs[6 + MB : 13 + MB]
    (
        w_send,
        w_recv,
        small_sems,
        local_sem,
        stage_sem,
        send_sem,
        recv_sem,
        back_send,
        back_recv,
        keep_sem,
    ) = refs[13 + MB :]
    c, w = lax.axis_index("ctx"), lax.axis_index("wsh")
    o = 1 - w
    by_x, by_y, by_z, by_core = (c, o), (flip(c, 2), w), (flip(c, 4), w), (flip(c, 1), w)
    core, y, z = bit_of(c, 1), bit_of(c, 2), bit_of(c, 4)
    peers = plane_peers(c, w, heads)
    targets = tuple(near) + tuple(wholes[3:])
    staged, locals_ = [], []
    for index, shard in enumerate(shards):
        rows = shard.shape[0]
        spot = pl.ds(pl.multiple_of(w * rows, rows), rows)
        dst = near[index].at[spot] if index < 3 else stages[index - 3]
        copy = pltpu.make_async_copy(shard, dst, stage_sem.at[index])
        copy.start()
        staged.append(copy)
    line, lanes = 0, small.shape[1]
    for vector in vectors:
        for first in range(0, vector.shape[0], lanes):
            piece = vector[pl.ds(first, lanes)].astype(F32)
            small[line : line + 1, :] = piece.reshape(1, lanes)
            line += 1
    greet(peers + [by_x])
    small_sent = send(small, small_in, small_sems.at[0], small_sems.at[1], by_x)

    def part(chunk, side, piece, start, count):
        tensor, first, rows, way = plan[chunk]
        half = shards[tensor].shape[0]
        at = side * half + first + piece * (rows // way) + start
        return targets[tensor].at[pl.ds(pl.multiple_of(at, 8), count)]

    steps = {}

    def sem(kind, chunk):
        return w_send.at[kind, chunk], w_recv.at[kind, chunk]

    def own_piece(way):
        return {SQUARE: core * 4 + z * 2 + y, PAIR: core * 2 + y, ALONE: core}[way]

    for chunk, (tensor, first, rows, way) in enumerate(plan):
        size, mine = rows // way, own_piece(way)
        src = shards[tensor].at[pl.ds(pl.multiple_of(first + mine * size, 8), size)]
        steps[chunk, 0] = send(src, part(chunk, w, mine, 0, size), *sem(0, chunk), by_x)

    def second(chunk):
        _, _, rows, way = plan[chunk]
        if way == ALONE:
            return
        steps[chunk, 0].wait_recv()
        ref = part(chunk, o, own_piece(way), 0, rows // way)
        steps[chunk, 1] = send(ref, ref, *sem(1, chunk), by_y)
        if way == SQUARE:
            steps[chunk, 2] = send(ref, ref, *sem(2, chunk), by_z)

    def third(chunk):
        _, _, rows, way = plan[chunk]
        if way != SQUARE:
            return
        size = rows // way
        steps[chunk, 1].wait_recv()
        steps[chunk, 2].wait_recv()
        ref = part(chunk, o, core * 4 + (1 - z) * 2 + y, 0, size // 2)
        steps[chunk, 3] = send(ref, ref, *sem(3, chunk), by_y)
        ref = part(chunk, o, core * 4 + z * 2 + (1 - y), size // 2, size // 2)
        steps[chunk, 4] = send(ref, ref, *sem(4, chunk), by_z)

    def fourth(chunk):
        _, _, rows, way = plan[chunk]
        for kind in {SQUARE: (3, 4), PAIR: (1,), ALONE: (0,)}[way]:
            steps[chunk, kind].wait_recv()
        ref = part(chunk, o, core * (way // 2), 0, rows // 2)
        steps[chunk, 5] = send(ref, ref, *sem(5, chunk), by_core)

    for index in range(3):
        staged[index].wait()
    for turn in range(5):
        for stage, act in enumerate((second, third, fourth)):
            if 0 <= turn - stage < 3:
                act(turn - stage)
    small_sent.wait()
    small_whole[w] = small[...]
    small_whole[o] = small_in[...]
    for side in range(2):
        for row in range(2):
            bias[row : row + 1, side * lanes : (side + 1) * lanes] = small_whole[
                side, row : row + 1, :
            ]
    width = x_ref.shape[1]
    step = 256
    for index, (weight, out) in enumerate(zip(near, (q_ref, k_ref, v_ref))):
        steps[index, 5].wait_recv()

        def project(turn, carry):
            cols = pl.ds(pl.multiple_of(turn * step, step), step)
            total = jnp.dot(x_ref[...], weight[:, cols], preferred_element_type=F32)
            if index != 1:
                total = total + bias[index // 2 : index // 2 + 1, cols]
            out[:, cols] = total.astype(BF16)
            return carry

        lax.fori_loop(0, width // step, project, 0)
    for m in range(MB):
        for pair in range(heads // 2):
            pack_three(q_ref, k_ref, v_ref, m * BLK, pair, out_buf.at[m])
        for peer in peers:
            send(out_buf.at[m, peer[0]], in_buf[m].at[c], send_sem.at[m], recv_sem.at[m], peer)
        in_buf[m][c] = out_buf[m, c]
    for index in range(n_weights):
        if index < 3:
            copy = pltpu.make_async_copy(near[index], wholes[index], local_sem.at[index])
        else:
            rows = shards[index].shape[0]
            spot = pl.ds(pl.multiple_of(w * rows, rows), rows)
            staged[index].wait()
            copy = pltpu.make_async_copy(
                stages[index - 3], wholes[index].at[spot], local_sem.at[index]
            )
        copy.start()
        locals_.append(copy)

    bulk = range(3, len(plan))
    kinds = {way: [i for i in bulk if plan[i][3] == way] for way in (SQUARE, PAIR, ALONE)}
    squares, pairs, alone = kinds[SQUARE], kinds[PAIR], kinds[ALONE]
    moves = [(second, i) for i in squares + pairs[:2]]
    moves += [None]
    moves += [(third, i) for i in squares] + [(second, i) for i in pairs[2:3]]
    moves += [None]
    moves += [(fourth, i) for i in squares] + [(second, i) for i in pairs[3:4]]
    moves += [(fourth, i) for i in pairs[:2]]
    moves += [None]
    moves += [(second, i) for i in pairs[4:]] + [(fourth, i) for i in pairs[2:]]
    moves += [(fourth, i) for i in alone]

    def pump():
        while moves:
            move = moves.pop(0)
            if move is None:
                return
            move[0](move[1])

    blocks = heads
    span = BPS * BLK
    for m in range(MB):
        pump()
        all_bytes(in_buf[m], recv_sem.at[m], heads - 1).wait()
        keep = pltpu.make_async_copy(in_buf[m], kept_ref.at[m], keep_sem.at[m])
        keep.start()
        for b in range(blocks):
            got = in_buf[m][table_ref[m, SEQS + blocks + b]]
            q_s[b * BLK : (b + 1) * BLK, :] = got[:BLK, :HD]
            k_s[b * BLK : (b + 1) * BLK, :] = got[:BLK, HD:]
            v_s[b * BLK : (b + 1) * BLK, :] = unpack_fold(got[BLK:])

        def one_sequence(s, carry):
            rows = pl.ds(pl.multiple_of(s * span, span), span)
            scores = lax.dot_general(
                k_s[rows, :], q_s[rows, :], (((1,), (1,)), ((), ())), preferred_element_type=F32
            ) * (1.0 / math.sqrt(HD))
            place = lax.broadcasted_iota(jnp.int32, scores.shape, 0)
            scores = jnp.where(place < table_ref[m, s], scores, NEG_FILL)
            top = jnp.max(scores, axis=0, keepdims=True)
            weights = jnp.exp(scores - top)
            total = jnp.sum(weights, axis=0, keepdims=True)
            out_t = lax.dot_general(
                v_s[rows, :],
                weights.astype(BF16),
                (((0,), (0,)), ((), ())),
                preferred_element_type=F32,
            )
            a_s[pl.ds(s * BPS, BPS)] = (out_t / total).T.reshape(BPS, BLK, HD)
            lse_ref[pl.ds(m * (blocks // BPS) + s, 1), :] = top + jnp.log(total)
            return carry

        lax.fori_loop(0, blocks // BPS, one_sequence, 0)
        for t in range(blocks):
            back_out[m, t] = fold(a_s[table_ref[m, SEQS + t]]).astype(BF16)
        for peer in peers:
            send(
                back_out.at[m, peer[0]], back_in.at[m, c], back_send.at[m], back_recv.at[m], peer
            )
        back_in[m, c] = back_out[m, c]
    pump()
    for m in range(MB):
        all_bytes(back_in.at[m], back_recv.at[m], heads - 1).wait()
        for pair in range(heads // 2):
            a_ref[m * BLK : (m + 1) * BLK, pair * 128 : (pair + 1) * 128] = jnp.concatenate(
                [unpack_fold(back_in[m, 2 * pair]), unpack_fold(back_in[m, 2 * pair + 1])], axis=1
            )
    for m in range(MB):
        all_bytes(out_buf.at[m], send_sem.at[m], heads - 1).wait()
        all_bytes(back_out.at[m], back_send.at[m], heads - 1).wait()
        pltpu.make_async_copy(in_buf[m], kept_ref.at[m], keep_sem.at[m]).wait()
    for chunk in bulk:
        steps[chunk, 5].wait_recv()
    for flight in steps.values():
        flight.wait_send()
    for copy in locals_:
        copy.wait()


def forward(table, x, shards, vectors, heads):
    plan = weight_plan(shards)
    count = len(shards)
    anywhere, vmem = pl.BlockSpec(memory_space=pl.ANY), pl.BlockSpec(memory_space=pltpu.VMEM)
    smem = pl.BlockSpec(memory_space=pltpu.SMEM)
    rows, width = x.shape
    pack_rows = BLK + BLK // 2
    span = BPS * BLK
    lanes = min(item.shape[0] for item in vectors)
    lines = sum(item.shape[0] for item in vectors) // lanes
    whole = lambda s: (2 * s.shape[0],) + s.shape[1:]
    return pl.pallas_call(
        functools.partial(forward_kernel, heads, plan, count, len(vectors)),
        out_shape=[jax.ShapeDtypeStruct(whole(s), s.dtype) for s in shards]
        + [
            jax.ShapeDtypeStruct((2, lines, lanes), F32),
            jax.ShapeDtypeStruct((rows, width), BF16),
            jax.ShapeDtypeStruct((MB, heads, pack_rows, 128), BF16),
            jax.ShapeDtypeStruct((8, span), F32),
        ],
        in_specs=[smem] + [vmem] + [anywhere] * count + [vmem] * len(vectors),
        out_specs=[anywhere] * count + [vmem, vmem, anywhere, vmem],
        scratch_shapes=[pltpu.VMEM(whole(s), s.dtype) for s in shards[:3]]
        + [pltpu.VMEM(s.shape, s.dtype) for s in shards[3:]]
        + [pltpu.VMEM((lines, lanes), F32)] * 2
        + [pltpu.VMEM((2, width), F32)]
        + [pltpu.VMEM((rows, width), BF16)] * 3
        + [pltpu.VMEM((heads, pack_rows, 128), BF16)] * MB
        + [
            pltpu.VMEM((MB, heads, pack_rows, 128), BF16),
            pltpu.VMEM((MB, heads, BLK // 2, 128), BF16),
            pltpu.VMEM((MB, heads, BLK // 2, 128), BF16),
            pltpu.VMEM((heads * BLK, HD), BF16),
            pltpu.VMEM((heads * BLK, HD), BF16),
            pltpu.VMEM((heads * BLK, HD), BF16),
            pltpu.VMEM((heads, BLK, HD), F32),
            pltpu.SemaphoreType.DMA((6, len(plan))),
            pltpu.SemaphoreType.DMA((6, len(plan))),
            pltpu.SemaphoreType.DMA((2,)),
            pltpu.SemaphoreType.DMA((count,)),
            pltpu.SemaphoreType.DMA((count,)),
        ]
        + [pltpu.SemaphoreType.DMA((MB,))] * 5,
        compiler_params=pltpu.CompilerParams(
            collective_id=1, has_side_effects=True, vmem_limit_bytes=VMEM_BYTES
        ),
        name="forward",
    )(table, x, *shards, *vectors)


def norm_parts(summed):
    row_mean = jnp.mean(summed, axis=-1, keepdims=True)
    centred = summed - row_mean
    row_var = jnp.mean(centred * centred, axis=-1, keepdims=True)
    scale = lax.rsqrt(row_var + EPSILON)
    return centred * scale, scale


def norm_back(grad, unit, scale, gain):
    inner = grad * gain
    mean_one = jnp.mean(inner, axis=-1, keepdims=True)
    mean_two = jnp.mean(inner * unit, axis=-1, keepdims=True)
    return scale * (inner - mean_one - unit * mean_two)


def dot_minor(a, b):
    return lax.dot_general(a, b, (((1,), (1,)), ((), ())), preferred_element_type=F32)


ROW_OUT, ROW_UP, ROW_DOWN, ROW_GAIN_ONE, ROW_SHIFT_ONE, ROW_GAIN_TWO, ROW_SHIFT_TWO = 2, 3, 7, 8, 9, 10, 11


def dense_kernel(a_ref, x_ref, cot_ref, small_ref, wo_hbm, wu_hbm, wd_hbm, *refs):
    out_ref, n_ref, g_ref, do_ref, du_ref, dm_ref, dh_ref, da_ref, vec_ref = refs[:9]
    wo, wu, wd, slope, n_full, unit, total, wo_sem, wu_sem, wd_sem = refs[9:]
    lanes = small_ref.shape[2]
    hidden = g_ref.shape[1]
    per_half = hidden // 2 // lanes
    chunks = hidden // lanes
    loads = [pltpu.make_async_copy(wo_hbm, wo, wo_sem.at[0])]
    for j in range(chunks):
        cols = pl.ds(j * lanes, lanes)
        loads.append(pltpu.make_async_copy(wu_hbm.at[:, cols], wu.at[:, cols], wu_sem.at[j]))
        loads.append(pltpu.make_async_copy(wd_hbm.at[cols], wd.at[cols], wd_sem.at[j]))
    for load in loads:
        load.start()

    def line(row):
        return jnp.concatenate([small_ref[0, row : row + 1, :], small_ref[1, row : row + 1, :]], axis=1)

    def keep(row, values):
        summed = jnp.sum(values, axis=0, keepdims=True)
        for side in range(2):
            vec_ref[side, row : row + 1, :] = summed[:, side * lanes : (side + 1) * lanes]

    loads[0].wait()
    h_one = x_ref[...].astype(F32) + (
        jnp.dot(a_ref[...], wo[...], preferred_element_type=F32) + line(ROW_OUT)
    )
    unit_one, scale_one = norm_parts(h_one)
    unit[...] = unit_one
    n_one = unit_one * line(ROW_GAIN_ONE) + line(ROW_SHIFT_ONE)
    n_full[...] = n_one
    n_ref[...] = n_one.astype(BF16)
    total[...] = jnp.zeros_like(total)

    def up_and_down(j, carry):
        at = pl.multiple_of(j * lanes, lanes)
        cols = pl.ds(at, lanes)
        pltpu.make_async_copy(wu_hbm.at[:, cols], wu.at[:, cols], wu_sem.at[j]).wait()
        pltpu.make_async_copy(wd_hbm.at[cols], wd.at[cols], wd_sem.at[j]).wait()
        bias = small_ref[lax.div(j, per_half), pl.ds(ROW_UP + lax.rem(j, per_half), 1), :]
        u = jnp.dot(n_ref[...], wu[:, cols], preferred_element_type=F32) + bias
        below = 0.5 * (1.0 + lax.erf(u * math.sqrt(0.5)))
        slope[:, cols] = below + u * jnp.exp(-0.5 * u * u) * (1.0 / math.sqrt(2.0 * math.pi))
        g = (u * below).astype(BF16)
        g_ref[:, cols] = g
        total[...] += jnp.dot(g, wd[cols, :], preferred_element_type=F32)
        return carry

    lax.fori_loop(0, chunks, up_and_down, 0, unroll=True)
    h_two = n_full[...] + (total[...] + line(ROW_DOWN))
    unit_two, scale_two = norm_parts(h_two)
    out_ref[...] = (unit_two * line(ROW_GAIN_TWO) + line(ROW_SHIFT_TWO)).astype(BF16)
    cot = cot_ref[...].astype(F32)
    keep(ROW_GAIN_TWO, cot * unit_two)
    keep(ROW_SHIFT_TWO, cot)
    dh_two = norm_back(cot, unit_two, scale_two, line(ROW_GAIN_TWO))
    dm = dh_two.astype(BF16)
    dm_ref[...] = dm
    keep(ROW_DOWN, dm.astype(F32))
    total[...] = dh_two

    def down_and_up(j, carry):
        cols = pl.ds(pl.multiple_of(j * lanes, lanes), lanes)
        du = (slope[:, cols] * dot_minor(dm_ref[...], wd[cols, :])).astype(BF16)
        du_ref[:, cols] = du
        vec_ref[lax.div(j, per_half), pl.ds(ROW_UP + lax.rem(j, per_half), 1), :] = jnp.sum(
            du.astype(F32), axis=0, keepdims=True
        )
        total[...] += dot_minor(du, wu[:, cols])
        return carry

    lax.fori_loop(0, chunks, down_and_up, 0, unroll=True)
    dn = total[...]
    keep(ROW_GAIN_ONE, dn * unit[...])
    keep(ROW_SHIFT_ONE, dn)
    dh_one = norm_back(dn, unit[...], scale_one, line(ROW_GAIN_ONE))
    dh_ref[...] = dh_one
    do = dh_one.astype(BF16)
    do_ref[...] = do
    keep(ROW_OUT, do.astype(F32))
    da_ref[...] = dot_minor(do, wo[...]).astype(BF16)
    for side in range(2):
        vec_ref[side, 0:ROW_OUT, :] = jnp.zeros((ROW_OUT, lanes), F32)


def dense(a, x, cot, small, wo, wu, wd):
    vmem, anywhere = pl.BlockSpec(memory_space=pltpu.VMEM), pl.BlockSpec(memory_space=pl.ANY)
    rows, width = x.shape
    hidden = wu.shape[1]
    chunks = hidden // small.shape[2]
    low = lambda cols: jax.ShapeDtypeStruct((rows, cols), BF16)
    full = lambda cols: pltpu.VMEM((rows, cols), F32)
    return pl.pallas_call(
        dense_kernel,
        out_shape=[
            low(width),
            low(width),
            low(hidden),
            low(width),
            low(hidden),
            low(width),
            jax.ShapeDtypeStruct((rows, width), F32),
            low(width),
            jax.ShapeDtypeStruct(small.shape, F32),
        ],
        in_specs=[vmem] * 4 + [anywhere] * 3,
        out_specs=[vmem] * 9,
        scratch_shapes=[pltpu.VMEM(item.shape, BF16) for item in (wo, wu, wd)]
        + [full(hidden), full(width), full(width), full(width)]
        + [pltpu.SemaphoreType.DMA((n,)) for n in (1, chunks, chunks)],
        compiler_params=pltpu.CompilerParams(vmem_limit_bytes=VMEM_BYTES),
        name="dense",
    )(a, x, cot, small, wo, wu, wd)


ORDERS = (
    ("yxzZ", "xyzZ", "zxyZ", "yxzZ"),
    ("xzyZ", "zyxZ", "xyzZ", "yzxZ"),
    ("xyzZ", "zxyZ", "yxzZ", "xyzZ"),
)
PIECES = len(ORDERS[0])
KEYS = tuple((part, piece) for part in range(3) for piece in range(PIECES))


def default_schedule():
    early = [(part, piece) for piece in range(PIECES) for part in (1, 2)]
    late = [(0, piece) for piece in range(PIECES)]
    events = ["up", 0, "down", 1, 2] + early + ["back", "qkv", "rows"]
    for step in range(6):
        events += early + ["vec"] + late
    return events + late


def landing_shapes(order, shape):
    shards, sides, shapes = 8, 2, []
    for name in order:
        if name == "x":
            sides = 1
        else:
            shards //= 2
        shapes.append((sides, shards, shape[2] // PIECES, shape[3]))
    return shapes


def dot_t(a, b):
    return lax.dot_general(a, b, (((0,), (0,)), ((), ())), preferred_element_type=F32)


def lanes_at(first, size):
    return pl.ds(pl.multiple_of(first, 128), size)


def backward_kernel(heads, *refs):
    table_ref, da_ref, kept_ref, lse_ref = refs[:4]
    x_ref, a_ref, n_ref, g_ref, do_ref, du_ref, dm_ref, vec_ref, dh_ref = refs[4:13]
    weights = refs[13:16]
    rows_out, o_a, o_b, o_c, vec_out = refs[16:21]
    refs = refs[21:]
    in_buf = refs[:MB]
    out_buf, back_out, back_in, q_s, k_s, v_s, a_s, dq_s, dk_s, dv_s = refs[MB : MB + 10]
    refs = refs[MB + 10 :]
    dq_ref, dk_ref, dv_ref, m_x, m_a, m_n, m_dm, m_do, m_du, m_g, m_dqkv = refs[:11]
    near, (vec_s, v_recv, v_sum, s_a, s_b, s_c) = refs[11:14], refs[14:20]
    refs = refs[20:]
    r_bufs = {key: refs[4 * i : 4 * i + 4] for i, key in enumerate(KEYS)}
    (
        send_sem,
        recv_sem,
        back_send,
        back_recv,
        mate_send,
        mate_recv,
        near_sem,
        rs_send,
        rs_recv,
        ag_send,
        ag_recv,
        own_sem,
        v_send_sem,
        v_recv_sem,
    ) = refs[4 * len(KEYS) :]
    c, x = lax.axis_index("ctx"), lax.axis_index("wsh")
    core, y, z, zz = bit_of(c, 1), bit_of(c, 2), bit_of(c, 4), bit_of(c, 8)
    by_core = (flip(c, 1), x)
    by = {"x": (c, 1 - x), "y": (flip(c, 2), x), "z": (flip(c, 4), x), "Z": (flip(c, 8), x)}
    bits = {"y": y, "z": z, "Z": zz}
    peers = plane_peers(c, x, heads)
    blocks, span = heads, BPS * BLK
    width, hidden = da_ref.shape[1], g_ref.shape[1]
    for index, weight in enumerate(weights):
        pltpu.make_async_copy(weight, near[index], near_sem.at[index]).start()
    greet(peers + [by["x"]])

    for m in range(MB):
        row = slice(m * BLK, (m + 1) * BLK)
        for pair in range(heads // 2):
            both = da_ref[row, pair * 128 : (pair + 1) * 128]
            for head in range(2):
                out_buf[m, 2 * pair + head] = fold(both[:, head * HD : (head + 1) * HD])
        for peer in peers:
            send(out_buf.at[m, peer[0]], in_buf[m].at[c], send_sem.at[m], recv_sem.at[m], peer)
        in_buf[m][c] = out_buf[m, c]

    shared = {}

    def share(name, src, dst):
        index = len(shared)
        shared[name] = send(src, dst, mate_send.at[index], mate_recv.at[index], by_core)

    other = 1 - core
    share("n", n_ref, m_n)
    share("du", du_ref.at[:, lanes_at(other * (hidden // 2), hidden // 2)], m_du)
    for half in range(2):
        share(
            "g" + str(half),
            g_ref.at[:, lanes_at(half * (hidden // 2) + other * (hidden // 4), hidden // 4)],
            m_g.at[:, pl.ds(half * (hidden // 4), hidden // 4)],
        )
    share("dm", dm_ref, m_dm)
    share("a", a_ref, m_a)
    share("do", do_ref.at[:, lanes_at(other * (width // 2), width // 2)], m_do)
    share("x", x_ref, m_x)

    sums, outs = (s_a, s_b, s_c), (o_a, o_b, o_c)
    wide = 256

    def tile(pairs, out, first, count):
        def body(turn, carry):
            at = turn * wide
            total = sum(dot_t(lhs[...], rhs[:, lanes_at(col + at, wide)]) for lhs, rhs, col in pairs)
            cols = lanes_at(first + at, wide)
            out[..., cols] = total.astype(BF16).reshape(out.shape[:-1] + (wide,))
            return carry

        lax.fori_loop(0, count, body, 0)

    def grads_up():
        shared["n"].wait_recv()
        shared["du"].wait_recv()
        half = hidden // 2
        tile(((n_ref, du_ref, core * half), (m_n, m_du, 0)), s_b, 0, half // wide)

    def grads_down():
        for name in ("g0", "g1", "dm"):
            shared[name].wait_recv()
        quarter = hidden // 4
        for half in range(2):
            mine = g_ref.at[:, lanes_at(half * 2 * quarter + core * quarter, quarter)]
            others = m_g.at[:, pl.ds(half * quarter, quarter)]
            tile(((mine, dm_ref, 0), (others, m_dm, 0)), s_c.at[half], 0, width // wide)

    def grads_qkv():
        half = width // 2
        for name in ("a", "do", "x", "dq", "dk", "dv"):
            shared[name].wait_recv()
        tile(((a_ref, do_ref, core * half), (m_a, m_do, 0)), s_a, 3 * half, half // wide)
        for index, ref in enumerate((dq_ref, dk_ref, dv_ref)):
            pairs = ((x_ref, ref, core * half), (m_x, m_dqkv, index * half))
            tile(pairs, s_a, index * half, half // wide)

    def attention(m):
        all_bytes(in_buf[m], recv_sem.at[m], heads - 1).wait()
        for b in range(blocks):
            slot = table_ref[m, SEQS + blocks + b]
            got = kept_ref[m, slot]
            rows = slice(b * BLK, (b + 1) * BLK)
            q_s[rows, :] = got[:BLK, :HD]
            k_s[rows, :] = got[:BLK, HD:]
            v_s[rows, :] = unpack_fold(got[BLK:])
            a_s[rows, :] = unpack_fold(in_buf[m][slot])

        def one_sequence(s, carry):
            rows = pl.ds(pl.multiple_of(s * span, span), span)
            qq, kk, vv, dd = q_s[rows, :], k_s[rows, :], v_s[rows, :], a_s[rows, :]
            scale = 1.0 / math.sqrt(HD)
            minor = (((1,), (1,)), ((), ()))
            scores = lax.dot_general(kk, qq, minor, preferred_element_type=F32) * scale
            spot = lax.broadcasted_iota(jnp.int32, scores.shape, 0)
            total = lse_ref[pl.ds(m * (blocks // BPS) + s, 1), :]
            probs = jnp.exp(jnp.where(spot < table_ref[m, s], scores - total, NEG_FILL))
            dp = lax.dot_general(vv, dd, minor, preferred_element_type=F32)
            both = probs * dp
            delta = jnp.sum(both, axis=0, keepdims=True)
            ds = (both - probs * delta).astype(BF16)
            here, split = pl.ds(s * BPS, BPS), (BPS, BLK, HD)
            dv = jnp.dot(probs.astype(BF16), dd, preferred_element_type=F32)
            dv_s[here] = dv.reshape(split)
            dk_s[here] = (jnp.dot(ds, qq, preferred_element_type=F32) * scale).reshape(split)
            dq_s[here] = (dot_t(kk, ds).T * scale).reshape(split)
            return carry

        lax.fori_loop(0, blocks // BPS, one_sequence, 0)
        for t in range(blocks):
            at = table_ref[m, SEQS + t]
            back_out[m, t, 0:BLK, :] = jnp.concatenate([dq_s[at], dk_s[at]], axis=1).astype(BF16)
            back_out[m, t, BLK:, :] = fold(dv_s[at]).astype(BF16)
        for peer in peers:
            send(
                back_out.at[m, peer[0]], back_in.at[m, c], back_send.at[m], back_recv.at[m], peer
            )
        back_in[m, c] = back_out[m, c]

    vec_peers = (by["x"], by["y"], by["z"], by["Z"], by_core)
    vec_steps = []

    def vec_send(src):
        step = len(vec_steps)
        vec_steps.append(
            send(
                src, v_recv.at[step], v_send_sem.at[step], v_recv_sem.at[step], vec_peers[step]
            )
        )

    def vec_next():
        step = len(vec_steps) - 1
        vec_steps[step].wait_recv()
        before = vec_s[x] if step == 0 else v_sum[step - 1]
        v_sum[step] = before + v_recv[step]
        if step + 1 < len(vec_peers):
            vec_send(v_sum.at[step])

    def come_back():
        for m in range(MB):
            all_bytes(back_in.at[m], back_recv.at[m], heads - 1).wait()
            row = slice(m * BLK, (m + 1) * BLK)
            for pair in range(heads // 2):
                lanes = slice(pair * 128, (pair + 1) * 128)
                one, two = back_in[m, 2 * pair], back_in[m, 2 * pair + 1]
                dq_ref[row, lanes] = jnp.concatenate([one[:BLK, :HD], two[:BLK, :HD]], axis=1)
                dk_ref[row, lanes] = jnp.concatenate([one[:BLK, HD:], two[:BLK, HD:]], axis=1)
                dv_ref[row, lanes] = jnp.concatenate(
                    [unpack_fold(one[BLK:]), unpack_fold(two[BLK:])], axis=1
                )
        half = width // 2
        for index, (name, ref) in enumerate((("dq", dq_ref), ("dk", dk_ref), ("dv", dv_ref))):
            share(
                name,
                ref.at[:, lanes_at(other * half, half)],
                m_dqkv.at[:, pl.ds(index * half, half)],
            )
        vec_s[...] = vec_ref[...]
        lanes = vec_s.shape[2]
        for index, ref in enumerate((dq_ref, dv_ref)):
            total = jnp.sum(ref[...].astype(F32), axis=0, keepdims=True)
            for side in range(2):
                vec_s[side, index : index + 1, :] = total[:, side * lanes : (side + 1) * lanes]
        vec_send(vec_s.at[1 - x])

    def grad_rows():
        total = dh_ref[...]
        for index, ref in enumerate((dq_ref, dk_ref, dv_ref)):
            pltpu.make_async_copy(weights[index], near[index], near_sem.at[index]).wait()
            total = total + lax.dot_general(
                ref[...], near[index][...], (((1,), (1,)), ((), ())), preferred_element_type=F32
            )
        rows_out[...] = total.astype(BF16)

    plans, gathers = {}, {}
    for key in KEYS:
        first, count, sided = 0, 8, False
        plans[key], back = [], []
        for name in ORDERS[key[0]][key[1]]:
            if name == "x":
                plans[key].append((by["x"], 1 - x, x, first, first, count))
                sided = True
                continue
            count //= 2
            out, keep = first + (1 - bits[name]) * count, first + bits[name] * count
            side = x if sided else None
            plans[key].append((by[name], side, side, out, keep, count))
            back.append((by[name], keep, out, count))
            first = keep
        gathers[key] = back[::-1]
    flights, spread, owns, state = {}, {}, {}, {}

    def piece_rows(key):
        rows = sums[key[0]].shape[2] // PIECES
        return pl.ds(key[1] * rows, rows)

    def reduce_send(key, step):
        peer, side, _, first, _, count = plans[key][step]
        dst = r_bufs[key][step]
        if side is None:
            src = sums[key[0]].at[:, pl.ds(first, count), piece_rows(key)]
        else:
            src, dst = sums[key[0]].at[side, pl.ds(first, count), piece_rows(key)], dst.at[0]
        sems = rs_send.at[key[0], key[1], step], rs_recv.at[key[0], key[1], step]
        flights[key, step] = send(src, dst, *sems, peer)
        state[key] = step

    def reduce_add(key, step):
        _, _, side, _, first, count = plans[key][step]
        flights[key, step].wait_recv()
        total, fresh, rows = sums[key[0]], r_bufs[key][step], piece_rows(key)
        sides = ((0, 0), (1, 1)) if side is None else ((side, 0),)
        for here, there in sides:

            def body(index, carry):
                spot = first + index
                total[here, spot, rows] = (
                    total[here, spot, rows].astype(F32) + fresh[there, index].astype(F32)
                ).astype(BF16)
                return carry

            lax.fori_loop(0, count, body, 0)

    def spread_send(key, kind, src, dst, peer):
        sems = ag_send.at[key[0], key[1], kind], ag_recv.at[key[0], key[1], kind]
        spread[key, kind] = send(src, dst, *sems, peer)

    def advance(key):
        step = state[key]
        out, rows = outs[key[0]], piece_rows(key)
        if step < 4:
            reduce_add(key, step)
            if step < 3:
                reduce_send(key, step + 1)
                return
            peer, first, _, _ = gathers[key][0]
            src = sums[key[0]].at[x, pl.ds(first, 1), rows]
            dst = out.at[core, pl.ds(first, 1), rows]
            owns[key] = pltpu.make_async_copy(src, dst, own_sem.at[key[0], key[1]])
            owns[key].start()
            spread_send(key, 0, src, dst, peer)
            spread_send(key, 3, src, dst, by_core)
        else:
            turn = step - 3
            spread[key, turn - 1].wait_recv()
            if turn == 1:
                owns[key].wait()
            if turn < 3:
                peer, first, _, count = gathers[key][turn]
                ref = out.at[core, pl.ds(first, count), rows]
                spread_send(key, turn, ref, ref, peer)
            _, _, first, count = gathers[key][turn - 1]
            ref = out.at[core, pl.ds(first, count), rows]
            spread_send(key, 3 + turn, ref, ref, by_core)
        state[key] = step + 1

    actions = {
        "up": (grads_up, 1),
        "down": (grads_down, 2),
        "qkv": (grads_qkv, 0),
        "back": (come_back, None),
        "rows": (grad_rows, None),
        "vec": (vec_next, None),
    }
    for event in SCHEDULE:
        if isinstance(event, tuple):
            advance(event)
        elif isinstance(event, int):
            attention(event)
        else:
            action, part = actions[event]
            if event == "vec" and len(vec_steps) == len(vec_peers) and "vec" in state:
                continue
            if event == "vec" and len(vec_steps) == len(vec_peers):
                state["vec"] = True
            action()
            if part is not None:
                for piece in range(PIECES):
                    reduce_send((part, piece), 0)
    vec_out[...] = v_sum[len(vec_peers) - 1]
    for m in range(MB):
        all_bytes(out_buf.at[m], send_sem.at[m], heads - 1).wait()
        all_bytes(back_out.at[m], back_send.at[m], heads - 1).wait()
    for flight in shared.values():
        flight.wait_send()
    for flight in vec_steps:
        flight.wait_send()
    for flight in flights.values():
        flight.wait_send()
    for (_, kind), flight in spread.items():
        if kind >= 3:
            flight.wait_recv()
        flight.wait_send()


SCHEDULE = (
    "down", 0, "up", 1, 2, (2, 0), (1, 3), (1, 1), (2, 2), (1, 0), (2, 0), (1, 3), (1, 2),
    "back", (2, 2), (2, 0), (2, 3), (1, 2), (1, 3), "qkv", (1, 3), (2, 3), (1, 2), (1, 3),
    (1, 1), (2, 2), (2, 0), (1, 1), "vec", (2, 1), (2, 2), (2, 0), (2, 1), (0, 1), (1, 3),
    (2, 2), (1, 2), (2, 3), (0, 0), (2, 1), (1, 0), "vec", (2, 3), (0, 3), (0, 0), (2, 2),
    (2, 1), (0, 3), (2, 0), (1, 3), (1, 1), (2, 1), (0, 2), "vec", (1, 2), (2, 3), (1, 0),
    (1, 1), (0, 1), (0, 3), (0, 0), (2, 1), (1, 0), (2, 0), (2, 2), (0, 2), "vec", (0, 3),
    (0, 1), (1, 2), (0, 3), (0, 2), (2, 3), "rows", (0, 0), (1, 0), (1, 1), (0, 2), (0, 0),
    (0, 3), (0, 1), "vec", (0, 2), (0, 1), (1, 0), (0, 0), (1, 2), (0, 1), (0, 2), (0, 3),
    (0, 0), (0, 1), (1, 1), (2, 3), (1, 0), (2, 1), (0, 2),
)


def backward(table, da, kept, lse, x, a, n1, g, do, du, dm, vec, dh, weights, heads):
    vmem, smem = pl.BlockSpec(memory_space=pltpu.VMEM), pl.BlockSpec(memory_space=pltpu.SMEM)
    anywhere = pl.BlockSpec(memory_space=pl.ANY)
    rows, width = da.shape
    hidden = g.shape[1]
    pack_rows = BLK + BLK // 2
    low = lambda *dims: pltpu.VMEM(dims, BF16)
    a_shape, b_shape = (2, 8, width // 16, 2 * width), (2, 8, width // 16, hidden // 2)
    c_shape = (2, 8, hidden // 32, width)
    scratch = [low(heads, BLK // 2, 128)] * MB
    scratch += [low(MB, heads, BLK // 2, 128)]
    scratch += [low(MB, heads, pack_rows, 128)] * 2
    scratch += [low(heads * BLK, HD)] * 4
    scratch += [pltpu.VMEM((heads, BLK, HD), F32)] * 3
    scratch += [low(rows, width)] * 7
    scratch += [low(rows, width // 2), low(rows, hidden // 2), low(rows, hidden // 2)]
    scratch += [low(rows, 3 * width // 2)]
    scratch += [low(*item.shape) for item in weights]
    scratch += [pltpu.VMEM(vec.shape, F32)] + [pltpu.VMEM((5,) + vec.shape[1:], F32)] * 2
    scratch += [low(*shape) for shape in (a_shape, b_shape, c_shape)]
    for key in KEYS:
        shape = (a_shape, b_shape, c_shape)[key[0]]
        scratch += [low(*item) for item in landing_shapes(ORDERS[key[0]][key[1]], shape)]
    sems = lambda *dims: pltpu.SemaphoreType.DMA(dims)
    scratch += [sems(MB)] * 4 + [sems(11)] * 2 + [sems(3)]
    scratch += [sems(3, PIECES, 4)] * 2 + [sems(3, PIECES, 7)] * 2 + [sems(3, PIECES)]
    scratch += [sems(5)] * 2
    return pl.pallas_call(
        functools.partial(backward_kernel, heads),
        out_shape=[
            jax.ShapeDtypeStruct((rows, width), BF16),
            jax.ShapeDtypeStruct(a_shape, BF16),
            jax.ShapeDtypeStruct(b_shape, BF16),
            jax.ShapeDtypeStruct(c_shape, BF16),
            jax.ShapeDtypeStruct(vec.shape[1:], F32),
        ],
        in_specs=[smem] + [vmem] * 12 + [anywhere] * 3,
        out_specs=[vmem] + [anywhere] * 3 + [vmem],
        scratch_shapes=scratch,
        compiler_params=pltpu.CompilerParams(
            collective_id=2, has_side_effects=True, vmem_limit_bytes=VMEM_BYTES
        ),
        name="backward",
    )(table, da, kept, lse, x, a, n1, g, do, du, dm, vec, dh, *weights)


def widen_kernel(a_ref, b_ref, c_ref, vec_ref, *outs):
    @pl.when(pl.program_id(0) == 0)
    def _():
        line, lanes = 0, vec_ref.shape[1]
        for out in outs[6:]:
            for first in range(0, out.shape[0], lanes):
                out[pl.ds(first, lanes)] = vec_ref[line, :]
                line += 1

    half = outs[0].shape[1] // 2
    for index, out in enumerate(outs[:4]):
        for core in range(2):
            out[:, core * half : (core + 1) * half] = a_ref[
                core, 0, :, index * half : (index + 1) * half
            ].astype(F32)
    up, down = outs[4:6]
    half = up.shape[1] // 2
    for core in range(2):
        up[:, core * half : (core + 1) * half] = b_ref[core, 0].astype(F32)
        down[core, 0] = c_ref[core, 0].astype(F32)


def widen(o_a, o_b, o_c, vec, sizes):
    shards = o_a.shape[1]
    block = lambda item: pl.BlockSpec((2, 1) + item.shape[2:], lambda i: (0, i, 0, 0))
    rows = o_a.shape[2]
    square = (shards * rows, o_a.shape[3] // 2)
    wide = (shards * rows, 2 * o_b.shape[3])
    return pl.pallas_call(
        widen_kernel,
        grid=(shards,),
        out_shape=[jax.ShapeDtypeStruct(square, F32)] * 4
        + [jax.ShapeDtypeStruct(wide, F32), jax.ShapeDtypeStruct(o_c.shape, F32)]
        + [jax.ShapeDtypeStruct((size,), F32) for size in sizes],
        in_specs=[block(o_a), block(o_b), block(o_c), pl.BlockSpec(vec.shape, lambda i: (0, 0))],
        out_specs=[pl.BlockSpec((rows, square[1]), lambda i: (i, 0))] * 4
        + [pl.BlockSpec((rows, wide[1]), lambda i: (i, 0)), block(o_c)]
        + [pl.BlockSpec((size,), lambda i: (0,)) for size in sizes],
        compiler_params=pltpu.CompilerParams(vmem_limit_bytes=VMEM_BYTES),
        name="widen",
    )(o_a, o_b, o_c, vec)


def per_device_heads(tokens, cotangent, lengths, dealing, *params):
    rows_in = tokens.shape[2]
    width = tokens.shape[3]
    rows = MB * rows_in
    weights, vectors = params[:6], params[6:]
    sizes = [item.shape[0] for item in vectors]
    x = tokens.reshape(rows, width)
    blocks = jnp.arange(HEADS, dtype=jnp.int32)
    at_block = dealing[0][:, :, None] == blocks[None, None, :]
    slot_of = jnp.sum(jnp.where(at_block, blocks[None, :, None], 0), axis=1)
    table = jnp.concatenate([lengths[0], dealing[0], slot_of], axis=1)
    *wholes, small_whole, a, kept, lse = forward(table, x, weights, vectors, HEADS)
    query_w, key_w, value_w, out_w, up_w, down_w = wholes
    output, n_low, g, do, du, dm, dh_one, da, vec = dense(
        a, x, cotangent.reshape(rows, width), small_whole, out_w, up_w, down_w
    )
    grad_tokens, o_a, o_b, o_c, vec_sum = backward(
        table,
        da,
        kept,
        lse,
        x,
        a,
        n_low,
        g,
        do,
        du,
        dm,
        vec,
        dh_one,
        (query_w, key_w, value_w),
        HEADS,
    )
    grads = list(widen(o_a, o_b, o_c, vec_sum, sizes))
    grads[5] = grads[5].reshape(-1, width)
    shape = (1, MB, rows_in, width)
    return (
        (output.reshape(shape), grad_tokens.reshape(shape))
        + tuple(grads)
    )


def solution(mesh):
    placed = (
        P("wsh", None, "ctx", None),
        P("wsh", None, "ctx", None),
        P("wsh", None, None),
        P("wsh", None, None),
        P("wsh", None),
        P("wsh", None),
        P("wsh", None),
        P("wsh", None),
        P("wsh", None),
        P("wsh", None),
        P("wsh"),
        P("wsh"),
        P("wsh"),
        P("wsh"),
        P("wsh"),
        P("wsh"),
        P("wsh"),
        P("wsh"),
        P("wsh"),
    )
    by_heads = mesh.shape["ctx"] == HEADS and mesh.shape["wsh"] == 2
    return jax.shard_map(
        per_device_heads if by_heads else per_device,
        mesh=mesh,
        in_specs=placed,
        out_specs=(
            P("wsh", None, "ctx", None),
            P("wsh", None, "ctx", None),
            P("wsh", None),
            P("wsh", None),
            P("wsh", None),
            P("wsh", None),
            P("wsh", None),
            P("wsh", None),
            P("wsh"),
            P("wsh"),
            P("wsh"),
            P("wsh"),
            P("wsh"),
            P("wsh"),
            P("wsh"),
            P("wsh"),
            P("wsh"),
        ),
        check_vma=False,
    )
```

```python
import functools
import math

import jax
import jax.numpy as jnp
from jax import lax
from jax.experimental import pallas as pl
from jax.experimental.pallas import tpu as pltpu
from jax.sharding import PartitionSpec as P

HEADS = 16
BPS = 8
MB = 3
BLK = 64


EPSILON = 1e-12
NEG_FILL = -1e30


def as_sent(x):
    return jax.tree.map(lambda a: a.astype(jnp.bfloat16) if a.dtype == jnp.float32 else a, x)


def layer_norm(summed, gain_vec, shift_vec):
    row_mean = jnp.mean(summed, axis=-1, keepdims=True)
    centred = summed - row_mean
    row_var = jnp.mean(centred * centred, axis=-1, keepdims=True)
    return centred * lax.rsqrt(row_var + EPSILON) * gain_vec + shift_vec


def gelu_exact(values):
    return jax.nn.gelu(values, approximate=False)


def row_labels(dealt_order, seq_lengths):
    blocks_of_rows = jnp.repeat(dealt_order, BLK)
    within = jnp.tile(jnp.arange(BLK, dtype=jnp.int32), dealt_order.shape[0])
    seq_ids = blocks_of_rows // BPS
    places = blocks_of_rows % BPS * BLK + within
    numbers = jnp.arange(seq_lengths.shape[0], dtype=jnp.int32)
    seq_bound = jnp.sum(
        jnp.where(seq_ids[:, None] == numbers[None, :], seq_lengths[None, :], 0), axis=1
    )
    return (seq_ids, places < seq_bound)


def blockwise(carried, total_rows, step_rows, visit_block):
    return lax.fori_loop(
        0,
        total_rows // step_rows,
        lambda turn_index, running: visit_block(running, turn_index * step_rows),
        carried,
    )


def masked_scores(query_blk, key_blk, query_seq, key_seq, key_valid, scale_factor):
    allowed = (query_seq[:, None] == key_seq[None, :]) & key_valid[None, :]
    scores = (
        jnp.einsum("qhd,khd->hqk", query_blk, key_blk, preferred_element_type=jnp.float32)
        * scale_factor
    )
    return (jnp.where(allowed[None], scores, NEG_FILL), allowed[None].astype(jnp.float32))


def attention_grads(
    query_blk,
    grad_blk,
    key_blk,
    value_blk,
    query_seq,
    key_seq,
    key_valid,
    row_total,
    row_delta,
    scale_factor,
):
    scores, allowed = masked_scores(query_blk, key_blk, query_seq, key_seq, key_valid, scale_factor)
    probs = jnp.exp(scores - row_total[:, :, None]) * allowed
    grad_probs = jnp.einsum("qhd,khd->hqk", grad_blk, value_blk, preferred_element_type=jnp.float32)
    grad_scores = (probs * (grad_probs - row_delta[:, :, None])).astype(jnp.bfloat16)
    return (probs.astype(jnp.bfloat16), grad_scores)


def gather_params(params):
    return (
        lax.all_gather(params[0], "wsh", axis=0, tiled=True),
        lax.all_gather(params[1], "wsh", axis=0, tiled=True),
        lax.all_gather(params[2], "wsh", axis=0, tiled=True),
        lax.all_gather(params[3], "wsh", axis=0, tiled=True),
        lax.all_gather(params[4], "wsh", axis=0, tiled=True),
        lax.all_gather(params[5], "wsh", axis=0, tiled=True),
        lax.all_gather(params[6], "wsh", axis=0, tiled=True),
        lax.all_gather(params[7], "wsh", axis=0, tiled=True),
        lax.all_gather(params[8], "wsh", axis=0, tiled=True),
        lax.all_gather(params[9], "wsh", axis=0, tiled=True),
        lax.all_gather(params[10], "wsh", axis=0, tiled=True),
        lax.all_gather(params[11], "wsh", axis=0, tiled=True),
        lax.all_gather(params[12], "wsh", axis=0, tiled=True),
        lax.all_gather(params[13], "wsh", axis=0, tiled=True),
        lax.all_gather(params[14], "wsh", axis=0, tiled=True),
    )


def per_device(
    tokens,
    cotangent,
    lengths,
    dealing,
    w_query,
    w_key,
    w_value,
    w_out,
    w_up,
    w_down,
    b_query,
    b_value,
    b_out,
    b_up,
    b_down,
    gain_one,
    shift_one,
    gain_two,
    shift_two,
):
    params = (
        w_query,
        w_key,
        w_value,
        w_out,
        w_up,
        w_down,
        b_query,
        b_value,
        b_out,
        b_up,
        b_down,
        gain_one,
        shift_one,
        gain_two,
        shift_two,
    )
    own_rows = tokens.shape[2]
    width = tokens.shape[3]
    head_size = width // HEADS
    scale_factor = 1.0 / math.sqrt(head_size)
    my_start = lax.axis_index("ctx") * own_rows
    wsh_count = lax.axis_size("wsh")
    grads = tuple(
        (jnp.zeros((item.shape[0] * wsh_count,) + item.shape[1:], jnp.float32) for item in params)
    )
    results = []
    input_grads = []
    for micro in range(MB):
        whole = gather_params(params)
        query_weight, key_weight, value_weight, out_weight, up_weight, down_weight = whole[:6]
        (
            bias_query,
            bias_value,
            bias_out,
            bias_up,
            bias_down,
            gain_first,
            shift_first,
            gain_second,
            shift_second,
        ) = tuple((item.astype(jnp.float32) for item in whole[6:]))
        token_rows = tokens[0, micro]
        seq_all, valid_all = row_labels(dealing[0, micro], lengths[0, micro])
        my_seq = lax.dynamic_slice_in_dim(seq_all, my_start, own_rows)
        my_valid = lax.dynamic_slice_in_dim(valid_all, my_start, own_rows)
        query_low = (
            jnp.dot(token_rows, query_weight, preferred_element_type=jnp.float32) + bias_query
        ).astype(jnp.bfloat16)
        key_low = jnp.dot(token_rows, key_weight, preferred_element_type=jnp.float32).astype(
            jnp.bfloat16
        )
        value_low = (
            jnp.dot(token_rows, value_weight, preferred_element_type=jnp.float32) + bias_value
        ).astype(jnp.bfloat16)
        query_heads = query_low.reshape(own_rows, HEADS, head_size)
        my_key_heads = key_low.reshape(own_rows, HEADS, head_size)
        my_value_heads = value_low.reshape(own_rows, HEADS, head_size)
        start_state = (
            jnp.full((HEADS, own_rows), NEG_FILL, jnp.float32),
            jnp.zeros((HEADS, own_rows), jnp.float32),
            jnp.zeros((own_rows, HEADS, head_size), jnp.float32),
        )
        key_piece = lax.all_gather(key_low, "ctx", axis=0, tiled=True)
        value_piece = lax.all_gather(value_low, "ctx", axis=0, tiled=True)
        piece_rows = key_piece.shape[0]
        step_rows = math.gcd(piece_rows, 512)

        def visit_block(running, offset):
            run_max, run_sum, run_acc = running
            key_blk = lax.dynamic_slice_in_dim(key_piece, offset, step_rows).reshape(
                step_rows, HEADS, head_size
            )
            value_blk = lax.dynamic_slice_in_dim(value_piece, offset, step_rows).reshape(
                step_rows, HEADS, head_size
            )
            key_seq = lax.dynamic_slice_in_dim(seq_all, offset, step_rows)
            key_valid = lax.dynamic_slice_in_dim(valid_all, offset, step_rows)
            scores, allowed = masked_scores(
                query_heads, key_blk, my_seq, key_seq, key_valid, scale_factor
            )
            new_max = jnp.maximum(run_max, jnp.max(scores, axis=-1))
            rescale = jnp.exp(run_max - new_max)
            weights = jnp.exp(scores - new_max[:, :, None]) * allowed
            run_sum = run_sum * rescale + jnp.sum(weights, axis=-1)
            run_acc = run_acc * rescale.T[:, :, None] + jnp.einsum(
                "hqk,khd->qhd",
                weights.astype(jnp.bfloat16),
                value_blk,
                preferred_element_type=jnp.float32,
            )
            return (new_max, run_sum, run_acc)

        final_max, final_sum, final_acc = blockwise(start_state, piece_rows, step_rows, visit_block)
        attended = final_acc / final_sum.T[:, :, None]
        log_total = final_max + jnp.log(final_sum)
        attended_low = attended.reshape(own_rows, width).astype(jnp.bfloat16)
        out_proj = jnp.dot(attended_low, out_weight, preferred_element_type=jnp.float32) + bias_out
        first_sum = token_rows.astype(jnp.float32) + out_proj
        norm_one, norm_one_back = jax.vjp(layer_norm, first_sum, gain_first, shift_first)
        mlp_input = norm_one.astype(jnp.bfloat16)
        up_pre = jnp.dot(mlp_input, up_weight, preferred_element_type=jnp.float32) + bias_up
        activated, gelu_back = jax.vjp(gelu_exact, up_pre)
        activated_low = activated.astype(jnp.bfloat16)
        down_out = (
            jnp.dot(activated_low, down_weight, preferred_element_type=jnp.float32) + bias_down
        )
        result, norm_two_back = jax.vjp(layer_norm, norm_one + down_out, gain_second, shift_second)
        results.append(result.astype(jnp.bfloat16))
        grad_second, grad_gain_b, grad_shift_b = norm_two_back(
            cotangent[0, micro].astype(jnp.float32)
        )
        grad_down_low = grad_second.astype(jnp.bfloat16)
        grad_activated = jnp.einsum(
            "rd,fd->rf", grad_down_low, down_weight, preferred_element_type=jnp.float32
        )
        (grad_up_pre,) = gelu_back(grad_activated)
        grad_up_low = grad_up_pre.astype(jnp.bfloat16)
        grad_norm_one = (
            jnp.einsum("rf,df->rd", grad_up_low, up_weight, preferred_element_type=jnp.float32)
            + grad_second
        )
        grad_first, grad_gain_a, grad_shift_a = norm_one_back(grad_norm_one)
        grad_out_low = grad_first.astype(jnp.bfloat16)
        grad_att_low = jnp.einsum(
            "rd,ed->re", grad_out_low, out_weight, preferred_element_type=jnp.float32
        ).astype(jnp.bfloat16)
        grad_heads = grad_att_low.reshape(own_rows, HEADS, head_size)
        row_delta = jnp.sum(grad_heads.astype(jnp.float32) * attended, axis=-1).T
        empty_heads = jnp.zeros((own_rows, HEADS, head_size), jnp.float32)
        query_key_piece = lax.all_gather(key_low, "ctx", axis=0, tiled=True)
        query_value_piece = lax.all_gather(value_low, "ctx", axis=0, tiled=True)
        query_piece_rows = query_key_piece.shape[0]
        query_step_rows = math.gcd(query_piece_rows, 512)

        def query_visit_block(running, offset):
            key_blk = lax.dynamic_slice_in_dim(query_key_piece, offset, query_step_rows).reshape(
                query_step_rows, HEADS, head_size
            )
            value_blk = lax.dynamic_slice_in_dim(
                query_value_piece, offset, query_step_rows
            ).reshape(query_step_rows, HEADS, head_size)
            key_seq = lax.dynamic_slice_in_dim(seq_all, offset, query_step_rows)
            key_valid = lax.dynamic_slice_in_dim(valid_all, offset, query_step_rows)
            probs_low, grad_scores = attention_grads(
                query_heads,
                grad_heads,
                key_blk,
                value_blk,
                my_seq,
                key_seq,
                key_valid,
                log_total,
                row_delta,
                scale_factor,
            )
            return running + jnp.einsum(
                "hqk,khd->qhd", grad_scores, key_blk, preferred_element_type=jnp.float32
            )

        grad_query_sum = blockwise(
            empty_heads, query_piece_rows, query_step_rows, query_visit_block
        )
        total_all, delta_all = (
            lax.all_gather(log_total.T, "ctx", axis=0, tiled=True),
            lax.all_gather(row_delta.T, "ctx", axis=0, tiled=True),
        )
        query_piece = lax.all_gather(query_low, "ctx", axis=0, tiled=True)
        grad_piece = lax.all_gather(grad_att_low, "ctx", axis=0, tiled=True)
        key_piece_rows = query_piece.shape[0]
        key_step_rows = math.gcd(key_piece_rows, 512)

        def key_visit_block(running, offset):
            grad_key_run, grad_value_run = running
            query_blk = lax.dynamic_slice_in_dim(query_piece, offset, key_step_rows).reshape(
                key_step_rows, HEADS, head_size
            )
            grad_blk = lax.dynamic_slice_in_dim(grad_piece, offset, key_step_rows).reshape(
                key_step_rows, HEADS, head_size
            )
            total_blk = lax.dynamic_slice_in_dim(total_all, offset, key_step_rows)
            delta_blk = lax.dynamic_slice_in_dim(delta_all, offset, key_step_rows)
            query_seq = lax.dynamic_slice_in_dim(seq_all, offset, key_step_rows)
            probs_low, grad_scores = attention_grads(
                query_blk,
                grad_blk,
                my_key_heads,
                my_value_heads,
                query_seq,
                my_seq,
                my_valid,
                total_blk.T,
                delta_blk.T,
                scale_factor,
            )
            grad_key_run = grad_key_run + jnp.einsum(
                "hqk,qhd->khd", grad_scores, query_blk, preferred_element_type=jnp.float32
            )
            grad_value_run = grad_value_run + jnp.einsum(
                "hqk,qhd->khd", probs_low, grad_blk, preferred_element_type=jnp.float32
            )
            return (grad_key_run, grad_value_run)

        grad_key_sum, grad_value_sum = blockwise(
            (empty_heads, empty_heads), key_piece_rows, key_step_rows, key_visit_block
        )
        grad_key_flat = grad_key_sum.reshape(own_rows, width)
        grad_value_flat = grad_value_sum.reshape(own_rows, width)
        grad_query_low = (
            (grad_query_sum * scale_factor).reshape(own_rows, width).astype(jnp.bfloat16)
        )
        grad_key_low = (grad_key_flat * scale_factor).astype(jnp.bfloat16)
        grad_value_low = grad_value_flat.astype(jnp.bfloat16)
        terms = (
            jnp.einsum("rd,re->de", token_rows, grad_query_low, preferred_element_type=jnp.float32),
            jnp.einsum("rd,re->de", token_rows, grad_key_low, preferred_element_type=jnp.float32),
            jnp.einsum("rd,re->de", token_rows, grad_value_low, preferred_element_type=jnp.float32),
            jnp.einsum("rd,re->de", attended_low, grad_out_low, preferred_element_type=jnp.float32),
            jnp.einsum("rd,rf->df", mlp_input, grad_up_low, preferred_element_type=jnp.float32),
            jnp.einsum(
                "rf,rd->fd", activated_low, grad_down_low, preferred_element_type=jnp.float32
            ),
            jnp.sum(grad_query_low.astype(jnp.float32), axis=0),
            jnp.sum(grad_value_low.astype(jnp.float32), axis=0),
            jnp.sum(grad_out_low.astype(jnp.float32), axis=0),
            jnp.sum(grad_up_low.astype(jnp.float32), axis=0),
            jnp.sum(grad_down_low.astype(jnp.float32), axis=0),
            grad_gain_a,
            grad_shift_a,
            grad_gain_b,
            grad_shift_b,
        )
        grads = tuple((total_now + fresh for total_now, fresh in zip(grads, terms)))
        grad_rows = (
            grad_first
            + jnp.einsum(
                "re,de->rd", grad_query_low, query_weight, preferred_element_type=jnp.float32
            )
            + jnp.einsum("re,de->rd", grad_key_low, key_weight, preferred_element_type=jnp.float32)
            + jnp.einsum(
                "re,de->rd", grad_value_low, value_weight, preferred_element_type=jnp.float32
            )
        )
        input_grads.append(grad_rows.astype(jnp.bfloat16))
    shards = jax.tree.map(
        lambda part: part.astype(jnp.float32),
        lax.psum_scatter(as_sent(grads), "wsh", scatter_dimension=0, tiled=True),
    )
    summed = jax.tree.map(lambda part: part.astype(jnp.float32), lax.psum(as_sent(shards), "ctx"))
    return (jnp.stack(results)[None], jnp.stack(input_grads)[None]) + tuple(summed)


MESH_IDS = pl.DeviceIdType.MESH
F32 = jnp.float32
BF16 = jnp.bfloat16
HD = 64
VMEM_BYTES = 60 * 1024 * 1024


def flip(index, bit):
    return index + bit * (1 - 2 * lax.rem(lax.div(index, bit), 2))


def bit_of(index, bit):
    return lax.rem(lax.div(index, bit), 2)


def greet(peers):
    barrier = pltpu.get_barrier_semaphore()
    for peer in peers:
        pl.semaphore_signal(barrier, inc=1, device_id=peer, device_id_type=MESH_IDS)
    pl.semaphore_wait(barrier, len(peers))


def send(src, dst, send_sem, recv_sem, peer):
    copy = pltpu.make_async_remote_copy(
        src_ref=src,
        dst_ref=dst,
        send_sem=send_sem,
        recv_sem=recv_sem,
        device_id=peer,
        device_id_type=MESH_IDS,
    )
    copy.start()
    return copy


SEQS = HEADS // BPS


def plane_peers(c, w, count):
    return [(lax.rem(c + step, count), w) for step in range(1, count)]


def pack_three(first, second, third, row, pair, out):
    cols = pl.ds(pair * 128, 128)
    a, b, d = (ref[pl.ds(row, BLK), cols] for ref in (first, second, third))
    half = BLK // 2
    for head in range(2):
        lane = slice(head * HD, head * HD + HD)
        out[2 * pair + head, 0:BLK, :] = jnp.concatenate([a[:, lane], b[:, lane]], axis=1)
        out[2 * pair + head, BLK : BLK + half, :] = jnp.concatenate(
            [d[:half, lane], d[half:, lane]], axis=1
        )


def unpack_fold(block):
    return jnp.concatenate([block[:, :HD], block[:, HD:]], axis=0)


def fold(rows):
    half = rows.shape[0] // 2
    return jnp.concatenate([rows[:half], rows[half:]], axis=1)


def all_bytes(ref, sem, peers):
    view = ref.at[pl.ds(0, peers)]
    return pltpu.make_async_copy(view, view, sem)


def norm_parts(summed):
    row_mean = jnp.mean(summed, axis=-1, keepdims=True)
    centred = summed - row_mean
    row_var = jnp.mean(centred * centred, axis=-1, keepdims=True)
    scale = lax.rsqrt(row_var + EPSILON)
    return centred * scale, scale


def norm_back(grad, unit, scale, gain):
    inner = grad * gain
    mean_one = jnp.mean(inner, axis=-1, keepdims=True)
    mean_two = jnp.mean(inner * unit, axis=-1, keepdims=True)
    return scale * (inner - mean_one - unit * mean_two)


def dot_minor(a, b):
    return lax.dot_general(a, b, (((1,), (1,)), ((), ())), preferred_element_type=F32)


ROW_OUT, ROW_UP, ROW_DOWN, ROW_GAIN_ONE, ROW_SHIFT_ONE, ROW_GAIN_TWO, ROW_SHIFT_TWO = 2, 3, 7, 8, 9, 10, 11


SQUARE, PAIR, ALONE = 8, 4, 2
WAYS = (SQUARE,) * 3 + (SQUARE,) * 4 + (PAIR,) * 3 + (ALONE,) * 2


def weight_plan(shards):
    unit = shards[0].shape[0] * shards[0].shape[1]
    plan = []
    for index, (rows, cols) in enumerate(shard.shape for shard in shards):
        parts = max(1, rows * cols // unit)
        for part in range(parts):
            plan.append((index, part * (rows // parts), rows // parts, WAYS[len(plan)]))
    return plan


def forward_schedule():
    squares = [i for i, way in enumerate(WAYS) if way == SQUARE and i > 2]
    pairs = [i for i, way in enumerate(WAYS) if way == PAIR]
    alone = [i for i, way in enumerate(WAYS) if way == ALONE]
    events = [("second", i) for i in squares + pairs[:1]] + [("att", 0)]
    events += [("third", i) for i in squares] + [("second", i) for i in pairs[1:2]] + [("att", 1)]
    events += [("fourth", i) for i in squares] + [("second", i) for i in pairs[2:3]] + [("att", 2)]
    events += [("fourth", i) for i in pairs[:2]] + [("rows", 0)]
    events += [("fourth", i) for i in pairs[2:] + alone] + [("out", 0)]
    return events + [("hidden", t) for t in range(8)]


FORWARD_SCHEDULE = forward_schedule()


def forward_kernel(heads, plan, n_weights, n_vectors, *refs):
    table_ref, x_ref, cot_ref = refs[:3]
    refs = refs[3:]
    shards, vectors = refs[:n_weights], refs[n_weights : n_weights + n_vectors]
    refs = refs[n_weights + n_vectors :]
    wholes, kept_ref, lse_ref, a_ref = refs[:3], *refs[3:6]
    out_ref, n_ref, g_ref, do_ref, du_ref, dm_ref, dh_ref, da_ref, vec_ref = refs[6:15]
    refs = refs[15:]
    near, refs = refs[:n_weights], refs[n_weights:]
    small, small_in, small_whole, bias, q_ref, k_ref, v_ref = refs[:7]
    slope, n_full, unit, total = refs[7:11]
    refs = refs[11:]
    in_buf = refs[:MB]
    out_buf, back_out, back_in, q_s, k_s, v_s, a_s = refs[MB : 7 + MB]
    (
        w_send,
        w_recv,
        small_sems,
        local_sem,
        stage_sem,
        send_sem,
        recv_sem,
        back_send,
        back_recv,
        keep_sem,
    ) = refs[7 + MB :]
    c, w = lax.axis_index("ctx"), lax.axis_index("wsh")
    o = 1 - w
    by_x, by_y, by_z, by_core = (c, o), (flip(c, 2), w), (flip(c, 4), w), (flip(c, 1), w)
    core, y, z = bit_of(c, 1), bit_of(c, 2), bit_of(c, 4)
    peers = plane_peers(c, w, heads)
    staged = []
    for index, shard in enumerate(shards):
        rows = shard.shape[0]
        spot = pl.ds(pl.multiple_of(w * rows, rows), rows)
        copy = pltpu.make_async_copy(shard, near[index].at[spot], stage_sem.at[index])
        copy.start()
        staged.append(copy)
    line, lanes = 0, small.shape[1]
    for vector in vectors:
        for first in range(0, vector.shape[0], lanes):
            piece = vector[pl.ds(first, lanes)].astype(F32)
            small[line : line + 1, :] = piece.reshape(1, lanes)
            line += 1
    greet(peers + [by_x])
    small_sent = send(small, small_in, small_sems.at[0], small_sems.at[1], by_x)

    def part(chunk, side, piece, start, count):
        tensor, first, rows, way = plan[chunk]
        half = shards[tensor].shape[0]
        at = side * half + first + piece * (rows // way) + start
        return near[tensor].at[pl.ds(pl.multiple_of(at, 8), count)]

    steps = {}

    def sem(kind, chunk):
        return w_send.at[kind, chunk], w_recv.at[kind, chunk]

    def own_piece(way):
        return {SQUARE: core * 4 + z * 2 + y, PAIR: core * 2 + y, ALONE: core}[way]

    for chunk, (tensor, first, rows, way) in enumerate(plan):
        size, mine = rows // way, own_piece(way)
        src = shards[tensor].at[pl.ds(pl.multiple_of(first + mine * size, 8), size)]
        steps[chunk, 0] = send(src, part(chunk, w, mine, 0, size), *sem(0, chunk), by_x)

    def second(chunk):
        _, _, rows, way = plan[chunk]
        steps[chunk, 0].wait_recv()
        ref = part(chunk, o, own_piece(way), 0, rows // way)
        steps[chunk, 1] = send(ref, ref, *sem(1, chunk), by_y)
        if way == SQUARE:
            steps[chunk, 2] = send(ref, ref, *sem(2, chunk), by_z)

    def third(chunk):
        _, _, rows, way = plan[chunk]
        size = rows // way
        steps[chunk, 1].wait_recv()
        steps[chunk, 2].wait_recv()
        ref = part(chunk, o, core * 4 + (1 - z) * 2 + y, 0, size // 2)
        steps[chunk, 3] = send(ref, ref, *sem(3, chunk), by_y)
        ref = part(chunk, o, core * 4 + z * 2 + (1 - y), size // 2, size // 2)
        steps[chunk, 4] = send(ref, ref, *sem(4, chunk), by_z)

    def fourth(chunk):
        _, _, rows, way = plan[chunk]
        for kind in {SQUARE: (3, 4), PAIR: (1,), ALONE: (0,)}[way]:
            steps[chunk, kind].wait_recv()
        ref = part(chunk, o, core * (way // 2), 0, rows // 2)
        steps[chunk, 5] = send(ref, ref, *sem(5, chunk), by_core)

    for index in range(3):
        staged[index].wait()
    for turn in range(5):
        for stage, act in enumerate((second, third, fourth)):
            if 0 <= turn - stage < 3:
                act(turn - stage)
    small_sent.wait()
    small_whole[w] = small[...]
    small_whole[o] = small_in[...]
    for side in range(2):
        for row in range(2):
            bias[row : row + 1, side * lanes : (side + 1) * lanes] = small_whole[
                side, row : row + 1, :
            ]
    width = x_ref.shape[1]
    step = 256
    for index, (weight, out) in enumerate(zip(near, (q_ref, k_ref, v_ref))):
        steps[index, 5].wait_recv()

        def project(turn, carry):
            cols = pl.ds(pl.multiple_of(turn * step, step), step)
            product = jnp.dot(x_ref[...], weight[:, cols], preferred_element_type=F32)
            if index != 1:
                product = product + bias[index // 2 : index // 2 + 1, cols]
            out[:, cols] = product.astype(BF16)
            return carry

        lax.fori_loop(0, width // step, project, 0)
    for m in range(MB):
        for pair in range(heads // 2):
            pack_three(q_ref, k_ref, v_ref, m * BLK, pair, out_buf.at[m])
        for peer in peers:
            send(out_buf.at[m, peer[0]], in_buf[m].at[c], send_sem.at[m], recv_sem.at[m], peer)
        in_buf[m][c] = out_buf[m, c]
    for index in range(3):
        pltpu.make_async_copy(near[index], wholes[index], local_sem.at[index]).start()
    blocks = heads
    span = BPS * BLK

    def attention(m):
        all_bytes(in_buf[m], recv_sem.at[m], heads - 1).wait()
        pltpu.make_async_copy(in_buf[m], kept_ref.at[m], keep_sem.at[m]).start()
        for b in range(blocks):
            got = in_buf[m][table_ref[m, SEQS + blocks + b]]
            q_s[b * BLK : (b + 1) * BLK, :] = got[:BLK, :HD]
            k_s[b * BLK : (b + 1) * BLK, :] = got[:BLK, HD:]
            v_s[b * BLK : (b + 1) * BLK, :] = unpack_fold(got[BLK:])

        def one_sequence(s, carry):
            rows = pl.ds(pl.multiple_of(s * span, span), span)
            scores = lax.dot_general(
                k_s[rows, :], q_s[rows, :], (((1,), (1,)), ((), ())), preferred_element_type=F32
            ) * (1.0 / math.sqrt(HD))
            place = lax.broadcasted_iota(jnp.int32, scores.shape, 0)
            scores = jnp.where(place < table_ref[m, s], scores, NEG_FILL)
            top = jnp.max(scores, axis=0, keepdims=True)
            weights = jnp.exp(scores - top)
            summed = jnp.sum(weights, axis=0, keepdims=True)
            out_t = lax.dot_general(
                v_s[rows, :],
                weights.astype(BF16),
                (((0,), (0,)), ((), ())),
                preferred_element_type=F32,
            )
            a_s[pl.ds(s * BPS, BPS)] = (out_t / summed).T.reshape(BPS, BLK, HD)
            lse_ref[pl.ds(m * (blocks // BPS) + s, 1), :] = top + jnp.log(summed)
            return carry

        lax.fori_loop(0, blocks // BPS, one_sequence, 0)
        for t in range(blocks):
            back_out[m, t] = fold(a_s[table_ref[m, SEQS + t]]).astype(BF16)
        for peer in peers:
            send(
                back_out.at[m, peer[0]], back_in.at[m, c], back_send.at[m], back_recv.at[m], peer
            )
        back_in[m, c] = back_out[m, c]

    def come_back(_):
        for m in range(MB):
            all_bytes(back_in.at[m], back_recv.at[m], heads - 1).wait()
            for pair in range(heads // 2):
                a_ref[m * BLK : (m + 1) * BLK, pair * 128 : (pair + 1) * 128] = jnp.concatenate(
                    [unpack_fold(back_in[m, 2 * pair]), unpack_fold(back_in[m, 2 * pair + 1])],
                    axis=1,
                )

    def line_of(row):
        return jnp.concatenate(
            [small_whole[0, row : row + 1, :], small_whole[1, row : row + 1, :]], axis=1
        )

    def keep(row, values):
        summed = jnp.sum(values, axis=0, keepdims=True)
        for side in range(2):
            vec_ref[side, row : row + 1, :] = summed[:, side * lanes : (side + 1) * lanes]

    out_w, up_w, down_w = near[3:]
    chunks_of = {t: [i for i, item in enumerate(plan) if item[0] == t] for t in range(n_weights)}

    def arrived(tensor, chunks):
        for chunk in chunks:
            steps[chunk, 5].wait_recv()

    def out_project(_):
        staged[3].wait()
        arrived(3, chunks_of[3])
        h_one = x_ref[...].astype(F32) + (
            jnp.dot(a_ref[...], out_w[...], preferred_element_type=F32) + line_of(ROW_OUT)
        )
        unit_one, scale_one = norm_parts(h_one)
        unit[...] = unit_one
        n_one = unit_one * line_of(ROW_GAIN_ONE) + line_of(ROW_SHIFT_ONE)
        n_full[...] = n_one
        n_ref[...] = n_one.astype(BF16)
        total[...] = jnp.zeros_like(total)
        kept_scale.append(scale_one)

    kept_scale = []
    hidden = g_ref.shape[1]
    hidden_steps = hidden // lanes
    per_half = hidden_steps // 2

    def hidden_at(turn):
        j = lax.rem(w * per_half + turn, hidden_steps)
        cols = pl.ds(pl.multiple_of(j * lanes, lanes), lanes)
        return cols, lax.div(j, per_half), pl.ds(ROW_UP + lax.rem(j, per_half), 1)

    def hidden_up(turn):
        if turn == 0:
            staged[4].wait()
            arrived(4, chunks_of[4])
            staged[5].wait()
        elif turn >= per_half:
            share = len(chunks_of[5]) // per_half
            first = (turn - per_half) * share
            arrived(5, chunks_of[5][first : first + share])
        cols, side, row = hidden_at(turn)
        u = jnp.dot(n_ref[...], up_w[:, cols], preferred_element_type=F32) + small_whole[side, row, :]
        below = 0.5 * (1.0 + lax.erf(u * math.sqrt(0.5)))
        slope[:, cols] = below + u * jnp.exp(-0.5 * u * u) * (1.0 / math.sqrt(2.0 * math.pi))
        g = (u * below).astype(BF16)
        g_ref[:, cols] = g
        total[...] += jnp.dot(g, down_w[cols, :], preferred_element_type=F32)

    acts = {
        "second": second,
        "third": third,
        "fourth": fourth,
        "att": attention,
        "rows": come_back,
        "out": out_project,
        "hidden": hidden_up,
    }
    for name, value in FORWARD_SCHEDULE:
        acts[name](value)

    h_two = n_full[...] + (total[...] + line_of(ROW_DOWN))
    unit_two, scale_two = norm_parts(h_two)
    out_ref[...] = (unit_two * line_of(ROW_GAIN_TWO) + line_of(ROW_SHIFT_TWO)).astype(BF16)
    cot = cot_ref[...].astype(F32)
    keep(ROW_GAIN_TWO, cot * unit_two)
    keep(ROW_SHIFT_TWO, cot)
    dh_two = norm_back(cot, unit_two, scale_two, line_of(ROW_GAIN_TWO))
    dm = dh_two.astype(BF16)
    dm_ref[...] = dm
    keep(ROW_DOWN, dm.astype(F32))
    total[...] = dh_two
    for turn in range(hidden_steps):
        cols, side, row = hidden_at(turn)
        du = (slope[:, cols] * dot_minor(dm_ref[...], down_w[cols, :])).astype(BF16)
        du_ref[:, cols] = du
        vec_ref[side, row, :] = jnp.sum(du.astype(F32), axis=0, keepdims=True)
        total[...] += dot_minor(du, up_w[:, cols])
    dn = total[...]
    keep(ROW_GAIN_ONE, dn * unit[...])
    keep(ROW_SHIFT_ONE, dn)
    dh_one = norm_back(dn, unit[...], kept_scale[0], line_of(ROW_GAIN_ONE))
    dh_ref[...] = dh_one
    do = dh_one.astype(BF16)
    do_ref[...] = do
    keep(ROW_OUT, do.astype(F32))
    da_ref[...] = dot_minor(do, out_w[...]).astype(BF16)
    for side in range(2):
        vec_ref[side, 0:ROW_OUT, :] = jnp.zeros((ROW_OUT, lanes), F32)

    for m in range(MB):
        all_bytes(out_buf.at[m], send_sem.at[m], heads - 1).wait()
        all_bytes(back_out.at[m], back_send.at[m], heads - 1).wait()
        pltpu.make_async_copy(in_buf[m], kept_ref.at[m], keep_sem.at[m]).wait()
    for flight in steps.values():
        flight.wait_send()
    for index in range(3):
        pltpu.make_async_copy(near[index], wholes[index], local_sem.at[index]).wait()


def forward(table, x, cot, shards, vectors, heads):
    plan = weight_plan(shards)
    count = len(shards)
    anywhere, vmem = pl.BlockSpec(memory_space=pl.ANY), pl.BlockSpec(memory_space=pltpu.VMEM)
    smem = pl.BlockSpec(memory_space=pltpu.SMEM)
    rows, width = x.shape
    hidden = shards[4].shape[1]
    pack_rows = BLK + BLK // 2
    span = BPS * BLK
    lanes = min(item.shape[0] for item in vectors)
    lines = sum(item.shape[0] for item in vectors) // lanes
    whole = lambda s: (2 * s.shape[0],) + s.shape[1:]
    low = lambda cols: jax.ShapeDtypeStruct((rows, cols), BF16)
    full = lambda cols: pltpu.VMEM((rows, cols), F32)
    sems = lambda *dims: pltpu.SemaphoreType.DMA(dims)
    return pl.pallas_call(
        functools.partial(forward_kernel, heads, plan, count, len(vectors)),
        out_shape=[jax.ShapeDtypeStruct(whole(s), s.dtype) for s in shards[:3]]
        + [
            jax.ShapeDtypeStruct((MB, heads, pack_rows, 128), BF16),
            jax.ShapeDtypeStruct((8, span), F32),
            low(width),
            low(width),
            low(width),
            low(hidden),
            low(width),
            low(hidden),
            low(width),
            jax.ShapeDtypeStruct((rows, width), F32),
            low(width),
            jax.ShapeDtypeStruct((2, lines, lanes), F32),
        ],
        in_specs=[smem, vmem, vmem] + [anywhere] * count + [vmem] * len(vectors),
        out_specs=[anywhere] * 4 + [vmem] * 11,
        scratch_shapes=[pltpu.VMEM(whole(s), s.dtype) for s in shards]
        + [pltpu.VMEM((lines, lanes), F32)] * 2
        + [pltpu.VMEM((2, lines, lanes), F32), pltpu.VMEM((2, width), F32)]
        + [pltpu.VMEM((rows, width), BF16)] * 3
        + [full(hidden), full(width), full(width), full(width)]
        + [pltpu.VMEM((heads, pack_rows, 128), BF16)] * MB
        + [
            pltpu.VMEM((MB, heads, pack_rows, 128), BF16),
            pltpu.VMEM((MB, heads, BLK // 2, 128), BF16),
            pltpu.VMEM((MB, heads, BLK // 2, 128), BF16),
            pltpu.VMEM((heads * BLK, HD), BF16),
            pltpu.VMEM((heads * BLK, HD), BF16),
            pltpu.VMEM((heads * BLK, HD), BF16),
            pltpu.VMEM((heads, BLK, HD), F32),
        ]
        + [sems(6, len(plan)), sems(6, len(plan)), sems(2), sems(3), sems(count)]
        + [sems(MB)] * 5,
        compiler_params=pltpu.CompilerParams(
            collective_id=1, has_side_effects=True, vmem_limit_bytes=VMEM_BYTES
        ),
        name="forward",
    )(table, x, cot, *shards, *vectors)


ORDERS = (
    ("yxzZ", "xyzZ", "zxyZ", "yxzZ"),
    ("xzyZ", "zyxZ", "xyzZ", "yzxZ"),
    ("xyzZ", "zxyZ", "yxzZ", "xyzZ"),
)
PIECES = len(ORDERS[0])
KEYS = tuple((part, piece) for part in range(3) for piece in range(PIECES))


def default_schedule():
    early = [(part, piece) for piece in range(PIECES) for part in (1, 2)]
    late = [(0, piece) for piece in range(PIECES)]
    events = ["up", 0, "down", 1, 2] + early + ["back", "qkv", "rows"]
    for step in range(6):
        events += early + ["vec"] + late
    return events + late


def landing_shapes(order, shape):
    shards, sides, shapes = 8, 2, []
    for name in order:
        if name == "x":
            sides = 1
        else:
            shards //= 2
        shapes.append((sides, shards, shape[2] // PIECES, shape[3]))
    return shapes


def dot_t(a, b):
    return lax.dot_general(a, b, (((0,), (0,)), ((), ())), preferred_element_type=F32)


def lanes_at(first, size):
    return pl.ds(pl.multiple_of(first, 128), size)


def backward_kernel(heads, *refs):
    table_ref, da_ref, kept_ref, lse_ref = refs[:4]
    x_ref, a_ref, n_ref, g_ref, do_ref, du_ref, dm_ref, vec_ref, dh_ref = refs[4:13]
    weights = refs[13:16]
    rows_out, o_a, o_b, o_c, vec_out = refs[16:21]
    refs = refs[21:]
    in_buf = refs[:MB]
    out_buf, back_out, back_in, q_s, k_s, v_s, a_s, dq_s, dk_s, dv_s = refs[MB : MB + 10]
    refs = refs[MB + 10 :]
    dq_ref, dk_ref, dv_ref, m_x, m_a, m_n, m_dm, m_do, m_du, m_g, m_dqkv = refs[:11]
    near, (vec_s, v_recv, v_sum, s_a, s_b, s_c) = refs[11:14], refs[14:20]
    refs = refs[20:]
    r_bufs = {key: refs[4 * i : 4 * i + 4] for i, key in enumerate(KEYS)}
    (
        send_sem,
        recv_sem,
        back_send,
        back_recv,
        mate_send,
        mate_recv,
        near_sem,
        rs_send,
        rs_recv,
        ag_send,
        ag_recv,
        own_sem,
        v_send_sem,
        v_recv_sem,
    ) = refs[4 * len(KEYS) :]
    c, x = lax.axis_index("ctx"), lax.axis_index("wsh")
    core, y, z, zz = bit_of(c, 1), bit_of(c, 2), bit_of(c, 4), bit_of(c, 8)
    by_core = (flip(c, 1), x)
    by = {"x": (c, 1 - x), "y": (flip(c, 2), x), "z": (flip(c, 4), x), "Z": (flip(c, 8), x)}
    bits = {"y": y, "z": z, "Z": zz}
    peers = plane_peers(c, x, heads)
    blocks, span = heads, BPS * BLK
    width, hidden = da_ref.shape[1], g_ref.shape[1]
    for index, weight in enumerate(weights):
        pltpu.make_async_copy(weight, near[index], near_sem.at[index]).start()
    greet(peers + [by["x"]])

    for m in range(MB):
        row = slice(m * BLK, (m + 1) * BLK)
        for pair in range(heads // 2):
            both = da_ref[row, pair * 128 : (pair + 1) * 128]
            for head in range(2):
                out_buf[m, 2 * pair + head] = fold(both[:, head * HD : (head + 1) * HD])
        for peer in peers:
            send(out_buf.at[m, peer[0]], in_buf[m].at[c], send_sem.at[m], recv_sem.at[m], peer)
        in_buf[m][c] = out_buf[m, c]

    shared = {}

    def share(name, src, dst):
        index = len(shared)
        shared[name] = send(src, dst, mate_send.at[index], mate_recv.at[index], by_core)

    other = 1 - core
    share("n", n_ref, m_n)
    share("du", du_ref.at[:, lanes_at(other * (hidden // 2), hidden // 2)], m_du)
    for half in range(2):
        share(
            "g" + str(half),
            g_ref.at[:, lanes_at(half * (hidden // 2) + other * (hidden // 4), hidden // 4)],
            m_g.at[:, pl.ds(half * (hidden // 4), hidden // 4)],
        )
    share("dm", dm_ref, m_dm)
    share("a", a_ref, m_a)
    share("do", do_ref.at[:, lanes_at(other * (width // 2), width // 2)], m_do)
    share("x", x_ref, m_x)

    sums, outs = (s_a, s_b, s_c), (o_a, o_b, o_c)
    wide = 256

    def tile(pairs, out, first, count):
        def body(turn, carry):
            at = turn * wide
            total = sum(dot_t(lhs[...], rhs[:, lanes_at(col + at, wide)]) for lhs, rhs, col in pairs)
            cols = lanes_at(first + at, wide)
            out[..., cols] = total.astype(BF16).reshape(out.shape[:-1] + (wide,))
            return carry

        lax.fori_loop(0, count, body, 0)

    def grads_up():
        shared["n"].wait_recv()
        shared["du"].wait_recv()
        half = hidden // 2
        tile(((n_ref, du_ref, core * half), (m_n, m_du, 0)), s_b, 0, half // wide)

    def grads_down():
        for name in ("g0", "g1", "dm"):
            shared[name].wait_recv()
        quarter = hidden // 4
        for half in range(2):
            mine = g_ref.at[:, lanes_at(half * 2 * quarter + core * quarter, quarter)]
            others = m_g.at[:, pl.ds(half * quarter, quarter)]
            tile(((mine, dm_ref, 0), (others, m_dm, 0)), s_c.at[half], 0, width // wide)

    def grads_qkv():
        half = width // 2
        for name in ("a", "do", "x", "dq", "dk", "dv"):
            shared[name].wait_recv()
        tile(((a_ref, do_ref, core * half), (m_a, m_do, 0)), s_a, 3 * half, half // wide)
        for index, ref in enumerate((dq_ref, dk_ref, dv_ref)):
            pairs = ((x_ref, ref, core * half), (m_x, m_dqkv, index * half))
            tile(pairs, s_a, index * half, half // wide)

    def attention(m):
        all_bytes(in_buf[m], recv_sem.at[m], heads - 1).wait()
        for b in range(blocks):
            slot = table_ref[m, SEQS + blocks + b]
            got = kept_ref[m, slot]
            rows = slice(b * BLK, (b + 1) * BLK)
            q_s[rows, :] = got[:BLK, :HD]
            k_s[rows, :] = got[:BLK, HD:]
            v_s[rows, :] = unpack_fold(got[BLK:])
            a_s[rows, :] = unpack_fold(in_buf[m][slot])

        def one_sequence(s, carry):
            rows = pl.ds(pl.multiple_of(s * span, span), span)
            qq, kk, vv, dd = q_s[rows, :], k_s[rows, :], v_s[rows, :], a_s[rows, :]
            scale = 1.0 / math.sqrt(HD)
            minor = (((1,), (1,)), ((), ()))
            scores = lax.dot_general(kk, qq, minor, preferred_element_type=F32) * scale
            spot = lax.broadcasted_iota(jnp.int32, scores.shape, 0)
            total = lse_ref[pl.ds(m * (blocks // BPS) + s, 1), :]
            probs = jnp.exp(jnp.where(spot < table_ref[m, s], scores - total, NEG_FILL))
            dp = lax.dot_general(vv, dd, minor, preferred_element_type=F32)
            both = probs * dp
            delta = jnp.sum(both, axis=0, keepdims=True)
            ds = (both - probs * delta).astype(BF16)
            here, split = pl.ds(s * BPS, BPS), (BPS, BLK, HD)
            dv = jnp.dot(probs.astype(BF16), dd, preferred_element_type=F32)
            dv_s[here] = dv.reshape(split)
            dk_s[here] = (jnp.dot(ds, qq, preferred_element_type=F32) * scale).reshape(split)
            dq_s[here] = (dot_t(kk, ds).T * scale).reshape(split)
            return carry

        lax.fori_loop(0, blocks // BPS, one_sequence, 0)
        for t in range(blocks):
            at = table_ref[m, SEQS + t]
            back_out[m, t, 0:BLK, :] = jnp.concatenate([dq_s[at], dk_s[at]], axis=1).astype(BF16)
            back_out[m, t, BLK:, :] = fold(dv_s[at]).astype(BF16)
        for peer in peers:
            send(
                back_out.at[m, peer[0]], back_in.at[m, c], back_send.at[m], back_recv.at[m], peer
            )
        back_in[m, c] = back_out[m, c]

    vec_peers = (by["x"], by["y"], by["z"], by["Z"], by_core)
    vec_steps = []

    def vec_send(src):
        step = len(vec_steps)
        vec_steps.append(
            send(
                src, v_recv.at[step], v_send_sem.at[step], v_recv_sem.at[step], vec_peers[step]
            )
        )

    def vec_next():
        step = len(vec_steps) - 1
        vec_steps[step].wait_recv()
        before = vec_s[x] if step == 0 else v_sum[step - 1]
        v_sum[step] = before + v_recv[step]
        if step + 1 < len(vec_peers):
            vec_send(v_sum.at[step])

    def come_back():
        for m in range(MB):
            all_bytes(back_in.at[m], back_recv.at[m], heads - 1).wait()
            row = slice(m * BLK, (m + 1) * BLK)
            for pair in range(heads // 2):
                lanes = slice(pair * 128, (pair + 1) * 128)
                one, two = back_in[m, 2 * pair], back_in[m, 2 * pair + 1]
                dq_ref[row, lanes] = jnp.concatenate([one[:BLK, :HD], two[:BLK, :HD]], axis=1)
                dk_ref[row, lanes] = jnp.concatenate([one[:BLK, HD:], two[:BLK, HD:]], axis=1)
                dv_ref[row, lanes] = jnp.concatenate(
                    [unpack_fold(one[BLK:]), unpack_fold(two[BLK:])], axis=1
                )
        half = width // 2
        for index, (name, ref) in enumerate((("dq", dq_ref), ("dk", dk_ref), ("dv", dv_ref))):
            share(
                name,
                ref.at[:, lanes_at(other * half, half)],
                m_dqkv.at[:, pl.ds(index * half, half)],
            )
        vec_s[...] = vec_ref[...]
        lanes = vec_s.shape[2]
        for index, ref in enumerate((dq_ref, dv_ref)):
            total = jnp.sum(ref[...].astype(F32), axis=0, keepdims=True)
            for side in range(2):
                vec_s[side, index : index + 1, :] = total[:, side * lanes : (side + 1) * lanes]
        vec_send(vec_s.at[1 - x])

    def grad_rows():
        total = dh_ref[...]
        for index, ref in enumerate((dq_ref, dk_ref, dv_ref)):
            pltpu.make_async_copy(weights[index], near[index], near_sem.at[index]).wait()
            total = total + lax.dot_general(
                ref[...], near[index][...], (((1,), (1,)), ((), ())), preferred_element_type=F32
            )
        rows_out[...] = total.astype(BF16)

    plans, gathers = {}, {}
    for key in KEYS:
        first, count, sided = 0, 8, False
        plans[key], back = [], []
        for name in ORDERS[key[0]][key[1]]:
            if name == "x":
                plans[key].append((by["x"], 1 - x, x, first, first, count))
                sided = True
                continue
            count //= 2
            out, keep = first + (1 - bits[name]) * count, first + bits[name] * count
            side = x if sided else None
            plans[key].append((by[name], side, side, out, keep, count))
            back.append((by[name], keep, out, count))
            first = keep
        gathers[key] = back[::-1]
    flights, spread, owns, state = {}, {}, {}, {}

    def piece_rows(key):
        rows = sums[key[0]].shape[2] // PIECES
        return pl.ds(key[1] * rows, rows)

    def reduce_send(key, step):
        peer, side, _, first, _, count = plans[key][step]
        dst = r_bufs[key][step]
        if side is None:
            src = sums[key[0]].at[:, pl.ds(first, count), piece_rows(key)]
        else:
            src, dst = sums[key[0]].at[side, pl.ds(first, count), piece_rows(key)], dst.at[0]
        sems = rs_send.at[key[0], key[1], step], rs_recv.at[key[0], key[1], step]
        flights[key, step] = send(src, dst, *sems, peer)
        state[key] = step

    def reduce_add(key, step):
        _, _, side, _, first, count = plans[key][step]
        flights[key, step].wait_recv()
        total, fresh, rows = sums[key[0]], r_bufs[key][step], piece_rows(key)
        sides = ((0, 0), (1, 1)) if side is None else ((side, 0),)
        for here, there in sides:

            def body(index, carry):
                spot = first + index
                total[here, spot, rows] = (
                    total[here, spot, rows].astype(F32) + fresh[there, index].astype(F32)
                ).astype(BF16)
                return carry

            lax.fori_loop(0, count, body, 0)

    def spread_send(key, kind, src, dst, peer):
        sems = ag_send.at[key[0], key[1], kind], ag_recv.at[key[0], key[1], kind]
        spread[key, kind] = send(src, dst, *sems, peer)

    def advance(key):
        step = state[key]
        out, rows = outs[key[0]], piece_rows(key)
        if step < 4:
            reduce_add(key, step)
            if step < 3:
                reduce_send(key, step + 1)
                return
            peer, first, _, _ = gathers[key][0]
            src = sums[key[0]].at[x, pl.ds(first, 1), rows]
            dst = out.at[core, pl.ds(first, 1), rows]
            owns[key] = pltpu.make_async_copy(src, dst, own_sem.at[key[0], key[1]])
            owns[key].start()
            spread_send(key, 0, src, dst, peer)
            spread_send(key, 3, src, dst, by_core)
        else:
            turn = step - 3
            spread[key, turn - 1].wait_recv()
            if turn == 1:
                owns[key].wait()
            if turn < 3:
                peer, first, _, count = gathers[key][turn]
                ref = out.at[core, pl.ds(first, count), rows]
                spread_send(key, turn, ref, ref, peer)
            _, _, first, count = gathers[key][turn - 1]
            ref = out.at[core, pl.ds(first, count), rows]
            spread_send(key, 3 + turn, ref, ref, by_core)
        state[key] = step + 1

    actions = {
        "up": (grads_up, 1),
        "down": (grads_down, 2),
        "qkv": (grads_qkv, 0),
        "back": (come_back, None),
        "rows": (grad_rows, None),
        "vec": (vec_next, None),
    }
    for event in SCHEDULE:
        if isinstance(event, tuple):
            advance(event)
        elif isinstance(event, int):
            attention(event)
        else:
            action, part = actions[event]
            if event == "vec" and len(vec_steps) == len(vec_peers) and "vec" in state:
                continue
            if event == "vec" and len(vec_steps) == len(vec_peers):
                state["vec"] = True
            action()
            if part is not None:
                for piece in range(PIECES):
                    reduce_send((part, piece), 0)
    vec_out[...] = v_sum[len(vec_peers) - 1]
    for m in range(MB):
        all_bytes(out_buf.at[m], send_sem.at[m], heads - 1).wait()
        all_bytes(back_out.at[m], back_send.at[m], heads - 1).wait()
    for flight in shared.values():
        flight.wait_send()
    for flight in vec_steps:
        flight.wait_send()
    for flight in flights.values():
        flight.wait_send()
    for (_, kind), flight in spread.items():
        if kind >= 3:
            flight.wait_recv()
        flight.wait_send()


SCHEDULE = (
    "down", 0, "up", 1, 2, (2, 0), (1, 3), (1, 1), (2, 2), (1, 0), (2, 0), (1, 3), (1, 2),
    "back", (2, 2), (2, 0), (2, 3), (1, 2), (1, 3), "qkv", (1, 3), (2, 3), (1, 2), (1, 3),
    (1, 1), (2, 2), (2, 0), (1, 1), "vec", (2, 1), (2, 2), (2, 0), (2, 1), (0, 1), (1, 3),
    (2, 2), (1, 2), (2, 3), (0, 0), (2, 1), (1, 0), "vec", (2, 3), (0, 3), (0, 0), (2, 2),
    (2, 1), (0, 3), (2, 0), (1, 3), (1, 1), (2, 1), (0, 2), "vec", (1, 2), (2, 3), (1, 0),
    (1, 1), (0, 1), (0, 3), (0, 0), (2, 1), (1, 0), (2, 0), (2, 2), (0, 2), "vec", (0, 3),
    (0, 1), (1, 2), (0, 3), (0, 2), (2, 3), "rows", (0, 0), (1, 0), (1, 1), (0, 2), (0, 0),
    (0, 3), (0, 1), "vec", (0, 2), (0, 1), (1, 0), (0, 0), (1, 2), (0, 1), (0, 2), (0, 3),
    (0, 0), (0, 1), (1, 1), (2, 3), (1, 0), (2, 1), (0, 2),
)


def backward(table, da, kept, lse, x, a, n1, g, do, du, dm, vec, dh, weights, heads):
    vmem, smem = pl.BlockSpec(memory_space=pltpu.VMEM), pl.BlockSpec(memory_space=pltpu.SMEM)
    anywhere = pl.BlockSpec(memory_space=pl.ANY)
    rows, width = da.shape
    hidden = g.shape[1]
    pack_rows = BLK + BLK // 2
    low = lambda *dims: pltpu.VMEM(dims, BF16)
    a_shape, b_shape = (2, 8, width // 16, 2 * width), (2, 8, width // 16, hidden // 2)
    c_shape = (2, 8, hidden // 32, width)
    scratch = [low(heads, BLK // 2, 128)] * MB
    scratch += [low(MB, heads, BLK // 2, 128)]
    scratch += [low(MB, heads, pack_rows, 128)] * 2
    scratch += [low(heads * BLK, HD)] * 4
    scratch += [pltpu.VMEM((heads, BLK, HD), F32)] * 3
    scratch += [low(rows, width)] * 7
    scratch += [low(rows, width // 2), low(rows, hidden // 2), low(rows, hidden // 2)]
    scratch += [low(rows, 3 * width // 2)]
    scratch += [low(*item.shape) for item in weights]
    scratch += [pltpu.VMEM(vec.shape, F32)] + [pltpu.VMEM((5,) + vec.shape[1:], F32)] * 2
    scratch += [low(*shape) for shape in (a_shape, b_shape, c_shape)]
    for key in KEYS:
        shape = (a_shape, b_shape, c_shape)[key[0]]
        scratch += [low(*item) for item in landing_shapes(ORDERS[key[0]][key[1]], shape)]
    sems = lambda *dims: pltpu.SemaphoreType.DMA(dims)
    scratch += [sems(MB)] * 4 + [sems(11)] * 2 + [sems(3)]
    scratch += [sems(3, PIECES, 4)] * 2 + [sems(3, PIECES, 7)] * 2 + [sems(3, PIECES)]
    scratch += [sems(5)] * 2
    return pl.pallas_call(
        functools.partial(backward_kernel, heads),
        out_shape=[
            jax.ShapeDtypeStruct((rows, width), BF16),
            jax.ShapeDtypeStruct(a_shape, BF16),
            jax.ShapeDtypeStruct(b_shape, BF16),
            jax.ShapeDtypeStruct(c_shape, BF16),
            jax.ShapeDtypeStruct(vec.shape[1:], F32),
        ],
        in_specs=[smem] + [vmem] * 12 + [anywhere] * 3,
        out_specs=[vmem] + [anywhere] * 3 + [vmem],
        scratch_shapes=scratch,
        compiler_params=pltpu.CompilerParams(
            collective_id=2, has_side_effects=True, vmem_limit_bytes=VMEM_BYTES
        ),
        name="backward",
    )(table, da, kept, lse, x, a, n1, g, do, du, dm, vec, dh, *weights)


def widen_kernel(a_ref, b_ref, c_ref, vec_ref, *outs):
    @pl.when(pl.program_id(0) == 0)
    def _():
        line, lanes = 0, vec_ref.shape[1]
        for out in outs[6:]:
            for first in range(0, out.shape[0], lanes):
                out[pl.ds(first, lanes)] = vec_ref[line, :]
                line += 1

    half = outs[0].shape[1] // 2
    for index, out in enumerate(outs[:4]):
        for core in range(2):
            out[:, core * half : (core + 1) * half] = a_ref[
                core, 0, :, index * half : (index + 1) * half
            ].astype(F32)
    up, down = outs[4:6]
    half = up.shape[1] // 2
    for core in range(2):
        up[:, core * half : (core + 1) * half] = b_ref[core, 0].astype(F32)
        down[core, 0] = c_ref[core, 0].astype(F32)


def widen(o_a, o_b, o_c, vec, sizes):
    shards = o_a.shape[1]
    block = lambda item: pl.BlockSpec((2, 1) + item.shape[2:], lambda i: (0, i, 0, 0))
    rows = o_a.shape[2]
    square = (shards * rows, o_a.shape[3] // 2)
    wide = (shards * rows, 2 * o_b.shape[3])
    return pl.pallas_call(
        widen_kernel,
        grid=(shards,),
        out_shape=[jax.ShapeDtypeStruct(square, F32)] * 4
        + [jax.ShapeDtypeStruct(wide, F32), jax.ShapeDtypeStruct(o_c.shape, F32)]
        + [jax.ShapeDtypeStruct((size,), F32) for size in sizes],
        in_specs=[block(o_a), block(o_b), block(o_c), pl.BlockSpec(vec.shape, lambda i: (0, 0))],
        out_specs=[pl.BlockSpec((rows, square[1]), lambda i: (i, 0))] * 4
        + [pl.BlockSpec((rows, wide[1]), lambda i: (i, 0)), block(o_c)]
        + [pl.BlockSpec((size,), lambda i: (0,)) for size in sizes],
        compiler_params=pltpu.CompilerParams(vmem_limit_bytes=VMEM_BYTES),
        name="widen",
    )(o_a, o_b, o_c, vec)


def per_device_heads(tokens, cotangent, lengths, dealing, *params):
    rows_in = tokens.shape[2]
    width = tokens.shape[3]
    rows = MB * rows_in
    weights, vectors = params[:6], params[6:]
    sizes = [item.shape[0] for item in vectors]
    x = tokens.reshape(rows, width)
    blocks = jnp.arange(HEADS, dtype=jnp.int32)
    at_block = dealing[0][:, :, None] == blocks[None, None, :]
    slot_of = jnp.sum(jnp.where(at_block, blocks[None, :, None], 0), axis=1)
    table = jnp.concatenate([lengths[0], dealing[0], slot_of], axis=1)
    query_w, key_w, value_w, kept, lse, a, output, n_low, g, do, du, dm, dh_one, da, vec = forward(
        table, x, cotangent.reshape(rows, width), weights, vectors, HEADS
    )
    grad_tokens, o_a, o_b, o_c, vec_sum = backward(
        table,
        da,
        kept,
        lse,
        x,
        a,
        n_low,
        g,
        do,
        du,
        dm,
        vec,
        dh_one,
        (query_w, key_w, value_w),
        HEADS,
    )
    grads = list(widen(o_a, o_b, o_c, vec_sum, sizes))
    grads[5] = grads[5].reshape(-1, width)
    shape = (1, MB, rows_in, width)
    return (
        (output.reshape(shape), grad_tokens.reshape(shape))
        + tuple(grads)
    )


def solution(mesh):
    placed = (
        P("wsh", None, "ctx", None),
        P("wsh", None, "ctx", None),
        P("wsh", None, None),
        P("wsh", None, None),
        P("wsh", None),
        P("wsh", None),
        P("wsh", None),
        P("wsh", None),
        P("wsh", None),
        P("wsh", None),
        P("wsh"),
        P("wsh"),
        P("wsh"),
        P("wsh"),
        P("wsh"),
        P("wsh"),
        P("wsh"),
        P("wsh"),
        P("wsh"),
    )
    by_heads = mesh.shape["ctx"] == HEADS and mesh.shape["wsh"] == 2
    return jax.shard_map(
        per_device_heads if by_heads else per_device,
        mesh=mesh,
        in_specs=placed,
        out_specs=(
            P("wsh", None, "ctx", None),
            P("wsh", None, "ctx", None),
            P("wsh", None),
            P("wsh", None),
            P("wsh", None),
            P("wsh", None),
            P("wsh", None),
            P("wsh", None),
            P("wsh"),
            P("wsh"),
            P("wsh"),
            P("wsh"),
            P("wsh"),
            P("wsh"),
            P("wsh"),
            P("wsh"),
            P("wsh"),
        ),
        check_vma=False,
    )
```

```python
import functools
import math

import jax
import jax.numpy as jnp
from jax import lax
from jax.experimental import pallas as pl
from jax.experimental.pallas import tpu as pltpu
from jax.sharding import PartitionSpec as P

HEADS = 16
BPS = 8
MB = 3
BLK = 64


EPSILON = 1e-12
NEG_FILL = -1e30


def as_sent(x):
    return jax.tree.map(lambda a: a.astype(jnp.bfloat16) if a.dtype == jnp.float32 else a, x)


def layer_norm(summed, gain_vec, shift_vec):
    row_mean = jnp.mean(summed, axis=-1, keepdims=True)
    centred = summed - row_mean
    row_var = jnp.mean(centred * centred, axis=-1, keepdims=True)
    return centred * lax.rsqrt(row_var + EPSILON) * gain_vec + shift_vec


def gelu_exact(values):
    return jax.nn.gelu(values, approximate=False)


def row_labels(dealt_order, seq_lengths):
    blocks_of_rows = jnp.repeat(dealt_order, BLK)
    within = jnp.tile(jnp.arange(BLK, dtype=jnp.int32), dealt_order.shape[0])
    seq_ids = blocks_of_rows // BPS
    places = blocks_of_rows % BPS * BLK + within
    numbers = jnp.arange(seq_lengths.shape[0], dtype=jnp.int32)
    seq_bound = jnp.sum(
        jnp.where(seq_ids[:, None] == numbers[None, :], seq_lengths[None, :], 0), axis=1
    )
    return (seq_ids, places < seq_bound)


def blockwise(carried, total_rows, step_rows, visit_block):
    return lax.fori_loop(
        0,
        total_rows // step_rows,
        lambda turn_index, running: visit_block(running, turn_index * step_rows),
        carried,
    )


def masked_scores(query_blk, key_blk, query_seq, key_seq, key_valid, scale_factor):
    allowed = (query_seq[:, None] == key_seq[None, :]) & key_valid[None, :]
    scores = (
        jnp.einsum("qhd,khd->hqk", query_blk, key_blk, preferred_element_type=jnp.float32)
        * scale_factor
    )
    return (jnp.where(allowed[None], scores, NEG_FILL), allowed[None].astype(jnp.float32))


def attention_grads(
    query_blk,
    grad_blk,
    key_blk,
    value_blk,
    query_seq,
    key_seq,
    key_valid,
    row_total,
    row_delta,
    scale_factor,
):
    scores, allowed = masked_scores(query_blk, key_blk, query_seq, key_seq, key_valid, scale_factor)
    probs = jnp.exp(scores - row_total[:, :, None]) * allowed
    grad_probs = jnp.einsum("qhd,khd->hqk", grad_blk, value_blk, preferred_element_type=jnp.float32)
    grad_scores = (probs * (grad_probs - row_delta[:, :, None])).astype(jnp.bfloat16)
    return (probs.astype(jnp.bfloat16), grad_scores)


def gather_params(params):
    return (
        lax.all_gather(params[0], "wsh", axis=0, tiled=True),
        lax.all_gather(params[1], "wsh", axis=0, tiled=True),
        lax.all_gather(params[2], "wsh", axis=0, tiled=True),
        lax.all_gather(params[3], "wsh", axis=0, tiled=True),
        lax.all_gather(params[4], "wsh", axis=0, tiled=True),
        lax.all_gather(params[5], "wsh", axis=0, tiled=True),
        lax.all_gather(params[6], "wsh", axis=0, tiled=True),
        lax.all_gather(params[7], "wsh", axis=0, tiled=True),
        lax.all_gather(params[8], "wsh", axis=0, tiled=True),
        lax.all_gather(params[9], "wsh", axis=0, tiled=True),
        lax.all_gather(params[10], "wsh", axis=0, tiled=True),
        lax.all_gather(params[11], "wsh", axis=0, tiled=True),
        lax.all_gather(params[12], "wsh", axis=0, tiled=True),
        lax.all_gather(params[13], "wsh", axis=0, tiled=True),
        lax.all_gather(params[14], "wsh", axis=0, tiled=True),
    )


def per_device(
    tokens,
    cotangent,
    lengths,
    dealing,
    w_query,
    w_key,
    w_value,
    w_out,
    w_up,
    w_down,
    b_query,
    b_value,
    b_out,
    b_up,
    b_down,
    gain_one,
    shift_one,
    gain_two,
    shift_two,
):
    params = (
        w_query,
        w_key,
        w_value,
        w_out,
        w_up,
        w_down,
        b_query,
        b_value,
        b_out,
        b_up,
        b_down,
        gain_one,
        shift_one,
        gain_two,
        shift_two,
    )
    own_rows = tokens.shape[2]
    width = tokens.shape[3]
    head_size = width // HEADS
    scale_factor = 1.0 / math.sqrt(head_size)
    my_start = lax.axis_index("ctx") * own_rows
    wsh_count = lax.axis_size("wsh")
    grads = tuple(
        (jnp.zeros((item.shape[0] * wsh_count,) + item.shape[1:], jnp.float32) for item in params)
    )
    results = []
    input_grads = []
    for micro in range(MB):
        whole = gather_params(params)
        query_weight, key_weight, value_weight, out_weight, up_weight, down_weight = whole[:6]
        (
            bias_query,
            bias_value,
            bias_out,
            bias_up,
            bias_down,
            gain_first,
            shift_first,
            gain_second,
            shift_second,
        ) = tuple((item.astype(jnp.float32) for item in whole[6:]))
        token_rows = tokens[0, micro]
        seq_all, valid_all = row_labels(dealing[0, micro], lengths[0, micro])
        my_seq = lax.dynamic_slice_in_dim(seq_all, my_start, own_rows)
        my_valid = lax.dynamic_slice_in_dim(valid_all, my_start, own_rows)
        query_low = (
            jnp.dot(token_rows, query_weight, preferred_element_type=jnp.float32) + bias_query
        ).astype(jnp.bfloat16)
        key_low = jnp.dot(token_rows, key_weight, preferred_element_type=jnp.float32).astype(
            jnp.bfloat16
        )
        value_low = (
            jnp.dot(token_rows, value_weight, preferred_element_type=jnp.float32) + bias_value
        ).astype(jnp.bfloat16)
        query_heads = query_low.reshape(own_rows, HEADS, head_size)
        my_key_heads = key_low.reshape(own_rows, HEADS, head_size)
        my_value_heads = value_low.reshape(own_rows, HEADS, head_size)
        start_state = (
            jnp.full((HEADS, own_rows), NEG_FILL, jnp.float32),
            jnp.zeros((HEADS, own_rows), jnp.float32),
            jnp.zeros((own_rows, HEADS, head_size), jnp.float32),
        )
        key_piece = lax.all_gather(key_low, "ctx", axis=0, tiled=True)
        value_piece = lax.all_gather(value_low, "ctx", axis=0, tiled=True)
        piece_rows = key_piece.shape[0]
        step_rows = math.gcd(piece_rows, 512)

        def visit_block(running, offset):
            run_max, run_sum, run_acc = running
            key_blk = lax.dynamic_slice_in_dim(key_piece, offset, step_rows).reshape(
                step_rows, HEADS, head_size
            )
            value_blk = lax.dynamic_slice_in_dim(value_piece, offset, step_rows).reshape(
                step_rows, HEADS, head_size
            )
            key_seq = lax.dynamic_slice_in_dim(seq_all, offset, step_rows)
            key_valid = lax.dynamic_slice_in_dim(valid_all, offset, step_rows)
            scores, allowed = masked_scores(
                query_heads, key_blk, my_seq, key_seq, key_valid, scale_factor
            )
            new_max = jnp.maximum(run_max, jnp.max(scores, axis=-1))
            rescale = jnp.exp(run_max - new_max)
            weights = jnp.exp(scores - new_max[:, :, None]) * allowed
            run_sum = run_sum * rescale + jnp.sum(weights, axis=-1)
            run_acc = run_acc * rescale.T[:, :, None] + jnp.einsum(
                "hqk,khd->qhd",
                weights.astype(jnp.bfloat16),
                value_blk,
                preferred_element_type=jnp.float32,
            )
            return (new_max, run_sum, run_acc)

        final_max, final_sum, final_acc = blockwise(start_state, piece_rows, step_rows, visit_block)
        attended = final_acc / final_sum.T[:, :, None]
        log_total = final_max + jnp.log(final_sum)
        attended_low = attended.reshape(own_rows, width).astype(jnp.bfloat16)
        out_proj = jnp.dot(attended_low, out_weight, preferred_element_type=jnp.float32) + bias_out
        first_sum = token_rows.astype(jnp.float32) + out_proj
        norm_one, norm_one_back = jax.vjp(layer_norm, first_sum, gain_first, shift_first)
        mlp_input = norm_one.astype(jnp.bfloat16)
        up_pre = jnp.dot(mlp_input, up_weight, preferred_element_type=jnp.float32) + bias_up
        activated, gelu_back = jax.vjp(gelu_exact, up_pre)
        activated_low = activated.astype(jnp.bfloat16)
        down_out = (
            jnp.dot(activated_low, down_weight, preferred_element_type=jnp.float32) + bias_down
        )
        result, norm_two_back = jax.vjp(layer_norm, norm_one + down_out, gain_second, shift_second)
        results.append(result.astype(jnp.bfloat16))
        grad_second, grad_gain_b, grad_shift_b = norm_two_back(
            cotangent[0, micro].astype(jnp.float32)
        )
        grad_down_low = grad_second.astype(jnp.bfloat16)
        grad_activated = jnp.einsum(
            "rd,fd->rf", grad_down_low, down_weight, preferred_element_type=jnp.float32
        )
        (grad_up_pre,) = gelu_back(grad_activated)
        grad_up_low = grad_up_pre.astype(jnp.bfloat16)
        grad_norm_one = (
            jnp.einsum("rf,df->rd", grad_up_low, up_weight, preferred_element_type=jnp.float32)
            + grad_second
        )
        grad_first, grad_gain_a, grad_shift_a = norm_one_back(grad_norm_one)
        grad_out_low = grad_first.astype(jnp.bfloat16)
        grad_att_low = jnp.einsum(
            "rd,ed->re", grad_out_low, out_weight, preferred_element_type=jnp.float32
        ).astype(jnp.bfloat16)
        grad_heads = grad_att_low.reshape(own_rows, HEADS, head_size)
        row_delta = jnp.sum(grad_heads.astype(jnp.float32) * attended, axis=-1).T
        empty_heads = jnp.zeros((own_rows, HEADS, head_size), jnp.float32)
        query_key_piece = lax.all_gather(key_low, "ctx", axis=0, tiled=True)
        query_value_piece = lax.all_gather(value_low, "ctx", axis=0, tiled=True)
        query_piece_rows = query_key_piece.shape[0]
        query_step_rows = math.gcd(query_piece_rows, 512)

        def query_visit_block(running, offset):
            key_blk = lax.dynamic_slice_in_dim(query_key_piece, offset, query_step_rows).reshape(
                query_step_rows, HEADS, head_size
            )
            value_blk = lax.dynamic_slice_in_dim(
                query_value_piece, offset, query_step_rows
            ).reshape(query_step_rows, HEADS, head_size)
            key_seq = lax.dynamic_slice_in_dim(seq_all, offset, query_step_rows)
            key_valid = lax.dynamic_slice_in_dim(valid_all, offset, query_step_rows)
            probs_low, grad_scores = attention_grads(
                query_heads,
                grad_heads,
                key_blk,
                value_blk,
                my_seq,
                key_seq,
                key_valid,
                log_total,
                row_delta,
                scale_factor,
            )
            return running + jnp.einsum(
                "hqk,khd->qhd", grad_scores, key_blk, preferred_element_type=jnp.float32
            )

        grad_query_sum = blockwise(
            empty_heads, query_piece_rows, query_step_rows, query_visit_block
        )
        total_all, delta_all = (
            lax.all_gather(log_total.T, "ctx", axis=0, tiled=True),
            lax.all_gather(row_delta.T, "ctx", axis=0, tiled=True),
        )
        query_piece = lax.all_gather(query_low, "ctx", axis=0, tiled=True)
        grad_piece = lax.all_gather(grad_att_low, "ctx", axis=0, tiled=True)
        key_piece_rows = query_piece.shape[0]
        key_step_rows = math.gcd(key_piece_rows, 512)

        def key_visit_block(running, offset):
            grad_key_run, grad_value_run = running
            query_blk = lax.dynamic_slice_in_dim(query_piece, offset, key_step_rows).reshape(
                key_step_rows, HEADS, head_size
            )
            grad_blk = lax.dynamic_slice_in_dim(grad_piece, offset, key_step_rows).reshape(
                key_step_rows, HEADS, head_size
            )
            total_blk = lax.dynamic_slice_in_dim(total_all, offset, key_step_rows)
            delta_blk = lax.dynamic_slice_in_dim(delta_all, offset, key_step_rows)
            query_seq = lax.dynamic_slice_in_dim(seq_all, offset, key_step_rows)
            probs_low, grad_scores = attention_grads(
                query_blk,
                grad_blk,
                my_key_heads,
                my_value_heads,
                query_seq,
                my_seq,
                my_valid,
                total_blk.T,
                delta_blk.T,
                scale_factor,
            )
            grad_key_run = grad_key_run + jnp.einsum(
                "hqk,qhd->khd", grad_scores, query_blk, preferred_element_type=jnp.float32
            )
            grad_value_run = grad_value_run + jnp.einsum(
                "hqk,qhd->khd", probs_low, grad_blk, preferred_element_type=jnp.float32
            )
            return (grad_key_run, grad_value_run)

        grad_key_sum, grad_value_sum = blockwise(
            (empty_heads, empty_heads), key_piece_rows, key_step_rows, key_visit_block
        )
        grad_key_flat = grad_key_sum.reshape(own_rows, width)
        grad_value_flat = grad_value_sum.reshape(own_rows, width)
        grad_query_low = (
            (grad_query_sum * scale_factor).reshape(own_rows, width).astype(jnp.bfloat16)
        )
        grad_key_low = (grad_key_flat * scale_factor).astype(jnp.bfloat16)
        grad_value_low = grad_value_flat.astype(jnp.bfloat16)
        terms = (
            jnp.einsum("rd,re->de", token_rows, grad_query_low, preferred_element_type=jnp.float32),
            jnp.einsum("rd,re->de", token_rows, grad_key_low, preferred_element_type=jnp.float32),
            jnp.einsum("rd,re->de", token_rows, grad_value_low, preferred_element_type=jnp.float32),
            jnp.einsum("rd,re->de", attended_low, grad_out_low, preferred_element_type=jnp.float32),
            jnp.einsum("rd,rf->df", mlp_input, grad_up_low, preferred_element_type=jnp.float32),
            jnp.einsum(
                "rf,rd->fd", activated_low, grad_down_low, preferred_element_type=jnp.float32
            ),
            jnp.sum(grad_query_low.astype(jnp.float32), axis=0),
            jnp.sum(grad_value_low.astype(jnp.float32), axis=0),
            jnp.sum(grad_out_low.astype(jnp.float32), axis=0),
            jnp.sum(grad_up_low.astype(jnp.float32), axis=0),
            jnp.sum(grad_down_low.astype(jnp.float32), axis=0),
            grad_gain_a,
            grad_shift_a,
            grad_gain_b,
            grad_shift_b,
        )
        grads = tuple((total_now + fresh for total_now, fresh in zip(grads, terms)))
        grad_rows = (
            grad_first
            + jnp.einsum(
                "re,de->rd", grad_query_low, query_weight, preferred_element_type=jnp.float32
            )
            + jnp.einsum("re,de->rd", grad_key_low, key_weight, preferred_element_type=jnp.float32)
            + jnp.einsum(
                "re,de->rd", grad_value_low, value_weight, preferred_element_type=jnp.float32
            )
        )
        input_grads.append(grad_rows.astype(jnp.bfloat16))
    shards = jax.tree.map(
        lambda part: part.astype(jnp.float32),
        lax.psum_scatter(as_sent(grads), "wsh", scatter_dimension=0, tiled=True),
    )
    summed = jax.tree.map(lambda part: part.astype(jnp.float32), lax.psum(as_sent(shards), "ctx"))
    return (jnp.stack(results)[None], jnp.stack(input_grads)[None]) + tuple(summed)


MESH_IDS = pl.DeviceIdType.MESH
F32 = jnp.float32
BF16 = jnp.bfloat16
HD = 64
VMEM_BYTES = 60 * 1024 * 1024


def flip(index, bit):
    return index + bit * (1 - 2 * lax.rem(lax.div(index, bit), 2))


def bit_of(index, bit):
    return lax.rem(lax.div(index, bit), 2)


def greet(peers):
    barrier = pltpu.get_barrier_semaphore()
    for peer in peers:
        pl.semaphore_signal(barrier, inc=1, device_id=peer, device_id_type=MESH_IDS)
    pl.semaphore_wait(barrier, len(peers))


def send(src, dst, send_sem, recv_sem, peer):
    copy = pltpu.make_async_remote_copy(
        src_ref=src,
        dst_ref=dst,
        send_sem=send_sem,
        recv_sem=recv_sem,
        device_id=peer,
        device_id_type=MESH_IDS,
    )
    copy.start()
    return copy


SEQS = HEADS // BPS


def plane_peers(c, w, count):
    return [(lax.rem(c + step, count), w) for step in range(1, count)]


def pack_three(first, second, third, row, pair, out):
    cols = pl.ds(pair * 128, 128)
    a, b, d = (ref[pl.ds(row, BLK), cols] for ref in (first, second, third))
    half = BLK // 2
    for head in range(2):
        lane = slice(head * HD, head * HD + HD)
        out[2 * pair + head, 0:BLK, :] = jnp.concatenate([a[:, lane], b[:, lane]], axis=1)
        out[2 * pair + head, BLK : BLK + half, :] = jnp.concatenate(
            [d[:half, lane], d[half:, lane]], axis=1
        )


def unpack_fold(block):
    return jnp.concatenate([block[:, :HD], block[:, HD:]], axis=0)


def fold(rows):
    half = rows.shape[0] // 2
    return jnp.concatenate([rows[:half], rows[half:]], axis=1)


def all_bytes(ref, sem, peers):
    view = ref.at[pl.ds(0, peers)]
    return pltpu.make_async_copy(view, view, sem)


def norm_parts(summed):
    row_mean = jnp.mean(summed, axis=-1, keepdims=True)
    centred = summed - row_mean
    row_var = jnp.mean(centred * centred, axis=-1, keepdims=True)
    scale = lax.rsqrt(row_var + EPSILON)
    return centred * scale, scale


def norm_back(grad, unit, scale, gain):
    inner = grad * gain
    mean_one = jnp.mean(inner, axis=-1, keepdims=True)
    mean_two = jnp.mean(inner * unit, axis=-1, keepdims=True)
    return scale * (inner - mean_one - unit * mean_two)


def dot_minor(a, b):
    return lax.dot_general(a, b, (((1,), (1,)), ((), ())), preferred_element_type=F32)


ROW_OUT, ROW_UP, ROW_DOWN, ROW_GAIN_ONE, ROW_SHIFT_ONE, ROW_GAIN_TWO, ROW_SHIFT_TWO = 2, 3, 7, 8, 9, 10, 11


SQUARE, PAIR_Y, PAIR_Z, ALONE = (8, "yz"), (4, "y"), (4, "z"), (2, "")
WAYS = (
    SQUARE, SQUARE, SQUARE, SQUARE, PAIR_Y, SQUARE, PAIR_Z, PAIR_Y, ALONE, PAIR_Z, PAIR_Y, ALONE,
)
SEND_ORDER = (2, 0, 1, 3, 5, 7, 4, 6, 9, 10, 8, 11)
FORWARD_SCHEDULE = (
    ("second", 2), ("second", 0), ("third", 2), ("second", 1), ("third", 0), ("fourth", 2),
    ("third", 1), ("second", 3), ("second", 5), ("fourth", 0), ("project", 2), ("fourth", 1),
    ("project", 0), ("project", 1), ("pack", 0), ("second", 7), ("third", 3), ("second", 4),
    ("second", 6), ("att", 0), ("fourth", 7), ("third", 5), ("fourth", 3), ("att", 1), ("att",
    2), ("fourth", 5), ("fourth", 8), ("second", 10), ("second", 9), ("fourth", 6), ("fourth",
    4), ("rows", 0), ("out", 0), ("hidden", 0), ("fourth", 10), ("hidden", 1), ("hidden", 2),
    ("fourth", 9), ("hidden", 3), ("hidden", 4), ("fourth", 11), ("hidden", 5), ("hidden", 6),
    ("hidden", 7),
)


def weight_plan(shards):
    unit = shards[0].shape[0] * shards[0].shape[1]
    plan = []
    for index, (rows, cols) in enumerate(shard.shape for shard in shards):
        parts = max(1, rows * cols // unit)
        for part in range(parts):
            plan.append((index, part * (rows // parts), rows // parts, WAYS[len(plan)]))
    return plan


def forward_kernel(heads, plan, n_weights, n_vectors, *refs):
    table_ref, x_ref, cot_ref = refs[:3]
    refs = refs[3:]
    shards, vectors = refs[:n_weights], refs[n_weights : n_weights + n_vectors]
    refs = refs[n_weights + n_vectors :]
    wholes, kept_ref, lse_ref, a_ref = refs[:3], *refs[3:6]
    out_ref, n_ref, g_ref, do_ref, du_ref, dm_ref, dh_ref, da_ref, vec_ref = refs[6:15]
    refs = refs[15:]
    near, refs = refs[:n_weights], refs[n_weights:]
    small, small_in, small_whole, bias, q_ref, k_ref, v_ref = refs[:7]
    slope, n_full, unit, total = refs[7:11]
    refs = refs[11:]
    in_buf = refs[:MB]
    out_buf, back_out, back_in, q_s, k_s, v_s, a_s = refs[MB : 7 + MB]
    (
        w_send,
        w_recv,
        small_sems,
        local_sem,
        stage_sem,
        send_sem,
        recv_sem,
        back_send,
        back_recv,
        keep_sem,
    ) = refs[7 + MB :]
    c, w = lax.axis_index("ctx"), lax.axis_index("wsh")
    o = 1 - w
    by_x, by_y, by_z, by_core = (c, o), (flip(c, 2), w), (flip(c, 4), w), (flip(c, 1), w)
    core, y, z = bit_of(c, 1), bit_of(c, 2), bit_of(c, 4)
    peers = plane_peers(c, w, heads)
    staged = []
    for index, shard in enumerate(shards):
        rows = shard.shape[0]
        spot = pl.ds(pl.multiple_of(w * rows, rows), rows)
        copy = pltpu.make_async_copy(shard, near[index].at[spot], stage_sem.at[index])
        copy.start()
        staged.append(copy)
    line, lanes = 0, small.shape[1]
    for vector in vectors:
        for first in range(0, vector.shape[0], lanes):
            piece = vector[pl.ds(first, lanes)].astype(F32)
            small[line : line + 1, :] = piece.reshape(1, lanes)
            line += 1
    greet(peers + [by_x])
    small_sent = send(small, small_in, small_sems.at[0], small_sems.at[1], by_x)

    def part(chunk, side, piece, start, count):
        tensor, first, rows, way = plan[chunk]
        half = shards[tensor].shape[0]
        at = side * half + first + piece * (rows // way[0]) + start
        return near[tensor].at[pl.ds(pl.multiple_of(at, 8), count)]

    steps = {}

    def sem(kind, chunk):
        return w_send.at[kind, chunk], w_recv.at[kind, chunk]

    def own_piece(way):
        return {
            SQUARE: core * 4 + z * 2 + y,
            PAIR_Y: core * 2 + y,
            PAIR_Z: core * 2 + z,
            ALONE: core,
        }[way]

    for chunk in SEND_ORDER:
        tensor, first, rows, way = plan[chunk]
        size, mine = rows // way[0], own_piece(way)
        src = shards[tensor].at[pl.ds(pl.multiple_of(first + mine * size, 8), size)]
        steps[chunk, 0] = send(src, part(chunk, w, mine, 0, size), *sem(0, chunk), by_x)

    def second(chunk):
        _, _, rows, way = plan[chunk]
        steps[chunk, 0].wait_recv()
        ref = part(chunk, o, own_piece(way), 0, rows // way[0])
        for name in way[1]:
            kind, peer = {"y": (1, by_y), "z": (2, by_z)}[name]
            steps[chunk, kind] = send(ref, ref, *sem(kind, chunk), peer)

    def third(chunk):
        _, _, rows, way = plan[chunk]
        size = rows // way[0]
        steps[chunk, 1].wait_recv()
        steps[chunk, 2].wait_recv()
        ref = part(chunk, o, core * 4 + (1 - z) * 2 + y, 0, size // 2)
        steps[chunk, 3] = send(ref, ref, *sem(3, chunk), by_y)
        ref = part(chunk, o, core * 4 + z * 2 + (1 - y), size // 2, size // 2)
        steps[chunk, 4] = send(ref, ref, *sem(4, chunk), by_z)

    def fourth(chunk):
        _, _, rows, way = plan[chunk]
        for kind in {SQUARE: (3, 4), PAIR_Y: (1,), PAIR_Z: (2,), ALONE: (0,)}[way]:
            steps[chunk, kind].wait_recv()
        ref = part(chunk, o, core * (way[0] // 2), 0, rows // 2)
        steps[chunk, 5] = send(ref, ref, *sem(5, chunk), by_core)

    width = x_ref.shape[1]
    step = 256
    projected = []

    def project(index):
        if not projected:
            small_sent.wait()
            small_whole[w] = small[...]
            small_whole[o] = small_in[...]
            for side in range(2):
                for row in range(2):
                    bias[row : row + 1, side * lanes : (side + 1) * lanes] = small_whole[
                        side, row : row + 1, :
                    ]
        projected.append(index)
        staged[index].wait()
        steps[index, 5].wait_recv()
        weight, out = near[index], (q_ref, k_ref, v_ref)[index]

        def some_columns(turn, carry):
            cols = pl.ds(pl.multiple_of(turn * step, step), step)
            product = jnp.dot(x_ref[...], weight[:, cols], preferred_element_type=F32)
            if index != 1:
                product = product + bias[index // 2 : index // 2 + 1, cols]
            out[:, cols] = product.astype(BF16)
            return carry

        lax.fori_loop(0, width // step, some_columns, 0)
        pltpu.make_async_copy(near[index], wholes[index], local_sem.at[index]).start()

    def pack(_):
        for m in range(MB):
            for pair in range(heads // 2):
                pack_three(q_ref, k_ref, v_ref, m * BLK, pair, out_buf.at[m])
            for peer in peers:
                send(
                    out_buf.at[m, peer[0]], in_buf[m].at[c], send_sem.at[m], recv_sem.at[m], peer
                )
            in_buf[m][c] = out_buf[m, c]

    blocks = heads
    span = BPS * BLK

    def attention(m):
        all_bytes(in_buf[m], recv_sem.at[m], heads - 1).wait()
        pltpu.make_async_copy(in_buf[m], kept_ref.at[m], keep_sem.at[m]).start()
        for b in range(blocks):
            got = in_buf[m][table_ref[m, SEQS + blocks + b]]
            q_s[b * BLK : (b + 1) * BLK, :] = got[:BLK, :HD]
            k_s[b * BLK : (b + 1) * BLK, :] = got[:BLK, HD:]
            v_s[b * BLK : (b + 1) * BLK, :] = unpack_fold(got[BLK:])

        def one_sequence(s, carry):
            rows = pl.ds(pl.multiple_of(s * span, span), span)
            scores = lax.dot_general(
                k_s[rows, :], q_s[rows, :], (((1,), (1,)), ((), ())), preferred_element_type=F32
            ) * (1.0 / math.sqrt(HD))
            place = lax.broadcasted_iota(jnp.int32, scores.shape, 0)
            scores = jnp.where(place < table_ref[m, s], scores, NEG_FILL)
            top = jnp.max(scores, axis=0, keepdims=True)
            weights = jnp.exp(scores - top)
            summed = jnp.sum(weights, axis=0, keepdims=True)
            out_t = lax.dot_general(
                v_s[rows, :],
                weights.astype(BF16),
                (((0,), (0,)), ((), ())),
                preferred_element_type=F32,
            )
            a_s[pl.ds(s * BPS, BPS)] = (out_t / summed).T.reshape(BPS, BLK, HD)
            lse_ref[pl.ds(m * (blocks // BPS) + s, 1), :] = top + jnp.log(summed)
            return carry

        lax.fori_loop(0, blocks // BPS, one_sequence, 0)
        for t in range(blocks):
            back_out[m, t] = fold(a_s[table_ref[m, SEQS + t]]).astype(BF16)
        for peer in peers:
            send(
                back_out.at[m, peer[0]], back_in.at[m, c], back_send.at[m], back_recv.at[m], peer
            )
        back_in[m, c] = back_out[m, c]

    def come_back(_):
        for m in range(MB):
            all_bytes(back_in.at[m], back_recv.at[m], heads - 1).wait()
            for pair in range(heads // 2):
                a_ref[m * BLK : (m + 1) * BLK, pair * 128 : (pair + 1) * 128] = jnp.concatenate(
                    [unpack_fold(back_in[m, 2 * pair]), unpack_fold(back_in[m, 2 * pair + 1])],
                    axis=1,
                )

    def line_of(row):
        return jnp.concatenate(
            [small_whole[0, row : row + 1, :], small_whole[1, row : row + 1, :]], axis=1
        )

    def keep(row, values):
        summed = jnp.sum(values, axis=0, keepdims=True)
        for side in range(2):
            vec_ref[side, row : row + 1, :] = summed[:, side * lanes : (side + 1) * lanes]

    out_w, up_w, down_w = near[3:]
    chunks_of = {t: [i for i, item in enumerate(plan) if item[0] == t] for t in range(n_weights)}

    def arrived(tensor, chunks):
        for chunk in chunks:
            steps[chunk, 5].wait_recv()

    def out_project(_):
        staged[3].wait()
        arrived(3, chunks_of[3])
        h_one = x_ref[...].astype(F32) + (
            jnp.dot(a_ref[...], out_w[...], preferred_element_type=F32) + line_of(ROW_OUT)
        )
        unit_one, scale_one = norm_parts(h_one)
        unit[...] = unit_one
        n_one = unit_one * line_of(ROW_GAIN_ONE) + line_of(ROW_SHIFT_ONE)
        n_full[...] = n_one
        n_ref[...] = n_one.astype(BF16)
        total[...] = jnp.zeros_like(total)
        kept_scale.append(scale_one)

    kept_scale = []
    hidden = g_ref.shape[1]
    hidden_steps = hidden // lanes
    per_half = hidden_steps // 2

    def hidden_at(turn):
        j = lax.rem(w * per_half + turn, hidden_steps)
        cols = pl.ds(pl.multiple_of(j * lanes, lanes), lanes)
        return cols, lax.div(j, per_half), pl.ds(ROW_UP + lax.rem(j, per_half), 1)

    def hidden_up(turn):
        if turn == 0:
            staged[4].wait()
            arrived(4, chunks_of[4])
            staged[5].wait()
        elif turn >= per_half:
            share = len(chunks_of[5]) // per_half
            first = (turn - per_half) * share
            arrived(5, chunks_of[5][first : first + share])
        cols, side, row = hidden_at(turn)
        u = jnp.dot(n_ref[...], up_w[:, cols], preferred_element_type=F32) + small_whole[side, row, :]
        below = 0.5 * (1.0 + lax.erf(u * math.sqrt(0.5)))
        slope[:, cols] = below + u * jnp.exp(-0.5 * u * u) * (1.0 / math.sqrt(2.0 * math.pi))
        g = (u * below).astype(BF16)
        g_ref[:, cols] = g
        total[...] += jnp.dot(g, down_w[cols, :], preferred_element_type=F32)

    acts = {
        "second": second,
        "third": third,
        "fourth": fourth,
        "project": project,
        "pack": pack,
        "att": attention,
        "rows": come_back,
        "out": out_project,
        "hidden": hidden_up,
    }
    for name, value in FORWARD_SCHEDULE:
        acts[name](value)

    h_two = n_full[...] + (total[...] + line_of(ROW_DOWN))
    unit_two, scale_two = norm_parts(h_two)
    out_ref[...] = (unit_two * line_of(ROW_GAIN_TWO) + line_of(ROW_SHIFT_TWO)).astype(BF16)
    cot = cot_ref[...].astype(F32)
    keep(ROW_GAIN_TWO, cot * unit_two)
    keep(ROW_SHIFT_TWO, cot)
    dh_two = norm_back(cot, unit_two, scale_two, line_of(ROW_GAIN_TWO))
    dm = dh_two.astype(BF16)
    dm_ref[...] = dm
    keep(ROW_DOWN, dm.astype(F32))
    total[...] = dh_two
    for turn in range(hidden_steps):
        cols, side, row = hidden_at(turn)
        du = (slope[:, cols] * dot_minor(dm_ref[...], down_w[cols, :])).astype(BF16)
        du_ref[:, cols] = du
        vec_ref[side, row, :] = jnp.sum(du.astype(F32), axis=0, keepdims=True)
        total[...] += dot_minor(du, up_w[:, cols])
    dn = total[...]
    keep(ROW_GAIN_ONE, dn * unit[...])
    keep(ROW_SHIFT_ONE, dn)
    dh_one = norm_back(dn, unit[...], kept_scale[0], line_of(ROW_GAIN_ONE))
    dh_ref[...] = dh_one
    do = dh_one.astype(BF16)
    do_ref[...] = do
    keep(ROW_OUT, do.astype(F32))
    da_ref[...] = dot_minor(do, out_w[...]).astype(BF16)
    for side in range(2):
        vec_ref[side, 0:ROW_OUT, :] = jnp.zeros((ROW_OUT, lanes), F32)

    for m in range(MB):
        all_bytes(out_buf.at[m], send_sem.at[m], heads - 1).wait()
        all_bytes(back_out.at[m], back_send.at[m], heads - 1).wait()
        pltpu.make_async_copy(in_buf[m], kept_ref.at[m], keep_sem.at[m]).wait()
    for flight in steps.values():
        flight.wait_send()
    for index in range(3):
        pltpu.make_async_copy(near[index], wholes[index], local_sem.at[index]).wait()


def forward(table, x, cot, shards, vectors, heads):
    plan = weight_plan(shards)
    count = len(shards)
    anywhere, vmem = pl.BlockSpec(memory_space=pl.ANY), pl.BlockSpec(memory_space=pltpu.VMEM)
    smem = pl.BlockSpec(memory_space=pltpu.SMEM)
    rows, width = x.shape
    hidden = shards[4].shape[1]
    pack_rows = BLK + BLK // 2
    span = BPS * BLK
    lanes = min(item.shape[0] for item in vectors)
    lines = sum(item.shape[0] for item in vectors) // lanes
    whole = lambda s: (2 * s.shape[0],) + s.shape[1:]
    low = lambda cols: jax.ShapeDtypeStruct((rows, cols), BF16)
    full = lambda cols: pltpu.VMEM((rows, cols), F32)
    sems = lambda *dims: pltpu.SemaphoreType.DMA(dims)
    return pl.pallas_call(
        functools.partial(forward_kernel, heads, plan, count, len(vectors)),
        out_shape=[jax.ShapeDtypeStruct(whole(s), s.dtype) for s in shards[:3]]
        + [
            jax.ShapeDtypeStruct((MB, heads, pack_rows, 128), BF16),
            jax.ShapeDtypeStruct((8, span), F32),
            low(width),
            low(width),
            low(width),
            low(hidden),
            low(width),
            low(hidden),
            low(width),
            jax.ShapeDtypeStruct((rows, width), F32),
            low(width),
            jax.ShapeDtypeStruct((2, lines, lanes), F32),
        ],
        in_specs=[smem, vmem, vmem] + [anywhere] * count + [vmem] * len(vectors),
        out_specs=[anywhere] * 4 + [vmem] * 11,
        scratch_shapes=[pltpu.VMEM(whole(s), s.dtype) for s in shards]
        + [pltpu.VMEM((lines, lanes), F32)] * 2
        + [pltpu.VMEM((2, lines, lanes), F32), pltpu.VMEM((2, width), F32)]
        + [pltpu.VMEM((rows, width), BF16)] * 3
        + [full(hidden), full(width), full(width), full(width)]
        + [pltpu.VMEM((heads, pack_rows, 128), BF16)] * MB
        + [
            pltpu.VMEM((MB, heads, pack_rows, 128), BF16),
            pltpu.VMEM((MB, heads, BLK // 2, 128), BF16),
            pltpu.VMEM((MB, heads, BLK // 2, 128), BF16),
            pltpu.VMEM((heads * BLK, HD), BF16),
            pltpu.VMEM((heads * BLK, HD), BF16),
            pltpu.VMEM((heads * BLK, HD), BF16),
            pltpu.VMEM((heads, BLK, HD), F32),
        ]
        + [sems(6, len(plan)), sems(6, len(plan)), sems(2), sems(3), sems(count)]
        + [sems(MB)] * 5,
        compiler_params=pltpu.CompilerParams(
            collective_id=1, has_side_effects=True, vmem_limit_bytes=VMEM_BYTES
        ),
        name="forward",
    )(table, x, cot, *shards, *vectors)


ORDERS = (
    ("xyzZ", "xyzZ", "yxzZ", "xyzZ"),
    ("yzxZ", "xZyz", "zxyZ", "xyzZ"),
    ("yxzZ", "xyZz", "zyxZ", "xyzZ"),
)
PIECES = len(ORDERS[0])
SCHEDULE = (
    "up", 0, 1, 2, "down", (1, 3), "back", (1, 1), (2, 0), (2, 1), "qkv", (1, 3), (2, 1),
    (1, 1), (1, 3), (2, 0), (2, 3), (1, 0), (2, 1), (1, 3), "vec", (2, 0), (2, 1), (0, 0),
    (1, 1), (2, 3), (2, 2), (2, 1), (2, 3), (1, 0), (2, 0), (1, 1), (1, 3), (2, 1), "vec",
    (2, 2), (0, 0), (0, 1), (1, 2), (2, 0), (0, 2), (0, 3), (0, 0), (2, 3), (2, 0), (1, 0),
    (0, 1), (2, 3), "vec", (2, 2), (1, 0), (1, 2), (2, 3), (0, 1), (0, 3), (0, 0), (1, 2),
    (1, 0), (2, 1), (0, 3), (0, 2), (0, 1), "vec", (1, 3), (2, 3), (1, 2), (1, 0), (1, 1),
    (0, 0), (0, 2), (0, 3), "rows", (0, 1), (2, 0), (1, 2), (0, 0), (2, 2), (1, 0), (0, 2),
    "vec", (0, 3), (2, 2), (0, 2), (0, 1), (1, 3), (1, 1), (0, 3), (0, 2), (0, 0), (2, 2),
    (0, 1), (1, 2), (1, 1), (2, 2), (0, 3), (1, 2), (0, 2),
)
KEYS = tuple((part, piece) for part in range(3) for piece in range(PIECES))


def landing_shapes(order, shape):
    shards, sides, shapes = 8, 2, []
    for name in order:
        if name == "x":
            sides = 1
        else:
            shards //= 2
        shapes.append((sides, shards, shape[2] // PIECES, shape[3]))
    return shapes


def dot_t(a, b):
    return lax.dot_general(a, b, (((0,), (0,)), ((), ())), preferred_element_type=F32)


def lanes_at(first, size):
    return pl.ds(pl.multiple_of(first, 128), size)


def backward_kernel(heads, *refs):
    table_ref, da_ref, kept_ref, lse_ref = refs[:4]
    x_ref, a_ref, n_ref, g_ref, do_ref, du_ref, dm_ref, vec_ref, dh_ref = refs[4:13]
    weights = refs[13:16]
    rows_out, o_a, o_b, o_c, vec_out = refs[16:21]
    refs = refs[21:]
    in_buf = refs[:MB]
    out_buf, back_out, back_in, q_s, k_s, v_s, a_s, dq_s, dk_s, dv_s = refs[MB : MB + 10]
    refs = refs[MB + 10 :]
    dq_ref, dk_ref, dv_ref, m_x, m_a, m_n, m_dm, m_do, m_du, m_g, m_dqkv = refs[:11]
    near, (vec_s, v_recv, v_sum, s_a, s_b, s_c) = refs[11:14], refs[14:20]
    refs = refs[20:]
    r_bufs = {key: refs[4 * i : 4 * i + 4] for i, key in enumerate(KEYS)}
    (
        send_sem,
        recv_sem,
        back_send,
        back_recv,
        mate_send,
        mate_recv,
        near_sem,
        rs_send,
        rs_recv,
        ag_send,
        ag_recv,
        own_sem,
        v_send_sem,
        v_recv_sem,
    ) = refs[4 * len(KEYS) :]
    c, x = lax.axis_index("ctx"), lax.axis_index("wsh")
    core, y, z, zz = bit_of(c, 1), bit_of(c, 2), bit_of(c, 4), bit_of(c, 8)
    by_core = (flip(c, 1), x)
    by = {"x": (c, 1 - x), "y": (flip(c, 2), x), "z": (flip(c, 4), x), "Z": (flip(c, 8), x)}
    bits = {"y": y, "z": z, "Z": zz}
    peers = plane_peers(c, x, heads)
    blocks, span = heads, BPS * BLK
    width, hidden = da_ref.shape[1], g_ref.shape[1]
    for index, weight in enumerate(weights):
        pltpu.make_async_copy(weight, near[index], near_sem.at[index]).start()
    greet(peers + [by["x"]])

    for m in range(MB):
        row = slice(m * BLK, (m + 1) * BLK)
        for pair in range(heads // 2):
            both = da_ref[row, pair * 128 : (pair + 1) * 128]
            for head in range(2):
                out_buf[m, 2 * pair + head] = fold(both[:, head * HD : (head + 1) * HD])
        for peer in peers:
            send(out_buf.at[m, peer[0]], in_buf[m].at[c], send_sem.at[m], recv_sem.at[m], peer)
        in_buf[m][c] = out_buf[m, c]

    shared = {}

    def share(name, src, dst):
        index = len(shared)
        shared[name] = send(src, dst, mate_send.at[index], mate_recv.at[index], by_core)

    other = 1 - core
    share("n", n_ref, m_n)
    share("du", du_ref.at[:, lanes_at(other * (hidden // 2), hidden // 2)], m_du)
    for half in range(2):
        share(
            "g" + str(half),
            g_ref.at[:, lanes_at(half * (hidden // 2) + other * (hidden // 4), hidden // 4)],
            m_g.at[:, pl.ds(half * (hidden // 4), hidden // 4)],
        )
    share("dm", dm_ref, m_dm)
    share("a", a_ref, m_a)
    share("do", do_ref.at[:, lanes_at(other * (width // 2), width // 2)], m_do)
    share("x", x_ref, m_x)

    sums, outs = (s_a, s_b, s_c), (o_a, o_b, o_c)
    wide = 512

    def tile(pairs, out, first, count):
        def body(turn, carry):
            at = turn * wide
            total = sum(dot_t(lhs[...], rhs[:, lanes_at(col + at, wide)]) for lhs, rhs, col in pairs)
            cols = lanes_at(first + at, wide)
            out[..., cols] = total.astype(BF16).reshape(out.shape[:-1] + (wide,))
            return carry

        lax.fori_loop(0, count, body, 0)

    def grads_up():
        shared["n"].wait_recv()
        shared["du"].wait_recv()
        half = hidden // 2
        tile(((n_ref, du_ref, core * half), (m_n, m_du, 0)), s_b, 0, half // wide)

    def grads_down():
        for name in ("g0", "g1", "dm"):
            shared[name].wait_recv()
        quarter = hidden // 4
        for half in range(2):
            mine = g_ref.at[:, lanes_at(half * 2 * quarter + core * quarter, quarter)]
            others = m_g.at[:, pl.ds(half * quarter, quarter)]
            tile(((mine, dm_ref, 0), (others, m_dm, 0)), s_c.at[half], 0, width // wide)

    def grads_qkv():
        half = width // 2
        for name in ("a", "do", "x", "dq", "dk", "dv"):
            shared[name].wait_recv()
        tile(((a_ref, do_ref, core * half), (m_a, m_do, 0)), s_a, 3 * half, half // wide)
        for index, ref in enumerate((dq_ref, dk_ref, dv_ref)):
            pairs = ((x_ref, ref, core * half), (m_x, m_dqkv, index * half))
            tile(pairs, s_a, index * half, half // wide)

    def attention(m):
        all_bytes(in_buf[m], recv_sem.at[m], heads - 1).wait()
        for b in range(blocks):
            slot = table_ref[m, SEQS + blocks + b]
            got = kept_ref[m, slot]
            rows = slice(b * BLK, (b + 1) * BLK)
            q_s[rows, :] = got[:BLK, :HD]
            k_s[rows, :] = got[:BLK, HD:]
            v_s[rows, :] = unpack_fold(got[BLK:])
            a_s[rows, :] = unpack_fold(in_buf[m][slot])

        def one_sequence(s, carry):
            rows = pl.ds(pl.multiple_of(s * span, span), span)
            qq, kk, vv, dd = q_s[rows, :], k_s[rows, :], v_s[rows, :], a_s[rows, :]
            scale = 1.0 / math.sqrt(HD)
            minor = (((1,), (1,)), ((), ()))
            scores = lax.dot_general(kk, qq, minor, preferred_element_type=F32) * scale
            spot = lax.broadcasted_iota(jnp.int32, scores.shape, 0)
            total = lse_ref[pl.ds(m * (blocks // BPS) + s, 1), :]
            probs = jnp.exp(jnp.where(spot < table_ref[m, s], scores - total, NEG_FILL))
            dp = lax.dot_general(vv, dd, minor, preferred_element_type=F32)
            both = probs * dp
            delta = jnp.sum(both, axis=0, keepdims=True)
            ds = (both - probs * delta).astype(BF16)
            here, split = pl.ds(s * BPS, BPS), (BPS, BLK, HD)
            dv = jnp.dot(probs.astype(BF16), dd, preferred_element_type=F32)
            dv_s[here] = dv.reshape(split)
            dk_s[here] = (jnp.dot(ds, qq, preferred_element_type=F32) * scale).reshape(split)
            dq_s[here] = (dot_t(kk, ds).T * scale).reshape(split)
            return carry

        lax.fori_loop(0, blocks // BPS, one_sequence, 0)
        for t in range(blocks):
            at = table_ref[m, SEQS + t]
            back_out[m, t, 0:BLK, :] = jnp.concatenate([dq_s[at], dk_s[at]], axis=1).astype(BF16)
            back_out[m, t, BLK:, :] = fold(dv_s[at]).astype(BF16)
        for peer in peers:
            send(
                back_out.at[m, peer[0]], back_in.at[m, c], back_send.at[m], back_recv.at[m], peer
            )
        back_in[m, c] = back_out[m, c]

    vec_peers = (by["x"], by["y"], by["z"], by["Z"], by_core)
    vec_steps = []

    def vec_send(src):
        step = len(vec_steps)
        vec_steps.append(
            send(
                src, v_recv.at[step], v_send_sem.at[step], v_recv_sem.at[step], vec_peers[step]
            )
        )

    def vec_next():
        step = len(vec_steps) - 1
        vec_steps[step].wait_recv()
        before = vec_s[x] if step == 0 else v_sum[step - 1]
        v_sum[step] = before + v_recv[step]
        if step + 1 < len(vec_peers):
            vec_send(v_sum.at[step])

    def come_back():
        for m in range(MB):
            all_bytes(back_in.at[m], back_recv.at[m], heads - 1).wait()
            row = slice(m * BLK, (m + 1) * BLK)
            for pair in range(heads // 2):
                lanes = slice(pair * 128, (pair + 1) * 128)
                one, two = back_in[m, 2 * pair], back_in[m, 2 * pair + 1]
                dq_ref[row, lanes] = jnp.concatenate([one[:BLK, :HD], two[:BLK, :HD]], axis=1)
                dk_ref[row, lanes] = jnp.concatenate([one[:BLK, HD:], two[:BLK, HD:]], axis=1)
                dv_ref[row, lanes] = jnp.concatenate(
                    [unpack_fold(one[BLK:]), unpack_fold(two[BLK:])], axis=1
                )
        half = width // 2
        for index, (name, ref) in enumerate((("dq", dq_ref), ("dk", dk_ref), ("dv", dv_ref))):
            share(
                name,
                ref.at[:, lanes_at(other * half, half)],
                m_dqkv.at[:, pl.ds(index * half, half)],
            )
        vec_s[...] = vec_ref[...]
        lanes = vec_s.shape[2]
        for index, ref in enumerate((dq_ref, dv_ref)):
            total = jnp.sum(ref[...].astype(F32), axis=0, keepdims=True)
            for side in range(2):
                vec_s[side, index : index + 1, :] = total[:, side * lanes : (side + 1) * lanes]
        vec_send(vec_s.at[1 - x])

    def grad_rows():
        total = dh_ref[...]
        for index, ref in enumerate((dq_ref, dk_ref, dv_ref)):
            pltpu.make_async_copy(weights[index], near[index], near_sem.at[index]).wait()
            total = total + lax.dot_general(
                ref[...], near[index][...], (((1,), (1,)), ((), ())), preferred_element_type=F32
            )
        rows_out[...] = total.astype(BF16)

    plans, gathers = {}, {}
    for key in KEYS:
        first, count, sided = 0, 8, False
        plans[key], back = [], []
        for name in ORDERS[key[0]][key[1]]:
            if name == "x":
                plans[key].append((by["x"], 1 - x, x, first, first, count))
                sided = True
                continue
            count //= 2
            out, keep = first + (1 - bits[name]) * count, first + bits[name] * count
            side = x if sided else None
            plans[key].append((by[name], side, side, out, keep, count))
            back.append((by[name], keep, out, count))
            first = keep
        gathers[key] = back[::-1]
    flights, spread, owns, state = {}, {}, {}, {}

    def piece_rows(key):
        rows = sums[key[0]].shape[2] // PIECES
        return pl.ds(key[1] * rows, rows)

    def reduce_send(key, step):
        peer, side, _, first, _, count = plans[key][step]
        dst = r_bufs[key][step]
        if side is None:
            src = sums[key[0]].at[:, pl.ds(first, count), piece_rows(key)]
        else:
            src, dst = sums[key[0]].at[side, pl.ds(first, count), piece_rows(key)], dst.at[0]
        sems = rs_send.at[key[0], key[1], step], rs_recv.at[key[0], key[1], step]
        flights[key, step] = send(src, dst, *sems, peer)
        state[key] = step

    def reduce_add(key, step):
        _, _, side, _, first, count = plans[key][step]
        flights[key, step].wait_recv()
        total, fresh, rows = sums[key[0]], r_bufs[key][step], piece_rows(key)
        sides = ((0, 0), (1, 1)) if side is None else ((side, 0),)
        for here, there in sides:

            def body(index, carry):
                spot = first + index
                total[here, spot, rows] = (
                    total[here, spot, rows].astype(F32) + fresh[there, index].astype(F32)
                ).astype(BF16)
                return carry

            lax.fori_loop(0, count, body, 0)

    def spread_send(key, kind, src, dst, peer):
        sems = ag_send.at[key[0], key[1], kind], ag_recv.at[key[0], key[1], kind]
        spread[key, kind] = send(src, dst, *sems, peer)

    def advance(key):
        step = state[key]
        out, rows = outs[key[0]], piece_rows(key)
        if step < 4:
            reduce_add(key, step)
            if step < 3:
                reduce_send(key, step + 1)
                return
            peer, first, _, _ = gathers[key][0]
            src = sums[key[0]].at[x, pl.ds(first, 1), rows]
            dst = out.at[core, pl.ds(first, 1), rows]
            owns[key] = pltpu.make_async_copy(src, dst, own_sem.at[key[0], key[1]])
            owns[key].start()
            spread_send(key, 0, src, dst, peer)
            spread_send(key, 3, src, dst, by_core)
        else:
            turn = step - 3
            spread[key, turn - 1].wait_recv()
            if turn == 1:
                owns[key].wait()
            if turn < 3:
                peer, first, _, count = gathers[key][turn]
                ref = out.at[core, pl.ds(first, count), rows]
                spread_send(key, turn, ref, ref, peer)
            _, _, first, count = gathers[key][turn - 1]
            ref = out.at[core, pl.ds(first, count), rows]
            spread_send(key, 3 + turn, ref, ref, by_core)
        state[key] = step + 1

    actions = {
        "up": (grads_up, 1),
        "down": (grads_down, 2),
        "qkv": (grads_qkv, 0),
        "back": (come_back, None),
        "rows": (grad_rows, None),
        "vec": (vec_next, None),
    }
    for event in SCHEDULE:
        if isinstance(event, tuple):
            advance(event)
        elif isinstance(event, int):
            attention(event)
        else:
            action, part = actions[event]
            if event == "vec" and len(vec_steps) == len(vec_peers) and "vec" in state:
                continue
            if event == "vec" and len(vec_steps) == len(vec_peers):
                state["vec"] = True
            action()
            if part is not None:
                for piece in range(PIECES):
                    reduce_send((part, piece), 0)
    vec_out[...] = v_sum[len(vec_peers) - 1]
    for m in range(MB):
        all_bytes(out_buf.at[m], send_sem.at[m], heads - 1).wait()
        all_bytes(back_out.at[m], back_send.at[m], heads - 1).wait()
    for flight in shared.values():
        flight.wait_send()
    for flight in vec_steps:
        flight.wait_send()
    for flight in flights.values():
        flight.wait_send()
    for (_, kind), flight in spread.items():
        if kind >= 3:
            flight.wait_recv()
        flight.wait_send()


def backward(table, da, kept, lse, x, a, n1, g, do, du, dm, vec, dh, weights, heads):
    vmem, smem = pl.BlockSpec(memory_space=pltpu.VMEM), pl.BlockSpec(memory_space=pltpu.SMEM)
    anywhere = pl.BlockSpec(memory_space=pl.ANY)
    rows, width = da.shape
    hidden = g.shape[1]
    pack_rows = BLK + BLK // 2
    low = lambda *dims: pltpu.VMEM(dims, BF16)
    a_shape, b_shape = (2, 8, width // 16, 2 * width), (2, 8, width // 16, hidden // 2)
    c_shape = (2, 8, hidden // 32, width)
    scratch = [low(heads, BLK // 2, 128)] * MB
    scratch += [low(MB, heads, BLK // 2, 128)]
    scratch += [low(MB, heads, pack_rows, 128)] * 2
    scratch += [low(heads * BLK, HD)] * 4
    scratch += [pltpu.VMEM((heads, BLK, HD), F32)] * 3
    scratch += [low(rows, width)] * 7
    scratch += [low(rows, width // 2), low(rows, hidden // 2), low(rows, hidden // 2)]
    scratch += [low(rows, 3 * width // 2)]
    scratch += [low(*item.shape) for item in weights]
    scratch += [pltpu.VMEM(vec.shape, F32)] + [pltpu.VMEM((5,) + vec.shape[1:], F32)] * 2
    scratch += [low(*shape) for shape in (a_shape, b_shape, c_shape)]
    for key in KEYS:
        shape = (a_shape, b_shape, c_shape)[key[0]]
        scratch += [low(*item) for item in landing_shapes(ORDERS[key[0]][key[1]], shape)]
    sems = lambda *dims: pltpu.SemaphoreType.DMA(dims)
    scratch += [sems(MB)] * 4 + [sems(11)] * 2 + [sems(3)]
    scratch += [sems(3, PIECES, 4)] * 2 + [sems(3, PIECES, 7)] * 2 + [sems(3, PIECES)]
    scratch += [sems(5)] * 2
    return pl.pallas_call(
        functools.partial(backward_kernel, heads),
        out_shape=[
            jax.ShapeDtypeStruct((rows, width), BF16),
            jax.ShapeDtypeStruct(a_shape, BF16),
            jax.ShapeDtypeStruct(b_shape, BF16),
            jax.ShapeDtypeStruct(c_shape, BF16),
            jax.ShapeDtypeStruct(vec.shape[1:], F32),
        ],
        in_specs=[smem] + [vmem] * 12 + [anywhere] * 3,
        out_specs=[vmem] + [anywhere] * 3 + [vmem],
        scratch_shapes=scratch,
        compiler_params=pltpu.CompilerParams(
            collective_id=2, has_side_effects=True, vmem_limit_bytes=VMEM_BYTES
        ),
        name="backward",
    )(table, da, kept, lse, x, a, n1, g, do, du, dm, vec, dh, *weights)


def widen_kernel(a_ref, b_ref, c_ref, vec_ref, *outs):
    @pl.when(pl.program_id(0) == 0)
    def _():
        line, lanes = 0, vec_ref.shape[1]
        for out in outs[6:]:
            for first in range(0, out.shape[0], lanes):
                out[pl.ds(first, lanes)] = vec_ref[line, :]
                line += 1

    half = outs[0].shape[1] // 2
    for index, out in enumerate(outs[:4]):
        for core in range(2):
            out[:, core * half : (core + 1) * half] = a_ref[
                core, 0, :, index * half : (index + 1) * half
            ].astype(F32)
    up, down = outs[4:6]
    half = up.shape[1] // 2
    for core in range(2):
        up[:, core * half : (core + 1) * half] = b_ref[core, 0].astype(F32)
        down[core, 0] = c_ref[core, 0].astype(F32)


def widen(o_a, o_b, o_c, vec, sizes):
    shards = o_a.shape[1]
    block = lambda item: pl.BlockSpec((2, 1) + item.shape[2:], lambda i: (0, i, 0, 0))
    rows = o_a.shape[2]
    square = (shards * rows, o_a.shape[3] // 2)
    wide = (shards * rows, 2 * o_b.shape[3])
    return pl.pallas_call(
        widen_kernel,
        grid=(shards,),
        out_shape=[jax.ShapeDtypeStruct(square, F32)] * 4
        + [jax.ShapeDtypeStruct(wide, F32), jax.ShapeDtypeStruct(o_c.shape, F32)]
        + [jax.ShapeDtypeStruct((size,), F32) for size in sizes],
        in_specs=[block(o_a), block(o_b), block(o_c), pl.BlockSpec(vec.shape, lambda i: (0, 0))],
        out_specs=[pl.BlockSpec((rows, square[1]), lambda i: (i, 0))] * 4
        + [pl.BlockSpec((rows, wide[1]), lambda i: (i, 0)), block(o_c)]
        + [pl.BlockSpec((size,), lambda i: (0,)) for size in sizes],
        compiler_params=pltpu.CompilerParams(vmem_limit_bytes=VMEM_BYTES),
        name="widen",
    )(o_a, o_b, o_c, vec)


def per_device_heads(tokens, cotangent, lengths, dealing, *params):
    rows_in = tokens.shape[2]
    width = tokens.shape[3]
    rows = MB * rows_in
    weights, vectors = params[:6], params[6:]
    sizes = [item.shape[0] for item in vectors]
    x = tokens.reshape(rows, width)
    blocks = jnp.arange(HEADS, dtype=jnp.int32)
    at_block = dealing[0][:, :, None] == blocks[None, None, :]
    slot_of = jnp.sum(jnp.where(at_block, blocks[None, :, None], 0), axis=1)
    table = jnp.concatenate([lengths[0], dealing[0], slot_of], axis=1)
    query_w, key_w, value_w, kept, lse, a, output, n_low, g, do, du, dm, dh_one, da, vec = forward(
        table, x, cotangent.reshape(rows, width), weights, vectors, HEADS
    )
    grad_tokens, o_a, o_b, o_c, vec_sum = backward(
        table,
        da,
        kept,
        lse,
        x,
        a,
        n_low,
        g,
        do,
        du,
        dm,
        vec,
        dh_one,
        (query_w, key_w, value_w),
        HEADS,
    )
    grads = list(widen(o_a, o_b, o_c, vec_sum, sizes))
    grads[5] = grads[5].reshape(-1, width)
    shape = (1, MB, rows_in, width)
    return (
        (output.reshape(shape), grad_tokens.reshape(shape))
        + tuple(grads)
    )


def solution(mesh):
    placed = (
        P("wsh", None, "ctx", None),
        P("wsh", None, "ctx", None),
        P("wsh", None, None),
        P("wsh", None, None),
        P("wsh", None),
        P("wsh", None),
        P("wsh", None),
        P("wsh", None),
        P("wsh", None),
        P("wsh", None),
        P("wsh"),
        P("wsh"),
        P("wsh"),
        P("wsh"),
        P("wsh"),
        P("wsh"),
        P("wsh"),
        P("wsh"),
        P("wsh"),
    )
    by_heads = mesh.shape["ctx"] == HEADS and mesh.shape["wsh"] == 2
    return jax.shard_map(
        per_device_heads if by_heads else per_device,
        mesh=mesh,
        in_specs=placed,
        out_specs=(
            P("wsh", None, "ctx", None),
            P("wsh", None, "ctx", None),
            P("wsh", None),
            P("wsh", None),
            P("wsh", None),
            P("wsh", None),
            P("wsh", None),
            P("wsh", None),
            P("wsh"),
            P("wsh"),
            P("wsh"),
            P("wsh"),
            P("wsh"),
            P("wsh"),
            P("wsh"),
            P("wsh"),
            P("wsh"),
        ),
        check_vma=False,
    )
```

```python
import functools
import math

import jax
import jax.numpy as jnp
from jax import lax
from jax.experimental import pallas as pl
from jax.experimental.pallas import tpu as pltpu
from jax.sharding import PartitionSpec as P

HEADS = 16
BPS = 8
MB = 3
BLK = 64


EPSILON = 1e-12
NEG_FILL = -1e30


def as_sent(x):
    return jax.tree.map(lambda a: a.astype(jnp.bfloat16) if a.dtype == jnp.float32 else a, x)


def layer_norm(summed, gain_vec, shift_vec):
    row_mean = jnp.mean(summed, axis=-1, keepdims=True)
    centred = summed - row_mean
    row_var = jnp.mean(centred * centred, axis=-1, keepdims=True)
    return centred * lax.rsqrt(row_var + EPSILON) * gain_vec + shift_vec


def gelu_exact(values):
    return jax.nn.gelu(values, approximate=False)


def row_labels(dealt_order, seq_lengths):
    blocks_of_rows = jnp.repeat(dealt_order, BLK)
    within = jnp.tile(jnp.arange(BLK, dtype=jnp.int32), dealt_order.shape[0])
    seq_ids = blocks_of_rows // BPS
    places = blocks_of_rows % BPS * BLK + within
    numbers = jnp.arange(seq_lengths.shape[0], dtype=jnp.int32)
    seq_bound = jnp.sum(
        jnp.where(seq_ids[:, None] == numbers[None, :], seq_lengths[None, :], 0), axis=1
    )
    return (seq_ids, places < seq_bound)


def blockwise(carried, total_rows, step_rows, visit_block):
    return lax.fori_loop(
        0,
        total_rows // step_rows,
        lambda turn_index, running: visit_block(running, turn_index * step_rows),
        carried,
    )


def masked_scores(query_blk, key_blk, query_seq, key_seq, key_valid, scale_factor):
    allowed = (query_seq[:, None] == key_seq[None, :]) & key_valid[None, :]
    scores = (
        jnp.einsum("qhd,khd->hqk", query_blk, key_blk, preferred_element_type=jnp.float32)
        * scale_factor
    )
    return (jnp.where(allowed[None], scores, NEG_FILL), allowed[None].astype(jnp.float32))


def attention_grads(
    query_blk,
    grad_blk,
    key_blk,
    value_blk,
    query_seq,
    key_seq,
    key_valid,
    row_total,
    row_delta,
    scale_factor,
):
    scores, allowed = masked_scores(query_blk, key_blk, query_seq, key_seq, key_valid, scale_factor)
    probs = jnp.exp(scores - row_total[:, :, None]) * allowed
    grad_probs = jnp.einsum("qhd,khd->hqk", grad_blk, value_blk, preferred_element_type=jnp.float32)
    grad_scores = (probs * (grad_probs - row_delta[:, :, None])).astype(jnp.bfloat16)
    return (probs.astype(jnp.bfloat16), grad_scores)


def gather_params(params):
    return (
        lax.all_gather(params[0], "wsh", axis=0, tiled=True),
        lax.all_gather(params[1], "wsh", axis=0, tiled=True),
        lax.all_gather(params[2], "wsh", axis=0, tiled=True),
        lax.all_gather(params[3], "wsh", axis=0, tiled=True),
        lax.all_gather(params[4], "wsh", axis=0, tiled=True),
        lax.all_gather(params[5], "wsh", axis=0, tiled=True),
        lax.all_gather(params[6], "wsh", axis=0, tiled=True),
        lax.all_gather(params[7], "wsh", axis=0, tiled=True),
        lax.all_gather(params[8], "wsh", axis=0, tiled=True),
        lax.all_gather(params[9], "wsh", axis=0, tiled=True),
        lax.all_gather(params[10], "wsh", axis=0, tiled=True),
        lax.all_gather(params[11], "wsh", axis=0, tiled=True),
        lax.all_gather(params[12], "wsh", axis=0, tiled=True),
        lax.all_gather(params[13], "wsh", axis=0, tiled=True),
        lax.all_gather(params[14], "wsh", axis=0, tiled=True),
    )


def per_device(
    tokens,
    cotangent,
    lengths,
    dealing,
    w_query,
    w_key,
    w_value,
    w_out,
    w_up,
    w_down,
    b_query,
    b_value,
    b_out,
    b_up,
    b_down,
    gain_one,
    shift_one,
    gain_two,
    shift_two,
):
    params = (
        w_query,
        w_key,
        w_value,
        w_out,
        w_up,
        w_down,
        b_query,
        b_value,
        b_out,
        b_up,
        b_down,
        gain_one,
        shift_one,
        gain_two,
        shift_two,
    )
    own_rows = tokens.shape[2]
    width = tokens.shape[3]
    head_size = width // HEADS
    scale_factor = 1.0 / math.sqrt(head_size)
    my_start = lax.axis_index("ctx") * own_rows
    wsh_count = lax.axis_size("wsh")
    grads = tuple(
        (jnp.zeros((item.shape[0] * wsh_count,) + item.shape[1:], jnp.float32) for item in params)
    )
    results = []
    input_grads = []
    for micro in range(MB):
        whole = gather_params(params)
        query_weight, key_weight, value_weight, out_weight, up_weight, down_weight = whole[:6]
        (
            bias_query,
            bias_value,
            bias_out,
            bias_up,
            bias_down,
            gain_first,
            shift_first,
            gain_second,
            shift_second,
        ) = tuple((item.astype(jnp.float32) for item in whole[6:]))
        token_rows = tokens[0, micro]
        seq_all, valid_all = row_labels(dealing[0, micro], lengths[0, micro])
        my_seq = lax.dynamic_slice_in_dim(seq_all, my_start, own_rows)
        my_valid = lax.dynamic_slice_in_dim(valid_all, my_start, own_rows)
        query_low = (
            jnp.dot(token_rows, query_weight, preferred_element_type=jnp.float32) + bias_query
        ).astype(jnp.bfloat16)
        key_low = jnp.dot(token_rows, key_weight, preferred_element_type=jnp.float32).astype(
            jnp.bfloat16
        )
        value_low = (
            jnp.dot(token_rows, value_weight, preferred_element_type=jnp.float32) + bias_value
        ).astype(jnp.bfloat16)
        query_heads = query_low.reshape(own_rows, HEADS, head_size)
        my_key_heads = key_low.reshape(own_rows, HEADS, head_size)
        my_value_heads = value_low.reshape(own_rows, HEADS, head_size)
        start_state = (
            jnp.full((HEADS, own_rows), NEG_FILL, jnp.float32),
            jnp.zeros((HEADS, own_rows), jnp.float32),
            jnp.zeros((own_rows, HEADS, head_size), jnp.float32),
        )
        key_piece = lax.all_gather(key_low, "ctx", axis=0, tiled=True)
        value_piece = lax.all_gather(value_low, "ctx", axis=0, tiled=True)
        piece_rows = key_piece.shape[0]
        step_rows = math.gcd(piece_rows, 512)

        def visit_block(running, offset):
            run_max, run_sum, run_acc = running
            key_blk = lax.dynamic_slice_in_dim(key_piece, offset, step_rows).reshape(
                step_rows, HEADS, head_size
            )
            value_blk = lax.dynamic_slice_in_dim(value_piece, offset, step_rows).reshape(
                step_rows, HEADS, head_size
            )
            key_seq = lax.dynamic_slice_in_dim(seq_all, offset, step_rows)
            key_valid = lax.dynamic_slice_in_dim(valid_all, offset, step_rows)
            scores, allowed = masked_scores(
                query_heads, key_blk, my_seq, key_seq, key_valid, scale_factor
            )
            new_max = jnp.maximum(run_max, jnp.max(scores, axis=-1))
            rescale = jnp.exp(run_max - new_max)
            weights = jnp.exp(scores - new_max[:, :, None]) * allowed
            run_sum = run_sum * rescale + jnp.sum(weights, axis=-1)
            run_acc = run_acc * rescale.T[:, :, None] + jnp.einsum(
                "hqk,khd->qhd",
                weights.astype(jnp.bfloat16),
                value_blk,
                preferred_element_type=jnp.float32,
            )
            return (new_max, run_sum, run_acc)

        final_max, final_sum, final_acc = blockwise(start_state, piece_rows, step_rows, visit_block)
        attended = final_acc / final_sum.T[:, :, None]
        log_total = final_max + jnp.log(final_sum)
        attended_low = attended.reshape(own_rows, width).astype(jnp.bfloat16)
        out_proj = jnp.dot(attended_low, out_weight, preferred_element_type=jnp.float32) + bias_out
        first_sum = token_rows.astype(jnp.float32) + out_proj
        norm_one, norm_one_back = jax.vjp(layer_norm, first_sum, gain_first, shift_first)
        mlp_input = norm_one.astype(jnp.bfloat16)
        up_pre = jnp.dot(mlp_input, up_weight, preferred_element_type=jnp.float32) + bias_up
        activated, gelu_back = jax.vjp(gelu_exact, up_pre)
        activated_low = activated.astype(jnp.bfloat16)
        down_out = (
            jnp.dot(activated_low, down_weight, preferred_element_type=jnp.float32) + bias_down
        )
        result, norm_two_back = jax.vjp(layer_norm, norm_one + down_out, gain_second, shift_second)
        results.append(result.astype(jnp.bfloat16))
        grad_second, grad_gain_b, grad_shift_b = norm_two_back(
            cotangent[0, micro].astype(jnp.float32)
        )
        grad_down_low = grad_second.astype(jnp.bfloat16)
        grad_activated = jnp.einsum(
            "rd,fd->rf", grad_down_low, down_weight, preferred_element_type=jnp.float32
        )
        (grad_up_pre,) = gelu_back(grad_activated)
        grad_up_low = grad_up_pre.astype(jnp.bfloat16)
        grad_norm_one = (
            jnp.einsum("rf,df->rd", grad_up_low, up_weight, preferred_element_type=jnp.float32)
            + grad_second
        )
        grad_first, grad_gain_a, grad_shift_a = norm_one_back(grad_norm_one)
        grad_out_low = grad_first.astype(jnp.bfloat16)
        grad_att_low = jnp.einsum(
            "rd,ed->re", grad_out_low, out_weight, preferred_element_type=jnp.float32
        ).astype(jnp.bfloat16)
        grad_heads = grad_att_low.reshape(own_rows, HEADS, head_size)
        row_delta = jnp.sum(grad_heads.astype(jnp.float32) * attended, axis=-1).T
        empty_heads = jnp.zeros((own_rows, HEADS, head_size), jnp.float32)
        query_key_piece = lax.all_gather(key_low, "ctx", axis=0, tiled=True)
        query_value_piece = lax.all_gather(value_low, "ctx", axis=0, tiled=True)
        query_piece_rows = query_key_piece.shape[0]
        query_step_rows = math.gcd(query_piece_rows, 512)

        def query_visit_block(running, offset):
            key_blk = lax.dynamic_slice_in_dim(query_key_piece, offset, query_step_rows).reshape(
                query_step_rows, HEADS, head_size
            )
            value_blk = lax.dynamic_slice_in_dim(
                query_value_piece, offset, query_step_rows
            ).reshape(query_step_rows, HEADS, head_size)
            key_seq = lax.dynamic_slice_in_dim(seq_all, offset, query_step_rows)
            key_valid = lax.dynamic_slice_in_dim(valid_all, offset, query_step_rows)
            probs_low, grad_scores = attention_grads(
                query_heads,
                grad_heads,
                key_blk,
                value_blk,
                my_seq,
                key_seq,
                key_valid,
                log_total,
                row_delta,
                scale_factor,
            )
            return running + jnp.einsum(
                "hqk,khd->qhd", grad_scores, key_blk, preferred_element_type=jnp.float32
            )

        grad_query_sum = blockwise(
            empty_heads, query_piece_rows, query_step_rows, query_visit_block
        )
        total_all, delta_all = (
            lax.all_gather(log_total.T, "ctx", axis=0, tiled=True),
            lax.all_gather(row_delta.T, "ctx", axis=0, tiled=True),
        )
        query_piece = lax.all_gather(query_low, "ctx", axis=0, tiled=True)
        grad_piece = lax.all_gather(grad_att_low, "ctx", axis=0, tiled=True)
        key_piece_rows = query_piece.shape[0]
        key_step_rows = math.gcd(key_piece_rows, 512)

        def key_visit_block(running, offset):
            grad_key_run, grad_value_run = running
            query_blk = lax.dynamic_slice_in_dim(query_piece, offset, key_step_rows).reshape(
                key_step_rows, HEADS, head_size
            )
            grad_blk = lax.dynamic_slice_in_dim(grad_piece, offset, key_step_rows).reshape(
                key_step_rows, HEADS, head_size
            )
            total_blk = lax.dynamic_slice_in_dim(total_all, offset, key_step_rows)
            delta_blk = lax.dynamic_slice_in_dim(delta_all, offset, key_step_rows)
            query_seq = lax.dynamic_slice_in_dim(seq_all, offset, key_step_rows)
            probs_low, grad_scores = attention_grads(
                query_blk,
                grad_blk,
                my_key_heads,
                my_value_heads,
                query_seq,
                my_seq,
                my_valid,
                total_blk.T,
                delta_blk.T,
                scale_factor,
            )
            grad_key_run = grad_key_run + jnp.einsum(
                "hqk,qhd->khd", grad_scores, query_blk, preferred_element_type=jnp.float32
            )
            grad_value_run = grad_value_run + jnp.einsum(
                "hqk,qhd->khd", probs_low, grad_blk, preferred_element_type=jnp.float32
            )
            return (grad_key_run, grad_value_run)

        grad_key_sum, grad_value_sum = blockwise(
            (empty_heads, empty_heads), key_piece_rows, key_step_rows, key_visit_block
        )
        grad_key_flat = grad_key_sum.reshape(own_rows, width)
        grad_value_flat = grad_value_sum.reshape(own_rows, width)
        grad_query_low = (
            (grad_query_sum * scale_factor).reshape(own_rows, width).astype(jnp.bfloat16)
        )
        grad_key_low = (grad_key_flat * scale_factor).astype(jnp.bfloat16)
        grad_value_low = grad_value_flat.astype(jnp.bfloat16)
        terms = (
            jnp.einsum("rd,re->de", token_rows, grad_query_low, preferred_element_type=jnp.float32),
            jnp.einsum("rd,re->de", token_rows, grad_key_low, preferred_element_type=jnp.float32),
            jnp.einsum("rd,re->de", token_rows, grad_value_low, preferred_element_type=jnp.float32),
            jnp.einsum("rd,re->de", attended_low, grad_out_low, preferred_element_type=jnp.float32),
            jnp.einsum("rd,rf->df", mlp_input, grad_up_low, preferred_element_type=jnp.float32),
            jnp.einsum(
                "rf,rd->fd", activated_low, grad_down_low, preferred_element_type=jnp.float32
            ),
            jnp.sum(grad_query_low.astype(jnp.float32), axis=0),
            jnp.sum(grad_value_low.astype(jnp.float32), axis=0),
            jnp.sum(grad_out_low.astype(jnp.float32), axis=0),
            jnp.sum(grad_up_low.astype(jnp.float32), axis=0),
            jnp.sum(grad_down_low.astype(jnp.float32), axis=0),
            grad_gain_a,
            grad_shift_a,
            grad_gain_b,
            grad_shift_b,
        )
        grads = tuple((total_now + fresh for total_now, fresh in zip(grads, terms)))
        grad_rows = (
            grad_first
            + jnp.einsum(
                "re,de->rd", grad_query_low, query_weight, preferred_element_type=jnp.float32
            )
            + jnp.einsum("re,de->rd", grad_key_low, key_weight, preferred_element_type=jnp.float32)
            + jnp.einsum(
                "re,de->rd", grad_value_low, value_weight, preferred_element_type=jnp.float32
            )
        )
        input_grads.append(grad_rows.astype(jnp.bfloat16))
    shards = jax.tree.map(
        lambda part: part.astype(jnp.float32),
        lax.psum_scatter(as_sent(grads), "wsh", scatter_dimension=0, tiled=True),
    )
    summed = jax.tree.map(lambda part: part.astype(jnp.float32), lax.psum(as_sent(shards), "ctx"))
    return (jnp.stack(results)[None], jnp.stack(input_grads)[None]) + tuple(summed)


MESH_IDS = pl.DeviceIdType.MESH
F32 = jnp.float32
BF16 = jnp.bfloat16
HD = 64
VMEM_BYTES = 60 * 1024 * 1024


def flip(index, bit):
    return index + bit * (1 - 2 * lax.rem(lax.div(index, bit), 2))


def bit_of(index, bit):
    return lax.rem(lax.div(index, bit), 2)


def greet(peers):
    barrier = pltpu.get_barrier_semaphore()
    for peer in peers:
        pl.semaphore_signal(barrier, inc=1, device_id=peer, device_id_type=MESH_IDS)
    pl.semaphore_wait(barrier, len(peers))


def send(src, dst, send_sem, recv_sem, peer):
    copy = pltpu.make_async_remote_copy(
        src_ref=src,
        dst_ref=dst,
        send_sem=send_sem,
        recv_sem=recv_sem,
        device_id=peer,
        device_id_type=MESH_IDS,
    )
    copy.start()
    return copy


SEQS = HEADS // BPS


def plane_peers(c, w, count):
    return [(lax.rem(c + step, count), w) for step in range(1, count)]


def pack_three(first, second, third, row, pair, out):
    cols = pl.ds(pair * 128, 128)
    a, b, d = (ref[pl.ds(row, BLK), cols] for ref in (first, second, third))
    half = BLK // 2
    for head in range(2):
        lane = slice(head * HD, head * HD + HD)
        out[2 * pair + head, 0:BLK, :] = jnp.concatenate([a[:, lane], b[:, lane]], axis=1)
        out[2 * pair + head, BLK : BLK + half, :] = jnp.concatenate(
            [d[:half, lane], d[half:, lane]], axis=1
        )


def unpack_fold(block):
    return jnp.concatenate([block[:, :HD], block[:, HD:]], axis=0)


def fold(rows):
    half = rows.shape[0] // 2
    return jnp.concatenate([rows[:half], rows[half:]], axis=1)


def all_bytes(ref, sem, peers):
    view = ref.at[pl.ds(0, peers)]
    return pltpu.make_async_copy(view, view, sem)


def norm_parts(summed):
    row_mean = jnp.mean(summed, axis=-1, keepdims=True)
    centred = summed - row_mean
    row_var = jnp.mean(centred * centred, axis=-1, keepdims=True)
    scale = lax.rsqrt(row_var + EPSILON)
    return centred * scale, scale


def norm_back(grad, unit, scale, gain):
    inner = grad * gain
    mean_one = jnp.mean(inner, axis=-1, keepdims=True)
    mean_two = jnp.mean(inner * unit, axis=-1, keepdims=True)
    return scale * (inner - mean_one - unit * mean_two)


def dot_minor(a, b):
    return lax.dot_general(a, b, (((1,), (1,)), ((), ())), preferred_element_type=F32)


ROW_OUT, ROW_UP, ROW_DOWN, ROW_GAIN_ONE, ROW_SHIFT_ONE, ROW_GAIN_TWO, ROW_SHIFT_TWO = 2, 3, 7, 8, 9, 10, 11


SQUARE, PAIR_Y, PAIR_Z, ALONE = (8, "yz"), (4, "y"), (4, "z"), (2, "")
WAYS = (
    SQUARE, SQUARE, SQUARE, SQUARE, PAIR_Y, SQUARE, PAIR_Z, PAIR_Y, ALONE, PAIR_Z, PAIR_Y, ALONE,
)
SEND_ORDER = (2, 0, 1, 3, 5, 7, 4, 6, 9, 10, 8, 11)
FORWARD_SCHEDULE = (
    ("second", 2), ("second", 0), ("third", 2), ("second", 1), ("third", 0), ("fourth", 2),
    ("third", 1), ("second", 3), ("second", 5), ("fourth", 0), ("project", 2), ("fourth", 1),
    ("project", 0), ("project", 1), ("pack", 0), ("second", 7), ("third", 3), ("second", 4),
    ("second", 6), ("att", 0), ("fourth", 7), ("third", 5), ("fourth", 3), ("att", 1), ("att",
    2), ("fourth", 5), ("fourth", 8), ("second", 10), ("second", 9), ("fourth", 6), ("fourth",
    4), ("rows", 0), ("out", 0), ("hidden", 0), ("fourth", 10), ("hidden", 1), ("hidden", 2),
    ("fourth", 9), ("hidden", 3), ("hidden", 4), ("fourth", 11), ("hidden", 5), ("hidden", 6),
    ("hidden", 7),
)


def weight_plan(shards):
    unit = shards[0].shape[0] * shards[0].shape[1]
    plan = []
    for index, (rows, cols) in enumerate(shard.shape for shard in shards):
        parts = max(1, rows * cols // unit)
        for part in range(parts):
            plan.append((index, part * (rows // parts), rows // parts, WAYS[len(plan)]))
    return plan


def forward_kernel(heads, plan, n_weights, n_vectors, *refs):
    table_ref, x_ref, cot_ref = refs[:3]
    refs = refs[3:]
    shards, vectors = refs[:n_weights], refs[n_weights : n_weights + n_vectors]
    refs = refs[n_weights + n_vectors :]
    wholes, kept_ref, lse_ref, a_ref = refs[:3], *refs[3:6]
    out_ref, n_ref, g_ref, do_ref, du_ref, dm_ref, dh_ref, da_ref, vec_ref = refs[6:15]
    refs = refs[15:]
    near, refs = refs[:n_weights], refs[n_weights:]
    small, small_in, small_whole, bias, q_ref, k_ref, v_ref = refs[:7]
    slope, n_full, unit, total = refs[7:11]
    refs = refs[11:]
    in_buf = refs[:MB]
    out_buf, back_out, back_in, q_s, k_s, v_s, a_s = refs[MB : 7 + MB]
    (
        w_send,
        w_recv,
        small_sems,
        local_sem,
        stage_sem,
        send_sem,
        recv_sem,
        back_send,
        back_recv,
        keep_sem,
    ) = refs[7 + MB :]
    c, w = lax.axis_index("ctx"), lax.axis_index("wsh")
    o = 1 - w
    by_x, by_y, by_z, by_core = (c, o), (flip(c, 2), w), (flip(c, 4), w), (flip(c, 1), w)
    core, y, z = bit_of(c, 1), bit_of(c, 2), bit_of(c, 4)
    peers = plane_peers(c, w, heads)
    staged = []
    for index, shard in enumerate(shards):
        rows = shard.shape[0]
        spot = pl.ds(pl.multiple_of(w * rows, rows), rows)
        copy = pltpu.make_async_copy(shard, near[index].at[spot], stage_sem.at[index])
        copy.start()
        staged.append(copy)
    line, lanes = 0, small.shape[1]
    for vector in vectors:
        for first in range(0, vector.shape[0], lanes):
            piece = vector[pl.ds(first, lanes)].astype(F32)
            small[line : line + 1, :] = piece.reshape(1, lanes)
            line += 1
    greet(peers + [by_x])
    small_sent = send(small, small_in, small_sems.at[0], small_sems.at[1], by_x)

    def part(chunk, side, piece, start, count):
        tensor, first, rows, way = plan[chunk]
        half = shards[tensor].shape[0]
        at = side * half + first + piece * (rows // way[0]) + start
        return near[tensor].at[pl.ds(pl.multiple_of(at, 8), count)]

    steps = {}

    def sem(kind, chunk):
        return w_send.at[kind, chunk], w_recv.at[kind, chunk]

    def own_piece(way):
        return {
            SQUARE: core * 4 + z * 2 + y,
            PAIR_Y: core * 2 + y,
            PAIR_Z: core * 2 + z,
            ALONE: core,
        }[way]

    for chunk in SEND_ORDER:
        tensor, first, rows, way = plan[chunk]
        size, mine = rows // way[0], own_piece(way)
        src = shards[tensor].at[pl.ds(pl.multiple_of(first + mine * size, 8), size)]
        steps[chunk, 0] = send(src, part(chunk, w, mine, 0, size), *sem(0, chunk), by_x)

    def second(chunk):
        _, _, rows, way = plan[chunk]
        steps[chunk, 0].wait_recv()
        ref = part(chunk, o, own_piece(way), 0, rows // way[0])
        for name in way[1]:
            kind, peer = {"y": (1, by_y), "z": (2, by_z)}[name]
            steps[chunk, kind] = send(ref, ref, *sem(kind, chunk), peer)

    def third(chunk):
        _, _, rows, way = plan[chunk]
        size = rows // way[0]
        steps[chunk, 1].wait_recv()
        steps[chunk, 2].wait_recv()
        ref = part(chunk, o, core * 4 + (1 - z) * 2 + y, 0, size // 2)
        steps[chunk, 3] = send(ref, ref, *sem(3, chunk), by_y)
        ref = part(chunk, o, core * 4 + z * 2 + (1 - y), size // 2, size // 2)
        steps[chunk, 4] = send(ref, ref, *sem(4, chunk), by_z)

    def fourth(chunk):
        _, _, rows, way = plan[chunk]
        for kind in {SQUARE: (3, 4), PAIR_Y: (1,), PAIR_Z: (2,), ALONE: (0,)}[way]:
            steps[chunk, kind].wait_recv()
        ref = part(chunk, o, core * (way[0] // 2), 0, rows // 2)
        steps[chunk, 5] = send(ref, ref, *sem(5, chunk), by_core)

    width = x_ref.shape[1]
    step = 256
    projected = []

    def project(index):
        if not projected:
            small_sent.wait()
            small_whole[w] = small[...]
            small_whole[o] = small_in[...]
            for side in range(2):
                for row in range(2):
                    bias[row : row + 1, side * lanes : (side + 1) * lanes] = small_whole[
                        side, row : row + 1, :
                    ]
        projected.append(index)
        staged[index].wait()
        steps[index, 5].wait_recv()
        weight, out = near[index], (q_ref, k_ref, v_ref)[index]

        def some_columns(turn, carry):
            cols = pl.ds(pl.multiple_of(turn * step, step), step)
            product = jnp.dot(x_ref[...], weight[:, cols], preferred_element_type=F32)
            if index != 1:
                product = product + bias[index // 2 : index // 2 + 1, cols]
            out[:, cols] = product.astype(BF16)
            return carry

        lax.fori_loop(0, width // step, some_columns, 0)
        pltpu.make_async_copy(near[index], wholes[index], local_sem.at[index]).start()

    def pack(_):
        for m in range(MB):
            for pair in range(heads // 2):
                pack_three(q_ref, k_ref, v_ref, m * BLK, pair, out_buf.at[m])
            for peer in peers:
                send(
                    out_buf.at[m, peer[0]], in_buf[m].at[c], send_sem.at[m], recv_sem.at[m], peer
                )
            in_buf[m][c] = out_buf[m, c]

    blocks = heads
    span = BPS * BLK

    def attention(m):
        all_bytes(in_buf[m], recv_sem.at[m], heads - 1).wait()
        pltpu.make_async_copy(in_buf[m], kept_ref.at[m], keep_sem.at[m]).start()
        for b in range(blocks):
            got = in_buf[m][table_ref[m, SEQS + blocks + b]]
            q_s[b * BLK : (b + 1) * BLK, :] = got[:BLK, :HD]
            k_s[b * BLK : (b + 1) * BLK, :] = got[:BLK, HD:]
            v_s[b * BLK : (b + 1) * BLK, :] = unpack_fold(got[BLK:])

        def one_sequence(s, carry):
            rows = pl.ds(pl.multiple_of(s * span, span), span)
            scores = lax.dot_general(
                k_s[rows, :], q_s[rows, :], (((1,), (1,)), ((), ())), preferred_element_type=F32
            ) * (1.0 / math.sqrt(HD))
            place = lax.broadcasted_iota(jnp.int32, scores.shape, 0)
            scores = jnp.where(place < table_ref[m, s], scores, NEG_FILL)
            top = jnp.max(scores, axis=0, keepdims=True)
            weights = jnp.exp(scores - top)
            summed = jnp.sum(weights, axis=0, keepdims=True)
            out_t = lax.dot_general(
                v_s[rows, :],
                weights.astype(BF16),
                (((0,), (0,)), ((), ())),
                preferred_element_type=F32,
            )
            a_s[pl.ds(s * BPS, BPS)] = (out_t / summed).T.reshape(BPS, BLK, HD)
            lse_ref[pl.ds(m * (blocks // BPS) + s, 1), :] = top + jnp.log(summed)
            return carry

        lax.fori_loop(0, blocks // BPS, one_sequence, 0)
        for t in range(blocks):
            back_out[m, t] = fold(a_s[table_ref[m, SEQS + t]]).astype(BF16)
        for peer in peers:
            send(
                back_out.at[m, peer[0]], back_in.at[m, c], back_send.at[m], back_recv.at[m], peer
            )
        back_in[m, c] = back_out[m, c]

    def come_back(_):
        for m in range(MB):
            all_bytes(back_in.at[m], back_recv.at[m], heads - 1).wait()
            for pair in range(heads // 2):
                a_ref[m * BLK : (m + 1) * BLK, pair * 128 : (pair + 1) * 128] = jnp.concatenate(
                    [unpack_fold(back_in[m, 2 * pair]), unpack_fold(back_in[m, 2 * pair + 1])],
                    axis=1,
                )

    def line_of(row):
        return jnp.concatenate(
            [small_whole[0, row : row + 1, :], small_whole[1, row : row + 1, :]], axis=1
        )

    def keep(row, values):
        summed = jnp.sum(values, axis=0, keepdims=True)
        for side in range(2):
            vec_ref[side, row : row + 1, :] = summed[:, side * lanes : (side + 1) * lanes]

    out_w, up_w, down_w = near[3:]
    chunks_of = {t: [i for i, item in enumerate(plan) if item[0] == t] for t in range(n_weights)}

    def arrived(tensor, chunks):
        for chunk in chunks:
            steps[chunk, 5].wait_recv()

    def out_project(_):
        staged[3].wait()
        arrived(3, chunks_of[3])
        h_one = x_ref[...].astype(F32) + (
            jnp.dot(a_ref[...], out_w[...], preferred_element_type=F32) + line_of(ROW_OUT)
        )
        unit_one, scale_one = norm_parts(h_one)
        unit[...] = unit_one
        n_one = unit_one * line_of(ROW_GAIN_ONE) + line_of(ROW_SHIFT_ONE)
        n_full[...] = n_one
        n_ref[...] = n_one.astype(BF16)
        total[...] = jnp.zeros_like(total)
        kept_scale.append(scale_one)

    kept_scale = []
    hidden = g_ref.shape[1]
    hidden_steps = hidden // lanes
    per_half = hidden_steps // 2

    def hidden_at(turn):
        j = lax.rem(w * per_half + turn, hidden_steps)
        cols = pl.ds(pl.multiple_of(j * lanes, lanes), lanes)
        return cols, lax.div(j, per_half), pl.ds(ROW_UP + lax.rem(j, per_half), 1)

    def hidden_up(turn):
        if turn == 0:
            staged[4].wait()
            arrived(4, chunks_of[4])
            staged[5].wait()
        elif turn >= per_half:
            share = len(chunks_of[5]) // per_half
            first = (turn - per_half) * share
            arrived(5, chunks_of[5][first : first + share])
        cols, side, row = hidden_at(turn)
        u = jnp.dot(n_ref[...], up_w[:, cols], preferred_element_type=F32) + small_whole[side, row, :]
        below = 0.5 * (1.0 + lax.erf(u * math.sqrt(0.5)))
        slope[:, cols] = below + u * jnp.exp(-0.5 * u * u) * (1.0 / math.sqrt(2.0 * math.pi))
        g = (u * below).astype(BF16)
        g_ref[:, cols] = g
        total[...] += jnp.dot(g, down_w[cols, :], preferred_element_type=F32)

    acts = {
        "second": second,
        "third": third,
        "fourth": fourth,
        "project": project,
        "pack": pack,
        "att": attention,
        "rows": come_back,
        "out": out_project,
        "hidden": hidden_up,
    }
    for name, value in FORWARD_SCHEDULE:
        acts[name](value)

    h_two = n_full[...] + (total[...] + line_of(ROW_DOWN))
    unit_two, scale_two = norm_parts(h_two)
    out_ref[...] = (unit_two * line_of(ROW_GAIN_TWO) + line_of(ROW_SHIFT_TWO)).astype(BF16)
    cot = cot_ref[...].astype(F32)
    keep(ROW_GAIN_TWO, cot * unit_two)
    keep(ROW_SHIFT_TWO, cot)
    dh_two = norm_back(cot, unit_two, scale_two, line_of(ROW_GAIN_TWO))
    dm = dh_two.astype(BF16)
    dm_ref[...] = dm
    keep(ROW_DOWN, dm.astype(F32))
    total[...] = dh_two
    for turn in range(hidden_steps):
        cols, side, row = hidden_at(turn)
        du = (slope[:, cols] * dot_minor(dm_ref[...], down_w[cols, :])).astype(BF16)
        du_ref[:, cols] = du
        vec_ref[side, row, :] = jnp.sum(du.astype(F32), axis=0, keepdims=True)
        total[...] += dot_minor(du, up_w[:, cols])
    dn = total[...]
    keep(ROW_GAIN_ONE, dn * unit[...])
    keep(ROW_SHIFT_ONE, dn)
    dh_one = norm_back(dn, unit[...], kept_scale[0], line_of(ROW_GAIN_ONE))
    dh_ref[...] = dh_one
    do = dh_one.astype(BF16)
    do_ref[...] = do
    keep(ROW_OUT, do.astype(F32))
    da_ref[...] = dot_minor(do, out_w[...]).astype(BF16)
    for side in range(2):
        vec_ref[side, 0:ROW_OUT, :] = jnp.zeros((ROW_OUT, lanes), F32)

    for m in range(MB):
        all_bytes(out_buf.at[m], send_sem.at[m], heads - 1).wait()
        all_bytes(back_out.at[m], back_send.at[m], heads - 1).wait()
        pltpu.make_async_copy(in_buf[m], kept_ref.at[m], keep_sem.at[m]).wait()
    for flight in steps.values():
        flight.wait_send()
    for index in range(3):
        pltpu.make_async_copy(near[index], wholes[index], local_sem.at[index]).wait()


def forward(table, x, cot, shards, vectors, heads):
    plan = weight_plan(shards)
    count = len(shards)
    anywhere, vmem = pl.BlockSpec(memory_space=pl.ANY), pl.BlockSpec(memory_space=pltpu.VMEM)
    smem = pl.BlockSpec(memory_space=pltpu.SMEM)
    rows, width = x.shape
    hidden = shards[4].shape[1]
    pack_rows = BLK + BLK // 2
    span = BPS * BLK
    lanes = min(item.shape[0] for item in vectors)
    lines = sum(item.shape[0] for item in vectors) // lanes
    whole = lambda s: (2 * s.shape[0],) + s.shape[1:]
    low = lambda cols: jax.ShapeDtypeStruct((rows, cols), BF16)
    full = lambda cols: pltpu.VMEM((rows, cols), F32)
    sems = lambda *dims: pltpu.SemaphoreType.DMA(dims)
    return pl.pallas_call(
        functools.partial(forward_kernel, heads, plan, count, len(vectors)),
        out_shape=[jax.ShapeDtypeStruct(whole(s), s.dtype) for s in shards[:3]]
        + [
            jax.ShapeDtypeStruct((MB, heads, pack_rows, 128), BF16),
            jax.ShapeDtypeStruct((8, span), F32),
            low(width),
            low(width),
            low(width),
            low(hidden),
            low(width),
            low(hidden),
            low(width),
            jax.ShapeDtypeStruct((rows, width), F32),
            low(width),
            jax.ShapeDtypeStruct((2, lines, lanes), F32),
        ],
        in_specs=[smem, vmem, vmem] + [anywhere] * count + [vmem] * len(vectors),
        out_specs=[anywhere] * 4 + [vmem] * 11,
        scratch_shapes=[pltpu.VMEM(whole(s), s.dtype) for s in shards]
        + [pltpu.VMEM((lines, lanes), F32)] * 2
        + [pltpu.VMEM((2, lines, lanes), F32), pltpu.VMEM((2, width), F32)]
        + [pltpu.VMEM((rows, width), BF16)] * 3
        + [full(hidden), full(width), full(width), full(width)]
        + [pltpu.VMEM((heads, pack_rows, 128), BF16)] * MB
        + [
            pltpu.VMEM((MB, heads, pack_rows, 128), BF16),
            pltpu.VMEM((MB, heads, BLK // 2, 128), BF16),
            pltpu.VMEM((MB, heads, BLK // 2, 128), BF16),
            pltpu.VMEM((heads * BLK, HD), BF16),
            pltpu.VMEM((heads * BLK, HD), BF16),
            pltpu.VMEM((heads * BLK, HD), BF16),
            pltpu.VMEM((heads, BLK, HD), F32),
        ]
        + [sems(6, len(plan)), sems(6, len(plan)), sems(2), sems(3), sems(count)]
        + [sems(MB)] * 5,
        compiler_params=pltpu.CompilerParams(
            collective_id=1, has_side_effects=True, vmem_limit_bytes=VMEM_BYTES
        ),
        name="forward",
    )(table, x, cot, *shards, *vectors)


ORDERS = (
    ("yxzZ", "xyzZ", "xyzZ", "xyzZ"),
    ("xzyZ", "xyzZ", "yxzZ", "zxyZ"),
    ("yZz", "yzZ", "yZz", "zyZ"),
)
PIECES = len(ORDERS[0])
SCHEDULE = (
    "up", 0, 1, (1, 2), 2, "down", "back", (2, 0), (1, 0), (2, 3), "qkv", (2, 1), (1, 3),
    (2, 2), (1, 1), (1, 2), (2, 0), (2, 1), (1, 0), (2, 3), "vec", (2, 2), (2, 0), (2, 1),
    (2, 2), (1, 2), (0, 1), (2, 1), (2, 3), (1, 2), (2, 2), (2, 1), (0, 0), "vec", (0, 2),
    (1, 0), (2, 0), (1, 2), (2, 3), (0, 1), (1, 1), (0, 3), (2, 1), (0, 2), (0, 1), (1, 1),
    "vec", (1, 3), (0, 2), (0, 3), (2, 0), (1, 1), (0, 2), (0, 0), (1, 2), (2, 2), (0, 3),
    (1, 1), (1, 3), (0, 0), "vec", (0, 1), (1, 2), (0, 2), (0, 3), (1, 1), (1, 0), (0, 1),
    (0, 0), (2, 0), (0, 2), (0, 3), (1, 3), (2, 3), (0, 1), (1, 3), "vec", (1, 1), (0, 0),
    (0, 2), (1, 0), (0, 3), (1, 3), (1, 0), (2, 3), (0, 0), (0, 3), "rows", (1, 3), (0, 1),
    (2, 2), (1, 0), (0, 0),
)
KEYS = tuple((part, piece) for part in range(3) for piece in range(PIECES))


def landing_shapes(order, shape):
    shards, sides, shapes = 8, shape[0], []
    for name in order:
        if name == "x":
            sides = 1
        else:
            shards //= 2
        shapes.append((sides, shards, shape[2] // PIECES, shape[3]))
    return shapes


def dot_t(a, b):
    return lax.dot_general(a, b, (((0,), (0,)), ((), ())), preferred_element_type=F32)


def lanes_at(first, size):
    return pl.ds(pl.multiple_of(first, 128), size)


def backward_kernel(heads, *refs):
    table_ref, da_ref, kept_ref, lse_ref = refs[:4]
    x_ref, a_ref, n_ref, g_ref, do_ref, du_ref, dm_ref, vec_ref, dh_ref = refs[4:13]
    weights = refs[13:16]
    rows_out, o_a, o_b, o_c, vec_out = refs[16:21]
    refs = refs[21:]
    in_buf = refs[:MB]
    out_buf, back_out, back_in, q_s, k_s, v_s, a_s, dq_s, dk_s, dv_s = refs[MB : MB + 10]
    refs = refs[MB + 10 :]
    dq_ref, dk_ref, dv_ref, m_x, m_a, m_n, m_do, m_du, m_dqkv, m_g, m_dm = refs[:11]
    far_g, far_dm, cross_g, cross_dm = refs[11:15]
    near, (vec_s, v_recv, v_sum, s_a, s_b, s_c) = refs[15:18], refs[18:24]
    refs = refs[24:]
    r_bufs = {}
    for part, piece in KEYS:
        size = len(ORDERS[part][piece])
        r_bufs[part, piece], refs = refs[:size], refs[size:]
    (
        send_sem,
        recv_sem,
        back_send,
        back_recv,
        mate_send,
        mate_recv,
        near_sem,
        rs_send,
        rs_recv,
        ag_send,
        ag_recv,
        own_sem,
        v_send_sem,
        v_recv_sem,
    ) = refs
    c, x = lax.axis_index("ctx"), lax.axis_index("wsh")
    core, y, z, zz = bit_of(c, 1), bit_of(c, 2), bit_of(c, 4), bit_of(c, 8)
    by_core = (flip(c, 1), x)
    by = {"x": (c, 1 - x), "y": (flip(c, 2), x), "z": (flip(c, 4), x), "Z": (flip(c, 8), x)}
    bits = {"y": y, "z": z, "Z": zz}
    peers = plane_peers(c, x, heads)
    blocks, span = heads, BPS * BLK
    width, hidden = da_ref.shape[1], g_ref.shape[1]
    for index, weight in enumerate(weights):
        pltpu.make_async_copy(weight, near[index], near_sem.at[index]).start()
    by_cross = (flip(c, 1), 1 - x)
    greet(peers + [by["x"], by_cross])

    for m in range(MB):
        row = slice(m * BLK, (m + 1) * BLK)
        for pair in range(heads // 2):
            both = da_ref[row, pair * 128 : (pair + 1) * 128]
            for head in range(2):
                out_buf[m, 2 * pair + head] = fold(both[:, head * HD : (head + 1) * HD])
        for peer in peers:
            send(out_buf.at[m, peer[0]], in_buf[m].at[c], send_sem.at[m], recv_sem.at[m], peer)
        in_buf[m][c] = out_buf[m, c]

    shared = {}

    def share(name, src, dst, peer=by_core):
        index = len(shared)
        shared[name] = send(src, dst, mate_send.at[index], mate_recv.at[index], peer)

    other = 1 - core
    quarter = hidden // 4

    def hidden_rows(side, which):
        return g_ref.at[:, lanes_at(side * 2 * quarter + which * quarter, quarter)]

    share("far_g", hidden_rows(1 - x, core), far_g, by["x"])
    share("far_dm", dm_ref, far_dm, by["x"])
    share("cross_g", hidden_rows(1 - x, other), cross_g, by_cross)
    share("n", n_ref, m_n)
    share("du", du_ref.at[:, lanes_at(other * (hidden // 2), hidden // 2)], m_du)
    share("g", hidden_rows(x, other), m_g)
    share("dm", dm_ref, m_dm)
    share("a", a_ref, m_a)
    share("do", do_ref.at[:, lanes_at(other * (width // 2), width // 2)], m_do)
    share("x", x_ref, m_x)

    sums, outs = (s_a, s_b, s_c), (o_a, o_b, o_c)
    wide = 512

    def tile(pairs, out, first, count):
        def body(turn, carry):
            at = turn * wide
            total = sum(dot_t(lhs[...], rhs[:, lanes_at(col + at, wide)]) for lhs, rhs, col in pairs)
            cols = lanes_at(first + at, wide)
            out[..., cols] = total.astype(BF16).reshape(out.shape[:-1] + (wide,))
            return carry

        lax.fori_loop(0, count, body, 0)

    def grads_up():
        shared["n"].wait_recv()
        shared["du"].wait_recv()
        half = hidden // 2
        tile(((n_ref, du_ref, core * half), (m_n, m_du, 0)), s_b, 0, half // wide)

    def grads_down():
        shared["far_dm"].wait_recv()
        share("cross_dm", far_dm, cross_dm)
        for name in ("g", "dm", "far_g", "cross_g", "cross_dm"):
            shared[name].wait_recv()
        pairs = ((hidden_rows(x, core), dm_ref, 0), (m_g, m_dm, 0))
        pairs += ((far_g, far_dm, 0), (cross_g, cross_dm, 0))
        tile(pairs, s_c.at[0], 0, width // wide)

    def grads_qkv():
        half = width // 2
        for name in ("a", "do", "x", "dq", "dk", "dv"):
            shared[name].wait_recv()
        tile(((a_ref, do_ref, core * half), (m_a, m_do, 0)), s_a, 3 * half, half // wide)
        for index, ref in enumerate((dq_ref, dk_ref, dv_ref)):
            pairs = ((x_ref, ref, core * half), (m_x, m_dqkv, index * half))
            tile(pairs, s_a, index * half, half // wide)

    def attention(m):
        all_bytes(in_buf[m], recv_sem.at[m], heads - 1).wait()
        for b in range(blocks):
            slot = table_ref[m, SEQS + blocks + b]
            got = kept_ref[m, slot]
            rows = slice(b * BLK, (b + 1) * BLK)
            q_s[rows, :] = got[:BLK, :HD]
            k_s[rows, :] = got[:BLK, HD:]
            v_s[rows, :] = unpack_fold(got[BLK:])
            a_s[rows, :] = unpack_fold(in_buf[m][slot])

        def one_sequence(s, carry):
            rows = pl.ds(pl.multiple_of(s * span, span), span)
            qq, kk, vv, dd = q_s[rows, :], k_s[rows, :], v_s[rows, :], a_s[rows, :]
            scale = 1.0 / math.sqrt(HD)
            minor = (((1,), (1,)), ((), ()))
            scores = lax.dot_general(kk, qq, minor, preferred_element_type=F32) * scale
            spot = lax.broadcasted_iota(jnp.int32, scores.shape, 0)
            total = lse_ref[pl.ds(m * (blocks // BPS) + s, 1), :]
            probs = jnp.exp(jnp.where(spot < table_ref[m, s], scores - total, NEG_FILL))
            dp = lax.dot_general(vv, dd, minor, preferred_element_type=F32)
            both = probs * dp
            delta = jnp.sum(both, axis=0, keepdims=True)
            ds = (both - probs * delta).astype(BF16)
            here, split = pl.ds(s * BPS, BPS), (BPS, BLK, HD)
            dv = jnp.dot(probs.astype(BF16), dd, preferred_element_type=F32)
            dv_s[here] = dv.reshape(split)
            dk_s[here] = (jnp.dot(ds, qq, preferred_element_type=F32) * scale).reshape(split)
            dq_s[here] = (dot_t(kk, ds).T * scale).reshape(split)
            return carry

        lax.fori_loop(0, blocks // BPS, one_sequence, 0)
        for t in range(blocks):
            at = table_ref[m, SEQS + t]
            back_out[m, t, 0:BLK, :] = jnp.concatenate([dq_s[at], dk_s[at]], axis=1).astype(BF16)
            back_out[m, t, BLK:, :] = fold(dv_s[at]).astype(BF16)
        for peer in peers:
            send(
                back_out.at[m, peer[0]], back_in.at[m, c], back_send.at[m], back_recv.at[m], peer
            )
        back_in[m, c] = back_out[m, c]

    vec_peers = (by["x"], by["y"], by["z"], by["Z"], by_core)
    vec_steps = []

    def vec_send(src):
        step = len(vec_steps)
        vec_steps.append(
            send(
                src, v_recv.at[step], v_send_sem.at[step], v_recv_sem.at[step], vec_peers[step]
            )
        )

    def vec_next():
        step = len(vec_steps) - 1
        vec_steps[step].wait_recv()
        before = vec_s[x] if step == 0 else v_sum[step - 1]
        v_sum[step] = before + v_recv[step]
        if step + 1 < len(vec_peers):
            vec_send(v_sum.at[step])

    def come_back():
        for m in range(MB):
            all_bytes(back_in.at[m], back_recv.at[m], heads - 1).wait()
            row = slice(m * BLK, (m + 1) * BLK)
            for pair in range(heads // 2):
                lanes = slice(pair * 128, (pair + 1) * 128)
                one, two = back_in[m, 2 * pair], back_in[m, 2 * pair + 1]
                dq_ref[row, lanes] = jnp.concatenate([one[:BLK, :HD], two[:BLK, :HD]], axis=1)
                dk_ref[row, lanes] = jnp.concatenate([one[:BLK, HD:], two[:BLK, HD:]], axis=1)
                dv_ref[row, lanes] = jnp.concatenate(
                    [unpack_fold(one[BLK:]), unpack_fold(two[BLK:])], axis=1
                )
        half = width // 2
        for index, (name, ref) in enumerate((("dq", dq_ref), ("dk", dk_ref), ("dv", dv_ref))):
            share(
                name,
                ref.at[:, lanes_at(other * half, half)],
                m_dqkv.at[:, pl.ds(index * half, half)],
            )
        vec_s[...] = vec_ref[...]
        lanes = vec_s.shape[2]
        for index, ref in enumerate((dq_ref, dv_ref)):
            total = jnp.sum(ref[...].astype(F32), axis=0, keepdims=True)
            for side in range(2):
                vec_s[side, index : index + 1, :] = total[:, side * lanes : (side + 1) * lanes]
        vec_send(vec_s.at[1 - x])

    def grad_rows():
        total = dh_ref[...]
        for index, ref in enumerate((dq_ref, dk_ref, dv_ref)):
            pltpu.make_async_copy(weights[index], near[index], near_sem.at[index]).wait()
            total = total + lax.dot_general(
                ref[...], near[index][...], (((1,), (1,)), ((), ())), preferred_element_type=F32
            )
        rows_out[...] = total.astype(BF16)

    plans, gathers = {}, {}
    for key in KEYS:
        alone = sums[key[0]].shape[0] == 1
        first, count, sided = 0, 8, alone
        plans[key], back = [], []
        for name in ORDERS[key[0]][key[1]]:
            if name == "x":
                plans[key].append((by["x"], 1 - x, x, first, first, count))
                sided = True
                continue
            count //= 2
            out, keep = first + (1 - bits[name]) * count, first + bits[name] * count
            side = (0 if alone else x) if sided else None
            plans[key].append((by[name], side, side, out, keep, count))
            back.append((by[name], keep, out, count))
            first = keep
        gathers[key] = back[::-1]
    flights, spread, owns, state = {}, {}, {}, {}

    def piece_rows(key):
        rows = sums[key[0]].shape[2] // PIECES
        return pl.ds(key[1] * rows, rows)

    def reduce_send(key, step):
        peer, side, _, first, _, count = plans[key][step]
        dst = r_bufs[key][step]
        if side is None:
            src = sums[key[0]].at[:, pl.ds(first, count), piece_rows(key)]
        else:
            src, dst = sums[key[0]].at[side, pl.ds(first, count), piece_rows(key)], dst.at[0]
        sems = rs_send.at[key[0], key[1], step], rs_recv.at[key[0], key[1], step]
        flights[key, step] = send(src, dst, *sems, peer)
        state[key] = step

    def reduce_add(key, step):
        _, _, side, _, first, count = plans[key][step]
        flights[key, step].wait_recv()
        total, fresh, rows = sums[key[0]], r_bufs[key][step], piece_rows(key)
        sides = ((0, 0), (1, 1)) if side is None else ((side, 0),)
        for here, there in sides:

            def body(index, carry):
                spot = first + index
                total[here, spot, rows] = (
                    total[here, spot, rows].astype(F32) + fresh[there, index].astype(F32)
                ).astype(BF16)
                return carry

            lax.fori_loop(0, count, body, 0)

    def spread_send(key, kind, src, dst, peer):
        sems = ag_send.at[key[0], key[1], kind], ag_recv.at[key[0], key[1], kind]
        spread[key, kind] = send(src, dst, *sems, peer)

    def advance(key):
        step, steps = state[key], len(plans[key])
        out, rows = outs[key[0]], piece_rows(key)
        if step < steps:
            reduce_add(key, step)
            if step < steps - 1:
                reduce_send(key, step + 1)
                return
            peer, first, _, _ = gathers[key][0]
            side = x if sums[key[0]].shape[0] == 2 else 0
            src = sums[key[0]].at[side, pl.ds(first, 1), rows]
            dst = out.at[core, pl.ds(first, 1), rows]
            owns[key] = pltpu.make_async_copy(src, dst, own_sem.at[key[0], key[1]])
            owns[key].start()
            spread_send(key, 0, src, dst, peer)
            spread_send(key, 3, src, dst, by_core)
        else:
            turn = step - steps + 1
            spread[key, turn - 1].wait_recv()
            if turn == 1:
                owns[key].wait()
            if turn < 3:
                peer, first, _, count = gathers[key][turn]
                ref = out.at[core, pl.ds(first, count), rows]
                spread_send(key, turn, ref, ref, peer)
            _, _, first, count = gathers[key][turn - 1]
            ref = out.at[core, pl.ds(first, count), rows]
            spread_send(key, 3 + turn, ref, ref, by_core)
        state[key] = step + 1

    actions = {
        "up": (grads_up, 1),
        "down": (grads_down, 2),
        "qkv": (grads_qkv, 0),
        "back": (come_back, None),
        "rows": (grad_rows, None),
        "vec": (vec_next, None),
    }
    for event in SCHEDULE:
        if isinstance(event, tuple):
            advance(event)
        elif isinstance(event, int):
            attention(event)
        else:
            action, part = actions[event]
            if event == "vec" and len(vec_steps) == len(vec_peers) and "vec" in state:
                continue
            if event == "vec" and len(vec_steps) == len(vec_peers):
                state["vec"] = True
            action()
            if part is not None:
                for piece in range(PIECES):
                    reduce_send((part, piece), 0)
    vec_out[...] = v_sum[len(vec_peers) - 1]
    for m in range(MB):
        all_bytes(out_buf.at[m], send_sem.at[m], heads - 1).wait()
        all_bytes(back_out.at[m], back_send.at[m], heads - 1).wait()
    for flight in shared.values():
        flight.wait_send()
    for flight in vec_steps:
        flight.wait_send()
    for flight in flights.values():
        flight.wait_send()
    for (_, kind), flight in spread.items():
        if kind >= 3:
            flight.wait_recv()
        flight.wait_send()


def backward(table, da, kept, lse, x, a, n1, g, do, du, dm, vec, dh, weights, heads):
    vmem, smem = pl.BlockSpec(memory_space=pltpu.VMEM), pl.BlockSpec(memory_space=pltpu.SMEM)
    anywhere = pl.BlockSpec(memory_space=pl.ANY)
    rows, width = da.shape
    hidden = g.shape[1]
    pack_rows = BLK + BLK // 2
    low = lambda *dims: pltpu.VMEM(dims, BF16)
    a_shape, b_shape = (2, 8, width // 16, 2 * width), (2, 8, width // 16, hidden // 2)
    c_shape = (1, 8, hidden // 32, width)
    scratch = [low(heads, BLK // 2, 128)] * MB
    scratch += [low(MB, heads, BLK // 2, 128)]
    scratch += [low(MB, heads, pack_rows, 128)] * 2
    scratch += [low(heads * BLK, HD)] * 4
    scratch += [pltpu.VMEM((heads, BLK, HD), F32)] * 3
    scratch += [low(rows, width)] * 6
    scratch += [low(rows, width // 2), low(rows, hidden // 2), low(rows, 3 * width // 2)]
    scratch += [low(rows, hidden // 4), low(rows, width)] * 3
    scratch += [low(*item.shape) for item in weights]
    scratch += [pltpu.VMEM(vec.shape, F32)] + [pltpu.VMEM((5,) + vec.shape[1:], F32)] * 2
    scratch += [low(*shape) for shape in (a_shape, b_shape, c_shape)]
    for key in KEYS:
        shape = (a_shape, b_shape, c_shape)[key[0]]
        scratch += [low(*item) for item in landing_shapes(ORDERS[key[0]][key[1]], shape)]
    sems = lambda *dims: pltpu.SemaphoreType.DMA(dims)
    scratch += [sems(MB)] * 4 + [sems(14)] * 2 + [sems(3)]
    scratch += [sems(3, PIECES, 4)] * 2 + [sems(3, PIECES, 7)] * 2 + [sems(3, PIECES)]
    scratch += [sems(5)] * 2
    return pl.pallas_call(
        functools.partial(backward_kernel, heads),
        out_shape=[
            jax.ShapeDtypeStruct((rows, width), BF16),
            jax.ShapeDtypeStruct(a_shape, BF16),
            jax.ShapeDtypeStruct(b_shape, BF16),
            jax.ShapeDtypeStruct((2,) + c_shape[1:], BF16),
            jax.ShapeDtypeStruct(vec.shape[1:], F32),
        ],
        in_specs=[smem] + [vmem] * 12 + [anywhere] * 3,
        out_specs=[vmem] + [anywhere] * 3 + [vmem],
        scratch_shapes=scratch,
        compiler_params=pltpu.CompilerParams(
            collective_id=2, has_side_effects=True, vmem_limit_bytes=VMEM_BYTES
        ),
        name="backward",
    )(table, da, kept, lse, x, a, n1, g, do, du, dm, vec, dh, *weights)


def widen_kernel(a_ref, b_ref, c_ref, vec_ref, *outs):
    @pl.when(pl.program_id(0) == 0)
    def _():
        line, lanes = 0, vec_ref.shape[1]
        for out in outs[6:]:
            for first in range(0, out.shape[0], lanes):
                out[pl.ds(first, lanes)] = vec_ref[line, :]
                line += 1

    half = outs[0].shape[1] // 2
    for index, out in enumerate(outs[:4]):
        for core in range(2):
            out[:, core * half : (core + 1) * half] = a_ref[
                core, 0, :, index * half : (index + 1) * half
            ].astype(F32)
    up, down = outs[4:6]
    half = up.shape[1] // 2
    for core in range(2):
        up[:, core * half : (core + 1) * half] = b_ref[core, 0].astype(F32)
        down[core, 0] = c_ref[core, 0].astype(F32)


def widen(o_a, o_b, o_c, vec, sizes):
    shards = o_a.shape[1]
    block = lambda item: pl.BlockSpec((2, 1) + item.shape[2:], lambda i: (0, i, 0, 0))
    rows = o_a.shape[2]
    square = (shards * rows, o_a.shape[3] // 2)
    wide = (shards * rows, 2 * o_b.shape[3])
    return pl.pallas_call(
        widen_kernel,
        grid=(shards,),
        out_shape=[jax.ShapeDtypeStruct(square, F32)] * 4
        + [jax.ShapeDtypeStruct(wide, F32), jax.ShapeDtypeStruct(o_c.shape, F32)]
        + [jax.ShapeDtypeStruct((size,), F32) for size in sizes],
        in_specs=[block(o_a), block(o_b), block(o_c), pl.BlockSpec(vec.shape, lambda i: (0, 0))],
        out_specs=[pl.BlockSpec((rows, square[1]), lambda i: (i, 0))] * 4
        + [pl.BlockSpec((rows, wide[1]), lambda i: (i, 0)), block(o_c)]
        + [pl.BlockSpec((size,), lambda i: (0,)) for size in sizes],
        compiler_params=pltpu.CompilerParams(vmem_limit_bytes=VMEM_BYTES),
        name="widen",
    )(o_a, o_b, o_c, vec)


def per_device_heads(tokens, cotangent, lengths, dealing, *params):
    rows_in = tokens.shape[2]
    width = tokens.shape[3]
    rows = MB * rows_in
    weights, vectors = params[:6], params[6:]
    sizes = [item.shape[0] for item in vectors]
    x = tokens.reshape(rows, width)
    blocks = jnp.arange(HEADS, dtype=jnp.int32)
    at_block = dealing[0][:, :, None] == blocks[None, None, :]
    slot_of = jnp.sum(jnp.where(at_block, blocks[None, :, None], 0), axis=1)
    table = jnp.concatenate([lengths[0], dealing[0], slot_of], axis=1)
    query_w, key_w, value_w, kept, lse, a, output, n_low, g, do, du, dm, dh_one, da, vec = forward(
        table, x, cotangent.reshape(rows, width), weights, vectors, HEADS
    )
    grad_tokens, o_a, o_b, o_c, vec_sum = backward(
        table,
        da,
        kept,
        lse,
        x,
        a,
        n_low,
        g,
        do,
        du,
        dm,
        vec,
        dh_one,
        (query_w, key_w, value_w),
        HEADS,
    )
    grads = list(widen(o_a, o_b, o_c, vec_sum, sizes))
    grads[5] = grads[5].reshape(-1, width)
    shape = (1, MB, rows_in, width)
    return (
        (output.reshape(shape), grad_tokens.reshape(shape))
        + tuple(grads)
    )


def solution(mesh):
    placed = (
        P("wsh", None, "ctx", None),
        P("wsh", None, "ctx", None),
        P("wsh", None, None),
        P("wsh", None, None),
        P("wsh", None),
        P("wsh", None),
        P("wsh", None),
        P("wsh", None),
        P("wsh", None),
        P("wsh", None),
        P("wsh"),
        P("wsh"),
        P("wsh"),
        P("wsh"),
        P("wsh"),
        P("wsh"),
        P("wsh"),
        P("wsh"),
        P("wsh"),
    )
    by_heads = mesh.shape["ctx"] == HEADS and mesh.shape["wsh"] == 2
    return jax.shard_map(
        per_device_heads if by_heads else per_device,
        mesh=mesh,
        in_specs=placed,
        out_specs=(
            P("wsh", None, "ctx", None),
            P("wsh", None, "ctx", None),
            P("wsh", None),
            P("wsh", None),
            P("wsh", None),
            P("wsh", None),
            P("wsh", None),
            P("wsh", None),
            P("wsh"),
            P("wsh"),
            P("wsh"),
            P("wsh"),
            P("wsh"),
            P("wsh"),
            P("wsh"),
            P("wsh"),
            P("wsh"),
        ),
        check_vma=False,
    )
```

```python
import functools
import math

import jax
import jax.numpy as jnp
from jax import lax
from jax.experimental import pallas as pl
from jax.experimental.pallas import tpu as pltpu
from jax.sharding import PartitionSpec as P

HEADS = 16
BPS = 8
MB = 3
BLK = 64


EPSILON = 1e-12
NEG_FILL = -1e30


def as_sent(x):
    return jax.tree.map(lambda a: a.astype(jnp.bfloat16) if a.dtype == jnp.float32 else a, x)


def layer_norm(summed, gain_vec, shift_vec):
    row_mean = jnp.mean(summed, axis=-1, keepdims=True)
    centred = summed - row_mean
    row_var = jnp.mean(centred * centred, axis=-1, keepdims=True)
    return centred * lax.rsqrt(row_var + EPSILON) * gain_vec + shift_vec


def gelu_exact(values):
    return jax.nn.gelu(values, approximate=False)


def row_labels(dealt_order, seq_lengths):
    blocks_of_rows = jnp.repeat(dealt_order, BLK)
    within = jnp.tile(jnp.arange(BLK, dtype=jnp.int32), dealt_order.shape[0])
    seq_ids = blocks_of_rows // BPS
    places = blocks_of_rows % BPS * BLK + within
    numbers = jnp.arange(seq_lengths.shape[0], dtype=jnp.int32)
    seq_bound = jnp.sum(
        jnp.where(seq_ids[:, None] == numbers[None, :], seq_lengths[None, :], 0), axis=1
    )
    return (seq_ids, places < seq_bound)


def blockwise(carried, total_rows, step_rows, visit_block):
    return lax.fori_loop(
        0,
        total_rows // step_rows,
        lambda turn_index, running: visit_block(running, turn_index * step_rows),
        carried,
    )


def masked_scores(query_blk, key_blk, query_seq, key_seq, key_valid, scale_factor):
    allowed = (query_seq[:, None] == key_seq[None, :]) & key_valid[None, :]
    scores = (
        jnp.einsum("qhd,khd->hqk", query_blk, key_blk, preferred_element_type=jnp.float32)
        * scale_factor
    )
    return (jnp.where(allowed[None], scores, NEG_FILL), allowed[None].astype(jnp.float32))


def attention_grads(
    query_blk,
    grad_blk,
    key_blk,
    value_blk,
    query_seq,
    key_seq,
    key_valid,
    row_total,
    row_delta,
    scale_factor,
):
    scores, allowed = masked_scores(query_blk, key_blk, query_seq, key_seq, key_valid, scale_factor)
    probs = jnp.exp(scores - row_total[:, :, None]) * allowed
    grad_probs = jnp.einsum("qhd,khd->hqk", grad_blk, value_blk, preferred_element_type=jnp.float32)
    grad_scores = (probs * (grad_probs - row_delta[:, :, None])).astype(jnp.bfloat16)
    return (probs.astype(jnp.bfloat16), grad_scores)


def gather_params(params):
    return (
        lax.all_gather(params[0], "wsh", axis=0, tiled=True),
        lax.all_gather(params[1], "wsh", axis=0, tiled=True),
        lax.all_gather(params[2], "wsh", axis=0, tiled=True),
        lax.all_gather(params[3], "wsh", axis=0, tiled=True),
        lax.all_gather(params[4], "wsh", axis=0, tiled=True),
        lax.all_gather(params[5], "wsh", axis=0, tiled=True),
        lax.all_gather(params[6], "wsh", axis=0, tiled=True),
        lax.all_gather(params[7], "wsh", axis=0, tiled=True),
        lax.all_gather(params[8], "wsh", axis=0, tiled=True),
        lax.all_gather(params[9], "wsh", axis=0, tiled=True),
        lax.all_gather(params[10], "wsh", axis=0, tiled=True),
        lax.all_gather(params[11], "wsh", axis=0, tiled=True),
        lax.all_gather(params[12], "wsh", axis=0, tiled=True),
        lax.all_gather(params[13], "wsh", axis=0, tiled=True),
        lax.all_gather(params[14], "wsh", axis=0, tiled=True),
    )


def per_device(
    tokens,
    cotangent,
    lengths,
    dealing,
    w_query,
    w_key,
    w_value,
    w_out,
    w_up,
    w_down,
    b_query,
    b_value,
    b_out,
    b_up,
    b_down,
    gain_one,
    shift_one,
    gain_two,
    shift_two,
):
    params = (
        w_query,
        w_key,
        w_value,
        w_out,
        w_up,
        w_down,
        b_query,
        b_value,
        b_out,
        b_up,
        b_down,
        gain_one,
        shift_one,
        gain_two,
        shift_two,
    )
    own_rows = tokens.shape[2]
    width = tokens.shape[3]
    head_size = width // HEADS
    scale_factor = 1.0 / math.sqrt(head_size)
    my_start = lax.axis_index("ctx") * own_rows
    wsh_count = lax.axis_size("wsh")
    grads = tuple(
        (jnp.zeros((item.shape[0] * wsh_count,) + item.shape[1:], jnp.float32) for item in params)
    )
    results = []
    input_grads = []
    for micro in range(MB):
        whole = gather_params(params)
        query_weight, key_weight, value_weight, out_weight, up_weight, down_weight = whole[:6]
        (
            bias_query,
            bias_value,
            bias_out,
            bias_up,
            bias_down,
            gain_first,
            shift_first,
            gain_second,
            shift_second,
        ) = tuple((item.astype(jnp.float32) for item in whole[6:]))
        token_rows = tokens[0, micro]
        seq_all, valid_all = row_labels(dealing[0, micro], lengths[0, micro])
        my_seq = lax.dynamic_slice_in_dim(seq_all, my_start, own_rows)
        my_valid = lax.dynamic_slice_in_dim(valid_all, my_start, own_rows)
        query_low = (
            jnp.dot(token_rows, query_weight, preferred_element_type=jnp.float32) + bias_query
        ).astype(jnp.bfloat16)
        key_low = jnp.dot(token_rows, key_weight, preferred_element_type=jnp.float32).astype(
            jnp.bfloat16
        )
        value_low = (
            jnp.dot(token_rows, value_weight, preferred_element_type=jnp.float32) + bias_value
        ).astype(jnp.bfloat16)
        query_heads = query_low.reshape(own_rows, HEADS, head_size)
        my_key_heads = key_low.reshape(own_rows, HEADS, head_size)
        my_value_heads = value_low.reshape(own_rows, HEADS, head_size)
        start_state = (
            jnp.full((HEADS, own_rows), NEG_FILL, jnp.float32),
            jnp.zeros((HEADS, own_rows), jnp.float32),
            jnp.zeros((own_rows, HEADS, head_size), jnp.float32),
        )
        key_piece = lax.all_gather(key_low, "ctx", axis=0, tiled=True)
        value_piece = lax.all_gather(value_low, "ctx", axis=0, tiled=True)
        piece_rows = key_piece.shape[0]
        step_rows = math.gcd(piece_rows, 512)

        def visit_block(running, offset):
            run_max, run_sum, run_acc = running
            key_blk = lax.dynamic_slice_in_dim(key_piece, offset, step_rows).reshape(
                step_rows, HEADS, head_size
            )
            value_blk = lax.dynamic_slice_in_dim(value_piece, offset, step_rows).reshape(
                step_rows, HEADS, head_size
            )
            key_seq = lax.dynamic_slice_in_dim(seq_all, offset, step_rows)
            key_valid = lax.dynamic_slice_in_dim(valid_all, offset, step_rows)
            scores, allowed = masked_scores(
                query_heads, key_blk, my_seq, key_seq, key_valid, scale_factor
            )
            new_max = jnp.maximum(run_max, jnp.max(scores, axis=-1))
            rescale = jnp.exp(run_max - new_max)
            weights = jnp.exp(scores - new_max[:, :, None]) * allowed
            run_sum = run_sum * rescale + jnp.sum(weights, axis=-1)
            run_acc = run_acc * rescale.T[:, :, None] + jnp.einsum(
                "hqk,khd->qhd",
                weights.astype(jnp.bfloat16),
                value_blk,
                preferred_element_type=jnp.float32,
            )
            return (new_max, run_sum, run_acc)

        final_max, final_sum, final_acc = blockwise(start_state, piece_rows, step_rows, visit_block)
        attended = final_acc / final_sum.T[:, :, None]
        log_total = final_max + jnp.log(final_sum)
        attended_low = attended.reshape(own_rows, width).astype(jnp.bfloat16)
        out_proj = jnp.dot(attended_low, out_weight, preferred_element_type=jnp.float32) + bias_out
        first_sum = token_rows.astype(jnp.float32) + out_proj
        norm_one, norm_one_back = jax.vjp(layer_norm, first_sum, gain_first, shift_first)
        mlp_input = norm_one.astype(jnp.bfloat16)
        up_pre = jnp.dot(mlp_input, up_weight, preferred_element_type=jnp.float32) + bias_up
        activated, gelu_back = jax.vjp(gelu_exact, up_pre)
        activated_low = activated.astype(jnp.bfloat16)
        down_out = (
            jnp.dot(activated_low, down_weight, preferred_element_type=jnp.float32) + bias_down
        )
        result, norm_two_back = jax.vjp(layer_norm, norm_one + down_out, gain_second, shift_second)
        results.append(result.astype(jnp.bfloat16))
        grad_second, grad_gain_b, grad_shift_b = norm_two_back(
            cotangent[0, micro].astype(jnp.float32)
        )
        grad_down_low = grad_second.astype(jnp.bfloat16)
        grad_activated = jnp.einsum(
            "rd,fd->rf", grad_down_low, down_weight, preferred_element_type=jnp.float32
        )
        (grad_up_pre,) = gelu_back(grad_activated)
        grad_up_low = grad_up_pre.astype(jnp.bfloat16)
        grad_norm_one = (
            jnp.einsum("rf,df->rd", grad_up_low, up_weight, preferred_element_type=jnp.float32)
            + grad_second
        )
        grad_first, grad_gain_a, grad_shift_a = norm_one_back(grad_norm_one)
        grad_out_low = grad_first.astype(jnp.bfloat16)
        grad_att_low = jnp.einsum(
            "rd,ed->re", grad_out_low, out_weight, preferred_element_type=jnp.float32
        ).astype(jnp.bfloat16)
        grad_heads = grad_att_low.reshape(own_rows, HEADS, head_size)
        row_delta = jnp.sum(grad_heads.astype(jnp.float32) * attended, axis=-1).T
        empty_heads = jnp.zeros((own_rows, HEADS, head_size), jnp.float32)
        query_key_piece = lax.all_gather(key_low, "ctx", axis=0, tiled=True)
        query_value_piece = lax.all_gather(value_low, "ctx", axis=0, tiled=True)
        query_piece_rows = query_key_piece.shape[0]
        query_step_rows = math.gcd(query_piece_rows, 512)

        def query_visit_block(running, offset):
            key_blk = lax.dynamic_slice_in_dim(query_key_piece, offset, query_step_rows).reshape(
                query_step_rows, HEADS, head_size
            )
            value_blk = lax.dynamic_slice_in_dim(
                query_value_piece, offset, query_step_rows
            ).reshape(query_step_rows, HEADS, head_size)
            key_seq = lax.dynamic_slice_in_dim(seq_all, offset, query_step_rows)
            key_valid = lax.dynamic_slice_in_dim(valid_all, offset, query_step_rows)
            probs_low, grad_scores = attention_grads(
                query_heads,
                grad_heads,
                key_blk,
                value_blk,
                my_seq,
                key_seq,
                key_valid,
                log_total,
                row_delta,
                scale_factor,
            )
            return running + jnp.einsum(
                "hqk,khd->qhd", grad_scores, key_blk, preferred_element_type=jnp.float32
            )

        grad_query_sum = blockwise(
            empty_heads, query_piece_rows, query_step_rows, query_visit_block
        )
        total_all, delta_all = (
            lax.all_gather(log_total.T, "ctx", axis=0, tiled=True),
            lax.all_gather(row_delta.T, "ctx", axis=0, tiled=True),
        )
        query_piece = lax.all_gather(query_low, "ctx", axis=0, tiled=True)
        grad_piece = lax.all_gather(grad_att_low, "ctx", axis=0, tiled=True)
        key_piece_rows = query_piece.shape[0]
        key_step_rows = math.gcd(key_piece_rows, 512)

        def key_visit_block(running, offset):
            grad_key_run, grad_value_run = running
            query_blk = lax.dynamic_slice_in_dim(query_piece, offset, key_step_rows).reshape(
                key_step_rows, HEADS, head_size
            )
            grad_blk = lax.dynamic_slice_in_dim(grad_piece, offset, key_step_rows).reshape(
                key_step_rows, HEADS, head_size
            )
            total_blk = lax.dynamic_slice_in_dim(total_all, offset, key_step_rows)
            delta_blk = lax.dynamic_slice_in_dim(delta_all, offset, key_step_rows)
            query_seq = lax.dynamic_slice_in_dim(seq_all, offset, key_step_rows)
            probs_low, grad_scores = attention_grads(
                query_blk,
                grad_blk,
                my_key_heads,
                my_value_heads,
                query_seq,
                my_seq,
                my_valid,
                total_blk.T,
                delta_blk.T,
                scale_factor,
            )
            grad_key_run = grad_key_run + jnp.einsum(
                "hqk,qhd->khd", grad_scores, query_blk, preferred_element_type=jnp.float32
            )
            grad_value_run = grad_value_run + jnp.einsum(
                "hqk,qhd->khd", probs_low, grad_blk, preferred_element_type=jnp.float32
            )
            return (grad_key_run, grad_value_run)

        grad_key_sum, grad_value_sum = blockwise(
            (empty_heads, empty_heads), key_piece_rows, key_step_rows, key_visit_block
        )
        grad_key_flat = grad_key_sum.reshape(own_rows, width)
        grad_value_flat = grad_value_sum.reshape(own_rows, width)
        grad_query_low = (
            (grad_query_sum * scale_factor).reshape(own_rows, width).astype(jnp.bfloat16)
        )
        grad_key_low = (grad_key_flat * scale_factor).astype(jnp.bfloat16)
        grad_value_low = grad_value_flat.astype(jnp.bfloat16)
        terms = (
            jnp.einsum("rd,re->de", token_rows, grad_query_low, preferred_element_type=jnp.float32),
            jnp.einsum("rd,re->de", token_rows, grad_key_low, preferred_element_type=jnp.float32),
            jnp.einsum("rd,re->de", token_rows, grad_value_low, preferred_element_type=jnp.float32),
            jnp.einsum("rd,re->de", attended_low, grad_out_low, preferred_element_type=jnp.float32),
            jnp.einsum("rd,rf->df", mlp_input, grad_up_low, preferred_element_type=jnp.float32),
            jnp.einsum(
                "rf,rd->fd", activated_low, grad_down_low, preferred_element_type=jnp.float32
            ),
            jnp.sum(grad_query_low.astype(jnp.float32), axis=0),
            jnp.sum(grad_value_low.astype(jnp.float32), axis=0),
            jnp.sum(grad_out_low.astype(jnp.float32), axis=0),
            jnp.sum(grad_up_low.astype(jnp.float32), axis=0),
            jnp.sum(grad_down_low.astype(jnp.float32), axis=0),
            grad_gain_a,
            grad_shift_a,
            grad_gain_b,
            grad_shift_b,
        )
        grads = tuple((total_now + fresh for total_now, fresh in zip(grads, terms)))
        grad_rows = (
            grad_first
            + jnp.einsum(
                "re,de->rd", grad_query_low, query_weight, preferred_element_type=jnp.float32
            )
            + jnp.einsum("re,de->rd", grad_key_low, key_weight, preferred_element_type=jnp.float32)
            + jnp.einsum(
                "re,de->rd", grad_value_low, value_weight, preferred_element_type=jnp.float32
            )
        )
        input_grads.append(grad_rows.astype(jnp.bfloat16))
    shards = jax.tree.map(
        lambda part: part.astype(jnp.float32),
        lax.psum_scatter(as_sent(grads), "wsh", scatter_dimension=0, tiled=True),
    )
    summed = jax.tree.map(lambda part: part.astype(jnp.float32), lax.psum(as_sent(shards), "ctx"))
    return (jnp.stack(results)[None], jnp.stack(input_grads)[None]) + tuple(summed)


MESH_IDS = pl.DeviceIdType.MESH
F32 = jnp.float32
BF16 = jnp.bfloat16
HD = 64
VMEM_BYTES = 60 * 1024 * 1024


def flip(index, bit):
    return index + bit * (1 - 2 * lax.rem(lax.div(index, bit), 2))


def bit_of(index, bit):
    return lax.rem(lax.div(index, bit), 2)


def greet(peers):
    barrier = pltpu.get_barrier_semaphore()
    for peer in peers:
        pl.semaphore_signal(barrier, inc=1, device_id=peer, device_id_type=MESH_IDS)
    pl.semaphore_wait(barrier, len(peers))


def send(src, dst, send_sem, recv_sem, peer):
    copy = pltpu.make_async_remote_copy(
        src_ref=src,
        dst_ref=dst,
        send_sem=send_sem,
        recv_sem=recv_sem,
        device_id=peer,
        device_id_type=MESH_IDS,
    )
    copy.start()
    return copy


class Dealing:
    def __init__(self, lengths_hbm, dealing_hbm, lengths, dealing, slots, sems):
        self.lengths, self.dealing, self.slots = lengths, dealing, slots
        self.copies = (
            pltpu.make_async_copy(lengths_hbm, lengths, sems.at[0]),
            pltpu.make_async_copy(dealing_hbm, dealing, sems.at[1]),
        )
        for copy in self.copies:
            copy.start()

    def invert(self):
        for copy in self.copies:
            copy.wait()
        micros, _, count = self.dealing.shape

        def find(number, carry):
            m, block = lax.div(number, count), lax.rem(number, count)
            slot = jnp.int32(0)
            for t in range(count):
                slot = jnp.where(self.dealing[m, 0, t] == block, jnp.int32(t), slot)
            self.slots[m, block] = slot
            return carry

        lax.fori_loop(0, micros * count, find, 0)

    def length(self, m, s):
        return self.lengths[0, s, m]

    def block(self, m, t):
        return self.dealing[m, 0, t]

    def slot(self, m, b):
        return self.slots[m, b]


def dealing_scratch(lengths, dealing):
    return [
        pltpu.SMEM(lengths.shape, jnp.int32),
        pltpu.SMEM(dealing.shape, jnp.int32),
        pltpu.SMEM((dealing.shape[0], dealing.shape[2]), jnp.int32),
        pltpu.SemaphoreType.DMA((2,)),
    ]


def plane_peers(c, w, count):
    return [(lax.rem(c + step, count), w) for step in range(1, count)]


def pack_three(first, second, third, row, pair, out):
    cols = pl.ds(pair * 128, 128)
    a, b, d = (ref[pl.ds(row, BLK), cols] for ref in (first, second, third))
    half = BLK // 2
    for head in range(2):
        lane = slice(head * HD, head * HD + HD)
        out[2 * pair + head, 0:BLK, :] = jnp.concatenate([a[:, lane], b[:, lane]], axis=1)
        out[2 * pair + head, BLK : BLK + half, :] = jnp.concatenate(
            [d[:half, lane], d[half:, lane]], axis=1
        )


def unpack_fold(block):
    return jnp.concatenate([block[:, :HD], block[:, HD:]], axis=0)


def fold(rows):
    half = rows.shape[0] // 2
    return jnp.concatenate([rows[:half], rows[half:]], axis=1)


def all_bytes(ref, sem, peers):
    view = ref.at[pl.ds(0, peers)]
    return pltpu.make_async_copy(view, view, sem)


def norm_parts(summed):
    row_mean = jnp.mean(summed, axis=-1, keepdims=True)
    centred = summed - row_mean
    row_var = jnp.mean(centred * centred, axis=-1, keepdims=True)
    scale = lax.rsqrt(row_var + EPSILON)
    return centred * scale, scale


def norm_back(grad, unit, scale, gain):
    inner = grad * gain
    mean_one = jnp.mean(inner, axis=-1, keepdims=True)
    mean_two = jnp.mean(inner * unit, axis=-1, keepdims=True)
    return scale * (inner - mean_one - unit * mean_two)


def dot_minor(a, b):
    return lax.dot_general(a, b, (((1,), (1,)), ((), ())), preferred_element_type=F32)


ROW_OUT, ROW_UP, ROW_DOWN, ROW_GAIN_ONE, ROW_SHIFT_ONE, ROW_GAIN_TWO, ROW_SHIFT_TWO = 2, 3, 7, 8, 9, 10, 11


SQUARE, PAIR_Y, PAIR_Z, ALONE = (8, "yz"), (4, "y"), (4, "z"), (2, "")
WAYS = (
    SQUARE, SQUARE, SQUARE, SQUARE, PAIR_Y, SQUARE, PAIR_Z, PAIR_Y, ALONE, PAIR_Z, PAIR_Y, ALONE,
)
SEND_ORDER = (2, 0, 1, 3, 5, 7, 4, 6, 9, 10, 8, 11)
FORWARD_SCHEDULE = (
    ("second", 2), ("second", 0), ("third", 2), ("second", 1), ("third", 0), ("fourth", 2),
    ("third", 1), ("second", 3), ("second", 5), ("fourth", 0), ("project", 2), ("fourth", 1),
    ("project", 0), ("project", 1), ("pack", 0), ("second", 7), ("third", 3), ("second", 4),
    ("second", 6), ("att", 0), ("fourth", 7), ("third", 5), ("fourth", 3), ("att", 1), ("att",
    2), ("fourth", 5), ("fourth", 8), ("second", 10), ("second", 9), ("fourth", 6), ("fourth",
    4), ("rows", 0), ("out", 0), ("hidden", 0), ("fourth", 10), ("hidden", 1), ("hidden", 2),
    ("fourth", 9), ("hidden", 3), ("hidden", 4), ("fourth", 11), ("hidden", 5), ("hidden", 6),
    ("hidden", 7),
)


def weight_plan(shards):
    unit = shards[0].shape[0] * shards[0].shape[1]
    plan = []
    for index, (rows, cols) in enumerate(shard.shape for shard in shards):
        parts = max(1, rows * cols // unit)
        for part in range(parts):
            plan.append((index, part * (rows // parts), rows // parts, WAYS[len(plan)]))
    return plan


def forward_kernel(heads, plan, n_weights, n_vectors, *refs):
    integers, (x_ref, cot_ref), refs = refs[:2], refs[2:4], refs[4:]
    shards, vectors = refs[:n_weights], refs[n_weights : n_weights + n_vectors]
    refs = refs[n_weights + n_vectors :]
    wholes, kept_ref, lse_ref = refs[:3], *refs[3:5]
    results, refs = refs[5:15], refs[15:]
    a_ref, out_ref, n_ref, g_ref, do_ref, du_ref, dm_ref, dh_ref, da_ref, vec_ref = refs[:10]
    made, result_sem, refs = refs[:10], refs[10], refs[11:]
    dealt, refs = Dealing(*integers, *refs[:4]), refs[4:]
    near, refs = refs[:n_weights], refs[n_weights:]
    small, small_in, small_whole, bias, q_ref, k_ref, v_ref = refs[:7]
    slope, n_full, unit, total = refs[7:11]
    refs = refs[11:]
    in_buf = refs[:MB]
    out_buf, back_out, back_in, q_s, k_s, v_s, a_s = refs[MB : 7 + MB]
    (
        w_send,
        w_recv,
        small_sems,
        local_sem,
        stage_sem,
        send_sem,
        recv_sem,
        back_send,
        back_recv,
        keep_sem,
    ) = refs[7 + MB :]
    c, w = lax.axis_index("ctx"), lax.axis_index("wsh")
    o = 1 - w
    by_x, by_y, by_z, by_core = (c, o), (flip(c, 2), w), (flip(c, 4), w), (flip(c, 1), w)
    core, y, z = bit_of(c, 1), bit_of(c, 2), bit_of(c, 4)
    peers = plane_peers(c, w, heads)
    stores = []

    def store(target):
        index = [item is target for item in made].index(True)
        copy = pltpu.make_async_copy(target, results[index], result_sem.at[index])
        copy.start()
        stores.append(copy)

    staged = []
    for index, shard in enumerate(shards):
        rows = shard.shape[0]
        spot = pl.ds(pl.multiple_of(w * rows, rows), rows)
        copy = pltpu.make_async_copy(shard, near[index].at[spot], stage_sem.at[index])
        copy.start()
        staged.append(copy)
    line, lanes = 0, small.shape[1]
    for vector in vectors:
        for first in range(0, vector.shape[0], lanes):
            piece = vector[pl.ds(first, lanes)].astype(F32)
            small[line : line + 1, :] = piece.reshape(1, lanes)
            line += 1
    greet(peers + [by_x])
    small_sent = send(small, small_in, small_sems.at[0], small_sems.at[1], by_x)

    def part(chunk, side, piece, start, count):
        tensor, first, rows, way = plan[chunk]
        half = shards[tensor].shape[0]
        at = side * half + first + piece * (rows // way[0]) + start
        return near[tensor].at[pl.ds(pl.multiple_of(at, 8), count)]

    steps = {}

    def sem(kind, chunk):
        return w_send.at[kind, chunk], w_recv.at[kind, chunk]

    def own_piece(way):
        return {
            SQUARE: core * 4 + z * 2 + y,
            PAIR_Y: core * 2 + y,
            PAIR_Z: core * 2 + z,
            ALONE: core,
        }[way]

    for chunk in SEND_ORDER:
        tensor, first, rows, way = plan[chunk]
        size, mine = rows // way[0], own_piece(way)
        src = shards[tensor].at[pl.ds(pl.multiple_of(first + mine * size, 8), size)]
        steps[chunk, 0] = send(src, part(chunk, w, mine, 0, size), *sem(0, chunk), by_x)
    dealt.invert()

    def second(chunk):
        _, _, rows, way = plan[chunk]
        steps[chunk, 0].wait_recv()
        ref = part(chunk, o, own_piece(way), 0, rows // way[0])
        for name in way[1]:
            kind, peer = {"y": (1, by_y), "z": (2, by_z)}[name]
            steps[chunk, kind] = send(ref, ref, *sem(kind, chunk), peer)

    def third(chunk):
        _, _, rows, way = plan[chunk]
        size = rows // way[0]
        steps[chunk, 1].wait_recv()
        steps[chunk, 2].wait_recv()
        ref = part(chunk, o, core * 4 + (1 - z) * 2 + y, 0, size // 2)
        steps[chunk, 3] = send(ref, ref, *sem(3, chunk), by_y)
        ref = part(chunk, o, core * 4 + z * 2 + (1 - y), size // 2, size // 2)
        steps[chunk, 4] = send(ref, ref, *sem(4, chunk), by_z)

    def fourth(chunk):
        _, _, rows, way = plan[chunk]
        for kind in {SQUARE: (3, 4), PAIR_Y: (1,), PAIR_Z: (2,), ALONE: (0,)}[way]:
            steps[chunk, kind].wait_recv()
        ref = part(chunk, o, core * (way[0] // 2), 0, rows // 2)
        steps[chunk, 5] = send(ref, ref, *sem(5, chunk), by_core)

    width = x_ref.shape[1]
    step = 256
    projected = []

    def project(index):
        if not projected:
            small_sent.wait()
            small_whole[w] = small[...]
            small_whole[o] = small_in[...]
            for side in range(2):
                for row in range(2):
                    bias[row : row + 1, side * lanes : (side + 1) * lanes] = small_whole[
                        side, row : row + 1, :
                    ]
        projected.append(index)
        staged[index].wait()
        steps[index, 5].wait_recv()
        weight, out = near[index], (q_ref, k_ref, v_ref)[index]

        def some_columns(turn, carry):
            cols = pl.ds(pl.multiple_of(turn * step, step), step)
            product = jnp.dot(x_ref[...], weight[:, cols], preferred_element_type=F32)
            if index != 1:
                product = product + bias[index // 2 : index // 2 + 1, cols]
            out[:, cols] = product.astype(BF16)
            return carry

        lax.fori_loop(0, width // step, some_columns, 0)
        pltpu.make_async_copy(near[index], wholes[index], local_sem.at[index]).start()

    def pack(_):
        for m in range(MB):
            for pair in range(heads // 2):
                pack_three(q_ref, k_ref, v_ref, m * BLK, pair, out_buf.at[m])
            for peer in peers:
                send(
                    out_buf.at[m, peer[0]], in_buf[m].at[c], send_sem.at[m], recv_sem.at[m], peer
                )
            in_buf[m][c] = out_buf[m, c]

    blocks = heads
    span = BPS * BLK

    def attention(m):
        all_bytes(in_buf[m], recv_sem.at[m], heads - 1).wait()
        pltpu.make_async_copy(in_buf[m], kept_ref.at[m], keep_sem.at[m]).start()
        for b in range(blocks):
            got = in_buf[m][dealt.slot(m, b)]
            q_s[b * BLK : (b + 1) * BLK, :] = got[:BLK, :HD]
            k_s[b * BLK : (b + 1) * BLK, :] = got[:BLK, HD:]
            v_s[b * BLK : (b + 1) * BLK, :] = unpack_fold(got[BLK:])

        def one_sequence(s, carry):
            rows = pl.ds(pl.multiple_of(s * span, span), span)
            scores = lax.dot_general(
                k_s[rows, :], q_s[rows, :], (((1,), (1,)), ((), ())), preferred_element_type=F32
            ) * (1.0 / math.sqrt(HD))
            place = lax.broadcasted_iota(jnp.int32, scores.shape, 0)
            scores = jnp.where(place < dealt.length(m, s), scores, NEG_FILL)
            top = jnp.max(scores, axis=0, keepdims=True)
            weights = jnp.exp(scores - top)
            summed = jnp.sum(weights, axis=0, keepdims=True)
            out_t = lax.dot_general(
                v_s[rows, :],
                weights.astype(BF16),
                (((0,), (0,)), ((), ())),
                preferred_element_type=F32,
            )
            a_s[pl.ds(s * BPS, BPS)] = (out_t / summed).T.reshape(BPS, BLK, HD)
            lse_ref[pl.ds(m * (blocks // BPS) + s, 1), :] = top + jnp.log(summed)
            return carry

        lax.fori_loop(0, blocks // BPS, one_sequence, 0)
        for t in range(blocks):
            back_out[m, t] = fold(a_s[dealt.block(m, t)]).astype(BF16)
        for peer in peers:
            send(
                back_out.at[m, peer[0]], back_in.at[m, c], back_send.at[m], back_recv.at[m], peer
            )
        back_in[m, c] = back_out[m, c]

    def come_back(_):
        for m in range(MB):
            all_bytes(back_in.at[m], back_recv.at[m], heads - 1).wait()
            for pair in range(heads // 2):
                a_ref[m * BLK : (m + 1) * BLK, pair * 128 : (pair + 1) * 128] = jnp.concatenate(
                    [unpack_fold(back_in[m, 2 * pair]), unpack_fold(back_in[m, 2 * pair + 1])],
                    axis=1,
                )
        store(a_ref)

    def line_of(row):
        return jnp.concatenate(
            [small_whole[0, row : row + 1, :], small_whole[1, row : row + 1, :]], axis=1
        )

    def keep(row, values):
        summed = jnp.sum(values, axis=0, keepdims=True)
        for side in range(2):
            vec_ref[side, row : row + 1, :] = summed[:, side * lanes : (side + 1) * lanes]

    out_w, up_w, down_w = near[3:]
    chunks_of = {t: [i for i, item in enumerate(plan) if item[0] == t] for t in range(n_weights)}

    def arrived(tensor, chunks):
        for chunk in chunks:
            steps[chunk, 5].wait_recv()

    def out_project(_):
        staged[3].wait()
        arrived(3, chunks_of[3])
        h_one = x_ref[...].astype(F32) + (
            jnp.dot(a_ref[...], out_w[...], preferred_element_type=F32) + line_of(ROW_OUT)
        )
        unit_one, scale_one = norm_parts(h_one)
        unit[...] = unit_one
        n_one = unit_one * line_of(ROW_GAIN_ONE) + line_of(ROW_SHIFT_ONE)
        n_full[...] = n_one
        n_ref[...] = n_one.astype(BF16)
        store(n_ref)
        total[...] = jnp.zeros_like(total)
        kept_scale.append(scale_one)

    kept_scale = []
    hidden = g_ref.shape[1]
    hidden_steps = hidden // lanes
    per_half = hidden_steps // 2

    def hidden_at(turn):
        j = lax.rem(w * per_half + turn, hidden_steps)
        cols = pl.ds(pl.multiple_of(j * lanes, lanes), lanes)
        return cols, lax.div(j, per_half), pl.ds(ROW_UP + lax.rem(j, per_half), 1)

    def hidden_up(turn):
        if turn == 0:
            staged[4].wait()
            arrived(4, chunks_of[4])
            staged[5].wait()
        elif turn >= per_half:
            share = len(chunks_of[5]) // per_half
            first = (turn - per_half) * share
            arrived(5, chunks_of[5][first : first + share])
        cols, side, row = hidden_at(turn)
        u = jnp.dot(n_ref[...], up_w[:, cols], preferred_element_type=F32) + small_whole[side, row, :]
        below = 0.5 * (1.0 + lax.erf(u * math.sqrt(0.5)))
        slope[:, cols] = below + u * jnp.exp(-0.5 * u * u) * (1.0 / math.sqrt(2.0 * math.pi))
        g = (u * below).astype(BF16)
        g_ref[:, cols] = g
        total[...] += jnp.dot(g, down_w[cols, :], preferred_element_type=F32)

    acts = {
        "second": second,
        "third": third,
        "fourth": fourth,
        "project": project,
        "pack": pack,
        "att": attention,
        "rows": come_back,
        "out": out_project,
        "hidden": hidden_up,
    }
    for name, value in FORWARD_SCHEDULE:
        acts[name](value)

    store(g_ref)
    h_two = n_full[...] + (total[...] + line_of(ROW_DOWN))
    unit_two, scale_two = norm_parts(h_two)
    out_ref[...] = (unit_two * line_of(ROW_GAIN_TWO) + line_of(ROW_SHIFT_TWO)).astype(BF16)
    store(out_ref)
    cot = cot_ref[...].astype(F32)
    keep(ROW_GAIN_TWO, cot * unit_two)
    keep(ROW_SHIFT_TWO, cot)
    dh_two = norm_back(cot, unit_two, scale_two, line_of(ROW_GAIN_TWO))
    dm = dh_two.astype(BF16)
    dm_ref[...] = dm
    store(dm_ref)
    keep(ROW_DOWN, dm.astype(F32))
    total[...] = dh_two
    for turn in range(hidden_steps):
        cols, side, row = hidden_at(turn)
        du = (slope[:, cols] * dot_minor(dm_ref[...], down_w[cols, :])).astype(BF16)
        du_ref[:, cols] = du
        vec_ref[side, row, :] = jnp.sum(du.astype(F32), axis=0, keepdims=True)
        total[...] += dot_minor(du, up_w[:, cols])
    store(du_ref)
    dn = total[...]
    keep(ROW_GAIN_ONE, dn * unit[...])
    keep(ROW_SHIFT_ONE, dn)
    dh_one = norm_back(dn, unit[...], kept_scale[0], line_of(ROW_GAIN_ONE))
    dh_ref[...] = dh_one
    store(dh_ref)
    do = dh_one.astype(BF16)
    do_ref[...] = do
    store(do_ref)
    keep(ROW_OUT, do.astype(F32))
    for side in range(2):
        vec_ref[side, 0:ROW_OUT, :] = jnp.zeros((ROW_OUT, lanes), F32)
    store(vec_ref)
    da_ref[...] = dot_minor(do, out_w[...]).astype(BF16)
    store(da_ref)

    for m in range(MB):
        all_bytes(out_buf.at[m], send_sem.at[m], heads - 1).wait()
        all_bytes(back_out.at[m], back_send.at[m], heads - 1).wait()
        pltpu.make_async_copy(in_buf[m], kept_ref.at[m], keep_sem.at[m]).wait()
    for flight in steps.values():
        flight.wait_send()
    for copy in stores:
        copy.wait()
    for index in range(3):
        pltpu.make_async_copy(near[index], wholes[index], local_sem.at[index]).wait()


def forward(lengths, dealing, x, cot, shards, vectors, heads):
    plan = weight_plan(shards)
    count = len(shards)
    anywhere, vmem = pl.BlockSpec(memory_space=pl.ANY), pl.BlockSpec(memory_space=pltpu.VMEM)
    rows, width = x.shape
    hidden = shards[4].shape[1]
    pack_rows = BLK + BLK // 2
    span = BPS * BLK
    lanes = min(item.shape[0] for item in vectors)
    lines = sum(item.shape[0] for item in vectors) // lanes
    whole = lambda s: (2 * s.shape[0],) + s.shape[1:]
    low = lambda cols: jax.ShapeDtypeStruct((rows, cols), BF16)
    full = lambda cols: pltpu.VMEM((rows, cols), F32)
    sems = lambda *dims: pltpu.SemaphoreType.DMA(dims)
    kept_shapes = [
        jax.ShapeDtypeStruct((MB, heads, pack_rows, 128), BF16),
        jax.ShapeDtypeStruct((8, span), F32),
    ]
    results = [low(width)] * 3 + [low(hidden), low(width), low(hidden), low(width)]
    results += [jax.ShapeDtypeStruct((rows, width), F32), low(width)]
    results += [jax.ShapeDtypeStruct((2, lines, lanes), F32)]
    return pl.pallas_call(
        functools.partial(forward_kernel, heads, plan, count, len(vectors)),
        out_shape=[jax.ShapeDtypeStruct(whole(s), s.dtype) for s in shards[:3]]
        + kept_shapes
        + results,
        in_specs=[anywhere] * 2 + [vmem] * 2 + [anywhere] * count + [vmem] * len(vectors),
        out_specs=[anywhere] * 4 + [vmem] + [anywhere] * 10,
        scratch_shapes=[pltpu.VMEM(item.shape, item.dtype) for item in results]
        + [sems(len(results))]
        + dealing_scratch(lengths, dealing)
        + [pltpu.VMEM(whole(s), s.dtype) for s in shards]
        + [pltpu.VMEM((lines, lanes), F32)] * 2
        + [pltpu.VMEM((2, lines, lanes), F32), pltpu.VMEM((2, width), F32)]
        + [pltpu.VMEM((rows, width), BF16)] * 3
        + [full(hidden), full(width), full(width), full(width)]
        + [pltpu.VMEM((heads, pack_rows, 128), BF16)] * MB
        + [
            pltpu.VMEM((MB, heads, pack_rows, 128), BF16),
            pltpu.VMEM((MB, heads, BLK // 2, 128), BF16),
            pltpu.VMEM((MB, heads, BLK // 2, 128), BF16),
            pltpu.VMEM((heads * BLK, HD), BF16),
            pltpu.VMEM((heads * BLK, HD), BF16),
            pltpu.VMEM((heads * BLK, HD), BF16),
            pltpu.VMEM((heads, BLK, HD), F32),
        ]
        + [sems(6, len(plan)), sems(6, len(plan)), sems(2), sems(3), sems(count)]
        + [sems(MB)] * 5,
        compiler_params=pltpu.CompilerParams(
            collective_id=1, has_side_effects=True, vmem_limit_bytes=VMEM_BYTES
        ),
        name="forward",
    )(lengths, dealing, x, cot, *shards, *vectors)


ORDERS = (
    ("yxZz", "xyzZ", "xyzZ", "xyzZ"),
    ("yxzZ", "zxyZ", "xyzZ", "xyzZ"),
    ("yZz", "zyZ", "zyZ", "yzZ"),
)
PIECES = len(ORDERS[0])
SCHEDULE = (
    "up", 0, 1, 2, (1, 0), "down", (1, 2), "back", (2, 0), (2, 1), "qkv", (2, 3), (2, 0),
    (2, 1), (2, 3), (1, 2), (1, 0), (2, 3), (2, 2), (1, 2), "vec", (2, 1), (1, 3), (2, 3),
    (0, 1), (2, 0), (1, 2), (2, 2), (1, 3), (1, 0), (2, 3), (1, 2), (2, 0), "vec", (1, 3),
    (2, 2), (0, 2), "rows", (0, 1), (2, 3), (2, 0), (1, 1), (0, 2), (1, 0), (0, 3), (0, 1),
    "vec", (1, 3), (0, 0), (1, 1), (1, 2), (1, 0), (0, 1), (0, 3), (0, 2), (1, 1), (0, 1),
    (2, 1), (0, 0), (2, 2), "vec", (1, 0), (1, 2), (0, 2), (0, 3), (0, 0), (0, 1), (1, 3),
    (0, 2), (1, 1), (0, 3), (1, 3), (1, 0), (0, 0), (2, 2), (1, 1), "vec", (0, 2), (0, 3),
    (0, 0), (1, 1), (2, 1), (2, 2), (0, 1), (2, 0), (0, 3), (0, 2), (0, 0), (1, 3), (0, 3),
    (1, 1), (2, 1), (0, 0),
)
KEYS = tuple((part, piece) for part in range(3) for piece in range(PIECES))


def landing_shapes(order, shape):
    shards, sides, shapes = 8, shape[0], []
    for name in order:
        if name == "x":
            sides = 1
        else:
            shards //= 2
        shapes.append((sides, shards, shape[2] // PIECES, shape[3]))
    return shapes


def dot_t(a, b):
    return lax.dot_general(a, b, (((0,), (0,)), ((), ())), preferred_element_type=F32)


def lanes_at(first, size):
    return pl.ds(pl.multiple_of(first, 128), size)


def backward_kernel(heads, *refs):
    integers, operands, weights = refs[:2], refs[2:14], refs[14:17]
    rows_out, o_a, o_b, o_c, vec_out = refs[17:22]
    held, load_sem, refs = refs[22:34], refs[34], refs[35:]
    dealt, refs = Dealing(*integers, *refs[:4]), refs[4:]
    da_ref, g_ref, dm_ref, n_ref, du_ref, kept_ref = held[:6]
    lse_ref, a_ref, do_ref, x_ref, vec_ref, dh_ref = held[6:]
    loads = []
    for index, (source, target) in enumerate(zip(operands, held)):
        copy = pltpu.make_async_copy(source, target, load_sem.at[index])
        copy.start()
        loads.append((target, copy))

    def ready(*targets):
        for item in list(loads):
            if any(item[0] is target for target in targets):
                item[1].wait()
                loads.remove(item)

    in_buf = refs[:MB]
    out_buf, back_out, back_in, q_s, k_s, v_s, a_s, dq_s, dk_s, dv_s = refs[MB : MB + 10]
    refs = refs[MB + 10 :]
    dq_ref, dk_ref, dv_ref, m_x, m_a, m_n, m_do, m_du, m_dqkv, m_g, m_dm = refs[:11]
    far_g, far_dm, cross_g, cross_dm = refs[11:15]
    near, (vec_s, v_recv, v_sum, s_a, s_b, s_c) = refs[15:18], refs[18:24]
    refs = refs[24:]
    r_bufs = {}
    for part, piece in KEYS:
        size = len(ORDERS[part][piece])
        r_bufs[part, piece], refs = refs[:size], refs[size:]
    (
        send_sem,
        recv_sem,
        back_send,
        back_recv,
        mate_send,
        mate_recv,
        near_sem,
        rs_send,
        rs_recv,
        ag_send,
        ag_recv,
        own_sem,
        v_send_sem,
        v_recv_sem,
    ) = refs
    c, x = lax.axis_index("ctx"), lax.axis_index("wsh")
    core, y, z, zz = bit_of(c, 1), bit_of(c, 2), bit_of(c, 4), bit_of(c, 8)
    by_core = (flip(c, 1), x)
    by = {"x": (c, 1 - x), "y": (flip(c, 2), x), "z": (flip(c, 4), x), "Z": (flip(c, 8), x)}
    bits = {"y": y, "z": z, "Z": zz}
    peers = plane_peers(c, x, heads)
    blocks, span = heads, BPS * BLK
    width, hidden = da_ref.shape[1], g_ref.shape[1]
    for index, weight in enumerate(weights):
        pltpu.make_async_copy(weight, near[index], near_sem.at[index]).start()
    by_cross = (flip(c, 1), 1 - x)
    greet(peers + [by["x"], by_cross])

    ready(da_ref)
    for m in range(MB):
        row = slice(m * BLK, (m + 1) * BLK)
        for pair in range(heads // 2):
            both = da_ref[row, pair * 128 : (pair + 1) * 128]
            for head in range(2):
                out_buf[m, 2 * pair + head] = fold(both[:, head * HD : (head + 1) * HD])
        for peer in peers:
            send(out_buf.at[m, peer[0]], in_buf[m].at[c], send_sem.at[m], recv_sem.at[m], peer)
        in_buf[m][c] = out_buf[m, c]

    shared = {}

    def share(name, src, dst, peer=by_core):
        index = len(shared)
        shared[name] = send(src, dst, mate_send.at[index], mate_recv.at[index], peer)

    other = 1 - core
    quarter = hidden // 4

    def hidden_rows(side, which):
        return g_ref.at[:, lanes_at(side * 2 * quarter + which * quarter, quarter)]

    ready(g_ref, dm_ref)
    share("far_g", hidden_rows(1 - x, core), far_g, by["x"])
    share("far_dm", dm_ref, far_dm, by["x"])
    share("cross_g", hidden_rows(1 - x, other), cross_g, by_cross)
    ready(n_ref, du_ref)
    share("n", n_ref, m_n)
    share("du", du_ref.at[:, lanes_at(other * (hidden // 2), hidden // 2)], m_du)
    share("g", hidden_rows(x, other), m_g)
    share("dm", dm_ref, m_dm)
    ready(*held)
    share("a", a_ref, m_a)
    share("do", do_ref.at[:, lanes_at(other * (width // 2), width // 2)], m_do)
    share("x", x_ref, m_x)
    dealt.invert()

    sums, outs = (s_a, s_b, s_c), (o_a, o_b, o_c)
    wide = 512

    def tile(pairs, out, first, count):
        def body(turn, carry):
            at = turn * wide
            total = sum(dot_t(lhs[...], rhs[:, lanes_at(col + at, wide)]) for lhs, rhs, col in pairs)
            cols = lanes_at(first + at, wide)
            out[..., cols] = total.astype(BF16).reshape(out.shape[:-1] + (wide,))
            return carry

        lax.fori_loop(0, count, body, 0)

    def grads_up():
        shared["n"].wait_recv()
        shared["du"].wait_recv()
        half = hidden // 2
        tile(((n_ref, du_ref, core * half), (m_n, m_du, 0)), s_b, 0, half // wide)

    def grads_down():
        shared["far_dm"].wait_recv()
        share("cross_dm", far_dm, cross_dm)
        for name in ("g", "dm", "far_g", "cross_g", "cross_dm"):
            shared[name].wait_recv()
        pairs = ((hidden_rows(x, core), dm_ref, 0), (m_g, m_dm, 0))
        pairs += ((far_g, far_dm, 0), (cross_g, cross_dm, 0))
        tile(pairs, s_c.at[0], 0, width // wide)

    def grads_qkv():
        half = width // 2
        for name in ("a", "do", "x", "dq", "dk", "dv"):
            shared[name].wait_recv()
        tile(((a_ref, do_ref, core * half), (m_a, m_do, 0)), s_a, 3 * half, half // wide)
        for index, ref in enumerate((dq_ref, dk_ref, dv_ref)):
            pairs = ((x_ref, ref, core * half), (m_x, m_dqkv, index * half))
            tile(pairs, s_a, index * half, half // wide)

    def attention(m):
        all_bytes(in_buf[m], recv_sem.at[m], heads - 1).wait()
        for b in range(blocks):
            slot = dealt.slot(m, b)
            got = kept_ref[m, slot]
            rows = slice(b * BLK, (b + 1) * BLK)
            q_s[rows, :] = got[:BLK, :HD]
            k_s[rows, :] = got[:BLK, HD:]
            v_s[rows, :] = unpack_fold(got[BLK:])
            a_s[rows, :] = unpack_fold(in_buf[m][slot])

        def one_sequence(s, carry):
            rows = pl.ds(pl.multiple_of(s * span, span), span)
            qq, kk, vv, dd = q_s[rows, :], k_s[rows, :], v_s[rows, :], a_s[rows, :]
            scale = 1.0 / math.sqrt(HD)
            minor = (((1,), (1,)), ((), ()))
            scores = lax.dot_general(kk, qq, minor, preferred_element_type=F32) * scale
            spot = lax.broadcasted_iota(jnp.int32, scores.shape, 0)
            total = lse_ref[pl.ds(m * (blocks // BPS) + s, 1), :]
            probs = jnp.exp(jnp.where(spot < dealt.length(m, s), scores - total, NEG_FILL))
            dp = lax.dot_general(vv, dd, minor, preferred_element_type=F32)
            both = probs * dp
            delta = jnp.sum(both, axis=0, keepdims=True)
            ds = (both - probs * delta).astype(BF16)
            here, split = pl.ds(s * BPS, BPS), (BPS, BLK, HD)
            dv = jnp.dot(probs.astype(BF16), dd, preferred_element_type=F32)
            dv_s[here] = dv.reshape(split)
            dk_s[here] = (jnp.dot(ds, qq, preferred_element_type=F32) * scale).reshape(split)
            dq_s[here] = (dot_t(kk, ds).T * scale).reshape(split)
            return carry

        lax.fori_loop(0, blocks // BPS, one_sequence, 0)
        for t in range(blocks):
            at = dealt.block(m, t)
            back_out[m, t, 0:BLK, :] = jnp.concatenate([dq_s[at], dk_s[at]], axis=1).astype(BF16)
            back_out[m, t, BLK:, :] = fold(dv_s[at]).astype(BF16)
        for peer in peers:
            send(
                back_out.at[m, peer[0]], back_in.at[m, c], back_send.at[m], back_recv.at[m], peer
            )
        back_in[m, c] = back_out[m, c]

    vec_peers = (by["x"], by["y"], by["z"], by["Z"], by_core)
    vec_steps = []

    def vec_send(src):
        step = len(vec_steps)
        vec_steps.append(
            send(
                src, v_recv.at[step], v_send_sem.at[step], v_recv_sem.at[step], vec_peers[step]
            )
        )

    def vec_next():
        step = len(vec_steps) - 1
        vec_steps[step].wait_recv()
        before = vec_s[x] if step == 0 else v_sum[step - 1]
        v_sum[step] = before + v_recv[step]
        if step + 1 < len(vec_peers):
            vec_send(v_sum.at[step])

    def come_back():
        for m in range(MB):
            all_bytes(back_in.at[m], back_recv.at[m], heads - 1).wait()
            row = slice(m * BLK, (m + 1) * BLK)
            for pair in range(heads // 2):
                lanes = slice(pair * 128, (pair + 1) * 128)
                one, two = back_in[m, 2 * pair], back_in[m, 2 * pair + 1]
                dq_ref[row, lanes] = jnp.concatenate([one[:BLK, :HD], two[:BLK, :HD]], axis=1)
                dk_ref[row, lanes] = jnp.concatenate([one[:BLK, HD:], two[:BLK, HD:]], axis=1)
                dv_ref[row, lanes] = jnp.concatenate(
                    [unpack_fold(one[BLK:]), unpack_fold(two[BLK:])], axis=1
                )
        half = width // 2
        for index, (name, ref) in enumerate((("dq", dq_ref), ("dk", dk_ref), ("dv", dv_ref))):
            share(
                name,
                ref.at[:, lanes_at(other * half, half)],
                m_dqkv.at[:, pl.ds(index * half, half)],
            )
        vec_s[...] = vec_ref[...]
        lanes = vec_s.shape[2]
        for index, ref in enumerate((dq_ref, dv_ref)):
            total = jnp.sum(ref[...].astype(F32), axis=0, keepdims=True)
            for side in range(2):
                vec_s[side, index : index + 1, :] = total[:, side * lanes : (side + 1) * lanes]
        vec_send(vec_s.at[1 - x])

    def grad_rows():
        total = dh_ref[...]
        for index, ref in enumerate((dq_ref, dk_ref, dv_ref)):
            pltpu.make_async_copy(weights[index], near[index], near_sem.at[index]).wait()
            total = total + lax.dot_general(
                ref[...], near[index][...], (((1,), (1,)), ((), ())), preferred_element_type=F32
            )
        rows_out[...] = total.astype(BF16)

    plans, gathers = {}, {}
    for key in KEYS:
        alone = sums[key[0]].shape[0] == 1
        first, count, sided = 0, 8, alone
        plans[key], back = [], []
        for name in ORDERS[key[0]][key[1]]:
            if name == "x":
                plans[key].append((by["x"], 1 - x, x, first, first, count))
                sided = True
                continue
            count //= 2
            out, keep = first + (1 - bits[name]) * count, first + bits[name] * count
            side = (0 if alone else x) if sided else None
            plans[key].append((by[name], side, side, out, keep, count))
            back.append((by[name], keep, out, count))
            first = keep
        gathers[key] = back[::-1]
    flights, spread, owns, state = {}, {}, {}, {}

    def piece_rows(key):
        rows = sums[key[0]].shape[2] // PIECES
        return pl.ds(key[1] * rows, rows)

    def reduce_send(key, step):
        peer, side, _, first, _, count = plans[key][step]
        dst = r_bufs[key][step]
        if side is None:
            src = sums[key[0]].at[:, pl.ds(first, count), piece_rows(key)]
        else:
            src, dst = sums[key[0]].at[side, pl.ds(first, count), piece_rows(key)], dst.at[0]
        sems = rs_send.at[key[0], key[1], step], rs_recv.at[key[0], key[1], step]
        flights[key, step] = send(src, dst, *sems, peer)
        state[key] = step

    def reduce_add(key, step):
        _, _, side, _, first, count = plans[key][step]
        flights[key, step].wait_recv()
        total, fresh, rows = sums[key[0]], r_bufs[key][step], piece_rows(key)
        sides = ((0, 0), (1, 1)) if side is None else ((side, 0),)
        for here, there in sides:

            def body(index, carry):
                spot = first + index
                total[here, spot, rows] = (
                    total[here, spot, rows].astype(F32) + fresh[there, index].astype(F32)
                ).astype(BF16)
                return carry

            lax.fori_loop(0, count, body, 0)

    def spread_send(key, kind, src, dst, peer):
        sems = ag_send.at[key[0], key[1], kind], ag_recv.at[key[0], key[1], kind]
        spread[key, kind] = send(src, dst, *sems, peer)

    def advance(key):
        step, steps = state[key], len(plans[key])
        out, rows = outs[key[0]], piece_rows(key)
        if step < steps:
            reduce_add(key, step)
            if step < steps - 1:
                reduce_send(key, step + 1)
                return
            peer, first, _, _ = gathers[key][0]
            side = x if sums[key[0]].shape[0] == 2 else 0
            src = sums[key[0]].at[side, pl.ds(first, 1), rows]
            dst = out.at[core, pl.ds(first, 1), rows]
            owns[key] = pltpu.make_async_copy(src, dst, own_sem.at[key[0], key[1]])
            owns[key].start()
            spread_send(key, 0, src, dst, peer)
            spread_send(key, 3, src, dst, by_core)
        else:
            turn = step - steps + 1
            spread[key, turn - 1].wait_recv()
            if turn == 1:
                owns[key].wait()
            if turn < 3:
                peer, first, _, count = gathers[key][turn]
                ref = out.at[core, pl.ds(first, count), rows]
                spread_send(key, turn, ref, ref, peer)
            _, _, first, count = gathers[key][turn - 1]
            ref = out.at[core, pl.ds(first, count), rows]
            spread_send(key, 3 + turn, ref, ref, by_core)
        state[key] = step + 1

    actions = {
        "up": (grads_up, 1),
        "down": (grads_down, 2),
        "qkv": (grads_qkv, 0),
        "back": (come_back, None),
        "rows": (grad_rows, None),
        "vec": (vec_next, None),
    }
    for event in SCHEDULE:
        if isinstance(event, tuple):
            advance(event)
        elif isinstance(event, int):
            attention(event)
        else:
            action, part = actions[event]
            if event == "vec" and len(vec_steps) == len(vec_peers) and "vec" in state:
                continue
            if event == "vec" and len(vec_steps) == len(vec_peers):
                state["vec"] = True
            action()
            if part is not None:
                for piece in range(PIECES):
                    reduce_send((part, piece), 0)
    vec_out[...] = v_sum[len(vec_peers) - 1]
    for m in range(MB):
        all_bytes(out_buf.at[m], send_sem.at[m], heads - 1).wait()
        all_bytes(back_out.at[m], back_send.at[m], heads - 1).wait()
    for flight in shared.values():
        flight.wait_send()
    for flight in vec_steps:
        flight.wait_send()
    for flight in flights.values():
        flight.wait_send()
    for (_, kind), flight in spread.items():
        if kind >= 3:
            flight.wait_recv()
        flight.wait_send()


def backward(lengths, dealing, da, kept, lse, x, a, n1, g, do, du, dm, vec, dh, weights, heads):
    vmem, anywhere = pl.BlockSpec(memory_space=pltpu.VMEM), pl.BlockSpec(memory_space=pl.ANY)
    rows, width = da.shape
    hidden = g.shape[1]
    pack_rows = BLK + BLK // 2
    low = lambda *dims: pltpu.VMEM(dims, BF16)
    operands = (da, g, dm, n1, du, kept, lse, a, do, x, vec, dh)
    a_shape, b_shape = (2, 8, width // 16, 2 * width), (2, 8, width // 16, hidden // 2)
    c_shape = (1, 8, hidden // 32, width)
    scratch = [pltpu.VMEM(item.shape, item.dtype) for item in operands]
    scratch += [pltpu.SemaphoreType.DMA((len(operands),))]
    scratch += dealing_scratch(lengths, dealing)
    scratch += [low(heads, BLK // 2, 128)] * MB
    scratch += [low(MB, heads, BLK // 2, 128)]
    scratch += [low(MB, heads, pack_rows, 128)] * 2
    scratch += [low(heads * BLK, HD)] * 4
    scratch += [pltpu.VMEM((heads, BLK, HD), F32)] * 3
    scratch += [low(rows, width)] * 6
    scratch += [low(rows, width // 2), low(rows, hidden // 2), low(rows, 3 * width // 2)]
    scratch += [low(rows, hidden // 4), low(rows, width)] * 3
    scratch += [low(*item.shape) for item in weights]
    scratch += [pltpu.VMEM(vec.shape, F32)] + [pltpu.VMEM((5,) + vec.shape[1:], F32)] * 2
    scratch += [low(*shape) for shape in (a_shape, b_shape, c_shape)]
    for key in KEYS:
        shape = (a_shape, b_shape, c_shape)[key[0]]
        scratch += [low(*item) for item in landing_shapes(ORDERS[key[0]][key[1]], shape)]
    sems = lambda *dims: pltpu.SemaphoreType.DMA(dims)
    scratch += [sems(MB)] * 4 + [sems(14)] * 2 + [sems(3)]
    scratch += [sems(3, PIECES, 4)] * 2 + [sems(3, PIECES, 7)] * 2 + [sems(3, PIECES)]
    scratch += [sems(5)] * 2
    return pl.pallas_call(
        functools.partial(backward_kernel, heads),
        out_shape=[
            jax.ShapeDtypeStruct((rows, width), BF16),
            jax.ShapeDtypeStruct(a_shape, BF16),
            jax.ShapeDtypeStruct(b_shape, BF16),
            jax.ShapeDtypeStruct((2,) + c_shape[1:], BF16),
            jax.ShapeDtypeStruct(vec.shape[1:], F32),
        ],
        in_specs=[anywhere] * 17,
        out_specs=[vmem] + [anywhere] * 3 + [vmem],
        scratch_shapes=scratch,
        compiler_params=pltpu.CompilerParams(
            collective_id=2, has_side_effects=True, vmem_limit_bytes=VMEM_BYTES
        ),
        name="backward",
    )(lengths, dealing, *operands, *weights)


def widen_kernel(a_ref, b_ref, c_ref, vec_ref, one_ref, two_ref, one_out, two_out, *outs):
    one_out[...] = one_ref[...]
    two_out[...] = two_ref[...]

    @pl.when(pl.program_id(0) == 0)
    def _():
        line, lanes = 0, vec_ref.shape[1]
        for out in outs[6:]:
            for first in range(0, out.shape[0], lanes):
                out[pl.ds(first, lanes)] = vec_ref[line, :]
                line += 1

    half = outs[0].shape[1] // 2
    for index, out in enumerate(outs[:4]):
        for core in range(2):
            out[:, core * half : (core + 1) * half] = a_ref[
                core, 0, :, index * half : (index + 1) * half
            ].astype(F32)
    up, down = outs[4:6]
    half = up.shape[1] // 2
    for core in range(2):
        up[:, core * half : (core + 1) * half] = b_ref[core, 0].astype(F32)
        down[core, 0] = c_ref[core, 0].astype(F32)


def widen(o_a, o_b, o_c, vec, sizes, one, two):
    shards = o_a.shape[1]
    block = lambda item: pl.BlockSpec((2, 1) + item.shape[2:], lambda i: (0, i, 0, 0))
    rows = o_a.shape[2]
    square = (shards * rows, o_a.shape[3] // 2)
    wide = (shards * rows, 2 * o_b.shape[3])
    strip = pl.BlockSpec((one.shape[0] // shards, one.shape[1]), lambda i: (i, 0))
    return pl.pallas_call(
        widen_kernel,
        grid=(shards,),
        out_shape=[jax.ShapeDtypeStruct(one.shape, one.dtype)] * 2
        + [jax.ShapeDtypeStruct(square, F32)] * 4
        + [jax.ShapeDtypeStruct(wide, F32), jax.ShapeDtypeStruct(o_c.shape, F32)]
        + [jax.ShapeDtypeStruct((size,), F32) for size in sizes],
        in_specs=[block(o_a), block(o_b), block(o_c), pl.BlockSpec(vec.shape, lambda i: (0, 0))]
        + [strip] * 2,
        out_specs=[strip] * 2
        + [pl.BlockSpec((rows, square[1]), lambda i: (i, 0))] * 4
        + [pl.BlockSpec((rows, wide[1]), lambda i: (i, 0)), block(o_c)]
        + [pl.BlockSpec((size,), lambda i: (0,)) for size in sizes],
        compiler_params=pltpu.CompilerParams(vmem_limit_bytes=VMEM_BYTES),
        name="widen",
    )(o_a, o_b, o_c, vec, one, two)


def per_device_heads(tokens, cotangent, lengths, dealing, *params):
    rows_in = tokens.shape[2]
    width = tokens.shape[3]
    rows = MB * rows_in
    weights, vectors = params[:6], params[6:]
    sizes = [item.shape[0] for item in vectors]
    x = tokens.reshape(rows, width)
    lengths, dealing = lengths.transpose(0, 2, 1), dealing.transpose(1, 0, 2)
    query_w, key_w, value_w, kept, lse, a, output, n_low, g, do, du, dm, dh_one, da, vec = forward(
        lengths, dealing, x, cotangent.reshape(rows, width), weights, vectors, HEADS
    )
    grad_tokens, o_a, o_b, o_c, vec_sum = backward(
        lengths,
        dealing,
        da,
        kept,
        lse,
        x,
        a,
        n_low,
        g,
        do,
        du,
        dm,
        vec,
        dh_one,
        (query_w, key_w, value_w),
        HEADS,
    )
    output, grad_tokens, *grads = widen(o_a, o_b, o_c, vec_sum, sizes, output, grad_tokens)
    grads[5] = grads[5].reshape(-1, width)
    shape = (1, MB, rows_in, width)
    return (
        (output.reshape(shape), grad_tokens.reshape(shape))
        + tuple(grads)
    )


def solution(mesh):
    placed = (
        P("wsh", None, "ctx", None),
        P("wsh", None, "ctx", None),
        P("wsh", None, None),
        P("wsh", None, None),
        P("wsh", None),
        P("wsh", None),
        P("wsh", None),
        P("wsh", None),
        P("wsh", None),
        P("wsh", None),
        P("wsh"),
        P("wsh"),
        P("wsh"),
        P("wsh"),
        P("wsh"),
        P("wsh"),
        P("wsh"),
        P("wsh"),
        P("wsh"),
    )
    by_heads = mesh.shape["ctx"] == HEADS and mesh.shape["wsh"] == 2
    return jax.shard_map(
        per_device_heads if by_heads else per_device,
        mesh=mesh,
        in_specs=placed,
        out_specs=(
            P("wsh", None, "ctx", None),
            P("wsh", None, "ctx", None),
            P("wsh", None),
            P("wsh", None),
            P("wsh", None),
            P("wsh", None),
            P("wsh", None),
            P("wsh", None),
            P("wsh"),
            P("wsh"),
            P("wsh"),
            P("wsh"),
            P("wsh"),
            P("wsh"),
            P("wsh"),
            P("wsh"),
            P("wsh"),
        ),
        check_vma=False,
    )
```

```python
import functools
import math

import jax
import jax.numpy as jnp
from jax import lax
from jax.experimental import pallas as pl
from jax.experimental.pallas import tpu as pltpu
from jax.sharding import PartitionSpec as P

HEADS = 16
BPS = 8
MB = 3
BLK = 64


EPSILON = 1e-12
NEG_FILL = -1e30


def as_sent(x):
    return jax.tree.map(lambda a: a.astype(jnp.bfloat16) if a.dtype == jnp.float32 else a, x)


def layer_norm(summed, gain_vec, shift_vec):
    row_mean = jnp.mean(summed, axis=-1, keepdims=True)
    centred = summed - row_mean
    row_var = jnp.mean(centred * centred, axis=-1, keepdims=True)
    return centred * lax.rsqrt(row_var + EPSILON) * gain_vec + shift_vec


def gelu_exact(values):
    return jax.nn.gelu(values, approximate=False)


def row_labels(dealt_order, seq_lengths):
    blocks_of_rows = jnp.repeat(dealt_order, BLK)
    within = jnp.tile(jnp.arange(BLK, dtype=jnp.int32), dealt_order.shape[0])
    seq_ids = blocks_of_rows // BPS
    places = blocks_of_rows % BPS * BLK + within
    numbers = jnp.arange(seq_lengths.shape[0], dtype=jnp.int32)
    seq_bound = jnp.sum(
        jnp.where(seq_ids[:, None] == numbers[None, :], seq_lengths[None, :], 0), axis=1
    )
    return (seq_ids, places < seq_bound)


def blockwise(carried, total_rows, step_rows, visit_block):
    return lax.fori_loop(
        0,
        total_rows // step_rows,
        lambda turn_index, running: visit_block(running, turn_index * step_rows),
        carried,
    )


def masked_scores(query_blk, key_blk, query_seq, key_seq, key_valid, scale_factor):
    allowed = (query_seq[:, None] == key_seq[None, :]) & key_valid[None, :]
    scores = (
        jnp.einsum("qhd,khd->hqk", query_blk, key_blk, preferred_element_type=jnp.float32)
        * scale_factor
    )
    return (jnp.where(allowed[None], scores, NEG_FILL), allowed[None].astype(jnp.float32))


def attention_grads(
    query_blk,
    grad_blk,
    key_blk,
    value_blk,
    query_seq,
    key_seq,
    key_valid,
    row_total,
    row_delta,
    scale_factor,
):
    scores, allowed = masked_scores(query_blk, key_blk, query_seq, key_seq, key_valid, scale_factor)
    probs = jnp.exp(scores - row_total[:, :, None]) * allowed
    grad_probs = jnp.einsum("qhd,khd->hqk", grad_blk, value_blk, preferred_element_type=jnp.float32)
    grad_scores = (probs * (grad_probs - row_delta[:, :, None])).astype(jnp.bfloat16)
    return (probs.astype(jnp.bfloat16), grad_scores)


def gather_params(params):
    return (
        lax.all_gather(params[0], "wsh", axis=0, tiled=True),
        lax.all_gather(params[1], "wsh", axis=0, tiled=True),
        lax.all_gather(params[2], "wsh", axis=0, tiled=True),
        lax.all_gather(params[3], "wsh", axis=0, tiled=True),
        lax.all_gather(params[4], "wsh", axis=0, tiled=True),
        lax.all_gather(params[5], "wsh", axis=0, tiled=True),
        lax.all_gather(params[6], "wsh", axis=0, tiled=True),
        lax.all_gather(params[7], "wsh", axis=0, tiled=True),
        lax.all_gather(params[8], "wsh", axis=0, tiled=True),
        lax.all_gather(params[9], "wsh", axis=0, tiled=True),
        lax.all_gather(params[10], "wsh", axis=0, tiled=True),
        lax.all_gather(params[11], "wsh", axis=0, tiled=True),
        lax.all_gather(params[12], "wsh", axis=0, tiled=True),
        lax.all_gather(params[13], "wsh", axis=0, tiled=True),
        lax.all_gather(params[14], "wsh", axis=0, tiled=True),
    )


def per_device(
    tokens,
    cotangent,
    lengths,
    dealing,
    w_query,
    w_key,
    w_value,
    w_out,
    w_up,
    w_down,
    b_query,
    b_value,
    b_out,
    b_up,
    b_down,
    gain_one,
    shift_one,
    gain_two,
    shift_two,
):
    params = (
        w_query,
        w_key,
        w_value,
        w_out,
        w_up,
        w_down,
        b_query,
        b_value,
        b_out,
        b_up,
        b_down,
        gain_one,
        shift_one,
        gain_two,
        shift_two,
    )
    own_rows = tokens.shape[2]
    width = tokens.shape[3]
    head_size = width // HEADS
    scale_factor = 1.0 / math.sqrt(head_size)
    my_start = lax.axis_index("ctx") * own_rows
    wsh_count = lax.axis_size("wsh")
    grads = tuple(
        (jnp.zeros((item.shape[0] * wsh_count,) + item.shape[1:], jnp.float32) for item in params)
    )
    results = []
    input_grads = []
    for micro in range(MB):
        whole = gather_params(params)
        query_weight, key_weight, value_weight, out_weight, up_weight, down_weight = whole[:6]
        (
            bias_query,
            bias_value,
            bias_out,
            bias_up,
            bias_down,
            gain_first,
            shift_first,
            gain_second,
            shift_second,
        ) = tuple((item.astype(jnp.float32) for item in whole[6:]))
        token_rows = tokens[0, micro]
        seq_all, valid_all = row_labels(dealing[0, micro], lengths[0, micro])
        my_seq = lax.dynamic_slice_in_dim(seq_all, my_start, own_rows)
        my_valid = lax.dynamic_slice_in_dim(valid_all, my_start, own_rows)
        query_low = (
            jnp.dot(token_rows, query_weight, preferred_element_type=jnp.float32) + bias_query
        ).astype(jnp.bfloat16)
        key_low = jnp.dot(token_rows, key_weight, preferred_element_type=jnp.float32).astype(
            jnp.bfloat16
        )
        value_low = (
            jnp.dot(token_rows, value_weight, preferred_element_type=jnp.float32) + bias_value
        ).astype(jnp.bfloat16)
        query_heads = query_low.reshape(own_rows, HEADS, head_size)
        my_key_heads = key_low.reshape(own_rows, HEADS, head_size)
        my_value_heads = value_low.reshape(own_rows, HEADS, head_size)
        start_state = (
            jnp.full((HEADS, own_rows), NEG_FILL, jnp.float32),
            jnp.zeros((HEADS, own_rows), jnp.float32),
            jnp.zeros((own_rows, HEADS, head_size), jnp.float32),
        )
        key_piece = lax.all_gather(key_low, "ctx", axis=0, tiled=True)
        value_piece = lax.all_gather(value_low, "ctx", axis=0, tiled=True)
        piece_rows = key_piece.shape[0]
        step_rows = math.gcd(piece_rows, 512)

        def visit_block(running, offset):
            run_max, run_sum, run_acc = running
            key_blk = lax.dynamic_slice_in_dim(key_piece, offset, step_rows).reshape(
                step_rows, HEADS, head_size
            )
            value_blk = lax.dynamic_slice_in_dim(value_piece, offset, step_rows).reshape(
                step_rows, HEADS, head_size
            )
            key_seq = lax.dynamic_slice_in_dim(seq_all, offset, step_rows)
            key_valid = lax.dynamic_slice_in_dim(valid_all, offset, step_rows)
            scores, allowed = masked_scores(
                query_heads, key_blk, my_seq, key_seq, key_valid, scale_factor
            )
            new_max = jnp.maximum(run_max, jnp.max(scores, axis=-1))
            rescale = jnp.exp(run_max - new_max)
            weights = jnp.exp(scores - new_max[:, :, None]) * allowed
            run_sum = run_sum * rescale + jnp.sum(weights, axis=-1)
            run_acc = run_acc * rescale.T[:, :, None] + jnp.einsum(
                "hqk,khd->qhd",
                weights.astype(jnp.bfloat16),
                value_blk,
                preferred_element_type=jnp.float32,
            )
            return (new_max, run_sum, run_acc)

        final_max, final_sum, final_acc = blockwise(start_state, piece_rows, step_rows, visit_block)
        attended = final_acc / final_sum.T[:, :, None]
        log_total = final_max + jnp.log(final_sum)
        attended_low = attended.reshape(own_rows, width).astype(jnp.bfloat16)
        out_proj = jnp.dot(attended_low, out_weight, preferred_element_type=jnp.float32) + bias_out
        first_sum = token_rows.astype(jnp.float32) + out_proj
        norm_one, norm_one_back = jax.vjp(layer_norm, first_sum, gain_first, shift_first)
        mlp_input = norm_one.astype(jnp.bfloat16)
        up_pre = jnp.dot(mlp_input, up_weight, preferred_element_type=jnp.float32) + bias_up
        activated, gelu_back = jax.vjp(gelu_exact, up_pre)
        activated_low = activated.astype(jnp.bfloat16)
        down_out = (
            jnp.dot(activated_low, down_weight, preferred_element_type=jnp.float32) + bias_down
        )
        result, norm_two_back = jax.vjp(layer_norm, norm_one + down_out, gain_second, shift_second)
        results.append(result.astype(jnp.bfloat16))
        grad_second, grad_gain_b, grad_shift_b = norm_two_back(
            cotangent[0, micro].astype(jnp.float32)
        )
        grad_down_low = grad_second.astype(jnp.bfloat16)
        grad_activated = jnp.einsum(
            "rd,fd->rf", grad_down_low, down_weight, preferred_element_type=jnp.float32
        )
        (grad_up_pre,) = gelu_back(grad_activated)
        grad_up_low = grad_up_pre.astype(jnp.bfloat16)
        grad_norm_one = (
            jnp.einsum("rf,df->rd", grad_up_low, up_weight, preferred_element_type=jnp.float32)
            + grad_second
        )
        grad_first, grad_gain_a, grad_shift_a = norm_one_back(grad_norm_one)
        grad_out_low = grad_first.astype(jnp.bfloat16)
        grad_att_low = jnp.einsum(
            "rd,ed->re", grad_out_low, out_weight, preferred_element_type=jnp.float32
        ).astype(jnp.bfloat16)
        grad_heads = grad_att_low.reshape(own_rows, HEADS, head_size)
        row_delta = jnp.sum(grad_heads.astype(jnp.float32) * attended, axis=-1).T
        empty_heads = jnp.zeros((own_rows, HEADS, head_size), jnp.float32)
        query_key_piece = lax.all_gather(key_low, "ctx", axis=0, tiled=True)
        query_value_piece = lax.all_gather(value_low, "ctx", axis=0, tiled=True)
        query_piece_rows = query_key_piece.shape[0]
        query_step_rows = math.gcd(query_piece_rows, 512)

        def query_visit_block(running, offset):
            key_blk = lax.dynamic_slice_in_dim(query_key_piece, offset, query_step_rows).reshape(
                query_step_rows, HEADS, head_size
            )
            value_blk = lax.dynamic_slice_in_dim(
                query_value_piece, offset, query_step_rows
            ).reshape(query_step_rows, HEADS, head_size)
            key_seq = lax.dynamic_slice_in_dim(seq_all, offset, query_step_rows)
            key_valid = lax.dynamic_slice_in_dim(valid_all, offset, query_step_rows)
            probs_low, grad_scores = attention_grads(
                query_heads,
                grad_heads,
                key_blk,
                value_blk,
                my_seq,
                key_seq,
                key_valid,
                log_total,
                row_delta,
                scale_factor,
            )
            return running + jnp.einsum(
                "hqk,khd->qhd", grad_scores, key_blk, preferred_element_type=jnp.float32
            )

        grad_query_sum = blockwise(
            empty_heads, query_piece_rows, query_step_rows, query_visit_block
        )
        total_all, delta_all = (
            lax.all_gather(log_total.T, "ctx", axis=0, tiled=True),
            lax.all_gather(row_delta.T, "ctx", axis=0, tiled=True),
        )
        query_piece = lax.all_gather(query_low, "ctx", axis=0, tiled=True)
        grad_piece = lax.all_gather(grad_att_low, "ctx", axis=0, tiled=True)
        key_piece_rows = query_piece.shape[0]
        key_step_rows = math.gcd(key_piece_rows, 512)

        def key_visit_block(running, offset):
            grad_key_run, grad_value_run = running
            query_blk = lax.dynamic_slice_in_dim(query_piece, offset, key_step_rows).reshape(
                key_step_rows, HEADS, head_size
            )
            grad_blk = lax.dynamic_slice_in_dim(grad_piece, offset, key_step_rows).reshape(
                key_step_rows, HEADS, head_size
            )
            total_blk = lax.dynamic_slice_in_dim(total_all, offset, key_step_rows)
            delta_blk = lax.dynamic_slice_in_dim(delta_all, offset, key_step_rows)
            query_seq = lax.dynamic_slice_in_dim(seq_all, offset, key_step_rows)
            probs_low, grad_scores = attention_grads(
                query_blk,
                grad_blk,
                my_key_heads,
                my_value_heads,
                query_seq,
                my_seq,
                my_valid,
                total_blk.T,
                delta_blk.T,
                scale_factor,
            )
            grad_key_run = grad_key_run + jnp.einsum(
                "hqk,qhd->khd", grad_scores, query_blk, preferred_element_type=jnp.float32
            )
            grad_value_run = grad_value_run + jnp.einsum(
                "hqk,qhd->khd", probs_low, grad_blk, preferred_element_type=jnp.float32
            )
            return (grad_key_run, grad_value_run)

        grad_key_sum, grad_value_sum = blockwise(
            (empty_heads, empty_heads), key_piece_rows, key_step_rows, key_visit_block
        )
        grad_key_flat = grad_key_sum.reshape(own_rows, width)
        grad_value_flat = grad_value_sum.reshape(own_rows, width)
        grad_query_low = (
            (grad_query_sum * scale_factor).reshape(own_rows, width).astype(jnp.bfloat16)
        )
        grad_key_low = (grad_key_flat * scale_factor).astype(jnp.bfloat16)
        grad_value_low = grad_value_flat.astype(jnp.bfloat16)
        terms = (
            jnp.einsum("rd,re->de", token_rows, grad_query_low, preferred_element_type=jnp.float32),
            jnp.einsum("rd,re->de", token_rows, grad_key_low, preferred_element_type=jnp.float32),
            jnp.einsum("rd,re->de", token_rows, grad_value_low, preferred_element_type=jnp.float32),
            jnp.einsum("rd,re->de", attended_low, grad_out_low, preferred_element_type=jnp.float32),
            jnp.einsum("rd,rf->df", mlp_input, grad_up_low, preferred_element_type=jnp.float32),
            jnp.einsum(
                "rf,rd->fd", activated_low, grad_down_low, preferred_element_type=jnp.float32
            ),
            jnp.sum(grad_query_low.astype(jnp.float32), axis=0),
            jnp.sum(grad_value_low.astype(jnp.float32), axis=0),
            jnp.sum(grad_out_low.astype(jnp.float32), axis=0),
            jnp.sum(grad_up_low.astype(jnp.float32), axis=0),
            jnp.sum(grad_down_low.astype(jnp.float32), axis=0),
            grad_gain_a,
            grad_shift_a,
            grad_gain_b,
            grad_shift_b,
        )
        grads = tuple((total_now + fresh for total_now, fresh in zip(grads, terms)))
        grad_rows = (
            grad_first
            + jnp.einsum(
                "re,de->rd", grad_query_low, query_weight, preferred_element_type=jnp.float32
            )
            + jnp.einsum("re,de->rd", grad_key_low, key_weight, preferred_element_type=jnp.float32)
            + jnp.einsum(
                "re,de->rd", grad_value_low, value_weight, preferred_element_type=jnp.float32
            )
        )
        input_grads.append(grad_rows.astype(jnp.bfloat16))
    shards = jax.tree.map(
        lambda part: part.astype(jnp.float32),
        lax.psum_scatter(as_sent(grads), "wsh", scatter_dimension=0, tiled=True),
    )
    summed = jax.tree.map(lambda part: part.astype(jnp.float32), lax.psum(as_sent(shards), "ctx"))
    return (jnp.stack(results)[None], jnp.stack(input_grads)[None]) + tuple(summed)


MESH_IDS = pl.DeviceIdType.MESH
F32 = jnp.float32
BF16 = jnp.bfloat16
HD = 64
VMEM_BYTES = 60 * 1024 * 1024


def flip(index, bit):
    return index + bit * (1 - 2 * lax.rem(lax.div(index, bit), 2))


def bit_of(index, bit):
    return lax.rem(lax.div(index, bit), 2)


def greet(peers):
    barrier = pltpu.get_barrier_semaphore()
    for peer in peers:
        pl.semaphore_signal(barrier, inc=1, device_id=peer, device_id_type=MESH_IDS)
    pl.semaphore_wait(barrier, len(peers))


def send(src, dst, send_sem, recv_sem, peer):
    copy = pltpu.make_async_remote_copy(
        src_ref=src,
        dst_ref=dst,
        send_sem=send_sem,
        recv_sem=recv_sem,
        device_id=peer,
        device_id_type=MESH_IDS,
    )
    copy.start()
    return copy


class Dealing:
    def __init__(self, lengths_hbm, dealing_hbm, lengths, dealing, slots, sems):
        self.lengths, self.dealing, self.slots = lengths, dealing, slots
        self.copies = (
            pltpu.make_async_copy(lengths_hbm, lengths, sems.at[0]),
            pltpu.make_async_copy(dealing_hbm, dealing, sems.at[1]),
        )
        for copy in self.copies:
            copy.start()

    def invert(self):
        for copy in self.copies:
            copy.wait()
        micros, _, count = self.dealing.shape

        def find(number, carry):
            m, block = lax.div(number, count), lax.rem(number, count)
            slot = jnp.int32(0)
            for t in range(count):
                slot = jnp.where(self.dealing[m, 0, t] == block, jnp.int32(t), slot)
            self.slots[m, block] = slot
            return carry

        lax.fori_loop(0, micros * count, find, 0)

    def length(self, m, s):
        return self.lengths[0, s, m]

    def block(self, m, t):
        return self.dealing[m, 0, t]

    def slot(self, m, b):
        return self.slots[m, b]


def dealing_scratch(lengths, dealing):
    return [
        pltpu.SMEM(lengths.shape, jnp.int32),
        pltpu.SMEM(dealing.shape, jnp.int32),
        pltpu.SMEM((dealing.shape[0], dealing.shape[2]), jnp.int32),
        pltpu.SemaphoreType.DMA((2,)),
    ]


def plane_peers(c, w, count):
    return [(lax.rem(c + step, count), w) for step in range(1, count)]


def pack_two(first, second, row, pair, out):
    cols = pl.ds(pair * 128, 128)
    a, b = first[pl.ds(row, BLK), cols], second[pl.ds(row, BLK), cols]
    for head in range(2):
        lane = slice(head * HD, head * HD + HD)
        out[2 * pair + head, 0:BLK, :] = jnp.concatenate([a[:, lane], b[:, lane]], axis=1)


def pack_one(source, row, pair, out):
    both = source[pl.ds(row, BLK), pl.ds(pair * 128, 128)]
    for head in range(2):
        lane = slice(head * HD, head * HD + HD)
        out[2 * pair + head, BLK : BLK + BLK // 2, :] = fold(both[:, lane])


def unpack_fold(block):
    return jnp.concatenate([block[:, :HD], block[:, HD:]], axis=0)


def fold(rows):
    half = rows.shape[0] // 2
    return jnp.concatenate([rows[:half], rows[half:]], axis=1)


def all_bytes(ref, sem, peers):
    view = ref.at[pl.ds(0, peers)]
    return pltpu.make_async_copy(view, view, sem)


def norm_parts(summed):
    row_mean = jnp.mean(summed, axis=-1, keepdims=True)
    centred = summed - row_mean
    row_var = jnp.mean(centred * centred, axis=-1, keepdims=True)
    scale = lax.rsqrt(row_var + EPSILON)
    return centred * scale, scale


def norm_back(grad, unit, scale, gain):
    inner = grad * gain
    mean_one = jnp.mean(inner, axis=-1, keepdims=True)
    mean_two = jnp.mean(inner * unit, axis=-1, keepdims=True)
    return scale * (inner - mean_one - unit * mean_two)


def dot_minor(a, b):
    return lax.dot_general(a, b, (((1,), (1,)), ((), ())), preferred_element_type=F32)


ROW_OUT, ROW_UP, ROW_DOWN, ROW_GAIN_ONE, ROW_SHIFT_ONE, ROW_GAIN_TWO, ROW_SHIFT_TWO = 2, 3, 7, 8, 9, 10, 11


SQUARE, PAIR_Y, PAIR_Z, ALONE = (8, "yz"), (4, "y"), (4, "z"), (2, "")
WAYS = (
    SQUARE, SQUARE, SQUARE, ALONE, PAIR_Y, PAIR_Y, SQUARE, SQUARE, SQUARE, PAIR_Z, ALONE, PAIR_Y,
)
SEND_ORDER = (1, 0, 2, 7, 6, 5, 11, 9, 4, 8, 3, 10)
FORWARD_SCHEDULE = (
    ("own", 0), ("own", 1), ("own", 2), ("second", 1), ("second", 0), ("third", 1), ("third",
    0), ("second", 2), ("fourth", 1), ("project", 1), ("second", 7), ("fourth", 0), ("third",
    2), ("project", 0), ("keys", 0), ("keys", 1), ("third", 7), ("second", 6), ("fourth", 2),
    ("project", 2), ("values", 0), ("values", 1), ("keys", 2), ("second", 5), ("values", 2),
    ("att", 0), ("second", 8), ("att", 1), ("second", 4), ("fourth", 7), ("att", 2), ("fourth",
    5), ("fourth", 3), ("third", 6), ("third", 8), ("second", 9), ("fourth", 4), ("rows", 0),
    ("second", 11), ("fourth", 6), ("out", 0), ("hidden", 0), ("hidden", 1), ("fourth", 8),
    ("hidden", 2), ("fourth", 9), ("hidden", 3), ("fourth", 10), ("hidden", 4), ("fourth", 11),
    ("hidden", 5), ("hidden", 6), ("hidden", 7),
)


def weight_plan(shards):
    unit = shards[0].shape[0] * shards[0].shape[1]
    plan = []
    for index, (rows, cols) in enumerate(shard.shape for shard in shards):
        parts = max(1, rows * cols // unit)
        for part in range(parts):
            plan.append((index, part * (rows // parts), rows // parts, WAYS[len(plan)]))
    return plan


def forward_kernel(heads, plan, n_weights, n_vectors, *refs):
    integers, (x_ref, cot_ref), refs = refs[:2], refs[2:4], refs[4:]
    shards, vectors = refs[:n_weights], refs[n_weights : n_weights + n_vectors]
    refs = refs[n_weights + n_vectors :]
    wholes, kept_ref, lse_ref = refs[:3], *refs[3:5]
    results, refs = refs[5:15], refs[15:]
    a_ref, out_ref, n_ref, g_ref, do_ref, du_ref, dm_ref, dh_ref, da_ref, vec_ref = refs[:10]
    made, result_sem, refs = refs[:10], refs[10], refs[11:]
    dealt, refs = Dealing(*integers, *refs[:4]), refs[4:]
    near, refs = refs[:n_weights], refs[n_weights:]
    small, small_in, small_whole, bias, q_ref, k_ref, v_ref = refs[:7]
    begun, slope, n_full, unit, total = refs[7:12]
    refs = refs[12:]
    in_buf = refs[:MB]
    out_buf, back_out, back_in, q_s, k_s, v_s, a_s = refs[MB : 7 + MB]
    (
        w_send,
        w_recv,
        small_sems,
        local_sem,
        stage_sem,
        send_sem,
        recv_sem,
        back_send,
        back_recv,
        keep_sem,
    ) = refs[7 + MB :]
    c, w = lax.axis_index("ctx"), lax.axis_index("wsh")
    o = 1 - w
    by_x, by_y, by_z, by_core = (c, o), (flip(c, 2), w), (flip(c, 4), w), (flip(c, 1), w)
    core, y, z = bit_of(c, 1), bit_of(c, 2), bit_of(c, 4)
    peers = plane_peers(c, w, heads)
    stores = []

    def store(target):
        index = [item is target for item in made].index(True)
        copy = pltpu.make_async_copy(target, results[index], result_sem.at[index])
        copy.start()
        stores.append(copy)

    staged = []
    for index, shard in enumerate(shards):
        rows = shard.shape[0]
        spot = pl.ds(pl.multiple_of(w * rows, rows), rows)
        copy = pltpu.make_async_copy(shard, near[index].at[spot], stage_sem.at[index])
        copy.start()
        staged.append(copy)
    line, lanes = 0, small.shape[1]
    for vector in vectors:
        for first in range(0, vector.shape[0], lanes):
            piece = vector[pl.ds(first, lanes)].astype(F32)
            small[line : line + 1, :] = piece.reshape(1, lanes)
            line += 1
    greet(peers + [by_x])
    small_sent = send(small, small_in, small_sems.at[0], small_sems.at[1], by_x)

    def part(chunk, side, piece, start, count):
        tensor, first, rows, way = plan[chunk]
        half = shards[tensor].shape[0]
        at = side * half + first + piece * (rows // way[0]) + start
        return near[tensor].at[pl.ds(pl.multiple_of(at, 8), count)]

    steps = {}

    def sem(kind, chunk):
        return w_send.at[kind, chunk], w_recv.at[kind, chunk]

    def own_piece(way):
        return {
            SQUARE: core * 4 + z * 2 + y,
            PAIR_Y: core * 2 + y,
            PAIR_Z: core * 2 + z,
            ALONE: core,
        }[way]

    for chunk in SEND_ORDER:
        tensor, first, rows, way = plan[chunk]
        size, mine = rows // way[0], own_piece(way)
        src = shards[tensor].at[pl.ds(pl.multiple_of(first + mine * size, 8), size)]
        steps[chunk, 0] = send(src, part(chunk, w, mine, 0, size), *sem(0, chunk), by_x)
    dealt.invert()

    def second(chunk):
        _, _, rows, way = plan[chunk]
        steps[chunk, 0].wait_recv()
        ref = part(chunk, o, own_piece(way), 0, rows // way[0])
        for name in way[1]:
            kind, peer = {"y": (1, by_y), "z": (2, by_z)}[name]
            steps[chunk, kind] = send(ref, ref, *sem(kind, chunk), peer)

    def third(chunk):
        _, _, rows, way = plan[chunk]
        size = rows // way[0]
        steps[chunk, 1].wait_recv()
        steps[chunk, 2].wait_recv()
        ref = part(chunk, o, core * 4 + (1 - z) * 2 + y, 0, size // 2)
        steps[chunk, 3] = send(ref, ref, *sem(3, chunk), by_y)
        ref = part(chunk, o, core * 4 + z * 2 + (1 - y), size // 2, size // 2)
        steps[chunk, 4] = send(ref, ref, *sem(4, chunk), by_z)

    def fourth(chunk):
        _, _, rows, way = plan[chunk]
        for kind in {SQUARE: (3, 4), PAIR_Y: (1,), PAIR_Z: (2,), ALONE: (0,)}[way]:
            steps[chunk, kind].wait_recv()
        ref = part(chunk, o, core * (way[0] // 2), 0, rows // 2)
        steps[chunk, 5] = send(ref, ref, *sem(5, chunk), by_core)

    width = x_ref.shape[1]
    step = 256
    projected = []

    def half_product(index, side, cols):
        rows = shards[index].shape[0]
        lanes_in = pl.ds(pl.multiple_of(side * rows, rows), rows)
        return jnp.dot(
            x_ref[:, lanes_in], near[index][lanes_in, cols], preferred_element_type=F32
        )

    def own_half(index):
        staged[index].wait()

        def some_columns(turn, carry):
            cols = pl.ds(pl.multiple_of(turn * step, step), step)
            begun[index, :, cols] = half_product(index, w, cols)
            return carry

        lax.fori_loop(0, width // step, some_columns, 0)

    def project(index):
        if not projected:
            small_sent.wait()
            small_whole[w] = small[...]
            small_whole[o] = small_in[...]
            for side in range(2):
                for row in range(2):
                    bias[row : row + 1, side * lanes : (side + 1) * lanes] = small_whole[
                        side, row : row + 1, :
                    ]
        projected.append(index)
        steps[index, 5].wait_recv()
        out = (q_ref, k_ref, v_ref)[index]

        def some_columns(turn, carry):
            cols = pl.ds(pl.multiple_of(turn * step, step), step)
            product = begun[index, :, cols] + half_product(index, o, cols)
            if index != 1:
                product = product + bias[index // 2 : index // 2 + 1, cols]
            out[:, cols] = product.astype(BF16)
            return carry

        lax.fori_loop(0, width // step, some_columns, 0)
        pltpu.make_async_copy(near[index], wholes[index], local_sem.at[index]).start()

    def pack(item, first, count, fill):
        for pair in range(heads // 2):
            fill(item, pair)
        rows = pl.ds(first, count)
        for peer in peers:
            send(
                out_buf.at[item, peer[0], rows],
                in_buf[item].at[c, rows],
                send_sem.at[item],
                recv_sem.at[item],
                peer,
            )
        in_buf[item][c, rows] = out_buf[item, c, rows]

    def pack_keys(m):
        pack(m, 0, BLK, lambda m, pair: pack_two(q_ref, k_ref, m * BLK, pair, out_buf.at[m]))

    def pack_values(m):
        pack(m, BLK, BLK // 2, lambda m, pair: pack_one(v_ref, m * BLK, pair, out_buf.at[m]))

    blocks = heads
    span = BPS * BLK

    def attention(m):
        all_bytes(in_buf[m], recv_sem.at[m], heads - 1).wait()
        pltpu.make_async_copy(in_buf[m], kept_ref.at[m], keep_sem.at[m]).start()
        for b in range(blocks):
            got = in_buf[m][dealt.slot(m, b)]
            q_s[b * BLK : (b + 1) * BLK, :] = got[:BLK, :HD]
            k_s[b * BLK : (b + 1) * BLK, :] = got[:BLK, HD:]
            v_s[b * BLK : (b + 1) * BLK, :] = unpack_fold(got[BLK:])

        def one_sequence(s, carry):
            rows = pl.ds(pl.multiple_of(s * span, span), span)
            scores = lax.dot_general(
                k_s[rows, :], q_s[rows, :], (((1,), (1,)), ((), ())), preferred_element_type=F32
            ) * (1.0 / math.sqrt(HD))
            place = lax.broadcasted_iota(jnp.int32, scores.shape, 0)
            scores = jnp.where(place < dealt.length(m, s), scores, NEG_FILL)
            top = jnp.max(scores, axis=0, keepdims=True)
            weights = jnp.exp(scores - top)
            summed = jnp.sum(weights, axis=0, keepdims=True)
            out_t = lax.dot_general(
                v_s[rows, :],
                weights.astype(BF16),
                (((0,), (0,)), ((), ())),
                preferred_element_type=F32,
            )
            a_s[pl.ds(s * BPS, BPS)] = (out_t / summed).T.reshape(BPS, BLK, HD)
            lse_ref[pl.ds(m * (blocks // BPS) + s, 1), :] = top + jnp.log(summed)
            return carry

        lax.fori_loop(0, blocks // BPS, one_sequence, 0)
        for t in range(blocks):
            back_out[m, t] = fold(a_s[dealt.block(m, t)]).astype(BF16)
        for peer in peers:
            send(
                back_out.at[m, peer[0]], back_in.at[m, c], back_send.at[m], back_recv.at[m], peer
            )
        back_in[m, c] = back_out[m, c]

    def come_back(_):
        for m in range(MB):
            all_bytes(back_in.at[m], back_recv.at[m], heads - 1).wait()
            for pair in range(heads // 2):
                a_ref[m * BLK : (m + 1) * BLK, pair * 128 : (pair + 1) * 128] = jnp.concatenate(
                    [unpack_fold(back_in[m, 2 * pair]), unpack_fold(back_in[m, 2 * pair + 1])],
                    axis=1,
                )
        store(a_ref)

    def line_of(row):
        return jnp.concatenate(
            [small_whole[0, row : row + 1, :], small_whole[1, row : row + 1, :]], axis=1
        )

    def keep(row, values):
        summed = jnp.sum(values, axis=0, keepdims=True)
        for side in range(2):
            vec_ref[side, row : row + 1, :] = summed[:, side * lanes : (side + 1) * lanes]

    out_w, up_w, down_w = near[3:]
    chunks_of = {t: [i for i, item in enumerate(plan) if item[0] == t] for t in range(n_weights)}

    def arrived(tensor, chunks):
        for chunk in chunks:
            steps[chunk, 5].wait_recv()

    def out_project(_):
        staged[3].wait()
        arrived(3, chunks_of[3])
        h_one = x_ref[...].astype(F32) + (
            jnp.dot(a_ref[...], out_w[...], preferred_element_type=F32) + line_of(ROW_OUT)
        )
        unit_one, scale_one = norm_parts(h_one)
        unit[...] = unit_one
        n_one = unit_one * line_of(ROW_GAIN_ONE) + line_of(ROW_SHIFT_ONE)
        n_full[...] = n_one
        n_ref[...] = n_one.astype(BF16)
        store(n_ref)
        total[...] = jnp.zeros_like(total)
        kept_scale.append(scale_one)

    kept_scale = []
    hidden = g_ref.shape[1]
    hidden_steps = hidden // lanes
    per_half = hidden_steps // 2

    def hidden_at(turn):
        j = lax.rem(w * per_half + turn, hidden_steps)
        cols = pl.ds(pl.multiple_of(j * lanes, lanes), lanes)
        return cols, lax.div(j, per_half), pl.ds(ROW_UP + lax.rem(j, per_half), 1)

    def hidden_up(turn):
        if turn == 0:
            staged[4].wait()
            arrived(4, chunks_of[4])
            staged[5].wait()
        elif turn >= per_half:
            share = len(chunks_of[5]) // per_half
            first = (turn - per_half) * share
            arrived(5, chunks_of[5][first : first + share])
        cols, side, row = hidden_at(turn)
        u = jnp.dot(n_ref[...], up_w[:, cols], preferred_element_type=F32) + small_whole[side, row, :]
        below = 0.5 * (1.0 + lax.erf(u * math.sqrt(0.5)))
        slope[:, cols] = below + u * jnp.exp(-0.5 * u * u) * (1.0 / math.sqrt(2.0 * math.pi))
        g = (u * below).astype(BF16)
        g_ref[:, cols] = g
        total[...] += jnp.dot(g, down_w[cols, :], preferred_element_type=F32)

    acts = {
        "second": second,
        "third": third,
        "fourth": fourth,
        "project": project,
        "own": own_half,
        "keys": pack_keys,
        "values": pack_values,
        "att": attention,
        "rows": come_back,
        "out": out_project,
        "hidden": hidden_up,
    }
    for name, value in FORWARD_SCHEDULE:
        acts[name](value)

    store(g_ref)
    h_two = n_full[...] + (total[...] + line_of(ROW_DOWN))
    unit_two, scale_two = norm_parts(h_two)
    out_ref[...] = (unit_two * line_of(ROW_GAIN_TWO) + line_of(ROW_SHIFT_TWO)).astype(BF16)
    store(out_ref)
    cot = cot_ref[...].astype(F32)
    keep(ROW_GAIN_TWO, cot * unit_two)
    keep(ROW_SHIFT_TWO, cot)
    dh_two = norm_back(cot, unit_two, scale_two, line_of(ROW_GAIN_TWO))
    dm = dh_two.astype(BF16)
    dm_ref[...] = dm
    store(dm_ref)
    keep(ROW_DOWN, dm.astype(F32))
    total[...] = dh_two
    for turn in range(hidden_steps):
        cols, side, row = hidden_at(turn)
        du = (slope[:, cols] * dot_minor(dm_ref[...], down_w[cols, :])).astype(BF16)
        du_ref[:, cols] = du
        vec_ref[side, row, :] = jnp.sum(du.astype(F32), axis=0, keepdims=True)
        total[...] += dot_minor(du, up_w[:, cols])
    store(du_ref)
    dn = total[...]
    keep(ROW_GAIN_ONE, dn * unit[...])
    keep(ROW_SHIFT_ONE, dn)
    dh_one = norm_back(dn, unit[...], kept_scale[0], line_of(ROW_GAIN_ONE))
    dh_ref[...] = dh_one
    store(dh_ref)
    do = dh_one.astype(BF16)
    do_ref[...] = do
    store(do_ref)
    keep(ROW_OUT, do.astype(F32))
    for side in range(2):
        vec_ref[side, 0:ROW_OUT, :] = jnp.zeros((ROW_OUT, lanes), F32)
    store(vec_ref)
    da_ref[...] = dot_minor(do, out_w[...]).astype(BF16)
    store(da_ref)

    for m in range(MB):
        all_bytes(out_buf.at[m], send_sem.at[m], heads - 1).wait()
        all_bytes(back_out.at[m], back_send.at[m], heads - 1).wait()
        pltpu.make_async_copy(in_buf[m], kept_ref.at[m], keep_sem.at[m]).wait()
    for flight in steps.values():
        flight.wait_send()
    for copy in stores:
        copy.wait()
    for index in range(3):
        pltpu.make_async_copy(near[index], wholes[index], local_sem.at[index]).wait()


def forward(lengths, dealing, x, cot, shards, vectors, heads):
    plan = weight_plan(shards)
    count = len(shards)
    anywhere, vmem = pl.BlockSpec(memory_space=pl.ANY), pl.BlockSpec(memory_space=pltpu.VMEM)
    rows, width = x.shape
    hidden = shards[4].shape[1]
    pack_rows = BLK + BLK // 2
    span = BPS * BLK
    lanes = min(item.shape[0] for item in vectors)
    lines = sum(item.shape[0] for item in vectors) // lanes
    whole = lambda s: (2 * s.shape[0],) + s.shape[1:]
    low = lambda cols: jax.ShapeDtypeStruct((rows, cols), BF16)
    full = lambda cols: pltpu.VMEM((rows, cols), F32)
    sems = lambda *dims: pltpu.SemaphoreType.DMA(dims)
    kept_shapes = [
        jax.ShapeDtypeStruct((MB, heads, pack_rows, 128), BF16),
        jax.ShapeDtypeStruct((8, span), F32),
    ]
    results = [low(width)] * 3 + [low(hidden), low(width), low(hidden), low(width)]
    results += [jax.ShapeDtypeStruct((rows, width), F32), low(width)]
    results += [jax.ShapeDtypeStruct((2, lines, lanes), F32)]
    return pl.pallas_call(
        functools.partial(forward_kernel, heads, plan, count, len(vectors)),
        out_shape=[jax.ShapeDtypeStruct(whole(s), s.dtype) for s in shards[:3]]
        + kept_shapes
        + results,
        in_specs=[anywhere] * 2 + [vmem] * 2 + [anywhere] * count + [vmem] * len(vectors),
        out_specs=[anywhere] * 4 + [vmem] + [anywhere] * 10,
        scratch_shapes=[pltpu.VMEM(item.shape, item.dtype) for item in results]
        + [sems(len(results))]
        + dealing_scratch(lengths, dealing)
        + [pltpu.VMEM(whole(s), s.dtype) for s in shards]
        + [pltpu.VMEM((lines, lanes), F32)] * 2
        + [pltpu.VMEM((2, lines, lanes), F32), pltpu.VMEM((2, width), F32)]
        + [pltpu.VMEM((rows, width), BF16)] * 3
        + [pltpu.VMEM((3, rows, width), F32)]
        + [full(hidden), full(width), full(width), full(width)]
        + [pltpu.VMEM((heads, pack_rows, 128), BF16)] * MB
        + [
            pltpu.VMEM((MB, heads, pack_rows, 128), BF16),
            pltpu.VMEM((MB, heads, BLK // 2, 128), BF16),
            pltpu.VMEM((MB, heads, BLK // 2, 128), BF16),
            pltpu.VMEM((heads * BLK, HD), BF16),
            pltpu.VMEM((heads * BLK, HD), BF16),
            pltpu.VMEM((heads * BLK, HD), BF16),
            pltpu.VMEM((heads, BLK, HD), F32),
        ]
        + [sems(6, len(plan)), sems(6, len(plan)), sems(2), sems(3), sems(count)]
        + [sems(MB)] * 5,
        compiler_params=pltpu.CompilerParams(
            collective_id=1, has_side_effects=True, vmem_limit_bytes=VMEM_BYTES
        ),
        name="forward",
    )(lengths, dealing, x, cot, *shards, *vectors)


ORDERS = (
    ("yxZz", "xyzZ", "xyzZ", "xyzZ"),
    ("yxzZ", "zxyZ", "xyzZ", "xyzZ"),
    ("yZz", "zyZ", "zyZ", "yzZ"),
)
PIECES = len(ORDERS[0])
SCHEDULE = (
    "up", 0, 1, 2, (1, 0), "down", (1, 2), "back", (2, 0), (2, 1), "qkv", (2, 3), (2, 0),
    (2, 1), (2, 3), (1, 2), (1, 0), (2, 3), (2, 2), (1, 2), "vec", (2, 1), (1, 3), (2, 3),
    (0, 1), (2, 0), (1, 2), (2, 2), (1, 3), (1, 0), (2, 3), (1, 2), (2, 0), "vec", (1, 3),
    (2, 2), (0, 2), "rows", (0, 1), (2, 3), (2, 0), (1, 1), (0, 2), (1, 0), (0, 3), (0, 1),
    "vec", (1, 3), (0, 0), (1, 1), (1, 2), (1, 0), (0, 1), (0, 3), (0, 2), (1, 1), (0, 1),
    (2, 1), (0, 0), (2, 2), "vec", (1, 0), (1, 2), (0, 2), (0, 3), (0, 0), (0, 1), (1, 3),
    (0, 2), (1, 1), (0, 3), (1, 3), (1, 0), (0, 0), (2, 2), (1, 1), "vec", (0, 2), (0, 3),
    (0, 0), (1, 1), (2, 1), (2, 2), (0, 1), (2, 0), (0, 3), (0, 2), (0, 0), (1, 3), (0, 3),
    (1, 1), (2, 1), (0, 0),
)
KEYS = tuple((part, piece) for part in range(3) for piece in range(PIECES))


def landing_shapes(order, shape):
    shards, sides, shapes = 8, shape[0], []
    for name in order:
        if name == "x":
            sides = 1
        else:
            shards //= 2
        shapes.append((sides, shards, shape[2] // PIECES, shape[3]))
    return shapes


def dot_t(a, b):
    return lax.dot_general(a, b, (((0,), (0,)), ((), ())), preferred_element_type=F32)


def lanes_at(first, size):
    return pl.ds(pl.multiple_of(first, 128), size)


def backward_kernel(heads, *refs):
    integers, operands, weights = refs[:2], refs[2:14], refs[14:17]
    rows_out, o_a, o_b, o_c, vec_out = refs[17:22]
    held, load_sem, refs = refs[22:34], refs[34], refs[35:]
    dealt, refs = Dealing(*integers, *refs[:4]), refs[4:]
    da_ref, g_ref, dm_ref, n_ref, du_ref, kept_ref = held[:6]
    lse_ref, a_ref, do_ref, x_ref, vec_ref, dh_ref = held[6:]
    loads = []
    for index, (source, target) in enumerate(zip(operands, held)):
        copy = pltpu.make_async_copy(source, target, load_sem.at[index])
        copy.start()
        loads.append((target, copy))

    def ready(*targets):
        for item in list(loads):
            if any(item[0] is target for target in targets):
                item[1].wait()
                loads.remove(item)

    in_buf = refs[:MB]
    out_buf, back_out, back_in, q_s, k_s, v_s, a_s, dq_s, dk_s, dv_s = refs[MB : MB + 10]
    refs = refs[MB + 10 :]
    dq_ref, dk_ref, dv_ref, m_x, m_a, m_n, m_do, m_du, m_dqkv, m_g, m_dm = refs[:11]
    far_g, far_dm, cross_g, cross_dm = refs[11:15]
    near, (vec_s, v_recv, v_sum, s_a, s_b, s_c) = refs[15:18], refs[18:24]
    refs = refs[24:]
    r_bufs = {}
    for part, piece in KEYS:
        size = len(ORDERS[part][piece])
        r_bufs[part, piece], refs = refs[:size], refs[size:]
    (
        send_sem,
        recv_sem,
        back_send,
        back_recv,
        mate_send,
        mate_recv,
        near_sem,
        rs_send,
        rs_recv,
        ag_send,
        ag_recv,
        own_sem,
        v_send_sem,
        v_recv_sem,
    ) = refs
    c, x = lax.axis_index("ctx"), lax.axis_index("wsh")
    core, y, z, zz = bit_of(c, 1), bit_of(c, 2), bit_of(c, 4), bit_of(c, 8)
    by_core = (flip(c, 1), x)
    by = {"x": (c, 1 - x), "y": (flip(c, 2), x), "z": (flip(c, 4), x), "Z": (flip(c, 8), x)}
    bits = {"y": y, "z": z, "Z": zz}
    peers = plane_peers(c, x, heads)
    blocks, span = heads, BPS * BLK
    width, hidden = da_ref.shape[1], g_ref.shape[1]
    for index, weight in enumerate(weights):
        pltpu.make_async_copy(weight, near[index], near_sem.at[index]).start()
    by_cross = (flip(c, 1), 1 - x)
    greet(peers + [by["x"], by_cross])

    ready(da_ref)
    for m in range(MB):
        row = slice(m * BLK, (m + 1) * BLK)
        for pair in range(heads // 2):
            both = da_ref[row, pair * 128 : (pair + 1) * 128]
            for head in range(2):
                out_buf[m, 2 * pair + head] = fold(both[:, head * HD : (head + 1) * HD])
        for peer in peers:
            send(out_buf.at[m, peer[0]], in_buf[m].at[c], send_sem.at[m], recv_sem.at[m], peer)
        in_buf[m][c] = out_buf[m, c]

    shared = {}

    def share(name, src, dst, peer=by_core):
        index = len(shared)
        shared[name] = send(src, dst, mate_send.at[index], mate_recv.at[index], peer)

    other = 1 - core
    quarter = hidden // 4

    def hidden_rows(side, which):
        return g_ref.at[:, lanes_at(side * 2 * quarter + which * quarter, quarter)]

    ready(g_ref, dm_ref)
    share("far_g", hidden_rows(1 - x, core), far_g, by["x"])
    share("far_dm", dm_ref, far_dm, by["x"])
    share("cross_g", hidden_rows(1 - x, other), cross_g, by_cross)
    ready(n_ref, du_ref)
    share("n", n_ref, m_n)
    share("du", du_ref.at[:, lanes_at(other * (hidden // 2), hidden // 2)], m_du)
    share("g", hidden_rows(x, other), m_g)
    share("dm", dm_ref, m_dm)
    ready(*held)
    share("a", a_ref, m_a)
    share("do", do_ref.at[:, lanes_at(other * (width // 2), width // 2)], m_do)
    share("x", x_ref, m_x)
    dealt.invert()

    sums, outs = (s_a, s_b, s_c), (o_a, o_b, o_c)
    wide = 512

    def tile(pairs, out, first, count):
        def body(turn, carry):
            at = turn * wide
            total = sum(dot_t(lhs[...], rhs[:, lanes_at(col + at, wide)]) for lhs, rhs, col in pairs)
            cols = lanes_at(first + at, wide)
            out[..., cols] = total.astype(BF16).reshape(out.shape[:-1] + (wide,))
            return carry

        lax.fori_loop(0, count, body, 0)

    def grads_up():
        shared["n"].wait_recv()
        shared["du"].wait_recv()
        half = hidden // 2
        tile(((n_ref, du_ref, core * half), (m_n, m_du, 0)), s_b, 0, half // wide)

    def grads_down():
        shared["far_dm"].wait_recv()
        share("cross_dm", far_dm, cross_dm)
        for name in ("g", "dm", "far_g", "cross_g", "cross_dm"):
            shared[name].wait_recv()
        pairs = ((hidden_rows(x, core), dm_ref, 0), (m_g, m_dm, 0))
        pairs += ((far_g, far_dm, 0), (cross_g, cross_dm, 0))
        tile(pairs, s_c.at[0], 0, width // wide)

    def grads_qkv():
        half = width // 2
        for name in ("a", "do", "x", "dq", "dk", "dv"):
            shared[name].wait_recv()
        tile(((a_ref, do_ref, core * half), (m_a, m_do, 0)), s_a, 3 * half, half // wide)
        for index, ref in enumerate((dq_ref, dk_ref, dv_ref)):
            pairs = ((x_ref, ref, core * half), (m_x, m_dqkv, index * half))
            tile(pairs, s_a, index * half, half // wide)

    def attention(m):
        all_bytes(in_buf[m], recv_sem.at[m], heads - 1).wait()
        for b in range(blocks):
            slot = dealt.slot(m, b)
            got = kept_ref[m, slot]
            rows = slice(b * BLK, (b + 1) * BLK)
            q_s[rows, :] = got[:BLK, :HD]
            k_s[rows, :] = got[:BLK, HD:]
            v_s[rows, :] = unpack_fold(got[BLK:])
            a_s[rows, :] = unpack_fold(in_buf[m][slot])

        def one_sequence(s, carry):
            rows = pl.ds(pl.multiple_of(s * span, span), span)
            qq, kk, vv, dd = q_s[rows, :], k_s[rows, :], v_s[rows, :], a_s[rows, :]
            scale = 1.0 / math.sqrt(HD)
            minor = (((1,), (1,)), ((), ()))
            scores = lax.dot_general(kk, qq, minor, preferred_element_type=F32) * scale
            spot = lax.broadcasted_iota(jnp.int32, scores.shape, 0)
            total = lse_ref[pl.ds(m * (blocks // BPS) + s, 1), :]
            probs = jnp.exp(jnp.where(spot < dealt.length(m, s), scores - total, NEG_FILL))
            dp = lax.dot_general(vv, dd, minor, preferred_element_type=F32)
            both = probs * dp
            delta = jnp.sum(both, axis=0, keepdims=True)
            ds = (both - probs * delta).astype(BF16)
            here, split = pl.ds(s * BPS, BPS), (BPS, BLK, HD)
            dv = jnp.dot(probs.astype(BF16), dd, preferred_element_type=F32)
            dv_s[here] = dv.reshape(split)
            dk_s[here] = (jnp.dot(ds, qq, preferred_element_type=F32) * scale).reshape(split)
            dq_s[here] = (dot_t(kk, ds).T * scale).reshape(split)
            return carry

        lax.fori_loop(0, blocks // BPS, one_sequence, 0)
        for t in range(blocks):
            at = dealt.block(m, t)
            back_out[m, t, 0:BLK, :] = jnp.concatenate([dq_s[at], dk_s[at]], axis=1).astype(BF16)
            back_out[m, t, BLK:, :] = fold(dv_s[at]).astype(BF16)
        for peer in peers:
            send(
                back_out.at[m, peer[0]], back_in.at[m, c], back_send.at[m], back_recv.at[m], peer
            )
        back_in[m, c] = back_out[m, c]

    vec_peers = (by["x"], by["y"], by["z"], by["Z"], by_core)
    vec_steps = []

    def vec_send(src):
        step = len(vec_steps)
        vec_steps.append(
            send(
                src, v_recv.at[step], v_send_sem.at[step], v_recv_sem.at[step], vec_peers[step]
            )
        )

    def vec_next():
        step = len(vec_steps) - 1
        vec_steps[step].wait_recv()
        before = vec_s[x] if step == 0 else v_sum[step - 1]
        v_sum[step] = before + v_recv[step]
        if step + 1 < len(vec_peers):
            vec_send(v_sum.at[step])

    def come_back():
        for m in range(MB):
            all_bytes(back_in.at[m], back_recv.at[m], heads - 1).wait()
            row = slice(m * BLK, (m + 1) * BLK)
            for pair in range(heads // 2):
                lanes = slice(pair * 128, (pair + 1) * 128)
                one, two = back_in[m, 2 * pair], back_in[m, 2 * pair + 1]
                dq_ref[row, lanes] = jnp.concatenate([one[:BLK, :HD], two[:BLK, :HD]], axis=1)
                dk_ref[row, lanes] = jnp.concatenate([one[:BLK, HD:], two[:BLK, HD:]], axis=1)
                dv_ref[row, lanes] = jnp.concatenate(
                    [unpack_fold(one[BLK:]), unpack_fold(two[BLK:])], axis=1
                )
        half = width // 2
        for index, (name, ref) in enumerate((("dq", dq_ref), ("dk", dk_ref), ("dv", dv_ref))):
            share(
                name,
                ref.at[:, lanes_at(other * half, half)],
                m_dqkv.at[:, pl.ds(index * half, half)],
            )
        vec_s[...] = vec_ref[...]
        lanes = vec_s.shape[2]
        for index, ref in enumerate((dq_ref, dv_ref)):
            total = jnp.sum(ref[...].astype(F32), axis=0, keepdims=True)
            for side in range(2):
                vec_s[side, index : index + 1, :] = total[:, side * lanes : (side + 1) * lanes]
        vec_send(vec_s.at[1 - x])

    def grad_rows():
        total = dh_ref[...]
        for index, ref in enumerate((dq_ref, dk_ref, dv_ref)):
            pltpu.make_async_copy(weights[index], near[index], near_sem.at[index]).wait()
            total = total + lax.dot_general(
                ref[...], near[index][...], (((1,), (1,)), ((), ())), preferred_element_type=F32
            )
        rows_out[...] = total.astype(BF16)

    plans, gathers = {}, {}
    for key in KEYS:
        alone = sums[key[0]].shape[0] == 1
        first, count, sided = 0, 8, alone
        plans[key], back = [], []
        for name in ORDERS[key[0]][key[1]]:
            if name == "x":
                plans[key].append((by["x"], 1 - x, x, first, first, count))
                sided = True
                continue
            count //= 2
            out, keep = first + (1 - bits[name]) * count, first + bits[name] * count
            side = (0 if alone else x) if sided else None
            plans[key].append((by[name], side, side, out, keep, count))
            back.append((by[name], keep, out, count))
            first = keep
        gathers[key] = back[::-1]
    flights, spread, owns, state = {}, {}, {}, {}

    def piece_rows(key):
        rows = sums[key[0]].shape[2] // PIECES
        return pl.ds(key[1] * rows, rows)

    def reduce_send(key, step):
        peer, side, _, first, _, count = plans[key][step]
        dst = r_bufs[key][step]
        if side is None:
            src = sums[key[0]].at[:, pl.ds(first, count), piece_rows(key)]
        else:
            src, dst = sums[key[0]].at[side, pl.ds(first, count), piece_rows(key)], dst.at[0]
        sems = rs_send.at[key[0], key[1], step], rs_recv.at[key[0], key[1], step]
        flights[key, step] = send(src, dst, *sems, peer)
        state[key] = step

    def reduce_add(key, step):
        _, _, side, _, first, count = plans[key][step]
        flights[key, step].wait_recv()
        total, fresh, rows = sums[key[0]], r_bufs[key][step], piece_rows(key)
        sides = ((0, 0), (1, 1)) if side is None else ((side, 0),)
        for here, there in sides:

            def body(index, carry):
                spot = first + index
                total[here, spot, rows] = (
                    total[here, spot, rows].astype(F32) + fresh[there, index].astype(F32)
                ).astype(BF16)
                return carry

            lax.fori_loop(0, count, body, 0)

    def spread_send(key, kind, src, dst, peer):
        sems = ag_send.at[key[0], key[1], kind], ag_recv.at[key[0], key[1], kind]
        spread[key, kind] = send(src, dst, *sems, peer)

    def advance(key):
        step, steps = state[key], len(plans[key])
        out, rows = outs[key[0]], piece_rows(key)
        if step < steps:
            reduce_add(key, step)
            if step < steps - 1:
                reduce_send(key, step + 1)
                return
            peer, first, _, _ = gathers[key][0]
            side = x if sums[key[0]].shape[0] == 2 else 0
            src = sums[key[0]].at[side, pl.ds(first, 1), rows]
            dst = out.at[core, pl.ds(first, 1), rows]
            owns[key] = pltpu.make_async_copy(src, dst, own_sem.at[key[0], key[1]])
            owns[key].start()
            spread_send(key, 0, src, dst, peer)
            spread_send(key, 3, src, dst, by_core)
        else:
            turn = step - steps + 1
            spread[key, turn - 1].wait_recv()
            if turn == 1:
                owns[key].wait()
            if turn < 3:
                peer, first, _, count = gathers[key][turn]
                ref = out.at[core, pl.ds(first, count), rows]
                spread_send(key, turn, ref, ref, peer)
            _, _, first, count = gathers[key][turn - 1]
            ref = out.at[core, pl.ds(first, count), rows]
            spread_send(key, 3 + turn, ref, ref, by_core)
        state[key] = step + 1

    actions = {
        "up": (grads_up, 1),
        "down": (grads_down, 2),
        "qkv": (grads_qkv, 0),
        "back": (come_back, None),
        "rows": (grad_rows, None),
        "vec": (vec_next, None),
    }
    for event in SCHEDULE:
        if isinstance(event, tuple):
            advance(event)
        elif isinstance(event, int):
            attention(event)
        else:
            action, part = actions[event]
            if event == "vec" and len(vec_steps) == len(vec_peers) and "vec" in state:
                continue
            if event == "vec" and len(vec_steps) == len(vec_peers):
                state["vec"] = True
            action()
            if part is not None:
                for piece in range(PIECES):
                    reduce_send((part, piece), 0)
    vec_out[...] = v_sum[len(vec_peers) - 1]
    for m in range(MB):
        all_bytes(out_buf.at[m], send_sem.at[m], heads - 1).wait()
        all_bytes(back_out.at[m], back_send.at[m], heads - 1).wait()
    for flight in shared.values():
        flight.wait_send()
    for flight in vec_steps:
        flight.wait_send()
    for flight in flights.values():
        flight.wait_send()
    for (_, kind), flight in spread.items():
        if kind >= 3:
            flight.wait_recv()
        flight.wait_send()


def backward(lengths, dealing, da, kept, lse, x, a, n1, g, do, du, dm, vec, dh, weights, heads):
    vmem, anywhere = pl.BlockSpec(memory_space=pltpu.VMEM), pl.BlockSpec(memory_space=pl.ANY)
    rows, width = da.shape
    hidden = g.shape[1]
    pack_rows = BLK + BLK // 2
    low = lambda *dims: pltpu.VMEM(dims, BF16)
    operands = (da, g, dm, n1, du, kept, lse, a, do, x, vec, dh)
    a_shape, b_shape = (2, 8, width // 16, 2 * width), (2, 8, width // 16, hidden // 2)
    c_shape = (1, 8, hidden // 32, width)
    scratch = [pltpu.VMEM(item.shape, item.dtype) for item in operands]
    scratch += [pltpu.SemaphoreType.DMA((len(operands),))]
    scratch += dealing_scratch(lengths, dealing)
    scratch += [low(heads, BLK // 2, 128)] * MB
    scratch += [low(MB, heads, BLK // 2, 128)]
    scratch += [low(MB, heads, pack_rows, 128)] * 2
    scratch += [low(heads * BLK, HD)] * 4
    scratch += [pltpu.VMEM((heads, BLK, HD), F32)] * 3
    scratch += [low(rows, width)] * 6
    scratch += [low(rows, width // 2), low(rows, hidden // 2), low(rows, 3 * width // 2)]
    scratch += [low(rows, hidden // 4), low(rows, width)] * 3
    scratch += [low(*item.shape) for item in weights]
    scratch += [pltpu.VMEM(vec.shape, F32)] + [pltpu.VMEM((5,) + vec.shape[1:], F32)] * 2
    scratch += [low(*shape) for shape in (a_shape, b_shape, c_shape)]
    for key in KEYS:
        shape = (a_shape, b_shape, c_shape)[key[0]]
        scratch += [low(*item) for item in landing_shapes(ORDERS[key[0]][key[1]], shape)]
    sems = lambda *dims: pltpu.SemaphoreType.DMA(dims)
    scratch += [sems(MB)] * 4 + [sems(14)] * 2 + [sems(3)]
    scratch += [sems(3, PIECES, 4)] * 2 + [sems(3, PIECES, 7)] * 2 + [sems(3, PIECES)]
    scratch += [sems(5)] * 2
    return pl.pallas_call(
        functools.partial(backward_kernel, heads),
        out_shape=[
            jax.ShapeDtypeStruct((rows, width), BF16),
            jax.ShapeDtypeStruct(a_shape, BF16),
            jax.ShapeDtypeStruct(b_shape, BF16),
            jax.ShapeDtypeStruct((2,) + c_shape[1:], BF16),
            jax.ShapeDtypeStruct(vec.shape[1:], F32),
        ],
        in_specs=[anywhere] * 17,
        out_specs=[vmem] + [anywhere] * 3 + [vmem],
        scratch_shapes=scratch,
        compiler_params=pltpu.CompilerParams(
            collective_id=2, has_side_effects=True, vmem_limit_bytes=VMEM_BYTES
        ),
        name="backward",
    )(lengths, dealing, *operands, *weights)


def widen_kernel(a_ref, b_ref, c_ref, vec_ref, one_ref, two_ref, one_out, two_out, *outs):
    one_out[...] = one_ref[...]
    two_out[...] = two_ref[...]

    @pl.when(pl.program_id(0) == 0)
    def _():
        line, lanes = 0, vec_ref.shape[1]
        for out in outs[6:]:
            for first in range(0, out.shape[0], lanes):
                out[pl.ds(first, lanes)] = vec_ref[line, :]
                line += 1

    half = outs[0].shape[1] // 2
    for index, out in enumerate(outs[:4]):
        for core in range(2):
            part = a_ref[core, :, :, index * half : (index + 1) * half]
            out[:, core * half : (core + 1) * half] = part.astype(F32).reshape(-1, half)
    up, down = outs[4:6]
    half = up.shape[1] // 2
    for core in range(2):
        part = b_ref[core].astype(F32)
        up[:, core * half : (core + 1) * half] = part.reshape(-1, half)
        down[core] = c_ref[core].astype(F32)


def widen(o_a, o_b, o_c, vec, sizes, one, two):
    shards = o_a.shape[1]
    turns = 2
    share = shards // turns
    block = lambda item: pl.BlockSpec((2, share) + item.shape[2:], lambda i: (0, i, 0, 0))
    rows = o_a.shape[2] * share
    square = (turns * rows, o_a.shape[3] // 2)
    wide = (turns * rows, 2 * o_b.shape[3])
    strip = pl.BlockSpec((one.shape[0] // turns, one.shape[1]), lambda i: (i, 0))
    return pl.pallas_call(
        widen_kernel,
        grid=(turns,),
        out_shape=[jax.ShapeDtypeStruct(one.shape, one.dtype)] * 2
        + [jax.ShapeDtypeStruct(square, F32)] * 4
        + [jax.ShapeDtypeStruct(wide, F32), jax.ShapeDtypeStruct(o_c.shape, F32)]
        + [jax.ShapeDtypeStruct((size,), F32) for size in sizes],
        in_specs=[block(o_a), block(o_b), block(o_c), pl.BlockSpec(vec.shape, lambda i: (0, 0))]
        + [strip] * 2,
        out_specs=[strip] * 2
        + [pl.BlockSpec((rows, square[1]), lambda i: (i, 0))] * 4
        + [pl.BlockSpec((rows, wide[1]), lambda i: (i, 0)), block(o_c)]
        + [pl.BlockSpec((size,), lambda i: (0,)) for size in sizes],
        compiler_params=pltpu.CompilerParams(vmem_limit_bytes=VMEM_BYTES),
        name="widen",
    )(o_a, o_b, o_c, vec, one, two)


def per_device_heads(tokens, cotangent, lengths, dealing, *params):
    rows_in = tokens.shape[2]
    width = tokens.shape[3]
    rows = MB * rows_in
    weights, vectors = params[:6], params[6:]
    sizes = [item.shape[0] for item in vectors]
    x = tokens.reshape(rows, width)
    lengths, dealing = lengths.transpose(0, 2, 1), dealing.transpose(1, 0, 2)
    query_w, key_w, value_w, kept, lse, a, output, n_low, g, do, du, dm, dh_one, da, vec = forward(
        lengths, dealing, x, cotangent.reshape(rows, width), weights, vectors, HEADS
    )
    grad_tokens, o_a, o_b, o_c, vec_sum = backward(
        lengths,
        dealing,
        da,
        kept,
        lse,
        x,
        a,
        n_low,
        g,
        do,
        du,
        dm,
        vec,
        dh_one,
        (query_w, key_w, value_w),
        HEADS,
    )
    output, grad_tokens, *grads = widen(o_a, o_b, o_c, vec_sum, sizes, output, grad_tokens)
    grads[5] = grads[5].reshape(-1, width)
    shape = (1, MB, rows_in, width)
    return (
        (output.reshape(shape), grad_tokens.reshape(shape))
        + tuple(grads)
    )


def solution(mesh):
    placed = (
        P("wsh", None, "ctx", None),
        P("wsh", None, "ctx", None),
        P("wsh", None, None),
        P("wsh", None, None),
        P("wsh", None),
        P("wsh", None),
        P("wsh", None),
        P("wsh", None),
        P("wsh", None),
        P("wsh", None),
        P("wsh"),
        P("wsh"),
        P("wsh"),
        P("wsh"),
        P("wsh"),
        P("wsh"),
        P("wsh"),
        P("wsh"),
        P("wsh"),
    )
    by_heads = mesh.shape["ctx"] == HEADS and mesh.shape["wsh"] == 2
    return jax.shard_map(
        per_device_heads if by_heads else per_device,
        mesh=mesh,
        in_specs=placed,
        out_specs=(
            P("wsh", None, "ctx", None),
            P("wsh", None, "ctx", None),
            P("wsh", None),
            P("wsh", None),
            P("wsh", None),
            P("wsh", None),
            P("wsh", None),
            P("wsh", None),
            P("wsh"),
            P("wsh"),
            P("wsh"),
            P("wsh"),
            P("wsh"),
            P("wsh"),
            P("wsh"),
            P("wsh"),
            P("wsh"),
        ),
        check_vma=False,
    )
```

```python
import functools
import math

import jax
import jax.numpy as jnp
from jax import lax
from jax.experimental import pallas as pl
from jax.experimental.pallas import tpu as pltpu
from jax.sharding import PartitionSpec as P

HEADS = 16
BPS = 8
MB = 3
BLK = 64


EPSILON = 1e-12
NEG_FILL = -1e30


def as_sent(x):
    return jax.tree.map(lambda a: a.astype(jnp.bfloat16) if a.dtype == jnp.float32 else a, x)


def layer_norm(summed, gain_vec, shift_vec):
    row_mean = jnp.mean(summed, axis=-1, keepdims=True)
    centred = summed - row_mean
    row_var = jnp.mean(centred * centred, axis=-1, keepdims=True)
    return centred * lax.rsqrt(row_var + EPSILON) * gain_vec + shift_vec


def gelu_exact(values):
    return jax.nn.gelu(values, approximate=False)


def row_labels(dealt_order, seq_lengths):
    blocks_of_rows = jnp.repeat(dealt_order, BLK)
    within = jnp.tile(jnp.arange(BLK, dtype=jnp.int32), dealt_order.shape[0])
    seq_ids = blocks_of_rows // BPS
    places = blocks_of_rows % BPS * BLK + within
    numbers = jnp.arange(seq_lengths.shape[0], dtype=jnp.int32)
    seq_bound = jnp.sum(
        jnp.where(seq_ids[:, None] == numbers[None, :], seq_lengths[None, :], 0), axis=1
    )
    return (seq_ids, places < seq_bound)


def blockwise(carried, total_rows, step_rows, visit_block):
    return lax.fori_loop(
        0,
        total_rows // step_rows,
        lambda turn_index, running: visit_block(running, turn_index * step_rows),
        carried,
    )


def masked_scores(query_blk, key_blk, query_seq, key_seq, key_valid, scale_factor):
    allowed = (query_seq[:, None] == key_seq[None, :]) & key_valid[None, :]
    scores = (
        jnp.einsum("qhd,khd->hqk", query_blk, key_blk, preferred_element_type=jnp.float32)
        * scale_factor
    )
    return (jnp.where(allowed[None], scores, NEG_FILL), allowed[None].astype(jnp.float32))


def attention_grads(
    query_blk,
    grad_blk,
    key_blk,
    value_blk,
    query_seq,
    key_seq,
    key_valid,
    row_total,
    row_delta,
    scale_factor,
):
    scores, allowed = masked_scores(query_blk, key_blk, query_seq, key_seq, key_valid, scale_factor)
    probs = jnp.exp(scores - row_total[:, :, None]) * allowed
    grad_probs = jnp.einsum("qhd,khd->hqk", grad_blk, value_blk, preferred_element_type=jnp.float32)
    grad_scores = (probs * (grad_probs - row_delta[:, :, None])).astype(jnp.bfloat16)
    return (probs.astype(jnp.bfloat16), grad_scores)


def gather_params(params):
    return (
        lax.all_gather(params[0], "wsh", axis=0, tiled=True),
        lax.all_gather(params[1], "wsh", axis=0, tiled=True),
        lax.all_gather(params[2], "wsh", axis=0, tiled=True),
        lax.all_gather(params[3], "wsh", axis=0, tiled=True),
        lax.all_gather(params[4], "wsh", axis=0, tiled=True),
        lax.all_gather(params[5], "wsh", axis=0, tiled=True),
        lax.all_gather(params[6], "wsh", axis=0, tiled=True),
        lax.all_gather(params[7], "wsh", axis=0, tiled=True),
        lax.all_gather(params[8], "wsh", axis=0, tiled=True),
        lax.all_gather(params[9], "wsh", axis=0, tiled=True),
        lax.all_gather(params[10], "wsh", axis=0, tiled=True),
        lax.all_gather(params[11], "wsh", axis=0, tiled=True),
        lax.all_gather(params[12], "wsh", axis=0, tiled=True),
        lax.all_gather(params[13], "wsh", axis=0, tiled=True),
        lax.all_gather(params[14], "wsh", axis=0, tiled=True),
    )


def per_device(
    tokens,
    cotangent,
    lengths,
    dealing,
    w_query,
    w_key,
    w_value,
    w_out,
    w_up,
    w_down,
    b_query,
    b_value,
    b_out,
    b_up,
    b_down,
    gain_one,
    shift_one,
    gain_two,
    shift_two,
):
    params = (
        w_query,
        w_key,
        w_value,
        w_out,
        w_up,
        w_down,
        b_query,
        b_value,
        b_out,
        b_up,
        b_down,
        gain_one,
        shift_one,
        gain_two,
        shift_two,
    )
    own_rows = tokens.shape[2]
    width = tokens.shape[3]
    head_size = width // HEADS
    scale_factor = 1.0 / math.sqrt(head_size)
    my_start = lax.axis_index("ctx") * own_rows
    wsh_count = lax.axis_size("wsh")
    grads = tuple(
        (jnp.zeros((item.shape[0] * wsh_count,) + item.shape[1:], jnp.float32) for item in params)
    )
    results = []
    input_grads = []
    for micro in range(MB):
        whole = gather_params(params)
        query_weight, key_weight, value_weight, out_weight, up_weight, down_weight = whole[:6]
        (
            bias_query,
            bias_value,
            bias_out,
            bias_up,
            bias_down,
            gain_first,
            shift_first,
            gain_second,
            shift_second,
        ) = tuple((item.astype(jnp.float32) for item in whole[6:]))
        token_rows = tokens[0, micro]
        seq_all, valid_all = row_labels(dealing[0, micro], lengths[0, micro])
        my_seq = lax.dynamic_slice_in_dim(seq_all, my_start, own_rows)
        my_valid = lax.dynamic_slice_in_dim(valid_all, my_start, own_rows)
        query_low = (
            jnp.dot(token_rows, query_weight, preferred_element_type=jnp.float32) + bias_query
        ).astype(jnp.bfloat16)
        key_low = jnp.dot(token_rows, key_weight, preferred_element_type=jnp.float32).astype(
            jnp.bfloat16
        )
        value_low = (
            jnp.dot(token_rows, value_weight, preferred_element_type=jnp.float32) + bias_value
        ).astype(jnp.bfloat16)
        query_heads = query_low.reshape(own_rows, HEADS, head_size)
        my_key_heads = key_low.reshape(own_rows, HEADS, head_size)
        my_value_heads = value_low.reshape(own_rows, HEADS, head_size)
        start_state = (
            jnp.full((HEADS, own_rows), NEG_FILL, jnp.float32),
            jnp.zeros((HEADS, own_rows), jnp.float32),
            jnp.zeros((own_rows, HEADS, head_size), jnp.float32),
        )
        key_piece = lax.all_gather(key_low, "ctx", axis=0, tiled=True)
        value_piece = lax.all_gather(value_low, "ctx", axis=0, tiled=True)
        piece_rows = key_piece.shape[0]
        step_rows = math.gcd(piece_rows, 512)

        def visit_block(running, offset):
            run_max, run_sum, run_acc = running
            key_blk = lax.dynamic_slice_in_dim(key_piece, offset, step_rows).reshape(
                step_rows, HEADS, head_size
            )
            value_blk = lax.dynamic_slice_in_dim(value_piece, offset, step_rows).reshape(
                step_rows, HEADS, head_size
            )
            key_seq = lax.dynamic_slice_in_dim(seq_all, offset, step_rows)
            key_valid = lax.dynamic_slice_in_dim(valid_all, offset, step_rows)
            scores, allowed = masked_scores(
                query_heads, key_blk, my_seq, key_seq, key_valid, scale_factor
            )
            new_max = jnp.maximum(run_max, jnp.max(scores, axis=-1))
            rescale = jnp.exp(run_max - new_max)
            weights = jnp.exp(scores - new_max[:, :, None]) * allowed
            run_sum = run_sum * rescale + jnp.sum(weights, axis=-1)
            run_acc = run_acc * rescale.T[:, :, None] + jnp.einsum(
                "hqk,khd->qhd",
                weights.astype(jnp.bfloat16),
                value_blk,
                preferred_element_type=jnp.float32,
            )
            return (new_max, run_sum, run_acc)

        final_max, final_sum, final_acc = blockwise(start_state, piece_rows, step_rows, visit_block)
        attended = final_acc / final_sum.T[:, :, None]
        log_total = final_max + jnp.log(final_sum)
        attended_low = attended.reshape(own_rows, width).astype(jnp.bfloat16)
        out_proj = jnp.dot(attended_low, out_weight, preferred_element_type=jnp.float32) + bias_out
        first_sum = token_rows.astype(jnp.float32) + out_proj
        norm_one, norm_one_back = jax.vjp(layer_norm, first_sum, gain_first, shift_first)
        mlp_input = norm_one.astype(jnp.bfloat16)
        up_pre = jnp.dot(mlp_input, up_weight, preferred_element_type=jnp.float32) + bias_up
        activated, gelu_back = jax.vjp(gelu_exact, up_pre)
        activated_low = activated.astype(jnp.bfloat16)
        down_out = (
            jnp.dot(activated_low, down_weight, preferred_element_type=jnp.float32) + bias_down
        )
        result, norm_two_back = jax.vjp(layer_norm, norm_one + down_out, gain_second, shift_second)
        results.append(result.astype(jnp.bfloat16))
        grad_second, grad_gain_b, grad_shift_b = norm_two_back(
            cotangent[0, micro].astype(jnp.float32)
        )
        grad_down_low = grad_second.astype(jnp.bfloat16)
        grad_activated = jnp.einsum(
            "rd,fd->rf", grad_down_low, down_weight, preferred_element_type=jnp.float32
        )
        (grad_up_pre,) = gelu_back(grad_activated)
        grad_up_low = grad_up_pre.astype(jnp.bfloat16)
        grad_norm_one = (
            jnp.einsum("rf,df->rd", grad_up_low, up_weight, preferred_element_type=jnp.float32)
            + grad_second
        )
        grad_first, grad_gain_a, grad_shift_a = norm_one_back(grad_norm_one)
        grad_out_low = grad_first.astype(jnp.bfloat16)
        grad_att_low = jnp.einsum(
            "rd,ed->re", grad_out_low, out_weight, preferred_element_type=jnp.float32
        ).astype(jnp.bfloat16)
        grad_heads = grad_att_low.reshape(own_rows, HEADS, head_size)
        row_delta = jnp.sum(grad_heads.astype(jnp.float32) * attended, axis=-1).T
        empty_heads = jnp.zeros((own_rows, HEADS, head_size), jnp.float32)
        query_key_piece = lax.all_gather(key_low, "ctx", axis=0, tiled=True)
        query_value_piece = lax.all_gather(value_low, "ctx", axis=0, tiled=True)
        query_piece_rows = query_key_piece.shape[0]
        query_step_rows = math.gcd(query_piece_rows, 512)

        def query_visit_block(running, offset):
            key_blk = lax.dynamic_slice_in_dim(query_key_piece, offset, query_step_rows).reshape(
                query_step_rows, HEADS, head_size
            )
            value_blk = lax.dynamic_slice_in_dim(
                query_value_piece, offset, query_step_rows
            ).reshape(query_step_rows, HEADS, head_size)
            key_seq = lax.dynamic_slice_in_dim(seq_all, offset, query_step_rows)
            key_valid = lax.dynamic_slice_in_dim(valid_all, offset, query_step_rows)
            probs_low, grad_scores = attention_grads(
                query_heads,
                grad_heads,
                key_blk,
                value_blk,
                my_seq,
                key_seq,
                key_valid,
                log_total,
                row_delta,
                scale_factor,
            )
            return running + jnp.einsum(
                "hqk,khd->qhd", grad_scores, key_blk, preferred_element_type=jnp.float32
            )

        grad_query_sum = blockwise(
            empty_heads, query_piece_rows, query_step_rows, query_visit_block
        )
        total_all, delta_all = (
            lax.all_gather(log_total.T, "ctx", axis=0, tiled=True),
            lax.all_gather(row_delta.T, "ctx", axis=0, tiled=True),
        )
        query_piece = lax.all_gather(query_low, "ctx", axis=0, tiled=True)
        grad_piece = lax.all_gather(grad_att_low, "ctx", axis=0, tiled=True)
        key_piece_rows = query_piece.shape[0]
        key_step_rows = math.gcd(key_piece_rows, 512)

        def key_visit_block(running, offset):
            grad_key_run, grad_value_run = running
            query_blk = lax.dynamic_slice_in_dim(query_piece, offset, key_step_rows).reshape(
                key_step_rows, HEADS, head_size
            )
            grad_blk = lax.dynamic_slice_in_dim(grad_piece, offset, key_step_rows).reshape(
                key_step_rows, HEADS, head_size
            )
            total_blk = lax.dynamic_slice_in_dim(total_all, offset, key_step_rows)
            delta_blk = lax.dynamic_slice_in_dim(delta_all, offset, key_step_rows)
            query_seq = lax.dynamic_slice_in_dim(seq_all, offset, key_step_rows)
            probs_low, grad_scores = attention_grads(
                query_blk,
                grad_blk,
                my_key_heads,
                my_value_heads,
                query_seq,
                my_seq,
                my_valid,
                total_blk.T,
                delta_blk.T,
                scale_factor,
            )
            grad_key_run = grad_key_run + jnp.einsum(
                "hqk,qhd->khd", grad_scores, query_blk, preferred_element_type=jnp.float32
            )
            grad_value_run = grad_value_run + jnp.einsum(
                "hqk,qhd->khd", probs_low, grad_blk, preferred_element_type=jnp.float32
            )
            return (grad_key_run, grad_value_run)

        grad_key_sum, grad_value_sum = blockwise(
            (empty_heads, empty_heads), key_piece_rows, key_step_rows, key_visit_block
        )
        grad_key_flat = grad_key_sum.reshape(own_rows, width)
        grad_value_flat = grad_value_sum.reshape(own_rows, width)
        grad_query_low = (
            (grad_query_sum * scale_factor).reshape(own_rows, width).astype(jnp.bfloat16)
        )
        grad_key_low = (grad_key_flat * scale_factor).astype(jnp.bfloat16)
        grad_value_low = grad_value_flat.astype(jnp.bfloat16)
        terms = (
            jnp.einsum("rd,re->de", token_rows, grad_query_low, preferred_element_type=jnp.float32),
            jnp.einsum("rd,re->de", token_rows, grad_key_low, preferred_element_type=jnp.float32),
            jnp.einsum("rd,re->de", token_rows, grad_value_low, preferred_element_type=jnp.float32),
            jnp.einsum("rd,re->de", attended_low, grad_out_low, preferred_element_type=jnp.float32),
            jnp.einsum("rd,rf->df", mlp_input, grad_up_low, preferred_element_type=jnp.float32),
            jnp.einsum(
                "rf,rd->fd", activated_low, grad_down_low, preferred_element_type=jnp.float32
            ),
            jnp.sum(grad_query_low.astype(jnp.float32), axis=0),
            jnp.sum(grad_value_low.astype(jnp.float32), axis=0),
            jnp.sum(grad_out_low.astype(jnp.float32), axis=0),
            jnp.sum(grad_up_low.astype(jnp.float32), axis=0),
            jnp.sum(grad_down_low.astype(jnp.float32), axis=0),
            grad_gain_a,
            grad_shift_a,
            grad_gain_b,
            grad_shift_b,
        )
        grads = tuple((total_now + fresh for total_now, fresh in zip(grads, terms)))
        grad_rows = (
            grad_first
            + jnp.einsum(
                "re,de->rd", grad_query_low, query_weight, preferred_element_type=jnp.float32
            )
            + jnp.einsum("re,de->rd", grad_key_low, key_weight, preferred_element_type=jnp.float32)
            + jnp.einsum(
                "re,de->rd", grad_value_low, value_weight, preferred_element_type=jnp.float32
            )
        )
        input_grads.append(grad_rows.astype(jnp.bfloat16))
    shards = jax.tree.map(
        lambda part: part.astype(jnp.float32),
        lax.psum_scatter(as_sent(grads), "wsh", scatter_dimension=0, tiled=True),
    )
    summed = jax.tree.map(lambda part: part.astype(jnp.float32), lax.psum(as_sent(shards), "ctx"))
    return (jnp.stack(results)[None], jnp.stack(input_grads)[None]) + tuple(summed)


MESH_IDS = pl.DeviceIdType.MESH
F32 = jnp.float32
BF16 = jnp.bfloat16
HD = 64
VMEM_BYTES = 60 * 1024 * 1024


def flip(index, bit):
    return index + bit * (1 - 2 * lax.rem(lax.div(index, bit), 2))


def bit_of(index, bit):
    return lax.rem(lax.div(index, bit), 2)


def greet(peers):
    barrier = pltpu.get_barrier_semaphore()
    for peer in peers:
        pl.semaphore_signal(barrier, inc=1, device_id=peer, device_id_type=MESH_IDS)
    pl.semaphore_wait(barrier, len(peers))


def send(src, dst, send_sem, recv_sem, peer):
    copy = pltpu.make_async_remote_copy(
        src_ref=src,
        dst_ref=dst,
        send_sem=send_sem,
        recv_sem=recv_sem,
        device_id=peer,
        device_id_type=MESH_IDS,
    )
    copy.start()
    return copy


class Dealing:
    def __init__(self, lengths_hbm, dealing_hbm, lengths, dealing, slots, sems):
        self.lengths, self.dealing, self.slots = lengths, dealing, slots
        self.copies = (
            pltpu.make_async_copy(lengths_hbm, lengths, sems.at[0]),
            pltpu.make_async_copy(dealing_hbm, dealing, sems.at[1]),
        )
        for copy in self.copies:
            copy.start()

    def invert(self):
        for copy in self.copies:
            copy.wait()
        micros, _, count = self.dealing.shape

        def find(number, carry):
            m, block = lax.div(number, count), lax.rem(number, count)
            slot = jnp.int32(0)
            for t in range(count):
                slot = jnp.where(self.dealing[m, 0, t] == block, jnp.int32(t), slot)
            self.slots[m, block] = slot
            return carry

        lax.fori_loop(0, micros * count, find, 0)

    def length(self, m, s):
        return self.lengths[0, s, m]

    def block(self, m, t):
        return self.dealing[m, 0, t]

    def slot(self, m, b):
        return self.slots[m, b]


def dealing_scratch(lengths, dealing):
    return [
        pltpu.SMEM(lengths.shape, jnp.int32),
        pltpu.SMEM(dealing.shape, jnp.int32),
        pltpu.SMEM((dealing.shape[0], dealing.shape[2]), jnp.int32),
        pltpu.SemaphoreType.DMA((2,)),
    ]


def plane_peers(c, w, count):
    return [(lax.rem(c + step, count), w) for step in range(1, count)]


def pack_two(first, second, row, pair, out):
    cols = pl.ds(pair * 128, 128)
    a, b = first[pl.ds(row, BLK), cols], second[pl.ds(row, BLK), cols]
    for head in range(2):
        lane = slice(head * HD, head * HD + HD)
        out[2 * pair + head, 0:BLK, :] = jnp.concatenate([a[:, lane], b[:, lane]], axis=1)


def pack_one(source, row, pair, out):
    both = source[pl.ds(row, BLK), pl.ds(pair * 128, 128)]
    for head in range(2):
        lane = slice(head * HD, head * HD + HD)
        out[2 * pair + head, BLK : BLK + BLK // 2, :] = fold(both[:, lane])


def unpack_fold(block):
    return jnp.concatenate([block[:, :HD], block[:, HD:]], axis=0)


def fold(rows):
    half = rows.shape[0] // 2
    return jnp.concatenate([rows[:half], rows[half:]], axis=1)


def all_bytes(ref, sem, peers):
    view = ref.at[pl.ds(0, peers)]
    return pltpu.make_async_copy(view, view, sem)


def norm_parts(summed):
    row_mean = jnp.mean(summed, axis=-1, keepdims=True)
    centred = summed - row_mean
    row_var = jnp.mean(centred * centred, axis=-1, keepdims=True)
    scale = lax.rsqrt(row_var + EPSILON)
    return centred * scale, scale


def norm_back(grad, unit, scale, gain):
    inner = grad * gain
    mean_one = jnp.mean(inner, axis=-1, keepdims=True)
    mean_two = jnp.mean(inner * unit, axis=-1, keepdims=True)
    return scale * (inner - mean_one - unit * mean_two)


def dot_minor(a, b):
    return lax.dot_general(a, b, (((1,), (1,)), ((), ())), preferred_element_type=F32)


ROW_OUT, ROW_UP, ROW_DOWN, ROW_GAIN_ONE, ROW_SHIFT_ONE, ROW_GAIN_TWO, ROW_SHIFT_TWO = 2, 3, 7, 8, 9, 10, 11


SQUARE, PAIR_Y, PAIR_Z, ALONE = (8, "yz"), (4, "y"), (4, "z"), (2, "")
WAYS = (
    SQUARE, SQUARE, SQUARE, ALONE, PAIR_Y, PAIR_Y, SQUARE, SQUARE, SQUARE, PAIR_Z, ALONE, PAIR_Y,
)
SEND_ORDER = (1, 0, 2, 7, 6, 5, 11, 9, 4, 8, 3, 10)
FORWARD_SCHEDULE = (
    ("own", 0), ("own", 1), ("own", 2), ("second", 1), ("second", 0), ("third", 1), ("third",
    0), ("second", 2), ("fourth", 1), ("project", 1), ("second", 7), ("fourth", 0), ("third",
    2), ("project", 0), ("keys", 0), ("keys", 1), ("third", 7), ("second", 6), ("fourth", 2),
    ("project", 2), ("values", 0), ("values", 1), ("keys", 2), ("second", 5), ("values", 2),
    ("att", 0), ("second", 8), ("att", 1), ("second", 4), ("fourth", 7), ("att", 2), ("fourth",
    5), ("fourth", 3), ("third", 6), ("third", 8), ("second", 9), ("fourth", 4), ("rows", 0),
    ("second", 11), ("fourth", 6), ("out", 0), ("hidden", 0), ("hidden", 1), ("fourth", 8),
    ("hidden", 2), ("fourth", 9), ("hidden", 3), ("fourth", 10), ("hidden", 4), ("fourth", 11),
    ("hidden", 5), ("hidden", 6), ("hidden", 7),
)


def weight_plan(shards):
    unit = shards[0].shape[0] * shards[0].shape[1]
    plan = []
    for index, (rows, cols) in enumerate(shard.shape for shard in shards):
        parts = max(1, rows * cols // unit)
        for part in range(parts):
            plan.append((index, part * (rows // parts), rows // parts, WAYS[len(plan)]))
    return plan


def forward_kernel(heads, plan, n_weights, n_vectors, *refs):
    integers, (x_ref, cot_ref), refs = refs[:2], refs[2:4], refs[4:]
    shards, vectors = refs[:n_weights], refs[n_weights : n_weights + n_vectors]
    refs = refs[n_weights + n_vectors :]
    wholes, kept_ref, lse_ref = refs[:3], *refs[3:5]
    results, refs = refs[5:15], refs[15:]
    a_ref, out_ref, n_ref, g_ref, do_ref, du_ref, dm_ref, dh_ref, da_ref, vec_ref = refs[:10]
    made, result_sem, refs = refs[:10], refs[10], refs[11:]
    dealt, refs = Dealing(*integers, *refs[:4]), refs[4:]
    near, refs = refs[:n_weights], refs[n_weights:]
    small, small_in, small_whole, bias, q_ref, k_ref, v_ref = refs[:7]
    begun, slope, n_full, unit, total = refs[7:12]
    refs = refs[12:]
    in_buf = refs[:MB]
    out_buf, back_out, back_in, q_s, k_s, v_s, a_s = refs[MB : 7 + MB]
    (
        w_send,
        w_recv,
        small_sems,
        local_sem,
        stage_sem,
        send_sem,
        recv_sem,
        back_send,
        back_recv,
        keep_sem,
    ) = refs[7 + MB :]
    c, w = lax.axis_index("ctx"), lax.axis_index("wsh")
    o = 1 - w
    by_x, by_y, by_z, by_core = (c, o), (flip(c, 2), w), (flip(c, 4), w), (flip(c, 1), w)
    core, y, z = bit_of(c, 1), bit_of(c, 2), bit_of(c, 4)
    peers = plane_peers(c, w, heads)
    stores = []

    def store(target):
        index = [item is target for item in made].index(True)
        copy = pltpu.make_async_copy(target, results[index], result_sem.at[index])
        copy.start()
        stores.append(copy)

    staged = []
    for index, shard in enumerate(shards):
        rows = shard.shape[0]
        spot = pl.ds(pl.multiple_of(w * rows, rows), rows)
        copy = pltpu.make_async_copy(shard, near[index].at[spot], stage_sem.at[index])
        copy.start()
        staged.append(copy)
    line, lanes = 0, small.shape[1]
    for vector in vectors:
        for first in range(0, vector.shape[0], lanes):
            piece = vector[pl.ds(first, lanes)].astype(F32)
            small[line : line + 1, :] = piece.reshape(1, lanes)
            line += 1
    greet(peers + [by_x])
    small_sent = send(small, small_in, small_sems.at[0], small_sems.at[1], by_x)

    def part(chunk, side, piece, start, count):
        tensor, first, rows, way = plan[chunk]
        half = shards[tensor].shape[0]
        at = side * half + first + piece * (rows // way[0]) + start
        return near[tensor].at[pl.ds(pl.multiple_of(at, 8), count)]

    steps = {}

    def sem(kind, chunk):
        return w_send.at[kind, chunk], w_recv.at[kind, chunk]

    def own_piece(way):
        return {
            SQUARE: core * 4 + z * 2 + y,
            PAIR_Y: core * 2 + y,
            PAIR_Z: core * 2 + z,
            ALONE: core,
        }[way]

    for chunk in SEND_ORDER:
        tensor, first, rows, way = plan[chunk]
        size, mine = rows // way[0], own_piece(way)
        src = shards[tensor].at[pl.ds(pl.multiple_of(first + mine * size, 8), size)]
        steps[chunk, 0] = send(src, part(chunk, w, mine, 0, size), *sem(0, chunk), by_x)
    dealt.invert()

    def second(chunk):
        _, _, rows, way = plan[chunk]
        steps[chunk, 0].wait_recv()
        ref = part(chunk, o, own_piece(way), 0, rows // way[0])
        for name in way[1]:
            kind, peer = {"y": (1, by_y), "z": (2, by_z)}[name]
            steps[chunk, kind] = send(ref, ref, *sem(kind, chunk), peer)

    def third(chunk):
        _, _, rows, way = plan[chunk]
        size = rows // way[0]
        steps[chunk, 1].wait_recv()
        steps[chunk, 2].wait_recv()
        ref = part(chunk, o, core * 4 + (1 - z) * 2 + y, 0, size // 2)
        steps[chunk, 3] = send(ref, ref, *sem(3, chunk), by_y)
        ref = part(chunk, o, core * 4 + z * 2 + (1 - y), size // 2, size // 2)
        steps[chunk, 4] = send(ref, ref, *sem(4, chunk), by_z)

    def fourth(chunk):
        _, _, rows, way = plan[chunk]
        for kind in {SQUARE: (3, 4), PAIR_Y: (1,), PAIR_Z: (2,), ALONE: (0,)}[way]:
            steps[chunk, kind].wait_recv()
        ref = part(chunk, o, core * (way[0] // 2), 0, rows // 2)
        steps[chunk, 5] = send(ref, ref, *sem(5, chunk), by_core)

    width = x_ref.shape[1]
    step = 256
    projected = []

    def half_product(index, side, cols):
        rows = shards[index].shape[0]
        lanes_in = pl.ds(pl.multiple_of(side * rows, rows), rows)
        return jnp.dot(
            x_ref[:, lanes_in], near[index][lanes_in, cols], preferred_element_type=F32
        )

    def own_half(index):
        staged[index].wait()

        def some_columns(turn, carry):
            cols = pl.ds(pl.multiple_of(turn * step, step), step)
            begun[index, :, cols] = half_product(index, w, cols)
            return carry

        lax.fori_loop(0, width // step, some_columns, 0)

    def project(index):
        if not projected:
            small_sent.wait()
            small_whole[w] = small[...]
            small_whole[o] = small_in[...]
            for side in range(2):
                for row in range(2):
                    bias[row : row + 1, side * lanes : (side + 1) * lanes] = small_whole[
                        side, row : row + 1, :
                    ]
        projected.append(index)
        steps[index, 5].wait_recv()
        out = (q_ref, k_ref, v_ref)[index]

        def some_columns(turn, carry):
            cols = pl.ds(pl.multiple_of(turn * step, step), step)
            product = begun[index, :, cols] + half_product(index, o, cols)
            if index != 1:
                product = product + bias[index // 2 : index // 2 + 1, cols]
            out[:, cols] = product.astype(BF16)
            return carry

        lax.fori_loop(0, width // step, some_columns, 0)
        pltpu.make_async_copy(near[index], wholes[index], local_sem.at[index]).start()

    def pack(item, first, count, fill):
        for pair in range(heads // 2):
            fill(item, pair)
        rows = pl.ds(first, count)
        for peer in peers:
            send(
                out_buf.at[item, peer[0], rows],
                in_buf[item].at[c, rows],
                send_sem.at[item],
                recv_sem.at[item],
                peer,
            )
        in_buf[item][c, rows] = out_buf[item, c, rows]

    def pack_keys(m):
        pack(m, 0, BLK, lambda m, pair: pack_two(q_ref, k_ref, m * BLK, pair, out_buf.at[m]))

    def pack_values(m):
        pack(m, BLK, BLK // 2, lambda m, pair: pack_one(v_ref, m * BLK, pair, out_buf.at[m]))

    blocks = heads
    span = BPS * BLK

    def attention(m):
        all_bytes(in_buf[m], recv_sem.at[m], heads - 1).wait()
        pltpu.make_async_copy(in_buf[m], kept_ref.at[m], keep_sem.at[m]).start()
        for b in range(blocks):
            got = in_buf[m][dealt.slot(m, b)]
            q_s[b * BLK : (b + 1) * BLK, :] = got[:BLK, :HD]
            k_s[b * BLK : (b + 1) * BLK, :] = got[:BLK, HD:]
            v_s[b * BLK : (b + 1) * BLK, :] = unpack_fold(got[BLK:])

        def one_sequence(s, carry):
            rows = pl.ds(pl.multiple_of(s * span, span), span)
            scores = lax.dot_general(
                k_s[rows, :], q_s[rows, :], (((1,), (1,)), ((), ())), preferred_element_type=F32
            ) * (1.0 / math.sqrt(HD))
            place = lax.broadcasted_iota(jnp.int32, scores.shape, 0)
            scores = jnp.where(place < dealt.length(m, s), scores, NEG_FILL)
            top = jnp.max(scores, axis=0, keepdims=True)
            weights = jnp.exp(scores - top)
            summed = jnp.sum(weights, axis=0, keepdims=True)
            out_t = lax.dot_general(
                v_s[rows, :],
                weights.astype(BF16),
                (((0,), (0,)), ((), ())),
                preferred_element_type=F32,
            )
            a_s[pl.ds(s * BPS, BPS)] = (out_t / summed).T.reshape(BPS, BLK, HD)
            lse_ref[pl.ds(m * (blocks // BPS) + s, 1), :] = top + jnp.log(summed)
            return carry

        lax.fori_loop(0, blocks // BPS, one_sequence, 0)
        for t in range(blocks):
            back_out[m, t] = fold(a_s[dealt.block(m, t)]).astype(BF16)
        for peer in peers:
            send(
                back_out.at[m, peer[0]], back_in.at[m, c], back_send.at[m], back_recv.at[m], peer
            )
        back_in[m, c] = back_out[m, c]

    def come_back(_):
        for m in range(MB):
            all_bytes(back_in.at[m], back_recv.at[m], heads - 1).wait()
            for pair in range(heads // 2):
                a_ref[m * BLK : (m + 1) * BLK, pair * 128 : (pair + 1) * 128] = jnp.concatenate(
                    [unpack_fold(back_in[m, 2 * pair]), unpack_fold(back_in[m, 2 * pair + 1])],
                    axis=1,
                )
        store(a_ref)

    def line_of(row):
        return jnp.concatenate(
            [small_whole[0, row : row + 1, :], small_whole[1, row : row + 1, :]], axis=1
        )

    def keep(row, values):
        summed = jnp.sum(values, axis=0, keepdims=True)
        for side in range(2):
            vec_ref[side, row : row + 1, :] = summed[:, side * lanes : (side + 1) * lanes]

    out_w, up_w, down_w = near[3:]
    chunks_of = {t: [i for i, item in enumerate(plan) if item[0] == t] for t in range(n_weights)}

    def arrived(tensor, chunks):
        for chunk in chunks:
            steps[chunk, 5].wait_recv()

    def out_project(_):
        staged[3].wait()
        arrived(3, chunks_of[3])
        h_one = x_ref[...].astype(F32) + (
            jnp.dot(a_ref[...], out_w[...], preferred_element_type=F32) + line_of(ROW_OUT)
        )
        unit_one, scale_one = norm_parts(h_one)
        unit[...] = unit_one
        n_one = unit_one * line_of(ROW_GAIN_ONE) + line_of(ROW_SHIFT_ONE)
        n_full[...] = n_one
        n_ref[...] = n_one.astype(BF16)
        store(n_ref)
        total[...] = jnp.zeros_like(total)
        kept_scale.append(scale_one)

    kept_scale = []
    hidden = g_ref.shape[1]
    hidden_steps = hidden // lanes
    per_half = hidden_steps // 2

    def hidden_at(turn):
        j = lax.rem(w * per_half + turn, hidden_steps)
        cols = pl.ds(pl.multiple_of(j * lanes, lanes), lanes)
        return cols, lax.div(j, per_half), pl.ds(ROW_UP + lax.rem(j, per_half), 1)

    def hidden_up(turn):
        if turn == 0:
            staged[4].wait()
            arrived(4, chunks_of[4])
            staged[5].wait()
        elif turn >= per_half:
            share = len(chunks_of[5]) // per_half
            first = (turn - per_half) * share
            arrived(5, chunks_of[5][first : first + share])
        cols, side, row = hidden_at(turn)
        u = jnp.dot(n_ref[...], up_w[:, cols], preferred_element_type=F32) + small_whole[side, row, :]
        below = 0.5 * (1.0 + lax.erf(u * math.sqrt(0.5)))
        slope[:, cols] = below + u * jnp.exp(-0.5 * u * u) * (1.0 / math.sqrt(2.0 * math.pi))
        g = (u * below).astype(BF16)
        g_ref[:, cols] = g
        total[...] += jnp.dot(g, down_w[cols, :], preferred_element_type=F32)

    acts = {
        "second": second,
        "third": third,
        "fourth": fourth,
        "project": project,
        "own": own_half,
        "keys": pack_keys,
        "values": pack_values,
        "att": attention,
        "rows": come_back,
        "out": out_project,
        "hidden": hidden_up,
    }
    for name, value in FORWARD_SCHEDULE:
        acts[name](value)

    store(g_ref)
    h_two = n_full[...] + (total[...] + line_of(ROW_DOWN))
    unit_two, scale_two = norm_parts(h_two)
    out_ref[...] = (unit_two * line_of(ROW_GAIN_TWO) + line_of(ROW_SHIFT_TWO)).astype(BF16)
    store(out_ref)
    cot = cot_ref[...].astype(F32)
    keep(ROW_GAIN_TWO, cot * unit_two)
    keep(ROW_SHIFT_TWO, cot)
    dh_two = norm_back(cot, unit_two, scale_two, line_of(ROW_GAIN_TWO))
    dm = dh_two.astype(BF16)
    dm_ref[...] = dm
    store(dm_ref)
    keep(ROW_DOWN, dm.astype(F32))
    total[...] = dh_two
    for turn in range(hidden_steps):
        cols, side, row = hidden_at(turn)
        du = (slope[:, cols] * dot_minor(dm_ref[...], down_w[cols, :])).astype(BF16)
        du_ref[:, cols] = du
        vec_ref[side, row, :] = jnp.sum(du.astype(F32), axis=0, keepdims=True)
        total[...] += dot_minor(du, up_w[:, cols])
    store(du_ref)
    dn = total[...]
    keep(ROW_GAIN_ONE, dn * unit[...])
    keep(ROW_SHIFT_ONE, dn)
    dh_one = norm_back(dn, unit[...], kept_scale[0], line_of(ROW_GAIN_ONE))
    dh_ref[...] = dh_one
    store(dh_ref)
    do = dh_one.astype(BF16)
    do_ref[...] = do
    store(do_ref)
    keep(ROW_OUT, do.astype(F32))
    for side in range(2):
        vec_ref[side, 0:ROW_OUT, :] = jnp.zeros((ROW_OUT, lanes), F32)
    store(vec_ref)
    da_ref[...] = dot_minor(do, out_w[...]).astype(BF16)
    store(da_ref)

    for m in range(MB):
        all_bytes(out_buf.at[m], send_sem.at[m], heads - 1).wait()
        all_bytes(back_out.at[m], back_send.at[m], heads - 1).wait()
        pltpu.make_async_copy(in_buf[m], kept_ref.at[m], keep_sem.at[m]).wait()
    for flight in steps.values():
        flight.wait_send()
    for copy in stores:
        copy.wait()
    for index in range(3):
        pltpu.make_async_copy(near[index], wholes[index], local_sem.at[index]).wait()


def forward(lengths, dealing, x, cot, shards, vectors, heads):
    plan = weight_plan(shards)
    count = len(shards)
    anywhere, vmem = pl.BlockSpec(memory_space=pl.ANY), pl.BlockSpec(memory_space=pltpu.VMEM)
    rows, width = x.shape
    hidden = shards[4].shape[1]
    pack_rows = BLK + BLK // 2
    span = BPS * BLK
    lanes = min(item.shape[0] for item in vectors)
    lines = sum(item.shape[0] for item in vectors) // lanes
    whole = lambda s: (2 * s.shape[0],) + s.shape[1:]
    low = lambda cols: jax.ShapeDtypeStruct((rows, cols), BF16)
    full = lambda cols: pltpu.VMEM((rows, cols), F32)
    sems = lambda *dims: pltpu.SemaphoreType.DMA(dims)
    kept_shapes = [
        jax.ShapeDtypeStruct((MB, heads, pack_rows, 128), BF16),
        jax.ShapeDtypeStruct((8, span), F32),
    ]
    results = [low(width)] * 3 + [low(hidden), low(width), low(hidden), low(width)]
    results += [jax.ShapeDtypeStruct((rows, width), F32), low(width)]
    results += [jax.ShapeDtypeStruct((2, lines, lanes), F32)]
    return pl.pallas_call(
        functools.partial(forward_kernel, heads, plan, count, len(vectors)),
        out_shape=[jax.ShapeDtypeStruct(whole(s), s.dtype) for s in shards[:3]]
        + kept_shapes
        + results,
        in_specs=[anywhere] * 2 + [vmem] * 2 + [anywhere] * count + [vmem] * len(vectors),
        out_specs=[anywhere] * 4 + [vmem] + [anywhere] * 10,
        scratch_shapes=[pltpu.VMEM(item.shape, item.dtype) for item in results]
        + [sems(len(results))]
        + dealing_scratch(lengths, dealing)
        + [pltpu.VMEM(whole(s), s.dtype) for s in shards]
        + [pltpu.VMEM((lines, lanes), F32)] * 2
        + [pltpu.VMEM((2, lines, lanes), F32), pltpu.VMEM((2, width), F32)]
        + [pltpu.VMEM((rows, width), BF16)] * 3
        + [pltpu.VMEM((3, rows, width), F32)]
        + [full(hidden), full(width), full(width), full(width)]
        + [pltpu.VMEM((heads, pack_rows, 128), BF16)] * MB
        + [
            pltpu.VMEM((MB, heads, pack_rows, 128), BF16),
            pltpu.VMEM((MB, heads, BLK // 2, 128), BF16),
            pltpu.VMEM((MB, heads, BLK // 2, 128), BF16),
            pltpu.VMEM((heads * BLK, HD), BF16),
            pltpu.VMEM((heads * BLK, HD), BF16),
            pltpu.VMEM((heads * BLK, HD), BF16),
            pltpu.VMEM((heads, BLK, HD), F32),
        ]
        + [sems(6, len(plan)), sems(6, len(plan)), sems(2), sems(3), sems(count)]
        + [sems(MB)] * 5,
        compiler_params=pltpu.CompilerParams(
            collective_id=1, has_side_effects=True, vmem_limit_bytes=VMEM_BYTES
        ),
        name="forward",
    )(lengths, dealing, x, cot, *shards, *vectors)


ORDERS = (
    ("xyzZ", "xyzZ", "yxzZ", "xyzZ"),
    ("zxyZ", "yxzZ", "xyzZ", "xzyZ"),
    ("yzZ", "zyZ", "yzZ", "yzZ"),
)
PIECES = len(ORDERS[0])
SCHEDULE = (
    "up", 0, 1, 2, "down", (1, 0), (2, 0), "back", (1, 2), (2, 2), (2, 0), (1, 1), (1, 3),
    (2, 2), (2, 1), (2, 3), (2, 0), "qkv", (1, 1), (2, 3), (2, 2), (1, 3), (2, 0), (2, 3),
    (1, 2), (0, 0), "vec", (2, 1), (1, 1), (2, 0), (1, 2), (1, 0), (2, 2), "rows", (0, 0),
    (1, 3), (1, 2), (0, 1), "vec", (0, 0), (1, 1), (2, 3), (1, 3), (2, 2), (0, 2), (2, 1),
    (0, 1), (0, 3), (1, 1), (0, 1), "vec", (1, 0), (2, 3), (0, 0), (1, 3), (0, 3), (0, 2),
    (2, 0), (1, 1), (1, 0), (0, 3), (0, 2), (0, 0), "vec", (2, 1), (0, 1), (1, 2), (1, 0),
    (0, 2), (0, 3), (0, 0), (0, 1), (1, 2), (2, 2), (0, 2), (0, 3), (2, 1), (0, 0), "vec",
    (1, 1), (0, 1), (1, 0), (1, 3), (0, 2), (0, 3), (2, 3), (0, 1), (1, 0), (1, 2), (0, 2),
    (2, 1), (0, 3), (1, 3),
)
KEYS = tuple((part, piece) for part in range(3) for piece in range(PIECES))


def landing_shapes(order, shape):
    shards, sides, shapes = 8, shape[0], []
    for name in order:
        if name == "x":
            sides = 1
        else:
            shards //= 2
        shapes.append((sides, shards, shape[2] // PIECES, shape[3]))
    return shapes


def dot_t(a, b):
    return lax.dot_general(a, b, (((0,), (0,)), ((), ())), preferred_element_type=F32)


def lanes_at(first, size):
    return pl.ds(pl.multiple_of(first, 128), size)


def backward_kernel(heads, *refs):
    integers, operands, weights = refs[:2], refs[2:14], refs[14:17]
    rows_out, o_a, o_b, o_c, vec_out = refs[17:22]
    held, load_sem, refs = refs[22:34], refs[34], refs[35:]
    dealt, refs = Dealing(*integers, *refs[:4]), refs[4:]
    da_ref, g_ref, dm_ref, n_ref, du_ref, kept_ref = held[:6]
    lse_ref, a_ref, do_ref, x_ref, vec_ref, dh_ref = held[6:]
    loads = []
    for index, (source, target) in enumerate(zip(operands, held)):
        copy = pltpu.make_async_copy(source, target, load_sem.at[index])
        copy.start()
        loads.append((target, copy))

    def ready(*targets):
        for item in list(loads):
            if any(item[0] is target for target in targets):
                item[1].wait()
                loads.remove(item)

    in_buf = refs[:MB]
    out_buf, back_out, back_in, q_s, k_s, v_s, a_s, dq_s, dk_s, dv_s = refs[MB : MB + 10]
    refs = refs[MB + 10 :]
    dq_ref, dk_ref, dv_ref, m_x, m_a, m_n, m_do, m_du, m_dqkv, m_g, m_dm = refs[:11]
    far_g, far_dm, cross_g, cross_dm = refs[11:15]
    near, (vec_s, v_recv, v_sum, s_a, s_b, s_c) = refs[15:18], refs[18:24]
    refs = refs[24:]
    r_bufs = {}
    for part, piece in KEYS:
        size = len(ORDERS[part][piece])
        r_bufs[part, piece], refs = refs[:size], refs[size:]
    (
        send_sem,
        recv_sem,
        back_send,
        back_recv,
        mate_send,
        mate_recv,
        near_sem,
        rs_send,
        rs_recv,
        ag_send,
        ag_recv,
        own_sem,
        v_send_sem,
        v_recv_sem,
    ) = refs
    c, x = lax.axis_index("ctx"), lax.axis_index("wsh")
    core, y, z, zz = bit_of(c, 1), bit_of(c, 2), bit_of(c, 4), bit_of(c, 8)
    by_core = (flip(c, 1), x)
    by = {"x": (c, 1 - x), "y": (flip(c, 2), x), "z": (flip(c, 4), x), "Z": (flip(c, 8), x)}
    bits = {"y": y, "z": z, "Z": zz}
    peers = plane_peers(c, x, heads)
    blocks, span = heads, BPS * BLK
    width, hidden = da_ref.shape[1], g_ref.shape[1]
    for index, weight in enumerate(weights):
        pltpu.make_async_copy(weight, near[index], near_sem.at[index]).start()
    by_cross = (flip(c, 1), 1 - x)
    greet(peers + [by["x"], by_cross])

    ready(da_ref)
    for m in range(MB):
        row = slice(m * BLK, (m + 1) * BLK)
        for pair in range(heads // 2):
            both = da_ref[row, pair * 128 : (pair + 1) * 128]
            for head in range(2):
                out_buf[m, 2 * pair + head] = fold(both[:, head * HD : (head + 1) * HD])
        for peer in peers:
            send(out_buf.at[m, peer[0]], in_buf[m].at[c], send_sem.at[m], recv_sem.at[m], peer)
        in_buf[m][c] = out_buf[m, c]

    shared = {}

    def share(name, src, dst, peer=by_core):
        index = len(shared)
        shared[name] = send(src, dst, mate_send.at[index], mate_recv.at[index], peer)

    other = 1 - core
    quarter = hidden // 4

    def hidden_rows(side, which):
        return g_ref.at[:, lanes_at(side * 2 * quarter + which * quarter, quarter)]

    ready(g_ref, dm_ref)
    share("far_g", hidden_rows(1 - x, core), far_g, by["x"])
    share("far_dm", dm_ref, far_dm, by["x"])
    share("cross_g", hidden_rows(1 - x, other), cross_g, by_cross)
    ready(n_ref, du_ref)
    share("n", n_ref, m_n)
    share("du", du_ref.at[:, lanes_at(other * (hidden // 2), hidden // 2)], m_du)
    share("g", hidden_rows(x, other), m_g)
    share("dm", dm_ref, m_dm)
    ready(*held)
    share("a", a_ref, m_a)
    share("do", do_ref.at[:, lanes_at(other * (width // 2), width // 2)], m_do)
    share("x", x_ref, m_x)
    dealt.invert()

    sums, outs = (s_a, s_b, s_c), (o_a, o_b, o_c)
    wide = 512

    def tile(pairs, out, first, count):
        def body(turn, carry):
            at = turn * wide
            total = sum(dot_t(lhs[...], rhs[:, lanes_at(col + at, wide)]) for lhs, rhs, col in pairs)
            cols = lanes_at(first + at, wide)
            out[..., cols] = total.astype(BF16).reshape(out.shape[:-1] + (wide,))
            return carry

        lax.fori_loop(0, count, body, 0)

    def grads_up():
        shared["n"].wait_recv()
        shared["du"].wait_recv()
        half = hidden // 2
        tile(((n_ref, du_ref, core * half), (m_n, m_du, 0)), s_b, 0, half // wide)

    def grads_down():
        shared["far_dm"].wait_recv()
        share("cross_dm", far_dm, cross_dm)
        for name in ("g", "dm", "far_g", "cross_g", "cross_dm"):
            shared[name].wait_recv()
        pairs = ((hidden_rows(x, core), dm_ref, 0), (m_g, m_dm, 0))
        pairs += ((far_g, far_dm, 0), (cross_g, cross_dm, 0))
        tile(pairs, s_c.at[0], 0, width // wide)

    def grads_qkv():
        half = width // 2
        for name in ("a", "do", "x", "dq", "dk", "dv"):
            shared[name].wait_recv()
        tile(((a_ref, do_ref, core * half), (m_a, m_do, 0)), s_a, 3 * half, half // wide)
        for index, ref in enumerate((dq_ref, dk_ref, dv_ref)):
            pairs = ((x_ref, ref, core * half), (m_x, m_dqkv, index * half))
            tile(pairs, s_a, index * half, half // wide)

    def attention(m):
        all_bytes(in_buf[m], recv_sem.at[m], heads - 1).wait()
        for b in range(blocks):
            slot = dealt.slot(m, b)
            got = kept_ref[m, slot]
            rows = slice(b * BLK, (b + 1) * BLK)
            q_s[rows, :] = got[:BLK, :HD]
            k_s[rows, :] = got[:BLK, HD:]
            v_s[rows, :] = unpack_fold(got[BLK:])
            a_s[rows, :] = unpack_fold(in_buf[m][slot])

        def one_sequence(s, carry):
            rows = pl.ds(pl.multiple_of(s * span, span), span)
            qq, kk, vv, dd = q_s[rows, :], k_s[rows, :], v_s[rows, :], a_s[rows, :]
            scale = 1.0 / math.sqrt(HD)
            minor = (((1,), (1,)), ((), ()))
            scores = lax.dot_general(kk, qq, minor, preferred_element_type=F32) * scale
            spot = lax.broadcasted_iota(jnp.int32, scores.shape, 0)
            total = lse_ref[pl.ds(m * (blocks // BPS) + s, 1), :]
            probs = jnp.exp(jnp.where(spot < dealt.length(m, s), scores - total, NEG_FILL))
            dp = lax.dot_general(vv, dd, minor, preferred_element_type=F32)
            both = probs * dp
            delta = jnp.sum(both, axis=0, keepdims=True)
            ds = (both - probs * delta).astype(BF16)
            here, split = pl.ds(s * BPS, BPS), (BPS, BLK, HD)
            dv = jnp.dot(probs.astype(BF16), dd, preferred_element_type=F32)
            dv_s[here] = dv.reshape(split)
            dk_s[here] = (jnp.dot(ds, qq, preferred_element_type=F32) * scale).reshape(split)
            dq_s[here] = (dot_t(kk, ds).T * scale).reshape(split)
            return carry

        lax.fori_loop(0, blocks // BPS, one_sequence, 0)
        for t in range(blocks):
            at = dealt.block(m, t)
            back_out[m, t, 0:BLK, :] = jnp.concatenate([dq_s[at], dk_s[at]], axis=1).astype(BF16)
            back_out[m, t, BLK:, :] = fold(dv_s[at]).astype(BF16)
        for peer in peers:
            send(
                back_out.at[m, peer[0]], back_in.at[m, c], back_send.at[m], back_recv.at[m], peer
            )
        back_in[m, c] = back_out[m, c]

    vec_peers = (by["x"], by["y"], by["z"], by["Z"], by_core)
    vec_steps = []

    def vec_send(src):
        step = len(vec_steps)
        vec_steps.append(
            send(
                src, v_recv.at[step], v_send_sem.at[step], v_recv_sem.at[step], vec_peers[step]
            )
        )

    def vec_next():
        step = len(vec_steps) - 1
        vec_steps[step].wait_recv()
        before = vec_s[x] if step == 0 else v_sum[step - 1]
        v_sum[step] = before + v_recv[step]
        if step + 1 < len(vec_peers):
            vec_send(v_sum.at[step])

    def come_back():
        for m in range(MB):
            all_bytes(back_in.at[m], back_recv.at[m], heads - 1).wait()
            row = slice(m * BLK, (m + 1) * BLK)
            for pair in range(heads // 2):
                lanes = slice(pair * 128, (pair + 1) * 128)
                one, two = back_in[m, 2 * pair], back_in[m, 2 * pair + 1]
                dq_ref[row, lanes] = jnp.concatenate([one[:BLK, :HD], two[:BLK, :HD]], axis=1)
                dk_ref[row, lanes] = jnp.concatenate([one[:BLK, HD:], two[:BLK, HD:]], axis=1)
                dv_ref[row, lanes] = jnp.concatenate(
                    [unpack_fold(one[BLK:]), unpack_fold(two[BLK:])], axis=1
                )
        half = width // 2
        for index, (name, ref) in enumerate((("dq", dq_ref), ("dk", dk_ref), ("dv", dv_ref))):
            share(
                name,
                ref.at[:, lanes_at(other * half, half)],
                m_dqkv.at[:, pl.ds(index * half, half)],
            )
        vec_s[...] = vec_ref[...]
        lanes = vec_s.shape[2]
        for index, ref in enumerate((dq_ref, dv_ref)):
            total = jnp.sum(ref[...].astype(F32), axis=0, keepdims=True)
            for side in range(2):
                vec_s[side, index : index + 1, :] = total[:, side * lanes : (side + 1) * lanes]
        vec_send(vec_s.at[1 - x])

    def grad_rows():
        total = dh_ref[...]
        for index, ref in enumerate((dq_ref, dk_ref, dv_ref)):
            pltpu.make_async_copy(weights[index], near[index], near_sem.at[index]).wait()
            total = total + lax.dot_general(
                ref[...], near[index][...], (((1,), (1,)), ((), ())), preferred_element_type=F32
            )
        rows_out[...] = total.astype(BF16)

    plans, gathers = {}, {}
    for key in KEYS:
        alone = sums[key[0]].shape[0] == 1
        first, count, sided = 0, 8, alone
        plans[key], back = [], []
        for name in ORDERS[key[0]][key[1]]:
            if name == "x":
                plans[key].append((by["x"], 1 - x, x, first, first, count))
                sided = True
                continue
            count //= 2
            out, keep = first + (1 - bits[name]) * count, first + bits[name] * count
            side = (0 if alone else x) if sided else None
            plans[key].append((by[name], side, side, out, keep, count))
            back.append((by[name], keep, out, count))
            first = keep
        gathers[key] = back[::-1]
    flights, spread, owns, state = {}, {}, {}, {}

    def piece_rows(key):
        rows = sums[key[0]].shape[2] // PIECES
        return pl.ds(key[1] * rows, rows)

    def reduce_send(key, step):
        peer, side, _, first, _, count = plans[key][step]
        dst = r_bufs[key][step]
        if side is None:
            src = sums[key[0]].at[:, pl.ds(first, count), piece_rows(key)]
        else:
            src, dst = sums[key[0]].at[side, pl.ds(first, count), piece_rows(key)], dst.at[0]
        sems = rs_send.at[key[0], key[1], step], rs_recv.at[key[0], key[1], step]
        flights[key, step] = send(src, dst, *sems, peer)
        state[key] = step

    def reduce_add(key, step):
        _, _, side, _, first, count = plans[key][step]
        flights[key, step].wait_recv()
        total, fresh, rows = sums[key[0]], r_bufs[key][step], piece_rows(key)
        sides = ((0, 0), (1, 1)) if side is None else ((side, 0),)
        for here, there in sides:

            def body(index, carry):
                spot = first + index
                total[here, spot, rows] = (
                    total[here, spot, rows].astype(F32) + fresh[there, index].astype(F32)
                ).astype(BF16)
                return carry

            lax.fori_loop(0, count, body, 0)

    def spread_send(key, kind, src, dst, peer):
        sems = ag_send.at[key[0], key[1], kind], ag_recv.at[key[0], key[1], kind]
        spread[key, kind] = send(src, dst, *sems, peer)

    def advance(key):
        step, steps = state[key], len(plans[key])
        out, rows = outs[key[0]], piece_rows(key)
        if step < steps:
            reduce_add(key, step)
            if step < steps - 1:
                reduce_send(key, step + 1)
                return
            peer, first, _, _ = gathers[key][0]
            side = x if sums[key[0]].shape[0] == 2 else 0
            src = sums[key[0]].at[side, pl.ds(first, 1), rows]
            dst = out.at[core, pl.ds(first, 1), rows]
            owns[key] = pltpu.make_async_copy(src, dst, own_sem.at[key[0], key[1]])
            owns[key].start()
            spread_send(key, 0, src, dst, peer)
            spread_send(key, 3, src, dst, by_core)
        else:
            turn = step - steps + 1
            spread[key, turn - 1].wait_recv()
            if turn == 1:
                owns[key].wait()
            if turn < 3:
                peer, first, _, count = gathers[key][turn]
                ref = out.at[core, pl.ds(first, count), rows]
                spread_send(key, turn, ref, ref, peer)
            _, _, first, count = gathers[key][turn - 1]
            ref = out.at[core, pl.ds(first, count), rows]
            spread_send(key, 3 + turn, ref, ref, by_core)
        state[key] = step + 1

    actions = {
        "up": (grads_up, 1),
        "down": (grads_down, 2),
        "qkv": (grads_qkv, 0),
        "back": (come_back, None),
        "rows": (grad_rows, None),
        "vec": (vec_next, None),
    }
    for event in SCHEDULE:
        if isinstance(event, tuple):
            advance(event)
        elif isinstance(event, int):
            attention(event)
        else:
            action, part = actions[event]
            if event == "vec" and len(vec_steps) == len(vec_peers) and "vec" in state:
                continue
            if event == "vec" and len(vec_steps) == len(vec_peers):
                state["vec"] = True
            action()
            if part is not None:
                for piece in range(PIECES):
                    reduce_send((part, piece), 0)
    vec_out[...] = v_sum[len(vec_peers) - 1]
    for m in range(MB):
        all_bytes(out_buf.at[m], send_sem.at[m], heads - 1).wait()
        all_bytes(back_out.at[m], back_send.at[m], heads - 1).wait()
    for flight in shared.values():
        flight.wait_send()
    for flight in vec_steps:
        flight.wait_send()
    for flight in flights.values():
        flight.wait_send()
    for (_, kind), flight in spread.items():
        if kind >= 3:
            flight.wait_recv()
        flight.wait_send()


def backward(lengths, dealing, da, kept, lse, x, a, n1, g, do, du, dm, vec, dh, weights, heads):
    vmem, anywhere = pl.BlockSpec(memory_space=pltpu.VMEM), pl.BlockSpec(memory_space=pl.ANY)
    rows, width = da.shape
    hidden = g.shape[1]
    pack_rows = BLK + BLK // 2
    low = lambda *dims: pltpu.VMEM(dims, BF16)
    operands = (da, g, dm, n1, du, kept, lse, a, do, x, vec, dh)
    a_shape, b_shape = (2, 8, width // 16, 2 * width), (2, 8, width // 16, hidden // 2)
    c_shape = (1, 8, hidden // 32, width)
    scratch = [pltpu.VMEM(item.shape, item.dtype) for item in operands]
    scratch += [pltpu.SemaphoreType.DMA((len(operands),))]
    scratch += dealing_scratch(lengths, dealing)
    scratch += [low(heads, BLK // 2, 128)] * MB
    scratch += [low(MB, heads, BLK // 2, 128)]
    scratch += [low(MB, heads, pack_rows, 128)] * 2
    scratch += [low(heads * BLK, HD)] * 4
    scratch += [pltpu.VMEM((heads, BLK, HD), F32)] * 3
    scratch += [low(rows, width)] * 6
    scratch += [low(rows, width // 2), low(rows, hidden // 2), low(rows, 3 * width // 2)]
    scratch += [low(rows, hidden // 4), low(rows, width)] * 3
    scratch += [low(*item.shape) for item in weights]
    scratch += [pltpu.VMEM(vec.shape, F32)] + [pltpu.VMEM((5,) + vec.shape[1:], F32)] * 2
    scratch += [low(*shape) for shape in (a_shape, b_shape, c_shape)]
    for key in KEYS:
        shape = (a_shape, b_shape, c_shape)[key[0]]
        scratch += [low(*item) for item in landing_shapes(ORDERS[key[0]][key[1]], shape)]
    sems = lambda *dims: pltpu.SemaphoreType.DMA(dims)
    scratch += [sems(MB)] * 4 + [sems(14)] * 2 + [sems(3)]
    scratch += [sems(3, PIECES, 4)] * 2 + [sems(3, PIECES, 7)] * 2 + [sems(3, PIECES)]
    scratch += [sems(5)] * 2
    return pl.pallas_call(
        functools.partial(backward_kernel, heads),
        out_shape=[
            jax.ShapeDtypeStruct((rows, width), BF16),
            jax.ShapeDtypeStruct(a_shape, BF16),
            jax.ShapeDtypeStruct(b_shape, BF16),
            jax.ShapeDtypeStruct((2,) + c_shape[1:], BF16),
            jax.ShapeDtypeStruct(vec.shape[1:], F32),
        ],
        in_specs=[anywhere] * 17,
        out_specs=[vmem] + [anywhere] * 3 + [vmem],
        scratch_shapes=scratch,
        compiler_params=pltpu.CompilerParams(
            collective_id=2, has_side_effects=True, vmem_limit_bytes=VMEM_BYTES
        ),
        name="backward",
    )(lengths, dealing, *operands, *weights)


def widen_kernel(a_ref, b_ref, c_ref, vec_ref, one_ref, two_ref, one_out, two_out, *outs):
    one_out[...] = one_ref[...]
    two_out[...] = two_ref[...]

    @pl.when(pl.program_id(0) == 0)
    def _():
        line, lanes = 0, vec_ref.shape[1]
        for out in outs[6:]:
            for first in range(0, out.shape[0], lanes):
                out[pl.ds(first, lanes)] = vec_ref[line, :]
                line += 1

    half = outs[0].shape[1] // 2
    for index, out in enumerate(outs[:4]):
        for core in range(2):
            part = a_ref[core, :, :, index * half : (index + 1) * half]
            out[:, core * half : (core + 1) * half] = part.astype(F32).reshape(-1, half)
    up, down = outs[4:6]
    half = up.shape[1] // 2
    for core in range(2):
        part = b_ref[core].astype(F32)
        up[:, core * half : (core + 1) * half] = part.reshape(-1, half)
        down[core] = c_ref[core].astype(F32)


def widen(o_a, o_b, o_c, vec, sizes, one, two):
    shards = o_a.shape[1]
    turns = 2
    share = shards // turns
    block = lambda item: pl.BlockSpec((2, share) + item.shape[2:], lambda i: (0, i, 0, 0))
    rows = o_a.shape[2] * share
    square = (turns * rows, o_a.shape[3] // 2)
    wide = (turns * rows, 2 * o_b.shape[3])
    strip = pl.BlockSpec((one.shape[0] // turns, one.shape[1]), lambda i: (i, 0))
    return pl.pallas_call(
        widen_kernel,
        grid=(turns,),
        out_shape=[jax.ShapeDtypeStruct(one.shape, one.dtype)] * 2
        + [jax.ShapeDtypeStruct(square, F32)] * 4
        + [jax.ShapeDtypeStruct(wide, F32), jax.ShapeDtypeStruct(o_c.shape, F32)]
        + [jax.ShapeDtypeStruct((size,), F32) for size in sizes],
        in_specs=[block(o_a), block(o_b), block(o_c), pl.BlockSpec(vec.shape, lambda i: (0, 0))]
        + [strip] * 2,
        out_specs=[strip] * 2
        + [pl.BlockSpec((rows, square[1]), lambda i: (i, 0))] * 4
        + [pl.BlockSpec((rows, wide[1]), lambda i: (i, 0)), block(o_c)]
        + [pl.BlockSpec((size,), lambda i: (0,)) for size in sizes],
        compiler_params=pltpu.CompilerParams(vmem_limit_bytes=VMEM_BYTES),
        name="widen",
    )(o_a, o_b, o_c, vec, one, two)


def per_device_heads(tokens, cotangent, lengths, dealing, *params):
    rows_in = tokens.shape[2]
    width = tokens.shape[3]
    rows = MB * rows_in
    weights, vectors = params[:6], params[6:]
    sizes = [item.shape[0] for item in vectors]
    x = tokens.reshape(rows, width)
    lengths, dealing = lengths.transpose(0, 2, 1), dealing.transpose(1, 0, 2)
    query_w, key_w, value_w, kept, lse, a, output, n_low, g, do, du, dm, dh_one, da, vec = forward(
        lengths, dealing, x, cotangent.reshape(rows, width), weights, vectors, HEADS
    )
    grad_tokens, o_a, o_b, o_c, vec_sum = backward(
        lengths,
        dealing,
        da,
        kept,
        lse,
        x,
        a,
        n_low,
        g,
        do,
        du,
        dm,
        vec,
        dh_one,
        (query_w, key_w, value_w),
        HEADS,
    )
    output, grad_tokens, *grads = widen(o_a, o_b, o_c, vec_sum, sizes, output, grad_tokens)
    grads[5] = grads[5].reshape(-1, width)
    shape = (1, MB, rows_in, width)
    return (
        (output.reshape(shape), grad_tokens.reshape(shape))
        + tuple(grads)
    )


def solution(mesh):
    placed = (
        P("wsh", None, "ctx", None),
        P("wsh", None, "ctx", None),
        P("wsh", None, None),
        P("wsh", None, None),
        P("wsh", None),
        P("wsh", None),
        P("wsh", None),
        P("wsh", None),
        P("wsh", None),
        P("wsh", None),
        P("wsh"),
        P("wsh"),
        P("wsh"),
        P("wsh"),
        P("wsh"),
        P("wsh"),
        P("wsh"),
        P("wsh"),
        P("wsh"),
    )
    by_heads = mesh.shape["ctx"] == HEADS and mesh.shape["wsh"] == 2
    return jax.shard_map(
        per_device_heads if by_heads else per_device,
        mesh=mesh,
        in_specs=placed,
        out_specs=(
            P("wsh", None, "ctx", None),
            P("wsh", None, "ctx", None),
            P("wsh", None),
            P("wsh", None),
            P("wsh", None),
            P("wsh", None),
            P("wsh", None),
            P("wsh", None),
            P("wsh"),
            P("wsh"),
            P("wsh"),
            P("wsh"),
            P("wsh"),
            P("wsh"),
            P("wsh"),
            P("wsh"),
            P("wsh"),
        ),
        check_vma=False,
    )
```

```python
import functools
import math

import jax
import jax.numpy as jnp
from jax import lax
from jax.experimental import pallas as pl
from jax.experimental.pallas import tpu as pltpu
from jax.sharding import PartitionSpec as P

HEADS = 16
BPS = 8
MB = 3
BLK = 64


EPSILON = 1e-12
NEG_FILL = -1e30


def as_sent(x):
    return jax.tree.map(lambda a: a.astype(jnp.bfloat16) if a.dtype == jnp.float32 else a, x)


def layer_norm(summed, gain_vec, shift_vec):
    row_mean = jnp.mean(summed, axis=-1, keepdims=True)
    centred = summed - row_mean
    row_var = jnp.mean(centred * centred, axis=-1, keepdims=True)
    return centred * lax.rsqrt(row_var + EPSILON) * gain_vec + shift_vec


def gelu_exact(values):
    return jax.nn.gelu(values, approximate=False)


def row_labels(dealt_order, seq_lengths):
    blocks_of_rows = jnp.repeat(dealt_order, BLK)
    within = jnp.tile(jnp.arange(BLK, dtype=jnp.int32), dealt_order.shape[0])
    seq_ids = blocks_of_rows // BPS
    places = blocks_of_rows % BPS * BLK + within
    numbers = jnp.arange(seq_lengths.shape[0], dtype=jnp.int32)
    seq_bound = jnp.sum(
        jnp.where(seq_ids[:, None] == numbers[None, :], seq_lengths[None, :], 0), axis=1
    )
    return (seq_ids, places < seq_bound)


def blockwise(carried, total_rows, step_rows, visit_block):
    return lax.fori_loop(
        0,
        total_rows // step_rows,
        lambda turn_index, running: visit_block(running, turn_index * step_rows),
        carried,
    )


def masked_scores(query_blk, key_blk, query_seq, key_seq, key_valid, scale_factor):
    allowed = (query_seq[:, None] == key_seq[None, :]) & key_valid[None, :]
    scores = (
        jnp.einsum("qhd,khd->hqk", query_blk, key_blk, preferred_element_type=jnp.float32)
        * scale_factor
    )
    return (jnp.where(allowed[None], scores, NEG_FILL), allowed[None].astype(jnp.float32))


def attention_grads(
    query_blk,
    grad_blk,
    key_blk,
    value_blk,
    query_seq,
    key_seq,
    key_valid,
    row_total,
    row_delta,
    scale_factor,
):
    scores, allowed = masked_scores(query_blk, key_blk, query_seq, key_seq, key_valid, scale_factor)
    probs = jnp.exp(scores - row_total[:, :, None]) * allowed
    grad_probs = jnp.einsum("qhd,khd->hqk", grad_blk, value_blk, preferred_element_type=jnp.float32)
    grad_scores = (probs * (grad_probs - row_delta[:, :, None])).astype(jnp.bfloat16)
    return (probs.astype(jnp.bfloat16), grad_scores)


def gather_params(params):
    return (
        lax.all_gather(params[0], "wsh", axis=0, tiled=True),
        lax.all_gather(params[1], "wsh", axis=0, tiled=True),
        lax.all_gather(params[2], "wsh", axis=0, tiled=True),
        lax.all_gather(params[3], "wsh", axis=0, tiled=True),
        lax.all_gather(params[4], "wsh", axis=0, tiled=True),
        lax.all_gather(params[5], "wsh", axis=0, tiled=True),
        lax.all_gather(params[6], "wsh", axis=0, tiled=True),
        lax.all_gather(params[7], "wsh", axis=0, tiled=True),
        lax.all_gather(params[8], "wsh", axis=0, tiled=True),
        lax.all_gather(params[9], "wsh", axis=0, tiled=True),
        lax.all_gather(params[10], "wsh", axis=0, tiled=True),
        lax.all_gather(params[11], "wsh", axis=0, tiled=True),
        lax.all_gather(params[12], "wsh", axis=0, tiled=True),
        lax.all_gather(params[13], "wsh", axis=0, tiled=True),
        lax.all_gather(params[14], "wsh", axis=0, tiled=True),
    )


def per_device(
    tokens,
    cotangent,
    lengths,
    dealing,
    w_query,
    w_key,
    w_value,
    w_out,
    w_up,
    w_down,
    b_query,
    b_value,
    b_out,
    b_up,
    b_down,
    gain_one,
    shift_one,
    gain_two,
    shift_two,
):
    params = (
        w_query,
        w_key,
        w_value,
        w_out,
        w_up,
        w_down,
        b_query,
        b_value,
        b_out,
        b_up,
        b_down,
        gain_one,
        shift_one,
        gain_two,
        shift_two,
    )
    own_rows = tokens.shape[2]
    width = tokens.shape[3]
    head_size = width // HEADS
    scale_factor = 1.0 / math.sqrt(head_size)
    my_start = lax.axis_index("ctx") * own_rows
    wsh_count = lax.axis_size("wsh")
    grads = tuple(
        (jnp.zeros((item.shape[0] * wsh_count,) + item.shape[1:], jnp.float32) for item in params)
    )
    results = []
    input_grads = []
    for micro in range(MB):
        whole = gather_params(params)
        query_weight, key_weight, value_weight, out_weight, up_weight, down_weight = whole[:6]
        (
            bias_query,
            bias_value,
            bias_out,
            bias_up,
            bias_down,
            gain_first,
            shift_first,
            gain_second,
            shift_second,
        ) = tuple((item.astype(jnp.float32) for item in whole[6:]))
        token_rows = tokens[0, micro]
        seq_all, valid_all = row_labels(dealing[0, micro], lengths[0, micro])
        my_seq = lax.dynamic_slice_in_dim(seq_all, my_start, own_rows)
        my_valid = lax.dynamic_slice_in_dim(valid_all, my_start, own_rows)
        query_low = (
            jnp.dot(token_rows, query_weight, preferred_element_type=jnp.float32) + bias_query
        ).astype(jnp.bfloat16)
        key_low = jnp.dot(token_rows, key_weight, preferred_element_type=jnp.float32).astype(
            jnp.bfloat16
        )
        value_low = (
            jnp.dot(token_rows, value_weight, preferred_element_type=jnp.float32) + bias_value
        ).astype(jnp.bfloat16)
        query_heads = query_low.reshape(own_rows, HEADS, head_size)
        my_key_heads = key_low.reshape(own_rows, HEADS, head_size)
        my_value_heads = value_low.reshape(own_rows, HEADS, head_size)
        start_state = (
            jnp.full((HEADS, own_rows), NEG_FILL, jnp.float32),
            jnp.zeros((HEADS, own_rows), jnp.float32),
            jnp.zeros((own_rows, HEADS, head_size), jnp.float32),
        )
        key_piece = lax.all_gather(key_low, "ctx", axis=0, tiled=True)
        value_piece = lax.all_gather(value_low, "ctx", axis=0, tiled=True)
        piece_rows = key_piece.shape[0]
        step_rows = math.gcd(piece_rows, 512)

        def visit_block(running, offset):
            run_max, run_sum, run_acc = running
            key_blk = lax.dynamic_slice_in_dim(key_piece, offset, step_rows).reshape(
                step_rows, HEADS, head_size
            )
            value_blk = lax.dynamic_slice_in_dim(value_piece, offset, step_rows).reshape(
                step_rows, HEADS, head_size
            )
            key_seq = lax.dynamic_slice_in_dim(seq_all, offset, step_rows)
            key_valid = lax.dynamic_slice_in_dim(valid_all, offset, step_rows)
            scores, allowed = masked_scores(
                query_heads, key_blk, my_seq, key_seq, key_valid, scale_factor
            )
            new_max = jnp.maximum(run_max, jnp.max(scores, axis=-1))
            rescale = jnp.exp(run_max - new_max)
            weights = jnp.exp(scores - new_max[:, :, None]) * allowed
            run_sum = run_sum * rescale + jnp.sum(weights, axis=-1)
            run_acc = run_acc * rescale.T[:, :, None] + jnp.einsum(
                "hqk,khd->qhd",
                weights.astype(jnp.bfloat16),
                value_blk,
                preferred_element_type=jnp.float32,
            )
            return (new_max, run_sum, run_acc)

        final_max, final_sum, final_acc = blockwise(start_state, piece_rows, step_rows, visit_block)
        attended = final_acc / final_sum.T[:, :, None]
        log_total = final_max + jnp.log(final_sum)
        attended_low = attended.reshape(own_rows, width).astype(jnp.bfloat16)
        out_proj = jnp.dot(attended_low, out_weight, preferred_element_type=jnp.float32) + bias_out
        first_sum = token_rows.astype(jnp.float32) + out_proj
        norm_one, norm_one_back = jax.vjp(layer_norm, first_sum, gain_first, shift_first)
        mlp_input = norm_one.astype(jnp.bfloat16)
        up_pre = jnp.dot(mlp_input, up_weight, preferred_element_type=jnp.float32) + bias_up
        activated, gelu_back = jax.vjp(gelu_exact, up_pre)
        activated_low = activated.astype(jnp.bfloat16)
        down_out = (
            jnp.dot(activated_low, down_weight, preferred_element_type=jnp.float32) + bias_down
        )
        result, norm_two_back = jax.vjp(layer_norm, norm_one + down_out, gain_second, shift_second)
        results.append(result.astype(jnp.bfloat16))
        grad_second, grad_gain_b, grad_shift_b = norm_two_back(
            cotangent[0, micro].astype(jnp.float32)
        )
        grad_down_low = grad_second.astype(jnp.bfloat16)
        grad_activated = jnp.einsum(
            "rd,fd->rf", grad_down_low, down_weight, preferred_element_type=jnp.float32
        )
        (grad_up_pre,) = gelu_back(grad_activated)
        grad_up_low = grad_up_pre.astype(jnp.bfloat16)
        grad_norm_one = (
            jnp.einsum("rf,df->rd", grad_up_low, up_weight, preferred_element_type=jnp.float32)
            + grad_second
        )
        grad_first, grad_gain_a, grad_shift_a = norm_one_back(grad_norm_one)
        grad_out_low = grad_first.astype(jnp.bfloat16)
        grad_att_low = jnp.einsum(
            "rd,ed->re", grad_out_low, out_weight, preferred_element_type=jnp.float32
        ).astype(jnp.bfloat16)
        grad_heads = grad_att_low.reshape(own_rows, HEADS, head_size)
        row_delta = jnp.sum(grad_heads.astype(jnp.float32) * attended, axis=-1).T
        empty_heads = jnp.zeros((own_rows, HEADS, head_size), jnp.float32)
        query_key_piece = lax.all_gather(key_low, "ctx", axis=0, tiled=True)
        query_value_piece = lax.all_gather(value_low, "ctx", axis=0, tiled=True)
        query_piece_rows = query_key_piece.shape[0]
        query_step_rows = math.gcd(query_piece_rows, 512)

        def query_visit_block(running, offset):
            key_blk = lax.dynamic_slice_in_dim(query_key_piece, offset, query_step_rows).reshape(
                query_step_rows, HEADS, head_size
            )
            value_blk = lax.dynamic_slice_in_dim(
                query_value_piece, offset, query_step_rows
            ).reshape(query_step_rows, HEADS, head_size)
            key_seq = lax.dynamic_slice_in_dim(seq_all, offset, query_step_rows)
            key_valid = lax.dynamic_slice_in_dim(valid_all, offset, query_step_rows)
            probs_low, grad_scores = attention_grads(
                query_heads,
                grad_heads,
                key_blk,
                value_blk,
                my_seq,
                key_seq,
                key_valid,
                log_total,
                row_delta,
                scale_factor,
            )
            return running + jnp.einsum(
                "hqk,khd->qhd", grad_scores, key_blk, preferred_element_type=jnp.float32
            )

        grad_query_sum = blockwise(
            empty_heads, query_piece_rows, query_step_rows, query_visit_block
        )
        total_all, delta_all = (
            lax.all_gather(log_total.T, "ctx", axis=0, tiled=True),
            lax.all_gather(row_delta.T, "ctx", axis=0, tiled=True),
        )
        query_piece = lax.all_gather(query_low, "ctx", axis=0, tiled=True)
        grad_piece = lax.all_gather(grad_att_low, "ctx", axis=0, tiled=True)
        key_piece_rows = query_piece.shape[0]
        key_step_rows = math.gcd(key_piece_rows, 512)

        def key_visit_block(running, offset):
            grad_key_run, grad_value_run = running
            query_blk = lax.dynamic_slice_in_dim(query_piece, offset, key_step_rows).reshape(
                key_step_rows, HEADS, head_size
            )
            grad_blk = lax.dynamic_slice_in_dim(grad_piece, offset, key_step_rows).reshape(
                key_step_rows, HEADS, head_size
            )
            total_blk = lax.dynamic_slice_in_dim(total_all, offset, key_step_rows)
            delta_blk = lax.dynamic_slice_in_dim(delta_all, offset, key_step_rows)
            query_seq = lax.dynamic_slice_in_dim(seq_all, offset, key_step_rows)
            probs_low, grad_scores = attention_grads(
                query_blk,
                grad_blk,
                my_key_heads,
                my_value_heads,
                query_seq,
                my_seq,
                my_valid,
                total_blk.T,
                delta_blk.T,
                scale_factor,
            )
            grad_key_run = grad_key_run + jnp.einsum(
                "hqk,qhd->khd", grad_scores, query_blk, preferred_element_type=jnp.float32
            )
            grad_value_run = grad_value_run + jnp.einsum(
                "hqk,qhd->khd", probs_low, grad_blk, preferred_element_type=jnp.float32
            )
            return (grad_key_run, grad_value_run)

        grad_key_sum, grad_value_sum = blockwise(
            (empty_heads, empty_heads), key_piece_rows, key_step_rows, key_visit_block
        )
        grad_key_flat = grad_key_sum.reshape(own_rows, width)
        grad_value_flat = grad_value_sum.reshape(own_rows, width)
        grad_query_low = (
            (grad_query_sum * scale_factor).reshape(own_rows, width).astype(jnp.bfloat16)
        )
        grad_key_low = (grad_key_flat * scale_factor).astype(jnp.bfloat16)
        grad_value_low = grad_value_flat.astype(jnp.bfloat16)
        terms = (
            jnp.einsum("rd,re->de", token_rows, grad_query_low, preferred_element_type=jnp.float32),
            jnp.einsum("rd,re->de", token_rows, grad_key_low, preferred_element_type=jnp.float32),
            jnp.einsum("rd,re->de", token_rows, grad_value_low, preferred_element_type=jnp.float32),
            jnp.einsum("rd,re->de", attended_low, grad_out_low, preferred_element_type=jnp.float32),
            jnp.einsum("rd,rf->df", mlp_input, grad_up_low, preferred_element_type=jnp.float32),
            jnp.einsum(
                "rf,rd->fd", activated_low, grad_down_low, preferred_element_type=jnp.float32
            ),
            jnp.sum(grad_query_low.astype(jnp.float32), axis=0),
            jnp.sum(grad_value_low.astype(jnp.float32), axis=0),
            jnp.sum(grad_out_low.astype(jnp.float32), axis=0),
            jnp.sum(grad_up_low.astype(jnp.float32), axis=0),
            jnp.sum(grad_down_low.astype(jnp.float32), axis=0),
            grad_gain_a,
            grad_shift_a,
            grad_gain_b,
            grad_shift_b,
        )
        grads = tuple((total_now + fresh for total_now, fresh in zip(grads, terms)))
        grad_rows = (
            grad_first
            + jnp.einsum(
                "re,de->rd", grad_query_low, query_weight, preferred_element_type=jnp.float32
            )
            + jnp.einsum("re,de->rd", grad_key_low, key_weight, preferred_element_type=jnp.float32)
            + jnp.einsum(
                "re,de->rd", grad_value_low, value_weight, preferred_element_type=jnp.float32
            )
        )
        input_grads.append(grad_rows.astype(jnp.bfloat16))
    shards = jax.tree.map(
        lambda part: part.astype(jnp.float32),
        lax.psum_scatter(as_sent(grads), "wsh", scatter_dimension=0, tiled=True),
    )
    summed = jax.tree.map(lambda part: part.astype(jnp.float32), lax.psum(as_sent(shards), "ctx"))
    return (jnp.stack(results)[None], jnp.stack(input_grads)[None]) + tuple(summed)


MESH_IDS = pl.DeviceIdType.MESH
F32 = jnp.float32
BF16 = jnp.bfloat16
HD = 64
VMEM_BYTES = 60 * 1024 * 1024


def flip(index, bit):
    return index + bit * (1 - 2 * lax.rem(lax.div(index, bit), 2))


def bit_of(index, bit):
    return lax.rem(lax.div(index, bit), 2)


def greet(peers):
    barrier = pltpu.get_barrier_semaphore()
    for peer in peers:
        pl.semaphore_signal(barrier, inc=1, device_id=peer, device_id_type=MESH_IDS)


def wait_for_all(peers):
    pl.semaphore_wait(pltpu.get_barrier_semaphore(), len(peers))


def send(src, dst, send_sem, recv_sem, peer):
    copy = pltpu.make_async_remote_copy(
        src_ref=src,
        dst_ref=dst,
        send_sem=send_sem,
        recv_sem=recv_sem,
        device_id=peer,
        device_id_type=MESH_IDS,
    )
    copy.start()
    return copy


class Dealing:
    def __init__(self, lengths_hbm, dealing_hbm, lengths, dealing, slots, sems):
        self.lengths, self.dealing, self.slots = lengths, dealing, slots
        self.copies = (
            pltpu.make_async_copy(lengths_hbm, lengths, sems.at[0]),
            pltpu.make_async_copy(dealing_hbm, dealing, sems.at[1]),
        )
        for copy in self.copies:
            copy.start()

    def invert(self):
        for copy in self.copies:
            copy.wait()
        micros, _, count = self.dealing.shape

        def find(number, carry):
            m, block = lax.div(number, count), lax.rem(number, count)
            slot = jnp.int32(0)
            for t in range(count):
                slot = jnp.where(self.dealing[m, 0, t] == block, jnp.int32(t), slot)
            self.slots[m, block] = slot
            return carry

        lax.fori_loop(0, micros * count, find, 0)

    def length(self, m, s):
        return self.lengths[0, s, m]

    def block(self, m, t):
        return self.dealing[m, 0, t]

    def slot(self, m, b):
        return self.slots[m, b]


def dealing_scratch(lengths, dealing):
    return [
        pltpu.SMEM(lengths.shape, jnp.int32),
        pltpu.SMEM(dealing.shape, jnp.int32),
        pltpu.SMEM((dealing.shape[0], dealing.shape[2]), jnp.int32),
        pltpu.SemaphoreType.DMA((2,)),
    ]


def plane_peers(c, w, count):
    return [(lax.rem(c + step, count), w) for step in range(1, count)]


def pack_two(first, second, row, pair, out):
    cols = pl.ds(pair * 128, 128)
    a, b = first[pl.ds(row, BLK), cols], second[pl.ds(row, BLK), cols]
    for head in range(2):
        lane = slice(head * HD, head * HD + HD)
        out[2 * pair + head, 0:BLK, :] = jnp.concatenate([a[:, lane], b[:, lane]], axis=1)


def pack_one(source, row, pair, out):
    both = source[pl.ds(row, BLK), pl.ds(pair * 128, 128)]
    for head in range(2):
        lane = slice(head * HD, head * HD + HD)
        out[2 * pair + head, BLK : BLK + BLK // 2, :] = fold(both[:, lane])


def unpack_fold(block):
    return jnp.concatenate([block[:, :HD], block[:, HD:]], axis=0)


def fold(rows):
    half = rows.shape[0] // 2
    return jnp.concatenate([rows[:half], rows[half:]], axis=1)


def all_bytes(ref, sem, peers):
    view = ref.at[pl.ds(0, peers)]
    return pltpu.make_async_copy(view, view, sem)


def norm_parts(summed):
    row_mean = jnp.mean(summed, axis=-1, keepdims=True)
    centred = summed - row_mean
    row_var = jnp.mean(centred * centred, axis=-1, keepdims=True)
    scale = lax.rsqrt(row_var + EPSILON)
    return centred * scale, scale


def norm_back(grad, unit, scale, gain):
    inner = grad * gain
    mean_one = jnp.mean(inner, axis=-1, keepdims=True)
    mean_two = jnp.mean(inner * unit, axis=-1, keepdims=True)
    return scale * (inner - mean_one - unit * mean_two)


def dot_minor(a, b):
    return lax.dot_general(a, b, (((1,), (1,)), ((), ())), preferred_element_type=F32)


ROW_OUT, ROW_UP, ROW_DOWN, ROW_GAIN_ONE, ROW_SHIFT_ONE, ROW_GAIN_TWO, ROW_SHIFT_TWO = 2, 3, 7, 8, 9, 10, 11


SQUARE, PAIR_Y, PAIR_Z, ALONE = (8, "yz"), (4, "y"), (4, "z"), (2, "")
WAYS = (
    SQUARE, SQUARE, SQUARE, ALONE, PAIR_Y, PAIR_Y, SQUARE, SQUARE, SQUARE, PAIR_Z, ALONE, PAIR_Y,
)
SEND_ORDER = (1, 0, 2, 7, 6, 5, 11, 9, 4, 8, 3, 10)
FORWARD_SCHEDULE = (
    ("own", 0), ("own", 1), ("own", 2), ("second", 1), ("second", 0), ("third", 1), ("third",
    0), ("second", 2), ("fourth", 1), ("project", 1), ("second", 7), ("fourth", 0), ("third",
    2), ("project", 0), ("keys", 0), ("keys", 1), ("third", 7), ("second", 6), ("fourth", 2),
    ("project", 2), ("values", 0), ("values", 1), ("keys", 2), ("second", 5), ("values", 2),
    ("att", 0), ("second", 8), ("att", 1), ("second", 4), ("fourth", 7), ("att", 2), ("fourth",
    5), ("fourth", 3), ("third", 6), ("third", 8), ("second", 9), ("fourth", 4), ("rows", 0),
    ("second", 11), ("fourth", 6), ("out", 0), ("hidden", 0), ("hidden", 1), ("fourth", 8),
    ("hidden", 2), ("fourth", 9), ("hidden", 3), ("fourth", 10), ("hidden", 4), ("fourth", 11),
    ("hidden", 5), ("hidden", 6), ("hidden", 7),
)


def weight_plan(shards):
    unit = shards[0].shape[0] * shards[0].shape[1]
    plan = []
    for index, (rows, cols) in enumerate(shard.shape for shard in shards):
        parts = max(1, rows * cols // unit)
        for part in range(parts):
            plan.append((index, part * (rows // parts), rows // parts, WAYS[len(plan)]))
    return plan


def forward_kernel(heads, plan, n_weights, n_vectors, *refs):
    integers, (x_ref, cot_ref), refs = refs[:2], refs[2:4], refs[4:]
    shards, vectors = refs[:n_weights], refs[n_weights : n_weights + n_vectors]
    refs = refs[n_weights + n_vectors :]
    wholes, kept_ref, lse_ref = refs[:3], *refs[3:5]
    results, refs = refs[5:15], refs[15:]
    a_ref, out_ref, n_ref, g_ref, do_ref, du_ref, dm_ref, dh_ref, da_ref, vec_ref = refs[:10]
    made, result_sem, refs = refs[:10], refs[10], refs[11:]
    dealt, refs = Dealing(*integers, *refs[:4]), refs[4:]
    near, refs = refs[:n_weights], refs[n_weights:]
    small, small_in, small_whole, bias, q_ref, k_ref, v_ref = refs[:7]
    begun, slope, n_full, unit, total = refs[7:12]
    refs = refs[12:]
    in_buf = refs[:MB]
    out_buf, back_out, back_in, q_s, k_s, v_s, a_s = refs[MB : 7 + MB]
    (
        w_send,
        w_recv,
        small_sems,
        local_sem,
        stage_sem,
        send_sem,
        recv_sem,
        back_send,
        back_recv,
        keep_sem,
    ) = refs[7 + MB :]
    c, w = lax.axis_index("ctx"), lax.axis_index("wsh")
    o = 1 - w
    by_x, by_y, by_z, by_core = (c, o), (flip(c, 2), w), (flip(c, 4), w), (flip(c, 1), w)
    core, y, z = bit_of(c, 1), bit_of(c, 2), bit_of(c, 4)
    peers = plane_peers(c, w, heads)
    stores = []

    def store(target):
        index = [item is target for item in made].index(True)
        copy = pltpu.make_async_copy(target, results[index], result_sem.at[index])
        copy.start()
        stores.append(copy)

    greet(peers + [by_x])
    staged = []
    for index, shard in enumerate(shards):
        rows = shard.shape[0]
        spot = pl.ds(pl.multiple_of(w * rows, rows), rows)
        copy = pltpu.make_async_copy(shard, near[index].at[spot], stage_sem.at[index])
        copy.start()
        staged.append(copy)
    line, lanes = 0, small.shape[1]
    for vector in vectors:
        for first in range(0, vector.shape[0], lanes):
            piece = vector[pl.ds(first, lanes)].astype(F32)
            small[line : line + 1, :] = piece.reshape(1, lanes)
            line += 1
    wait_for_all(peers + [by_x])
    small_sent = send(small, small_in, small_sems.at[0], small_sems.at[1], by_x)

    def part(chunk, side, piece, start, count):
        tensor, first, rows, way = plan[chunk]
        half = shards[tensor].shape[0]
        at = side * half + first + piece * (rows // way[0]) + start
        return near[tensor].at[pl.ds(pl.multiple_of(at, 8), count)]

    steps = {}

    def sem(kind, chunk):
        return w_send.at[kind, chunk], w_recv.at[kind, chunk]

    def own_piece(way):
        return {
            SQUARE: core * 4 + z * 2 + y,
            PAIR_Y: core * 2 + y,
            PAIR_Z: core * 2 + z,
            ALONE: core,
        }[way]

    for chunk in SEND_ORDER:
        tensor, first, rows, way = plan[chunk]
        size, mine = rows // way[0], own_piece(way)
        src = shards[tensor].at[pl.ds(pl.multiple_of(first + mine * size, 8), size)]
        steps[chunk, 0] = send(src, part(chunk, w, mine, 0, size), *sem(0, chunk), by_x)
    dealt.invert()

    def second(chunk):
        _, _, rows, way = plan[chunk]
        steps[chunk, 0].wait_recv()
        ref = part(chunk, o, own_piece(way), 0, rows // way[0])
        for name in way[1]:
            kind, peer = {"y": (1, by_y), "z": (2, by_z)}[name]
            steps[chunk, kind] = send(ref, ref, *sem(kind, chunk), peer)

    def third(chunk):
        _, _, rows, way = plan[chunk]
        size = rows // way[0]
        steps[chunk, 1].wait_recv()
        steps[chunk, 2].wait_recv()
        ref = part(chunk, o, core * 4 + (1 - z) * 2 + y, 0, size // 2)
        steps[chunk, 3] = send(ref, ref, *sem(3, chunk), by_y)
        ref = part(chunk, o, core * 4 + z * 2 + (1 - y), size // 2, size // 2)
        steps[chunk, 4] = send(ref, ref, *sem(4, chunk), by_z)

    def fourth(chunk):
        _, _, rows, way = plan[chunk]
        for kind in {SQUARE: (3, 4), PAIR_Y: (1,), PAIR_Z: (2,), ALONE: (0,)}[way]:
            steps[chunk, kind].wait_recv()
        ref = part(chunk, o, core * (way[0] // 2), 0, rows // 2)
        steps[chunk, 5] = send(ref, ref, *sem(5, chunk), by_core)

    width = x_ref.shape[1]
    step = 256
    projected = []

    def half_product(index, side, cols):
        rows = shards[index].shape[0]
        lanes_in = pl.ds(pl.multiple_of(side * rows, rows), rows)
        return jnp.dot(
            x_ref[:, lanes_in], near[index][lanes_in, cols], preferred_element_type=F32
        )

    def own_half(index):
        staged[index].wait()

        def some_columns(turn, carry):
            cols = pl.ds(pl.multiple_of(turn * step, step), step)
            begun[index, :, cols] = half_product(index, w, cols)
            return carry

        lax.fori_loop(0, width // step, some_columns, 0)

    def project(index):
        if not projected:
            small_sent.wait()
            small_whole[w] = small[...]
            small_whole[o] = small_in[...]
            for side in range(2):
                for row in range(2):
                    bias[row : row + 1, side * lanes : (side + 1) * lanes] = small_whole[
                        side, row : row + 1, :
                    ]
        projected.append(index)
        steps[index, 5].wait_recv()
        out = (q_ref, k_ref, v_ref)[index]

        def some_columns(turn, carry):
            cols = pl.ds(pl.multiple_of(turn * step, step), step)
            product = begun[index, :, cols] + half_product(index, o, cols)
            if index != 1:
                product = product + bias[index // 2 : index // 2 + 1, cols]
            out[:, cols] = product.astype(BF16)
            return carry

        lax.fori_loop(0, width // step, some_columns, 0)
        pltpu.make_async_copy(near[index], wholes[index], local_sem.at[index]).start()

    def pack(item, first, count, fill):
        for pair in range(heads // 2):
            fill(item, pair)
        rows = pl.ds(first, count)
        for peer in peers:
            send(
                out_buf.at[item, peer[0], rows],
                in_buf[item].at[c, rows],
                send_sem.at[item],
                recv_sem.at[item],
                peer,
            )
        in_buf[item][c, rows] = out_buf[item, c, rows]

    def pack_keys(m):
        pack(m, 0, BLK, lambda m, pair: pack_two(q_ref, k_ref, m * BLK, pair, out_buf.at[m]))

    def pack_values(m):
        pack(m, BLK, BLK // 2, lambda m, pair: pack_one(v_ref, m * BLK, pair, out_buf.at[m]))

    blocks = heads
    span = BPS * BLK

    def attention(m):
        all_bytes(in_buf[m], recv_sem.at[m], heads - 1).wait()
        pltpu.make_async_copy(in_buf[m], kept_ref.at[m], keep_sem.at[m]).start()
        for b in range(blocks):
            got = in_buf[m][dealt.slot(m, b)]
            q_s[b * BLK : (b + 1) * BLK, :] = got[:BLK, :HD]
            k_s[b * BLK : (b + 1) * BLK, :] = got[:BLK, HD:]
            v_s[b * BLK : (b + 1) * BLK, :] = unpack_fold(got[BLK:])

        def one_sequence(s, carry):
            rows = pl.ds(pl.multiple_of(s * span, span), span)
            scores = lax.dot_general(
                k_s[rows, :], q_s[rows, :], (((1,), (1,)), ((), ())), preferred_element_type=F32
            ) * (1.0 / math.sqrt(HD))
            place = lax.broadcasted_iota(jnp.int32, scores.shape, 0)
            scores = jnp.where(place < dealt.length(m, s), scores, NEG_FILL)
            top = jnp.max(scores, axis=0, keepdims=True)
            weights = jnp.exp(scores - top)
            summed = jnp.sum(weights, axis=0, keepdims=True)
            out_t = lax.dot_general(
                v_s[rows, :],
                weights.astype(BF16),
                (((0,), (0,)), ((), ())),
                preferred_element_type=F32,
            )
            a_s[pl.ds(s * BPS, BPS)] = (out_t / summed).T.reshape(BPS, BLK, HD)
            lse_ref[pl.ds(m * (blocks // BPS) + s, 1), :] = top + jnp.log(summed)
            return carry

        lax.fori_loop(0, blocks // BPS, one_sequence, 0)
        for t in range(blocks):
            back_out[m, t] = fold(a_s[dealt.block(m, t)]).astype(BF16)
        for peer in peers:
            send(
                back_out.at[m, peer[0]], back_in.at[m, c], back_send.at[m], back_recv.at[m], peer
            )
        back_in[m, c] = back_out[m, c]

    def come_back(_):
        for m in range(MB):
            all_bytes(back_in.at[m], back_recv.at[m], heads - 1).wait()
            for pair in range(heads // 2):
                a_ref[m * BLK : (m + 1) * BLK, pair * 128 : (pair + 1) * 128] = jnp.concatenate(
                    [unpack_fold(back_in[m, 2 * pair]), unpack_fold(back_in[m, 2 * pair + 1])],
                    axis=1,
                )
        store(a_ref)

    def line_of(row):
        return jnp.concatenate(
            [small_whole[0, row : row + 1, :], small_whole[1, row : row + 1, :]], axis=1
        )

    def keep(row, values):
        summed = jnp.sum(values, axis=0, keepdims=True)
        for side in range(2):
            vec_ref[side, row : row + 1, :] = summed[:, side * lanes : (side + 1) * lanes]

    out_w, up_w, down_w = near[3:]
    chunks_of = {t: [i for i, item in enumerate(plan) if item[0] == t] for t in range(n_weights)}

    def arrived(tensor, chunks):
        for chunk in chunks:
            steps[chunk, 5].wait_recv()

    def out_project(_):
        staged[3].wait()
        arrived(3, chunks_of[3])
        h_one = x_ref[...].astype(F32) + (
            jnp.dot(a_ref[...], out_w[...], preferred_element_type=F32) + line_of(ROW_OUT)
        )
        unit_one, scale_one = norm_parts(h_one)
        unit[...] = unit_one
        n_one = unit_one * line_of(ROW_GAIN_ONE) + line_of(ROW_SHIFT_ONE)
        n_full[...] = n_one
        n_ref[...] = n_one.astype(BF16)
        store(n_ref)
        total[...] = jnp.zeros_like(total)
        kept_scale.append(scale_one)

    kept_scale = []
    hidden = g_ref.shape[1]
    hidden_steps = hidden // lanes
    per_half = hidden_steps // 2

    def hidden_at(turn):
        j = lax.rem(w * per_half + turn, hidden_steps)
        cols = pl.ds(pl.multiple_of(j * lanes, lanes), lanes)
        return cols, lax.div(j, per_half), pl.ds(ROW_UP + lax.rem(j, per_half), 1)

    def hidden_up(turn):
        if turn == 0:
            staged[4].wait()
            arrived(4, chunks_of[4])
            staged[5].wait()
        elif turn >= per_half:
            share = len(chunks_of[5]) // per_half
            first = (turn - per_half) * share
            arrived(5, chunks_of[5][first : first + share])
        cols, side, row = hidden_at(turn)
        u = jnp.dot(n_ref[...], up_w[:, cols], preferred_element_type=F32) + small_whole[side, row, :]
        below = 0.5 * (1.0 + lax.erf(u * math.sqrt(0.5)))
        slope[:, cols] = below + u * jnp.exp(-0.5 * u * u) * (1.0 / math.sqrt(2.0 * math.pi))
        g = (u * below).astype(BF16)
        g_ref[:, cols] = g
        total[...] += jnp.dot(g, down_w[cols, :], preferred_element_type=F32)

    acts = {
        "second": second,
        "third": third,
        "fourth": fourth,
        "project": project,
        "own": own_half,
        "keys": pack_keys,
        "values": pack_values,
        "att": attention,
        "rows": come_back,
        "out": out_project,
        "hidden": hidden_up,
    }
    for name, value in FORWARD_SCHEDULE:
        acts[name](value)

    store(g_ref)
    h_two = n_full[...] + (total[...] + line_of(ROW_DOWN))
    unit_two, scale_two = norm_parts(h_two)
    out_ref[...] = (unit_two * line_of(ROW_GAIN_TWO) + line_of(ROW_SHIFT_TWO)).astype(BF16)
    store(out_ref)
    cot = cot_ref[...].astype(F32)
    keep(ROW_GAIN_TWO, cot * unit_two)
    keep(ROW_SHIFT_TWO, cot)
    dh_two = norm_back(cot, unit_two, scale_two, line_of(ROW_GAIN_TWO))
    dm = dh_two.astype(BF16)
    dm_ref[...] = dm
    store(dm_ref)
    keep(ROW_DOWN, dm.astype(F32))
    total[...] = dh_two
    for turn in range(hidden_steps):
        cols, side, row = hidden_at(turn)
        du = (slope[:, cols] * dot_minor(dm_ref[...], down_w[cols, :])).astype(BF16)
        du_ref[:, cols] = du
        vec_ref[side, row, :] = jnp.sum(du.astype(F32), axis=0, keepdims=True)
        total[...] += dot_minor(du, up_w[:, cols])
    store(du_ref)
    dn = total[...]
    keep(ROW_GAIN_ONE, dn * unit[...])
    keep(ROW_SHIFT_ONE, dn)
    dh_one = norm_back(dn, unit[...], kept_scale[0], line_of(ROW_GAIN_ONE))
    dh_ref[...] = dh_one
    store(dh_ref)
    do = dh_one.astype(BF16)
    do_ref[...] = do
    store(do_ref)
    keep(ROW_OUT, do.astype(F32))
    for side in range(2):
        vec_ref[side, 0:ROW_OUT, :] = jnp.zeros((ROW_OUT, lanes), F32)
    store(vec_ref)
    da_ref[...] = dot_minor(do, out_w[...]).astype(BF16)
    store(da_ref)

    for m in range(MB):
        all_bytes(out_buf.at[m], send_sem.at[m], heads - 1).wait()
        all_bytes(back_out.at[m], back_send.at[m], heads - 1).wait()
        pltpu.make_async_copy(in_buf[m], kept_ref.at[m], keep_sem.at[m]).wait()
    for flight in steps.values():
        flight.wait_send()
    for copy in stores:
        copy.wait()
    for index in range(3):
        pltpu.make_async_copy(near[index], wholes[index], local_sem.at[index]).wait()


def forward(lengths, dealing, x, cot, shards, vectors, heads):
    plan = weight_plan(shards)
    count = len(shards)
    anywhere, vmem = pl.BlockSpec(memory_space=pl.ANY), pl.BlockSpec(memory_space=pltpu.VMEM)
    rows, width = x.shape
    hidden = shards[4].shape[1]
    pack_rows = BLK + BLK // 2
    span = BPS * BLK
    lanes = min(item.shape[0] for item in vectors)
    lines = sum(item.shape[0] for item in vectors) // lanes
    whole = lambda s: (2 * s.shape[0],) + s.shape[1:]
    low = lambda cols: jax.ShapeDtypeStruct((rows, cols), BF16)
    full = lambda cols: pltpu.VMEM((rows, cols), F32)
    sems = lambda *dims: pltpu.SemaphoreType.DMA(dims)
    kept_shapes = [
        jax.ShapeDtypeStruct((MB, heads, pack_rows, 128), BF16),
        jax.ShapeDtypeStruct((8, span), F32),
    ]
    results = [low(width)] * 3 + [low(hidden), low(width), low(hidden), low(width)]
    results += [jax.ShapeDtypeStruct((rows, width), F32), low(width)]
    results += [jax.ShapeDtypeStruct((2, lines, lanes), F32)]
    return pl.pallas_call(
        functools.partial(forward_kernel, heads, plan, count, len(vectors)),
        out_shape=[jax.ShapeDtypeStruct(whole(s), s.dtype) for s in shards[:3]]
        + kept_shapes
        + results,
        in_specs=[anywhere] * 2 + [vmem] * 2 + [anywhere] * count + [vmem] * len(vectors),
        out_specs=[anywhere] * 4 + [vmem] + [anywhere] * 10,
        scratch_shapes=[pltpu.VMEM(item.shape, item.dtype) for item in results]
        + [sems(len(results))]
        + dealing_scratch(lengths, dealing)
        + [pltpu.VMEM(whole(s), s.dtype) for s in shards]
        + [pltpu.VMEM((lines, lanes), F32)] * 2
        + [pltpu.VMEM((2, lines, lanes), F32), pltpu.VMEM((2, width), F32)]
        + [pltpu.VMEM((rows, width), BF16)] * 3
        + [pltpu.VMEM((3, rows, width), F32)]
        + [full(hidden), full(width), full(width), full(width)]
        + [pltpu.VMEM((heads, pack_rows, 128), BF16)] * MB
        + [
            pltpu.VMEM((MB, heads, pack_rows, 128), BF16),
            pltpu.VMEM((MB, heads, BLK // 2, 128), BF16),
            pltpu.VMEM((MB, heads, BLK // 2, 128), BF16),
            pltpu.VMEM((heads * BLK, HD), BF16),
            pltpu.VMEM((heads * BLK, HD), BF16),
            pltpu.VMEM((heads * BLK, HD), BF16),
            pltpu.VMEM((heads, BLK, HD), F32),
        ]
        + [sems(6, len(plan)), sems(6, len(plan)), sems(2), sems(3), sems(count)]
        + [sems(MB)] * 5,
        compiler_params=pltpu.CompilerParams(
            collective_id=1, has_side_effects=True, vmem_limit_bytes=VMEM_BYTES
        ),
        name="forward",
    )(lengths, dealing, x, cot, *shards, *vectors)


ORDERS = (
    ("xyzZ", "xyzZ", "yxzZ", "xyzZ"),
    ("zxyZ", "yxzZ", "xyzZ", "xzyZ"),
    ("yzZ", "zyZ", "yzZ", "yzZ"),
)
PIECES = len(ORDERS[0])
SCHEDULE = (
    "up", 0, 1, 2, "down", (1, 0), (2, 0), "back", (1, 2), (2, 2), (2, 0), (1, 1), (1, 3),
    (2, 2), (2, 1), (2, 3), (2, 0), "qkv", (1, 1), (2, 3), (2, 2), (1, 3), (2, 0), (2, 3),
    (1, 2), (0, 0), "vec", (2, 1), (1, 1), (2, 0), (1, 2), (1, 0), (2, 2), "rows", (0, 0),
    (1, 3), (1, 2), (0, 1), "vec", (0, 0), (1, 1), (2, 3), (1, 3), (2, 2), (0, 2), (2, 1),
    (0, 1), (0, 3), (1, 1), (0, 1), "vec", (1, 0), (2, 3), (0, 0), (1, 3), (0, 3), (0, 2),
    (2, 0), (1, 1), (1, 0), (0, 3), (0, 2), (0, 0), "vec", (2, 1), (0, 1), (1, 2), (1, 0),
    (0, 2), (0, 3), (0, 0), (0, 1), (1, 2), (2, 2), (0, 2), (0, 3), (2, 1), (0, 0), "vec",
    (1, 1), (0, 1), (1, 0), (1, 3), (0, 2), (0, 3), (2, 3), (0, 1), (1, 0), (1, 2), (0, 2),
    (2, 1), (0, 3), (1, 3),
)
KEYS = tuple((part, piece) for part in range(3) for piece in range(PIECES))


def landing_shapes(order, shape):
    shards, sides, shapes = 8, shape[0], []
    for name in order:
        if name == "x":
            sides = 1
        else:
            shards //= 2
        shapes.append((sides, shards, shape[2] // PIECES, shape[3]))
    return shapes


def dot_t(a, b):
    return lax.dot_general(a, b, (((0,), (0,)), ((), ())), preferred_element_type=F32)


def lanes_at(first, size):
    return pl.ds(pl.multiple_of(first, 128), size)


def backward_kernel(heads, *refs):
    integers, operands, weights = refs[:2], refs[2:14], refs[14:17]
    rows_out, o_a, o_b, o_c, vec_out = refs[17:22]
    held, load_sem, refs = refs[22:34], refs[34], refs[35:]
    dealt, refs = Dealing(*integers, *refs[:4]), refs[4:]
    da_ref, g_ref, dm_ref, n_ref, du_ref, kept_ref = held[:6]
    lse_ref, a_ref, do_ref, x_ref, vec_ref, dh_ref = held[6:]
    loads = []
    for index, (source, target) in enumerate(zip(operands, held)):
        copy = pltpu.make_async_copy(source, target, load_sem.at[index])
        copy.start()
        loads.append((target, copy))

    def ready(*targets):
        for item in list(loads):
            if any(item[0] is target for target in targets):
                item[1].wait()
                loads.remove(item)

    in_buf = refs[:MB]
    out_buf, back_out, back_in, q_s, k_s, v_s, a_s, dq_s, dk_s, dv_s = refs[MB : MB + 10]
    refs = refs[MB + 10 :]
    dq_ref, dk_ref, dv_ref, m_x, m_a, m_n, m_do, m_du, m_dqkv, m_g, m_dm = refs[:11]
    far_g, far_dm, cross_g, cross_dm = refs[11:15]
    near, (vec_s, v_recv, v_sum, s_a, s_b, s_c) = refs[15:18], refs[18:24]
    refs = refs[24:]
    r_bufs = {}
    for part, piece in KEYS:
        size = len(ORDERS[part][piece])
        r_bufs[part, piece], refs = refs[:size], refs[size:]
    (
        send_sem,
        recv_sem,
        back_send,
        back_recv,
        mate_send,
        mate_recv,
        near_sem,
        rs_send,
        rs_recv,
        ag_send,
        ag_recv,
        own_sem,
        v_send_sem,
        v_recv_sem,
    ) = refs
    c, x = lax.axis_index("ctx"), lax.axis_index("wsh")
    core, y, z, zz = bit_of(c, 1), bit_of(c, 2), bit_of(c, 4), bit_of(c, 8)
    by_core = (flip(c, 1), x)
    by = {"x": (c, 1 - x), "y": (flip(c, 2), x), "z": (flip(c, 4), x), "Z": (flip(c, 8), x)}
    bits = {"y": y, "z": z, "Z": zz}
    peers = plane_peers(c, x, heads)
    by_cross = (flip(c, 1), 1 - x)
    greet(peers + [by["x"], by_cross])
    blocks, span = heads, BPS * BLK
    width, hidden = da_ref.shape[1], g_ref.shape[1]
    for index, weight in enumerate(weights):
        pltpu.make_async_copy(weight, near[index], near_sem.at[index]).start()
    ready(da_ref)
    for m in range(MB):
        row = slice(m * BLK, (m + 1) * BLK)
        for pair in range(heads // 2):
            both = da_ref[row, pair * 128 : (pair + 1) * 128]
            for head in range(2):
                out_buf[m, 2 * pair + head] = fold(both[:, head * HD : (head + 1) * HD])
        in_buf[m][c] = out_buf[m, c]
    wait_for_all(peers + [by["x"], by_cross])
    for m in range(MB):
        for peer in peers:
            send(out_buf.at[m, peer[0]], in_buf[m].at[c], send_sem.at[m], recv_sem.at[m], peer)

    shared = {}

    def share(name, src, dst, peer=by_core):
        index = len(shared)
        shared[name] = send(src, dst, mate_send.at[index], mate_recv.at[index], peer)

    other = 1 - core
    quarter = hidden // 4

    def hidden_rows(side, which):
        return g_ref.at[:, lanes_at(side * 2 * quarter + which * quarter, quarter)]

    ready(g_ref, dm_ref)
    share("far_g", hidden_rows(1 - x, core), far_g, by["x"])
    share("far_dm", dm_ref, far_dm, by["x"])
    share("cross_g", hidden_rows(1 - x, other), cross_g, by_cross)
    ready(n_ref, du_ref)
    share("n", n_ref, m_n)
    share("du", du_ref.at[:, lanes_at(other * (hidden // 2), hidden // 2)], m_du)
    share("g", hidden_rows(x, other), m_g)
    share("dm", dm_ref, m_dm)
    ready(*held)
    share("a", a_ref, m_a)
    share("do", do_ref.at[:, lanes_at(other * (width // 2), width // 2)], m_do)
    share("x", x_ref, m_x)
    dealt.invert()

    sums, outs = (s_a, s_b, s_c), (o_a, o_b, o_c)
    wide = 512

    def tile(pairs, out, first, count):
        def body(turn, carry):
            at = turn * wide
            total = sum(dot_t(lhs[...], rhs[:, lanes_at(col + at, wide)]) for lhs, rhs, col in pairs)
            cols = lanes_at(first + at, wide)
            out[..., cols] = total.astype(BF16).reshape(out.shape[:-1] + (wide,))
            return carry

        lax.fori_loop(0, count, body, 0)

    def grads_up():
        shared["n"].wait_recv()
        shared["du"].wait_recv()
        half = hidden // 2
        tile(((n_ref, du_ref, core * half), (m_n, m_du, 0)), s_b, 0, half // wide)

    def grads_down():
        shared["far_dm"].wait_recv()
        share("cross_dm", far_dm, cross_dm)
        for name in ("g", "dm", "far_g", "cross_g", "cross_dm"):
            shared[name].wait_recv()
        pairs = ((hidden_rows(x, core), dm_ref, 0), (m_g, m_dm, 0))
        pairs += ((far_g, far_dm, 0), (cross_g, cross_dm, 0))
        tile(pairs, s_c.at[0], 0, width // wide)

    def grads_qkv():
        half = width // 2
        for name in ("a", "do", "x", "dq", "dk", "dv"):
            shared[name].wait_recv()
        tile(((a_ref, do_ref, core * half), (m_a, m_do, 0)), s_a, 3 * half, half // wide)
        for index, ref in enumerate((dq_ref, dk_ref, dv_ref)):
            pairs = ((x_ref, ref, core * half), (m_x, m_dqkv, index * half))
            tile(pairs, s_a, index * half, half // wide)

    def attention(m):
        all_bytes(in_buf[m], recv_sem.at[m], heads - 1).wait()
        for b in range(blocks):
            slot = dealt.slot(m, b)
            got = kept_ref[m, slot]
            rows = slice(b * BLK, (b + 1) * BLK)
            q_s[rows, :] = got[:BLK, :HD]
            k_s[rows, :] = got[:BLK, HD:]
            v_s[rows, :] = unpack_fold(got[BLK:])
            a_s[rows, :] = unpack_fold(in_buf[m][slot])

        def one_sequence(s, carry):
            rows = pl.ds(pl.multiple_of(s * span, span), span)
            qq, kk, vv, dd = q_s[rows, :], k_s[rows, :], v_s[rows, :], a_s[rows, :]
            scale = 1.0 / math.sqrt(HD)
            minor = (((1,), (1,)), ((), ()))
            scores = lax.dot_general(kk, qq, minor, preferred_element_type=F32) * scale
            spot = lax.broadcasted_iota(jnp.int32, scores.shape, 0)
            total = lse_ref[pl.ds(m * (blocks // BPS) + s, 1), :]
            probs = jnp.exp(jnp.where(spot < dealt.length(m, s), scores - total, NEG_FILL))
            dp = lax.dot_general(vv, dd, minor, preferred_element_type=F32)
            both = probs * dp
            delta = jnp.sum(both, axis=0, keepdims=True)
            ds = (both - probs * delta).astype(BF16)
            here, split = pl.ds(s * BPS, BPS), (BPS, BLK, HD)
            dv = jnp.dot(probs.astype(BF16), dd, preferred_element_type=F32)
            dv_s[here] = dv.reshape(split)
            dk_s[here] = (jnp.dot(ds, qq, preferred_element_type=F32) * scale).reshape(split)
            dq_s[here] = (dot_t(kk, ds).T * scale).reshape(split)
            return carry

        lax.fori_loop(0, blocks // BPS, one_sequence, 0)
        for t in range(blocks):
            at = dealt.block(m, t)
            back_out[m, t, 0:BLK, :] = jnp.concatenate([dq_s[at], dk_s[at]], axis=1).astype(BF16)
            back_out[m, t, BLK:, :] = fold(dv_s[at]).astype(BF16)
        for peer in peers:
            send(
                back_out.at[m, peer[0]], back_in.at[m, c], back_send.at[m], back_recv.at[m], peer
            )
        back_in[m, c] = back_out[m, c]

    vec_peers = (by["x"], by["y"], by["z"], by["Z"], by_core)
    vec_steps = []

    def vec_send(src):
        step = len(vec_steps)
        vec_steps.append(
            send(
                src, v_recv.at[step], v_send_sem.at[step], v_recv_sem.at[step], vec_peers[step]
            )
        )

    def vec_next():
        step = len(vec_steps) - 1
        vec_steps[step].wait_recv()
        before = vec_s[x] if step == 0 else v_sum[step - 1]
        v_sum[step] = before + v_recv[step]
        if step + 1 < len(vec_peers):
            vec_send(v_sum.at[step])

    def come_back():
        for m in range(MB):
            all_bytes(back_in.at[m], back_recv.at[m], heads - 1).wait()
            row = slice(m * BLK, (m + 1) * BLK)
            for pair in range(heads // 2):
                lanes = slice(pair * 128, (pair + 1) * 128)
                one, two = back_in[m, 2 * pair], back_in[m, 2 * pair + 1]
                dq_ref[row, lanes] = jnp.concatenate([one[:BLK, :HD], two[:BLK, :HD]], axis=1)
                dk_ref[row, lanes] = jnp.concatenate([one[:BLK, HD:], two[:BLK, HD:]], axis=1)
                dv_ref[row, lanes] = jnp.concatenate(
                    [unpack_fold(one[BLK:]), unpack_fold(two[BLK:])], axis=1
                )
        half = width // 2
        for index, (name, ref) in enumerate((("dq", dq_ref), ("dk", dk_ref), ("dv", dv_ref))):
            share(
                name,
                ref.at[:, lanes_at(other * half, half)],
                m_dqkv.at[:, pl.ds(index * half, half)],
            )
        vec_s[...] = vec_ref[...]
        lanes = vec_s.shape[2]
        for index, ref in enumerate((dq_ref, dv_ref)):
            total = jnp.sum(ref[...].astype(F32), axis=0, keepdims=True)
            for side in range(2):
                vec_s[side, index : index + 1, :] = total[:, side * lanes : (side + 1) * lanes]
        vec_send(vec_s.at[1 - x])

    def grad_rows():
        total = dh_ref[...]
        for index, ref in enumerate((dq_ref, dk_ref, dv_ref)):
            pltpu.make_async_copy(weights[index], near[index], near_sem.at[index]).wait()
            total = total + lax.dot_general(
                ref[...], near[index][...], (((1,), (1,)), ((), ())), preferred_element_type=F32
            )
        rows_out[...] = total.astype(BF16)

    plans, gathers = {}, {}
    for key in KEYS:
        alone = sums[key[0]].shape[0] == 1
        first, count, sided = 0, 8, alone
        plans[key], back = [], []
        for name in ORDERS[key[0]][key[1]]:
            if name == "x":
                plans[key].append((by["x"], 1 - x, x, first, first, count))
                sided = True
                continue
            count //= 2
            out, keep = first + (1 - bits[name]) * count, first + bits[name] * count
            side = (0 if alone else x) if sided else None
            plans[key].append((by[name], side, side, out, keep, count))
            back.append((by[name], keep, out, count))
            first = keep
        gathers[key] = back[::-1]
    flights, spread, owns, state = {}, {}, {}, {}

    def piece_rows(key):
        rows = sums[key[0]].shape[2] // PIECES
        return pl.ds(key[1] * rows, rows)

    def reduce_send(key, step):
        peer, side, _, first, _, count = plans[key][step]
        dst = r_bufs[key][step]
        if side is None:
            src = sums[key[0]].at[:, pl.ds(first, count), piece_rows(key)]
        else:
            src, dst = sums[key[0]].at[side, pl.ds(first, count), piece_rows(key)], dst.at[0]
        sems = rs_send.at[key[0], key[1], step], rs_recv.at[key[0], key[1], step]
        flights[key, step] = send(src, dst, *sems, peer)
        state[key] = step

    def reduce_add(key, step):
        _, _, side, _, first, count = plans[key][step]
        flights[key, step].wait_recv()
        total, fresh, rows = sums[key[0]], r_bufs[key][step], piece_rows(key)
        sides = ((0, 0), (1, 1)) if side is None else ((side, 0),)
        for here, there in sides:

            def body(index, carry):
                spot = first + index
                total[here, spot, rows] = (
                    total[here, spot, rows].astype(F32) + fresh[there, index].astype(F32)
                ).astype(BF16)
                return carry

            lax.fori_loop(0, count, body, 0)

    def spread_send(key, kind, src, dst, peer):
        sems = ag_send.at[key[0], key[1], kind], ag_recv.at[key[0], key[1], kind]
        spread[key, kind] = send(src, dst, *sems, peer)

    def advance(key):
        step, steps = state[key], len(plans[key])
        out, rows = outs[key[0]], piece_rows(key)
        if step < steps:
            reduce_add(key, step)
            if step < steps - 1:
                reduce_send(key, step + 1)
                return
            peer, first, _, _ = gathers[key][0]
            side = x if sums[key[0]].shape[0] == 2 else 0
            src = sums[key[0]].at[side, pl.ds(first, 1), rows]
            dst = out.at[core, pl.ds(first, 1), rows]
            owns[key] = pltpu.make_async_copy(src, dst, own_sem.at[key[0], key[1]])
            owns[key].start()
            spread_send(key, 0, src, dst, peer)
            spread_send(key, 3, src, dst, by_core)
        else:
            turn = step - steps + 1
            spread[key, turn - 1].wait_recv()
            if turn == 1:
                owns[key].wait()
            if turn < 3:
                peer, first, _, count = gathers[key][turn]
                ref = out.at[core, pl.ds(first, count), rows]
                spread_send(key, turn, ref, ref, peer)
            _, _, first, count = gathers[key][turn - 1]
            ref = out.at[core, pl.ds(first, count), rows]
            spread_send(key, 3 + turn, ref, ref, by_core)
        state[key] = step + 1

    actions = {
        "up": (grads_up, 1),
        "down": (grads_down, 2),
        "qkv": (grads_qkv, 0),
        "back": (come_back, None),
        "rows": (grad_rows, None),
        "vec": (vec_next, None),
    }
    for event in SCHEDULE:
        if isinstance(event, tuple):
            advance(event)
        elif isinstance(event, int):
            attention(event)
        else:
            action, part = actions[event]
            if event == "vec" and len(vec_steps) == len(vec_peers) and "vec" in state:
                continue
            if event == "vec" and len(vec_steps) == len(vec_peers):
                state["vec"] = True
            action()
            if part is not None:
                for piece in range(PIECES):
                    reduce_send((part, piece), 0)
    vec_out[...] = v_sum[len(vec_peers) - 1]
    for m in range(MB):
        all_bytes(out_buf.at[m], send_sem.at[m], heads - 1).wait()
        all_bytes(back_out.at[m], back_send.at[m], heads - 1).wait()
    for flight in shared.values():
        flight.wait_send()
    for flight in vec_steps:
        flight.wait_send()
    for flight in flights.values():
        flight.wait_send()
    for (_, kind), flight in spread.items():
        if kind >= 3:
            flight.wait_recv()
        flight.wait_send()


def backward(lengths, dealing, da, kept, lse, x, a, n1, g, do, du, dm, vec, dh, weights, heads):
    vmem, anywhere = pl.BlockSpec(memory_space=pltpu.VMEM), pl.BlockSpec(memory_space=pl.ANY)
    rows, width = da.shape
    hidden = g.shape[1]
    pack_rows = BLK + BLK // 2
    low = lambda *dims: pltpu.VMEM(dims, BF16)
    operands = (da, g, dm, n1, du, kept, lse, a, do, x, vec, dh)
    a_shape, b_shape = (2, 8, width // 16, 2 * width), (2, 8, width // 16, hidden // 2)
    c_shape = (1, 8, hidden // 32, width)
    scratch = [pltpu.VMEM(item.shape, item.dtype) for item in operands]
    scratch += [pltpu.SemaphoreType.DMA((len(operands),))]
    scratch += dealing_scratch(lengths, dealing)
    scratch += [low(heads, BLK // 2, 128)] * MB
    scratch += [low(MB, heads, BLK // 2, 128)]
    scratch += [low(MB, heads, pack_rows, 128)] * 2
    scratch += [low(heads * BLK, HD)] * 4
    scratch += [pltpu.VMEM((heads, BLK, HD), F32)] * 3
    scratch += [low(rows, width)] * 6
    scratch += [low(rows, width // 2), low(rows, hidden // 2), low(rows, 3 * width // 2)]
    scratch += [low(rows, hidden // 4), low(rows, width)] * 3
    scratch += [low(*item.shape) for item in weights]
    scratch += [pltpu.VMEM(vec.shape, F32)] + [pltpu.VMEM((5,) + vec.shape[1:], F32)] * 2
    scratch += [low(*shape) for shape in (a_shape, b_shape, c_shape)]
    for key in KEYS:
        shape = (a_shape, b_shape, c_shape)[key[0]]
        scratch += [low(*item) for item in landing_shapes(ORDERS[key[0]][key[1]], shape)]
    sems = lambda *dims: pltpu.SemaphoreType.DMA(dims)
    scratch += [sems(MB)] * 4 + [sems(14)] * 2 + [sems(3)]
    scratch += [sems(3, PIECES, 4)] * 2 + [sems(3, PIECES, 7)] * 2 + [sems(3, PIECES)]
    scratch += [sems(5)] * 2
    return pl.pallas_call(
        functools.partial(backward_kernel, heads),
        out_shape=[
            jax.ShapeDtypeStruct((rows, width), BF16),
            jax.ShapeDtypeStruct(a_shape, BF16),
            jax.ShapeDtypeStruct(b_shape, BF16),
            jax.ShapeDtypeStruct((2,) + c_shape[1:], BF16),
            jax.ShapeDtypeStruct(vec.shape[1:], F32),
        ],
        in_specs=[anywhere] * 17,
        out_specs=[vmem] + [anywhere] * 3 + [vmem],
        scratch_shapes=scratch,
        compiler_params=pltpu.CompilerParams(
            collective_id=2, has_side_effects=True, vmem_limit_bytes=VMEM_BYTES
        ),
        name="backward",
    )(lengths, dealing, *operands, *weights)


def widen_kernel(a_ref, b_ref, c_ref, vec_ref, one_ref, two_ref, one_out, two_out, *outs):
    one_out[...] = one_ref[...]
    two_out[...] = two_ref[...]

    @pl.when(pl.program_id(0) == 0)
    def _():
        line, lanes = 0, vec_ref.shape[1]
        for out in outs[6:]:
            for first in range(0, out.shape[0], lanes):
                out[pl.ds(first, lanes)] = vec_ref[line, :]
                line += 1

    half = outs[0].shape[1] // 2
    for index, out in enumerate(outs[:4]):
        for core in range(2):
            part = a_ref[core, :, :, index * half : (index + 1) * half]
            out[:, core * half : (core + 1) * half] = part.astype(F32).reshape(-1, half)
    up, down = outs[4:6]
    half = up.shape[1] // 2
    for core in range(2):
        part = b_ref[core].astype(F32)
        up[:, core * half : (core + 1) * half] = part.reshape(-1, half)
        down[core] = c_ref[core].astype(F32)


def widen(o_a, o_b, o_c, vec, sizes, one, two):
    shards = o_a.shape[1]
    turns = 2
    share = shards // turns
    block = lambda item: pl.BlockSpec((2, share) + item.shape[2:], lambda i: (0, i, 0, 0))
    rows = o_a.shape[2] * share
    square = (turns * rows, o_a.shape[3] // 2)
    wide = (turns * rows, 2 * o_b.shape[3])
    strip = pl.BlockSpec((one.shape[0] // turns, one.shape[1]), lambda i: (i, 0))
    return pl.pallas_call(
        widen_kernel,
        grid=(turns,),
        out_shape=[jax.ShapeDtypeStruct(one.shape, one.dtype)] * 2
        + [jax.ShapeDtypeStruct(square, F32)] * 4
        + [jax.ShapeDtypeStruct(wide, F32), jax.ShapeDtypeStruct(o_c.shape, F32)]
        + [jax.ShapeDtypeStruct((size,), F32) for size in sizes],
        in_specs=[block(o_a), block(o_b), block(o_c), pl.BlockSpec(vec.shape, lambda i: (0, 0))]
        + [strip] * 2,
        out_specs=[strip] * 2
        + [pl.BlockSpec((rows, square[1]), lambda i: (i, 0))] * 4
        + [pl.BlockSpec((rows, wide[1]), lambda i: (i, 0)), block(o_c)]
        + [pl.BlockSpec((size,), lambda i: (0,)) for size in sizes],
        compiler_params=pltpu.CompilerParams(vmem_limit_bytes=VMEM_BYTES),
        name="widen",
    )(o_a, o_b, o_c, vec, one, two)


def per_device_heads(tokens, cotangent, lengths, dealing, *params):
    rows_in = tokens.shape[2]
    width = tokens.shape[3]
    rows = MB * rows_in
    weights, vectors = params[:6], params[6:]
    sizes = [item.shape[0] for item in vectors]
    x = tokens.reshape(rows, width)
    lengths, dealing = lengths.transpose(0, 2, 1), dealing.transpose(1, 0, 2)
    query_w, key_w, value_w, kept, lse, a, output, n_low, g, do, du, dm, dh_one, da, vec = forward(
        lengths, dealing, x, cotangent.reshape(rows, width), weights, vectors, HEADS
    )
    grad_tokens, o_a, o_b, o_c, vec_sum = backward(
        lengths,
        dealing,
        da,
        kept,
        lse,
        x,
        a,
        n_low,
        g,
        do,
        du,
        dm,
        vec,
        dh_one,
        (query_w, key_w, value_w),
        HEADS,
    )
    output, grad_tokens, *grads = widen(o_a, o_b, o_c, vec_sum, sizes, output, grad_tokens)
    grads[5] = grads[5].reshape(-1, width)
    shape = (1, MB, rows_in, width)
    return (
        (output.reshape(shape), grad_tokens.reshape(shape))
        + tuple(grads)
    )


def solution(mesh):
    placed = (
        P("wsh", None, "ctx", None),
        P("wsh", None, "ctx", None),
        P("wsh", None, None),
        P("wsh", None, None),
        P("wsh", None),
        P("wsh", None),
        P("wsh", None),
        P("wsh", None),
        P("wsh", None),
        P("wsh", None),
        P("wsh"),
        P("wsh"),
        P("wsh"),
        P("wsh"),
        P("wsh"),
        P("wsh"),
        P("wsh"),
        P("wsh"),
        P("wsh"),
    )
    by_heads = mesh.shape["ctx"] == HEADS and mesh.shape["wsh"] == 2
    return jax.shard_map(
        per_device_heads if by_heads else per_device,
        mesh=mesh,
        in_specs=placed,
        out_specs=(
            P("wsh", None, "ctx", None),
            P("wsh", None, "ctx", None),
            P("wsh", None),
            P("wsh", None),
            P("wsh", None),
            P("wsh", None),
            P("wsh", None),
            P("wsh", None),
            P("wsh"),
            P("wsh"),
            P("wsh"),
            P("wsh"),
            P("wsh"),
            P("wsh"),
            P("wsh"),
            P("wsh"),
            P("wsh"),
        ),
        check_vma=False,
    )
```
